32 devices in a mesh: ctx: 16 (over z, y, core), wa: 2 (over x).
Axes of the slice: x: 2, y: 2, z: 4, core: 2. Of those that a mesh axis runs over, the one named last changes fastest.
Arguments:
- query_in: bfloat16 [2, 4096, 512], P('wa', 'ctx'), may hold values from -6 to 6
- content_in: bfloat16 [2, 4096, 512], P('wa', 'ctx'), may hold values from -6 to 6
- encoder_in: bfloat16 [2, 4096, 512], P('wa', 'ctx'), may hold values from -6 to 6
- out_grad: bfloat16 [2, 4096, 512], P('wa', 'ctx'), may hold values from -6 to 6
- document_lengths: int32 [2, 4], P('wa'), may hold values from 1 to 2048, 4096 in all within a row
- key_ranks: int32 [2, 4096], P('wa'), may hold values from 0 to 15
- query_limits: int32 [2, 4096], P('wa'), may hold values from 1 to 16
- self_query_weight: bfloat16 [512, 512], P('wa'), may hold values from -0.25 to 0.25
- self_query_bias: bfloat16 [512], P('wa'), may hold values from -3 to 3
- self_key_weight: bfloat16 [512, 512], P('wa'), may hold values from -0.25 to 0.25
- self_value_weight: bfloat16 [512, 512], P('wa'), may hold values from -0.25 to 0.25
- self_value_bias: bfloat16 [512], P('wa'), may hold values from -0.29882812 to 0.29882812
- self_out_weight: bfloat16 [512, 512], P('wa'), may hold values from -3 to 3
- self_out_bias: bfloat16 [512], P('wa'), may hold values from -3 to 3
- norm_one_gain: bfloat16 [512], P('wa'), may hold values from 0.099609375 to 1.8984375
- norm_one_shift: bfloat16 [512], P('wa'), may hold values from -2 to 2
- cross_query_weight: bfloat16 [512, 512], P('wa'), may hold values from -0.25 to 0.25
- cross_query_bias: bfloat16 [512], P('wa'), may hold values from -3 to 3
- cross_key_weight: bfloat16 [512, 512], P('wa'), may hold values from -0.25 to 0.25
- cross_value_weight: bfloat16 [512, 512], P('wa'), may hold values from -0.25 to 0.25
- cross_value_bias: bfloat16 [512], P('wa'), may hold values from -0.29882812 to 0.29882812
- cross_out_weight: bfloat16 [512, 512], P('wa'), may hold values from -3 to 3
- cross_out_bias: bfloat16 [512], P('wa'), may hold values from -3 to 3
- norm_two_gain: bfloat16 [512], P('wa'), may hold values from 0.099609375 to 1.8984375
- norm_two_shift: bfloat16 [512], P('wa'), may hold values from -2 to 2
- expand_weight: bfloat16 [512, 2048], P('wa'), may hold values from -0.25 to 0.25
- expand_bias: bfloat16 [2048], P('wa'), may hold values from -2 to 2
- shrink_weight: bfloat16 [2048, 512], P('wa'), may hold values from -0.125 to 0.125
- shrink_bias: bfloat16 [512], P('wa'), may hold values from -2 to 2
- norm_three_gain: bfloat16 [512], P('wa'), may hold values from 0.099609375 to 1.8984375
- norm_three_shift: bfloat16 [512], P('wa'), may hold values from -2 to 2
Outputs:
- layer_out: float32 [2, 4096, 512], P('wa', 'ctx')
- query_grad: float32 [2, 4096, 512], P('wa', 'ctx')
- content_grad: float32 [2, 4096, 512], P('wa', 'ctx')
- encoder_grad: float32 [2, 4096, 512], P('wa', 'ctx')
- grad_self_query_weight: float32 [512, 512], P('wa')
- grad_self_query_bias: float32 [512], P('wa')
- grad_self_key_weight: float32 [512, 512], P('wa')
- grad_self_value_weight: float32 [512, 512], P('wa')
- grad_self_value_bias: float32 [512], P('wa')
- grad_self_out_weight: float32 [512, 512], P('wa')
- grad_self_out_bias: float32 [512], P('wa')
- grad_norm_one_gain: float32 [512], P('wa')
- grad_norm_one_shift: float32 [512], P('wa')
- grad_cross_query_weight: float32 [512, 512], P('wa')
- grad_cross_query_bias: float32 [512], P('wa')
- grad_cross_key_weight: float32 [512, 512], P('wa')
- grad_cross_value_weight: float32 [512, 512], P('wa')
- grad_cross_value_bias: float32 [512], P('wa')
- grad_cross_out_weight: float32 [512, 512], P('wa')
- grad_cross_out_bias: float32 [512], P('wa')
- grad_norm_two_gain: float32 [512], P('wa')
- grad_norm_two_shift: float32 [512], P('wa')
- grad_expand_weight: float32 [512, 2048], P('wa')
- grad_expand_bias: float32 [2048], P('wa')
- grad_shrink_weight: float32 [2048, 512], P('wa')
- grad_shrink_bias: float32 [512], P('wa')
- grad_norm_three_gain: float32 [512], P('wa')
- grad_norm_three_shift: float32 [512], P('wa')
The draws below stay inside these ranges and needn't reach their ends.
Inputs may be any that keep to these rules, and one draw needn't show every extreme that they name: `document_lengths`: each row gives the 4 document lengths of one packed sequence in order; they sum to 4096, and the longest is exactly 2048.
All inputs are finite; a program needn't handle non-finite values.
Results may differ from the reference program's by a relative error of at most 0.03.
Values may be sent and summed in bfloat16 or wider, within the bound.
A program may use at most 320 MiB of HBM per device.

```python
import math
import jax
import jax.numpy as jnp
import numpy as np
from jax import lax

D = 512
HEADS = 8
FF = 2048
TOK_DEV = 256
DOCLEN = 2048
RANKS = 16
HEAD_DIM = 64
PACK = 4096
NDOCS = 4
REACH = 8
N_WA = 2


def plant(array, stream_key, least, high):
    extent = array.shape
    place = [jax.random.randint(jax.random.fold_in(stream_key, axis), (), 0, extent[axis]) for axis in range(len(extent))]
    array = array.at[tuple(place)].set(least)
    longest = extent.index(max(extent))
    place[longest] = (place[longest] + 1) % extent[longest]
    return array.at[tuple(place)].set(high)


def steps_of(rng, dims, shards, smallest, top_value):
    def one(dim, blocks):
        draws = jax.random.uniform(jax.random.fold_in(jax.random.fold_in(rng, 6), dim), (blocks,), jnp.float32, smallest / len(shards), top_value / len(shards))
        return jnp.repeat(jnp.exp(draws), dims[dim] // blocks).reshape((-1,) + (1,) * (len(dims) - dim - 1))

    loudness = one(*shards[0])
    for cut in shards[1:]:
        loudness = loudness * one(*cut)
    return loudness


def profile(amount, total, limit, lean):
    portions = [(1 << 20) // math.isqrt(standing ** lean) + 1 for standing in range(2, amount + 1)]
    rest, counts = total - limit - (amount - 1), [1] * (amount - 1)
    while rest > 0:
        movable = [i for i in range(amount - 1) if counts[i] < limit]
        pool, remaining = sum([portions[i] for i in movable]), rest
        for i in movable:
            extra = min(limit - counts[i], max(1, remaining * portions[i] // pool), rest)
            counts[i] = counts[i] + extra
            rest = rest - extra
    return np.array([limit] + counts)


def uneven(rng, amount, total, limit, lean):
    if amount == 2:
        one = jax.random.randint(rng, (), max(1, total - limit), min(limit, total - 1) + 1)
        return jnp.stack([one, total - one])
    sizes = jnp.asarray(profile(amount, total, limit, lean), jnp.int32)
    twos = (amount - 1) // 2
    giver, sink = sizes[1:1 + 2 * twos:2], sizes[2:2 + 2 * twos:2]
    room = jnp.minimum(giver - 1, limit - sink)
    shifted = jax.random.randint(jax.random.fold_in(rng, 1), (twos,), 0, 1 << 20) % (room + 1)
    sizes = sizes.at[1:1 + 2 * twos:2].set(giver - shifted).at[2:2 + 2 * twos:2].set(sink + shifted)
    return sizes[jax.random.permutation(jax.random.fold_in(rng, 2), amount)]


def scatter_about(rng, dims, width, limit, cuts=(), held_as=jnp.bfloat16):
    level = steps_of(rng, dims, cuts, -0.22, 0.18) if cuts else 1.0
    values = jax.random.normal(rng, dims, jnp.float32) * width * level
    return jnp.minimum(jnp.maximum(values, -limit), limit).astype(held_as)


def setup_inputs(seed: int = 0) -> dict:
    key_list = jax.random.split(jax.random.key(seed), 32)
    query_in = scatter_about(key_list[0], (N_WA, PACK, D), 1.0, 6.0, ((0, 2), (1, 16)))
    content_in = scatter_about(key_list[1], (N_WA, PACK, D), 1.0, 6.0, ((0, 2), (1, 16)))
    encoder_in = scatter_about(key_list[2], (N_WA, PACK, D), 1.0, 6.0, ((0, 2), (1, 16)))
    out_grad = scatter_about(key_list[3], (N_WA, PACK, D), 1.0, 6.0, ((0, 2), (1, 16)))
    document_lengths = jax.vmap(lambda own: uneven(own, NDOCS, PACK, DOCLEN, 2))(jax.random.split(key_list[4], N_WA)).reshape((N_WA, NDOCS)).astype(jnp.int32)
    key_ranks = plant(jax.random.randint(key_list[5], (N_WA, PACK), 0, RANKS), jax.random.fold_in(key_list[5], 1), 0, RANKS - 1).astype(jnp.int32)
    query_limits = plant(jax.random.randint(key_list[6], (N_WA, PACK), 1, RANKS + 1), jax.random.fold_in(key_list[6], 1), 1, RANKS).astype(jnp.int32)
    self_query_weight = scatter_about(key_list[7], (D, D), D ** -0.5, 0.25, ((0, 2),))
    self_query_bias = scatter_about(key_list[8], (D,), 0.5, 3.0, ((0, 2),))
    self_key_weight = scatter_about(key_list[9], (D, D), D ** -0.5, 0.25, ((0, 2),))
    self_value_weight = scatter_about(key_list[10], (D, D), D ** -0.5, 0.25, ((0, 2),))
    self_value_bias = scatter_about(key_list[11], (D,), 0.05, 0.29882812, ((0, 2),))
    self_out_weight = scatter_about(key_list[12], (D, D), (D * 16 // DOCLEN) ** -0.5, 3.0, ((0, 2),))
    self_out_bias = scatter_about(key_list[13], (D,), 0.5, 3.0, ((0, 2),))
    norm_one_gain = jnp.clip(1.0 + 0.18 * jax.random.normal(key_list[14], (D,), jnp.float32), 0.099609375, 1.8984375).astype(jnp.bfloat16)
    norm_one_shift = scatter_about(key_list[15], (D,), 0.3, 2.0, ((0, 2),))
    cross_query_weight = scatter_about(key_list[16], (D, D), D ** -0.5, 0.25, ((0, 2),))
    cross_query_bias = scatter_about(key_list[17], (D,), 0.5, 3.0, ((0, 2),))
    cross_key_weight = scatter_about(key_list[18], (D, D), D ** -0.5, 0.25, ((0, 2),))
    cross_value_weight = scatter_about(key_list[19], (D, D), D ** -0.5, 0.25, ((0, 2),))
    cross_value_bias = scatter_about(key_list[20], (D,), 0.05, 0.29882812, ((0, 2),))
    cross_out_weight = scatter_about(key_list[21], (D, D), (D * 16 // DOCLEN) ** -0.5, 3.0, ((0, 2),))
    cross_out_bias = scatter_about(key_list[22], (D,), 0.5, 3.0, ((0, 2),))
    norm_two_gain = jnp.clip(1.0 + 0.18 * jax.random.normal(key_list[23], (D,), jnp.float32), 0.099609375, 1.8984375).astype(jnp.bfloat16)
    norm_two_shift = scatter_about(key_list[24], (D,), 0.3, 2.0, ((0, 2),))
    expand_weight = scatter_about(key_list[25], (D, FF), D ** -0.5, 0.25, ((0, 2),))
    expand_bias = scatter_about(key_list[26], (FF,), 0.3, 2.0, ((0, 2),))
    shrink_weight = scatter_about(key_list[27], (FF, D), FF ** -0.5, 0.125, ((0, 2),))
    shrink_bias = scatter_about(key_list[28], (D,), 0.3, 2.0, ((0, 2),))
    norm_three_gain = jnp.clip(1.0 + 0.18 * jax.random.normal(key_list[29], (D,), jnp.float32), 0.099609375, 1.8984375).astype(jnp.bfloat16)
    norm_three_shift = scatter_about(key_list[30], (D,), 0.3, 2.0, ((0, 2),))
    return {"query_in": query_in, "content_in": content_in, "encoder_in": encoder_in, "out_grad": out_grad, "document_lengths": document_lengths, "key_ranks": key_ranks, "query_limits": query_limits, "self_query_weight": self_query_weight, "self_query_bias": self_query_bias, "self_key_weight": self_key_weight, "self_value_weight": self_value_weight, "self_value_bias": self_value_bias, "self_out_weight": self_out_weight, "self_out_bias": self_out_bias, "norm_one_gain": norm_one_gain, "norm_one_shift": norm_one_shift, "cross_query_weight": cross_query_weight, "cross_query_bias": cross_query_bias, "cross_key_weight": cross_key_weight, "cross_value_weight": cross_value_weight, "cross_value_bias": cross_value_bias, "cross_out_weight": cross_out_weight, "cross_out_bias": cross_out_bias, "norm_two_gain": norm_two_gain, "norm_two_shift": norm_two_shift, "expand_weight": expand_weight, "expand_bias": expand_bias, "shrink_weight": shrink_weight, "shrink_bias": shrink_bias, "norm_three_gain": norm_three_gain, "norm_three_shift": norm_three_shift}


@jax.custom_vjp
def low(v):
    return lax.optimization_barrier(v.astype(jnp.bfloat16)).astype(jnp.float32)

@jax.custom_vjp
def low_back(v):
    return v

def low_keep(v):
    return (low(v), None)

def low_pass(kept, grad):
    return (grad,)

def back_keep(v):
    return (v, None)

def back_low(kept, grad):
    return (low(grad),)
low.defvjp(low_keep, low_pass)
low_back.defvjp(back_keep, back_low)
TOP_PRECISION = lax.Precision.HIGHEST
EPSILON = 1e-05
NEGATIVE = -1e+30

def rounded_pair(value):
    return low(low_back(value))

def layer_norm(value, gain_row, shift_row):
    middle = lax.optimization_barrier(jnp.mean(value, axis=-1, keepdims=True))
    centred = value - middle
    spread = lax.optimization_barrier(jnp.mean(centred * centred, axis=-1, keepdims=True))
    return centred * lax.rsqrt(spread + EPSILON) * gain_row + shift_row

def project(layer_inputs, weight_matrix, bias_vector_row):
    return jnp.einsum('fzu,ug->fzg', layer_inputs, weight_matrix, precision=TOP_PRECISION) + bias_vector_row

def layout(lengths):
    endings = jnp.cumsum(lengths).astype(jnp.int32)
    places = jnp.arange(PACK, dtype=jnp.int32)
    passed = endings[None, :] <= places[:, None]
    document = lax.optimization_barrier(jnp.sum(passed.astype(jnp.int32), axis=1)).astype(jnp.int32)
    opening = lax.optimization_barrier(jnp.sum(jnp.where(passed, lengths[None, :], 0), axis=1)).astype(jnp.int32)
    return (document, opening)

def attend_pack(queries, keys, values, document, opening, ranking, limits, with_ranks):
    margin = REACH * TOK_DEV
    window = (2 * REACH + 1) * TOK_DEV
    query_heads = queries.reshape(PACK, HEADS, HEAD_DIM)
    keys_padded = jnp.pad(keys.reshape(PACK, HEADS, HEAD_DIM), ((margin, margin), (0, 0), (0, 0)))
    values_padded = jnp.pad(values.reshape(PACK, HEADS, HEAD_DIM), ((margin, margin), (0, 0), (0, 0)))
    document_padded = jnp.pad(document, (margin, margin), constant_values=-1)
    ranking_padded = jnp.pad(ranking, (margin, margin))
    scaling = HEAD_DIM ** (-0.5)

    def one_block(block_index):
        begin = (block_index * TOK_DEV).astype(jnp.int32)
        query_block = lax.dynamic_slice_in_dim(query_heads, begin, TOK_DEV, 0)
        key_block = lax.dynamic_slice_in_dim(keys_padded, begin, window, 0)
        value_block = lax.dynamic_slice_in_dim(values_padded, begin, window, 0)
        key_document = lax.dynamic_slice_in_dim(document_padded, begin, window, 0)
        key_ranking = lax.dynamic_slice_in_dim(ranking_padded, begin, window, 0)
        query_document = lax.dynamic_slice_in_dim(document, begin, TOK_DEV, 0)
        query_opening = lax.dynamic_slice_in_dim(opening, begin, TOK_DEV, 0)
        query_limit = lax.dynamic_slice_in_dim(limits, begin, TOK_DEV, 0)
        query_places = begin + jnp.arange(TOK_DEV, dtype=jnp.int32)
        key_places = begin - margin + jnp.arange(window, dtype=jnp.int32)
        allowed = query_document[:, None] == key_document[None, :]
        if with_ranks:
            observed = jnp.logical_and(key_ranking[None, :] < query_limit[:, None], key_places[None, :] != query_places[:, None])
            allowed = jnp.logical_and(allowed, jnp.logical_or(observed, key_places[None, :] == query_opening[:, None]))
        scores = low_back(jnp.einsum('qhd,khd->hqk', query_block, key_block, precision=TOP_PRECISION) * scaling)
        scores = jnp.where(allowed[None], scores, NEGATIVE)
        row_max = lax.optimization_barrier(jnp.max(scores, axis=-1, keepdims=True))
        weights = jnp.where(allowed[None], jnp.exp(scores - row_max), 0.0)
        shares = low(weights / lax.optimization_barrier(jnp.sum(weights, axis=-1, keepdims=True)))
        return jnp.einsum('hqk,khd->qhd', shares, value_block, precision=TOP_PRECISION)
    blocks = lax.map(jax.checkpoint(one_block), jnp.arange(PACK // TOK_DEV, dtype=jnp.int32))
    return blocks.reshape(PACK, HEADS * HEAD_DIM)

def reference(query_in, content_in, encoder_in, out_grad, document_lengths, key_ranks, query_limits, self_query_weight, self_query_bias, self_key_weight, self_value_weight, self_value_bias, self_out_weight, self_out_bias, norm_one_gain, norm_one_shift, cross_query_weight, cross_query_bias, cross_key_weight, cross_value_weight, cross_value_bias, cross_out_weight, cross_out_bias, norm_two_gain, norm_two_shift, expand_weight, expand_bias, shrink_weight, shrink_bias, norm_three_gain, norm_three_shift):
    params = tuple((member.astype(jnp.float32) for member in (self_query_weight, self_query_bias, self_key_weight, self_value_weight, self_value_bias, self_out_weight, self_out_bias, norm_one_gain, norm_one_shift, cross_query_weight, cross_query_bias, cross_key_weight, cross_value_weight, cross_value_bias, cross_out_weight, cross_out_bias, norm_two_gain, norm_two_shift, expand_weight, expand_bias, shrink_weight, shrink_bias, norm_three_gain, norm_three_shift)))
    layer_inputs = (query_in.astype(jnp.float32), content_in.astype(jnp.float32), encoder_in.astype(jnp.float32))
    document, opening = jax.vmap(layout)(document_lengths)

    def self_pack(queries, keys, values, doc_row, open_row, rank_row, limit_row):
        return attend_pack(queries, keys, values, doc_row, open_row, rank_row, limit_row, True)

    def cross_pack(queries, keys, values, doc_row, open_row, rank_row, limit_row):
        return attend_pack(queries, keys, values, doc_row, open_row, rank_row, limit_row, False)

    def forward(weights_all, inputs_all):
        self_query_mat, self_query_vec, self_key_matrix, self_value_mat, self_value_vec, self_out_mat, self_out_vec, gain_one, shift_one, cross_query_mat, cross_query_vec, cross_key_matrix, cross_value_mat, cross_value_vec, cross_out_mat, cross_out_vec, gain_two, shift_two, expand_mat, expand_vec, shrink_mat, shrink_vec, gain_three, shift_three = weights_all
        source, content_states, encoder_output = inputs_all
        query_one = rounded_pair(project(source, self_query_mat, self_query_vec))
        first_key = rounded_pair(jnp.einsum('fzu,ug->fzg', content_states, self_key_matrix, precision=TOP_PRECISION))
        value_one = rounded_pair(project(content_states, self_value_mat, self_value_vec))
        mixed_one = rounded_pair(jax.vmap(self_pack)(query_one, first_key, value_one, document, opening, key_ranks, query_limits))
        branch_one = low_back(project(mixed_one, self_out_mat, self_out_vec))
        hidden_one = layer_norm(source + branch_one, gain_one, shift_one)
        query_two = rounded_pair(project(low(hidden_one), cross_query_mat, cross_query_vec))
        second_key = rounded_pair(jnp.einsum('fzu,ug->fzg', encoder_output, cross_key_matrix, precision=TOP_PRECISION))
        value_two = rounded_pair(project(encoder_output, cross_value_mat, cross_value_vec))
        mixed_two = rounded_pair(jax.vmap(cross_pack)(query_two, second_key, value_two, document, opening, key_ranks, query_limits))
        branch_two = low_back(project(mixed_two, cross_out_mat, cross_out_vec))
        hidden_two = layer_norm(hidden_one + branch_two, gain_two, shift_two)
        expanded = low_back(project(low(hidden_two), expand_mat, expand_vec))
        activated = low(jax.nn.gelu(expanded, approximate=False))
        branch_three = low_back(project(activated, shrink_mat, shrink_vec))
        return layer_norm(hidden_two + branch_three, gain_three, shift_three)
    layer_out, pullback = jax.vjp(forward, params, layer_inputs)
    param_grads, input_grads = pullback(out_grad.astype(jnp.float32))
    grad_a, grad_b, grad_c, grad_d, grad_e, grad_f, grad_g, grad_h, grad_i, grad_j, grad_k, grad_l, grad_m, grad_n, grad_o, grad_p, grad_q, grad_r, grad_s, grad_t, grad_u, grad_v, grad_w, grad_x = param_grads
    return (layer_out, input_grads[0], input_grads[1], input_grads[2], grad_a, grad_b, grad_c, grad_d, grad_e, grad_f, grad_g, grad_h, grad_i, grad_j, grad_k, grad_l, grad_m, grad_n, grad_o, grad_p, grad_q, grad_r, grad_s, grad_t, grad_u, grad_v, grad_w, grad_x)
```

```python
import functools
import jax
import jax.numpy as jnp
from jax import lax
from jax.experimental import pallas as pl
from jax.experimental.pallas import tpu as pltpu
from jax.sharding import Mesh
from jax.sharding import PartitionSpec as P

PLANE = 4
EPSILON = 1e-05
ROOT_HALF = 0.7071067811865476
INV_ROOT_TWO_PI = 0.3989422804014327

NEGATIVE = -1e29
HIDE = -(2.0 ** 100)
BLOCK = 256
WIDE = 512
STAT = 40


def dot(a, b, ca, cb):
    return lax.dot_general(a, b, (((ca,), (cb,)), ((), ())), preferred_element_type=jnp.float32)


def left_half(shape):
    return lax.broadcasted_iota(jnp.int32, shape, 1) < 64


def spans(lens_ref, first, count):
    low, high, total = 0, 0, 0
    for d in range(lens_ref.shape[1]):
        begin = total
        total = total + lens_ref[0, d]
        low = jnp.where(begin <= first, begin, low)
        high = jnp.where(begin <= first + count - 1, total, high)
    return low, high


def openings(lens_ref, places):
    total, found = 0, places == 0
    for d in range(lens_ref.shape[1] - 1):
        total = total + lens_ref[0, d]
        found = jnp.logical_or(found, places == total)
    return found


def over_blocks(low, high, first, size, step, carry, ranked):
    begin, end = low // size, (high + size - 1) // size
    own = first // size
    skip = 1 if ranked else 0

    def body(index, carry):
        if ranked:
            index = index + jnp.where(index >= own, 1, 0)
        return step(pl.multiple_of(index * size, size), carry)

    carry = lax.fori_loop(begin, end - skip, body, carry)
    if ranked:
        carry = step(pl.multiple_of(own * size, size), carry, True)
    return carry


def forward_kernel(ranked, lens_ref, own_ref, q_ref, qm_ref, k_ref, v_ref, km_ref, o_ref, lse_ref):
    rows = q_ref.shape[0]
    base = own_ref[0] * rows
    half = left_half((BLOCK, 128))
    khalf = left_half((WIDE, 128))
    one = jnp.ones((WIDE, 128), jnp.bfloat16)

    def one_block(block, _):
        start = pl.multiple_of(block * BLOCK, BLOCK)
        first = base + start
        low, high = spans(lens_ref, first, BLOCK)
        q = q_ref[pl.ds(start, BLOCK), :]
        qm = qm_ref[pl.ds(start, BLOCK), :]
        queries = (jnp.where(half, q, qm), jnp.where(half, qm, q))

        def step(at, carry, diagonal=False):
            k = k_ref[pl.ds(at, WIDE), :]
            v = v_ref[pl.ds(at, WIDE), :]
            km = km_ref[pl.ds(at, WIDE), :]
            keys = (jnp.where(khalf, k, km), jnp.where(khalf, km, k))
            values = (jnp.where(khalf, v, one), jnp.where(khalf, one, v))
            scores = [dot(queries[h], keys[h], 1, 1) for h in (0, 1)]
            if diagonal:
                place = first + lax.broadcasted_iota(jnp.int32, (BLOCK, WIDE), 0)
                other = at + lax.broadcasted_iota(jnp.int32, (BLOCK, WIDE), 1)
                column = first + lax.broadcasted_iota(jnp.int32, (BLOCK, 1), 0)
                banned = jnp.where(openings(lens_ref, column), -1, place) == other
                scores = [jnp.where(banned, HIDE, s) for s in scores]
            out = []
            for h in (0, 1):
                peak, acc = carry[h]
                new = jnp.maximum(peak, jnp.max(scores[h], axis=1, keepdims=True))
                p = jnp.exp(scores[h] - new).astype(jnp.bfloat16)
                acc = acc * jnp.exp(peak - new) + dot(p, values[h], 1, 0)
                out.append((new, acc))
            return tuple(out)

        empty = (jnp.full((BLOCK, 1), NEGATIVE, jnp.float32), jnp.zeros((BLOCK, 128), jnp.float32))
        (peak0, acc0), (peak1, acc1) = over_blocks(low, high, first, WIDE, step, (empty, empty), ranked)
        total = jnp.where(half, acc1, acc0)
        mixed = jnp.where(half, acc0, acc1)
        o_ref[pl.ds(start, BLOCK), :] = mixed / pltpu.roll(total, 64, 1)
        lse_ref[pl.ds(start, BLOCK), :] = jnp.where(half, peak1, peak0) + jnp.log(total)
        return 0

    lax.fori_loop(0, rows // BLOCK, one_block, 0)


def attend_forward(ranked, lens, own, q, qm, k, v, km):
    rows = q.shape[0]
    whole = pl.BlockSpec(memory_space=pltpu.VMEM)
    smem = pl.BlockSpec(memory_space=pltpu.SMEM)
    return pl.pallas_call(
        functools.partial(forward_kernel, ranked),
        out_shape=(jax.ShapeDtypeStruct((rows, 128), jnp.float32),) * 2,
        in_specs=[smem, smem] + [whole] * 5,
        out_specs=(whole, whole),
        compiler_params=pltpu.CompilerParams(vmem_limit_bytes=56 << 20),
    )(lens, own, q, qm, k, v, km)


def with_stat(marks, stat, lane, at):
    high = stat.astype(jnp.bfloat16)
    rest = stat - high.astype(jnp.float32)
    middle = rest.astype(jnp.bfloat16)
    tail = (rest - middle.astype(jnp.float32)).astype(jnp.bfloat16)
    side = jnp.where(lane == at, high, jnp.where(lane == at + 1, middle, jnp.where(lane == at + 2, tail, marks)))
    return side


def backward_kernel(ranked, lens_ref, own_ref, q_ref, qm_ref, k_ref, v_ref, km_ref, o_ref, lse_ref, do_ref,
                    dq_ref, dk_ref, dv_ref):
    rows = q_ref.shape[0]
    base = own_ref[0] * rows
    half = left_half((BLOCK, 128))
    lane = lax.broadcasted_iota(jnp.int32, (BLOCK, 128), 1)
    one = jnp.ones((BLOCK, 128), jnp.bfloat16)
    zero = jnp.zeros((BLOCK, 128), jnp.bfloat16)

    def clear(index, _):
        at = pl.multiple_of(index * BLOCK, BLOCK)
        dk_ref[pl.ds(at, BLOCK), :] = jnp.zeros((BLOCK, 128), jnp.float32)
        dv_ref[pl.ds(at, BLOCK), :] = jnp.zeros((BLOCK, 128), jnp.float32)
        return 0

    lax.fori_loop(0, k_ref.shape[0] // BLOCK, clear, 0)

    def one_block(block, _):
        start = pl.multiple_of(block * BLOCK, BLOCK)
        first = base + start
        low, high = spans(lens_ref, first, BLOCK)
        here = pl.ds(start, BLOCK)
        q, qm, do, lse = q_ref[here, :], qm_ref[here, :], do_ref[here, :], lse_ref[here, :]
        shared = do.astype(jnp.float32) * o_ref[here, :]
        delta0 = jnp.sum(jnp.where(half, shared, 0.0), axis=1, keepdims=True)
        delta1 = jnp.sum(jnp.where(half, 0.0, shared), axis=1, keepdims=True)
        side = with_stat(qm, lse, lane % 64, STAT)
        queries = (jnp.where(half, q, side), jnp.where(half, side, q))
        side = with_stat(zero, -jnp.where(half, delta1, delta0), lane % 64, STAT)
        grads = (jnp.where(half, do, side), jnp.where(half, side, do))

        def step(at, carry, diagonal=False):
            there = pl.ds(at, BLOCK)
            k, v, km = k_ref[there, :], v_ref[there, :], km_ref[there, :]
            keys = (jnp.where(half, k, km), jnp.where(half, km, k))
            values = (jnp.where(half, v, one), jnp.where(half, one, v))
            scores = [dot(keys[h], queries[h], 1, 1) for h in (0, 1)]
            if diagonal:
                other = first + lax.broadcasted_iota(jnp.int32, (BLOCK, BLOCK), 0)
                row = first + lax.broadcasted_iota(jnp.int32, (1, BLOCK), 1)
                banned = other == jnp.where(openings(lens_ref, row), -1, row)
                scores = [jnp.where(banned, HIDE, s) for s in scores]
            dvs, dks, dqs = [], [], []
            for h in (0, 1):
                p = jnp.exp(scores[h])
                dp = dot(values[h], grads[h], 1, 1)
                ds = (p * dp).astype(jnp.bfloat16)
                dvs.append(dot(p.astype(jnp.bfloat16), do, 1, 0))
                dks.append(dot(ds, q, 1, 0))
                dqs.append(dot(ds, k, 0, 0))
            dv_ref[there, :] += jnp.where(half, dvs[0], dvs[1])
            dk_ref[there, :] += jnp.where(half, dks[0], dks[1])
            return carry + jnp.where(half, dqs[0], dqs[1])

        dq = over_blocks(low, high, first, BLOCK, step, jnp.zeros((BLOCK, 128), jnp.float32), ranked)
        dq_ref[here, :] = (dq * 0.125).astype(dq_ref.dtype)
        return 0

    lax.fori_loop(0, rows // BLOCK, one_block, 0)


def attend_backward(ranked, lens, own, q, qm, k, v, km, o, lse, do):
    rows, keys = q.shape[0], k.shape[0]
    whole = pl.BlockSpec(memory_space=pltpu.VMEM)
    smem = pl.BlockSpec(memory_space=pltpu.SMEM)
    return pl.pallas_call(
        functools.partial(backward_kernel, ranked),
        out_shape=(jax.ShapeDtypeStruct((rows, 128), jnp.bfloat16),) + (jax.ShapeDtypeStruct((keys, 128), jnp.float32),) * 2,
        in_specs=[smem, smem] + [whole] * 8,
        out_specs=(whole, whole, whole),
        compiler_params=pltpu.CompilerParams(vmem_limit_bytes=56 << 20),
    )(lens, own, q, qm, k, v, km, o, lse, do)


def mark_tables(lengths, ranks, limits, offset, rows, ranked):
    total = ranks.shape[0]
    docs = lengths.shape[0]
    ends = jnp.stack([jnp.sum(lengths[: d + 1]) for d in range(docs)])
    begins = jnp.stack([jnp.sum(lengths[:d]) for d in range(docs)])
    place = lax.broadcasted_iota(jnp.int32, (total, 64), 0)
    lane = lax.broadcasted_iota(jnp.int32, (total, 64), 1)
    doc = jnp.zeros((total, 1), jnp.int32)
    is_open = jnp.zeros((total, 1), bool)
    for d in range(docs):
        doc = doc + (place[:, :1] >= ends[d]).astype(jnp.int32)
        is_open = jnp.logical_or(is_open, place[:, :1] == begins[d])
    rank = jnp.where(is_open, 0, ranks[:, None] + 1)
    key_marks = jnp.where(lane == doc, 1.0, 0.0)
    if ranked:
        key_marks = key_marks + jnp.where(lane == rank + 16, 1.0, 0.0)
    key_marks = key_marks - jnp.where(jnp.logical_and(lane >= STAT, lane < STAT + 3), 1.0, 0.0)
    hide = jnp.where(jnp.logical_and(lane < docs, lane != doc), HIDE, 0.0)
    if ranked:
        hide = hide + jnp.where(jnp.logical_and(lane >= 16, jnp.logical_and(lane < 33, lane - 17 >= limits[:, None])), HIDE, 0.0)
    query_marks = lax.dynamic_slice_in_dim(hide, offset, rows, 0)
    both = lambda m: jnp.concatenate([m, m], axis=1).astype(jnp.bfloat16)
    return both(key_marks), both(query_marks)


def matmul(left, right):
    return jnp.dot(left, right, preferred_element_type=jnp.float32)


def left_product(left, right):
    return jnp.einsum("ta,tb->ab", left, right, preferred_element_type=jnp.float32)


def right_product(left, right):
    return jnp.einsum("ta,ba->tb", left, right, preferred_element_type=jnp.float32)


def column_sum(value):
    return jnp.sum(value.astype(jnp.float32), axis=0)


def gelu_slope(value):
    cumulative = 0.5 * (1.0 + lax.erf(value * ROOT_HALF))
    return cumulative + value * jnp.exp(-0.5 * value * value) * INV_ROOT_TWO_PI


def norm_forward(value, gain_row, shift_row):
    middle = jnp.mean(value, axis=-1, keepdims=True)
    centred = value - middle
    spread = jnp.mean(centred * centred, axis=-1, keepdims=True)
    inverse = lax.rsqrt(spread + EPSILON)
    normed = centred * inverse
    return (normed * gain_row + shift_row, normed, inverse)


def norm_backward(incoming, normed, inverse, gain_row):
    scaled = incoming * gain_row
    centred = (
        scaled
        - jnp.mean(scaled, axis=-1, keepdims=True)
        - normed * jnp.mean(scaled * normed, axis=-1, keepdims=True)
    )
    return (inverse * centred, jnp.sum(incoming * normed, axis=0), jnp.sum(incoming, axis=0))


def gather_weights(mats, vecs):
    wa = lax.axis_size("wa")
    pack = jnp.concatenate([m.reshape(-1, 512) for m in mats])
    full = lax.all_gather(pack, "wa", axis=0)
    out, at = [], 0
    for m in mats:
        n = m.size // 512
        out.append(full[:, at : at + n].reshape((wa * m.shape[0],) + m.shape[1:]))
        at += n
    line = lax.all_gather(jnp.concatenate(vecs), "wa", axis=0)
    small, at = [], 0
    for v in vecs:
        small.append(line[:, at : at + v.shape[0]].reshape(-1).astype(jnp.float32))
        at += v.shape[0]
    return out, small


def to_pairs(value):
    return lax.all_to_all(value, "pln", 1, 0, tiled=True)


def to_tokens(value):
    return lax.all_to_all(value, "pln", 0, 1, tiled=True)


def gather_pairs(keys, values):
    both = jnp.concatenate([to_pairs(keys), to_pairs(values)], axis=1)
    full = lax.all_gather(both, "grp", axis=0, tiled=True)
    return full[:, :128], full[:, 128:]


def return_pairs(keys, values):
    both = jnp.concatenate([keys, values], axis=1).astype(jnp.bfloat16)
    mine = lax.psum_scatter(both, "grp", scatter_dimension=0, tiled=True).astype(jnp.bfloat16)
    return to_tokens(mine[:, :128]), to_tokens(mine[:, 128:])


def reduce_grads(grads):
    wa = lax.axis_size("wa")
    mats = [g.astype(jnp.bfloat16).reshape(wa, -1, 512) for g in grads if g.ndim == 2]
    vecs = [g.reshape(wa, -1) for g in grads if g.ndim == 1]
    pack = jnp.concatenate(mats, axis=1)
    mine = lax.psum_scatter(pack, "wa", scatter_dimension=0, tiled=False)
    total = lax.psum(mine, ("grp", "pln")).astype(jnp.float32)
    line = lax.psum(jnp.concatenate(vecs, axis=1).astype(jnp.bfloat16), ("grp", "pln", "wa")).astype(jnp.float32)
    line = lax.dynamic_index_in_dim(line, lax.axis_index("wa"), 0, False)
    out, at, vat = [], 0, 0
    for g in grads:
        if g.ndim == 2:
            n = g.size // wa // 512
            out.append(total[at : at + n].reshape(g.shape[0] // wa, g.shape[1]))
            at += n
        else:
            n = g.size // wa
            out.append(line[vat : vat + n])
            vat += n
    return tuple(out)


def shards(
    query_in,
    content_in,
    encoder_in,
    out_grad,
    document_lengths,
    key_ranks,
    query_limits,
    self_query_weight,
    self_query_bias,
    self_key_weight,
    self_value_weight,
    self_value_bias,
    self_out_weight,
    self_out_bias,
    norm_one_gain,
    norm_one_shift,
    cross_query_weight,
    cross_query_bias,
    cross_key_weight,
    cross_value_weight,
    cross_value_bias,
    cross_out_weight,
    cross_out_bias,
    norm_two_gain,
    norm_two_shift,
    expand_weight,
    expand_bias,
    shrink_weight,
    shrink_bias,
    norm_three_gain,
    norm_three_shift,
):
    grp_count = lax.axis_size("grp")
    own = lax.axis_index("grp")[None].astype(jnp.int32)
    lens = document_lengths
    tok = query_in.shape[1]
    rows = tok * PLANE
    row_at = lax.axis_index("grp") * rows
    cross_keys, cross_marks = mark_tables(lens[0], key_ranks[0], query_limits[0], row_at, rows, False)
    self_keys, self_marks = mark_tables(lens[0], key_ranks[0], query_limits[0], row_at, rows, True)
    mats, vecs = gather_weights((self_query_weight, self_key_weight, self_value_weight, self_out_weight, cross_query_weight,
        cross_key_weight, cross_value_weight, cross_out_weight, expand_weight, shrink_weight),
        (self_query_bias, self_value_bias, self_out_bias, norm_one_gain, norm_one_shift, cross_query_bias, cross_value_bias,
        cross_out_bias, norm_two_gain, norm_two_shift, expand_bias, shrink_bias, norm_three_gain, norm_three_shift))
    (self_query_mat, self_key_matrix, self_value_mat, self_out_mat, cross_query_mat, cross_key_matrix, cross_value_mat,
        cross_out_mat, expand_mat, shrink_mat) = mats
    (self_query_vec, self_value_vec, self_out_vec, gain_one, shift_one, cross_query_vec, cross_value_vec, cross_out_vec,
        gain_two, shift_two, expand_vec, shrink_vec, gain_three, shift_three) = vecs
    source = query_in[0]
    content_states = content_in[0]
    encoder_output = encoder_in[0]
    cotangent = out_grad[0].astype(jnp.float32)
    query_one = (matmul(source, self_query_mat) + self_query_vec).astype(jnp.bfloat16)
    first_key = matmul(content_states, self_key_matrix).astype(jnp.bfloat16)
    value_one = (matmul(content_states, self_value_mat) + self_value_vec).astype(jnp.bfloat16)
    second_key = matmul(encoder_output, cross_key_matrix).astype(jnp.bfloat16)
    value_two = (matmul(encoder_output, cross_value_mat) + cross_value_vec).astype(jnp.bfloat16)
    keys_one, values_one = gather_pairs(first_key, value_one)
    keys_two, values_two = gather_pairs(second_key, value_two)
    pair_one = to_pairs(query_one * jnp.bfloat16(0.125))
    attended_one, total_one = attend_forward(True, lens, own, pair_one, self_marks, keys_one, values_one, self_keys)
    mixed_one = to_tokens(attended_one.astype(jnp.bfloat16))
    hidden_one, normed_one, inverse_one = norm_forward(
        source.astype(jnp.float32) + matmul(mixed_one, self_out_mat) + self_out_vec, gain_one, shift_one)
    hidden_one_low = hidden_one.astype(jnp.bfloat16)
    query_two = (matmul(hidden_one_low, cross_query_mat) + cross_query_vec).astype(jnp.bfloat16)
    pair_two = to_pairs(query_two * jnp.bfloat16(0.125))
    attended_two, total_two = attend_forward(False, lens, own, pair_two, cross_marks, keys_two, values_two, cross_keys)
    mixed_two = to_tokens(attended_two.astype(jnp.bfloat16))
    hidden_two, normed_two, inverse_two = norm_forward(
        hidden_one + matmul(mixed_two, cross_out_mat) + cross_out_vec, gain_two, shift_two)
    hidden_two_low = hidden_two.astype(jnp.bfloat16)
    expanded = matmul(hidden_two_low, expand_mat) + expand_vec
    activated = jax.nn.gelu(expanded, approximate=False).astype(jnp.bfloat16)
    layer_out, normed_three, inverse_three = norm_forward(
        hidden_two + matmul(activated, shrink_mat) + shrink_vec, gain_three, shift_three)
    back_three, grad_gain_three, grad_shift_three = norm_backward(cotangent, normed_three, inverse_three, gain_three)
    shrink_in_grad = back_three.astype(jnp.bfloat16)
    grad_shrink_mat = left_product(activated, shrink_in_grad)
    grad_shrink_vec = column_sum(shrink_in_grad)
    activated_grad = right_product(shrink_in_grad, shrink_mat)
    expand_grad = (activated_grad * gelu_slope(expanded)).astype(jnp.bfloat16)
    grad_expand_mat = left_product(hidden_two_low, expand_grad)
    grad_expand_vec = column_sum(expand_grad)
    hidden_two_grad = back_three + right_product(expand_grad, expand_mat)
    back_two, grad_gain_two, grad_shift_two = norm_backward(hidden_two_grad, normed_two, inverse_two, gain_two)
    branch_two = back_two.astype(jnp.bfloat16)
    grad_cross_out_mat = left_product(mixed_two, branch_two)
    grad_cross_out_vec = column_sum(branch_two)
    mixed_two_grad = right_product(branch_two, cross_out_mat).astype(jnp.bfloat16)
    dq_two, dk_two, dv_two = attend_backward(False, lens, own, pair_two, cross_marks, keys_two, values_two, cross_keys,
        attended_two, total_two, to_pairs(mixed_two_grad))
    key_two_low, value_two_low = return_pairs(dk_two, dv_two)
    query_two_low = to_tokens(dq_two)
    grad_cross_query_mat = left_product(hidden_one_low, query_two_low)
    grad_cross_query_vec = column_sum(query_two_low)
    grad_cross_key_mat = left_product(encoder_output, key_two_low)
    grad_cross_value_mat = left_product(encoder_output, value_two_low)
    grad_cross_value_vec = column_sum(value_two_low)
    encoder_grad = right_product(key_two_low, cross_key_matrix) + right_product(value_two_low, cross_value_mat)
    hidden_one_grad = back_two + right_product(query_two_low, cross_query_mat)
    back_one, grad_gain_one, grad_shift_one = norm_backward(hidden_one_grad, normed_one, inverse_one, gain_one)
    branch_one = back_one.astype(jnp.bfloat16)
    grad_self_out_mat = left_product(mixed_one, branch_one)
    grad_self_out_vec = column_sum(branch_one)
    mixed_one_grad = right_product(branch_one, self_out_mat).astype(jnp.bfloat16)
    dq_one, dk_one, dv_one = attend_backward(True, lens, own, pair_one, self_marks, keys_one, values_one, self_keys,
        attended_one, total_one, to_pairs(mixed_one_grad))
    key_one_low, value_one_low = return_pairs(dk_one, dv_one)
    query_one_low = to_tokens(dq_one)
    grad_self_query_mat = left_product(source, query_one_low)
    grad_self_query_vec = column_sum(query_one_low)
    grad_self_key_mat = left_product(content_states, key_one_low)
    grad_self_value_mat = left_product(content_states, value_one_low)
    grad_self_value_vec = column_sum(value_one_low)
    query_grad = back_one + right_product(query_one_low, self_query_mat)
    content_grad = right_product(key_one_low, self_key_matrix) + right_product(value_one_low, self_value_mat)
    grads = reduce_grads((
        grad_self_query_mat, grad_self_query_vec, grad_self_key_mat, grad_self_value_mat, grad_self_value_vec, grad_self_out_mat, grad_self_out_vec, grad_gain_one, grad_shift_one, grad_cross_query_mat, grad_cross_query_vec, grad_cross_key_mat, grad_cross_value_mat, grad_cross_value_vec, grad_cross_out_mat, grad_cross_out_vec, grad_gain_two, grad_shift_two, grad_expand_mat, grad_expand_vec, grad_shrink_mat, grad_shrink_vec, grad_gain_three, grad_shift_three))
    return (layer_out[None], query_grad[None], content_grad[None], encoder_grad[None]) + grads


def solution(mesh):
    ctx, wa = mesh.devices.shape
    mesh = Mesh(mesh.devices.reshape(ctx // PLANE, PLANE, wa), ("grp", "pln", "wa"))
    in_specs = (
        P("wa", ("grp", "pln"), None),
        P("wa", ("grp", "pln"), None),
        P("wa", ("grp", "pln"), None),
        P("wa", ("grp", "pln"), None),
        P("wa", None),
        P("wa", None),
        P("wa", None),
        P("wa", None),
        P("wa"),
        P("wa", None),
        P("wa", None),
        P("wa"),
        P("wa", None),
        P("wa"),
        P("wa"),
        P("wa"),
        P("wa", None),
        P("wa"),
        P("wa", None),
        P("wa", None),
        P("wa"),
        P("wa", None),
        P("wa"),
        P("wa"),
        P("wa"),
        P("wa", None),
        P("wa"),
        P("wa", None),
        P("wa"),
        P("wa"),
        P("wa"),
    )
    out_specs = (
        P("wa", ("grp", "pln"), None),
        P("wa", ("grp", "pln"), None),
        P("wa", ("grp", "pln"), None),
        P("wa", ("grp", "pln"), None),
        P("wa", None),
        P("wa"),
        P("wa", None),
        P("wa", None),
        P("wa"),
        P("wa", None),
        P("wa"),
        P("wa"),
        P("wa"),
        P("wa", None),
        P("wa"),
        P("wa", None),
        P("wa", None),
        P("wa"),
        P("wa", None),
        P("wa"),
        P("wa"),
        P("wa"),
        P("wa", None),
        P("wa"),
        P("wa", None),
        P("wa"),
        P("wa"),
        P("wa"),
    )
    return jax.shard_map(shards, mesh=mesh, in_specs=in_specs, out_specs=out_specs, check_vma=False)
```

```python
import functools
import jax
import jax.numpy as jnp
from jax import lax
from jax.experimental import pallas as pl
from jax.experimental.pallas import tpu as pltpu
from jax.sharding import Mesh
from jax.sharding import PartitionSpec as P

PLANE = 4
DOCLEN = 2048
EPSILON = 1e-05
ROOT_HALF = 0.7071067811865476
INV_ROOT_TWO_PI = 0.3989422804014327

NEGATIVE = -1e29
HIDE = -(2.0 ** 100)
BLOCK = 256
WIDE = 512
STAT = 40


def dot(a, b, ca, cb):
    return lax.dot_general(a, b, (((ca,), (cb,)), ((), ())), preferred_element_type=jnp.float32)


def left_half(shape):
    return lax.broadcasted_iota(jnp.int32, shape, 1) < 64


def spans(lens_ref, first, count):
    low, high, total = 0, 0, 0
    for d in range(lens_ref.shape[1]):
        begin = total
        total = total + lens_ref[0, d]
        low = jnp.where(begin <= first, begin, low)
        high = jnp.where(begin <= first + count - 1, total, high)
    return low, high


def openings(lens_ref, places):
    total, found = 0, places == 0
    for d in range(lens_ref.shape[1] - 1):
        total = total + lens_ref[0, d]
        found = jnp.logical_or(found, places == total)
    return found


def over_blocks(low, high, first, size, step, carry, ranked):
    begin, end = low // size, (high + size - 1) // size
    own = first // size
    skip = 1 if ranked else 0

    def body(index, carry):
        if ranked:
            index = index + jnp.where(index >= own, 1, 0)
        return step(pl.multiple_of(index * size, size), carry)

    carry = lax.fori_loop(begin, end - skip, body, carry)
    if ranked:
        carry = step(pl.multiple_of(own * size, size), carry, True)
    return carry


def forward_kernel(ranked, lens_ref, own_ref, q_ref, qm_ref, k_ref, v_ref, km_ref, o_ref, lse_ref):
    rows = q_ref.shape[0]
    base = own_ref[0] * rows
    half = left_half((BLOCK, 128))
    khalf = left_half((WIDE, 128))
    one = jnp.ones((WIDE, 128), jnp.bfloat16)

    def one_block(block, _):
        start = pl.multiple_of(block * BLOCK, BLOCK)
        first = base + start
        low, high = spans(lens_ref, first, BLOCK)
        q = q_ref[pl.ds(start, BLOCK), :]
        qm = qm_ref[pl.ds(start, BLOCK), :]
        queries = (jnp.where(half, q, qm), jnp.where(half, qm, q))

        def step(at, carry, diagonal=False):
            k = k_ref[pl.ds(at, WIDE), :]
            v = v_ref[pl.ds(at, WIDE), :]
            km = km_ref[pl.ds(at, WIDE), :]
            keys = (jnp.where(khalf, k, km), jnp.where(khalf, km, k))
            values = (jnp.where(khalf, v, one), jnp.where(khalf, one, v))
            scores = [dot(queries[h], keys[h], 1, 1) for h in (0, 1)]
            if diagonal:
                place = first + lax.broadcasted_iota(jnp.int32, (BLOCK, WIDE), 0)
                other = at + lax.broadcasted_iota(jnp.int32, (BLOCK, WIDE), 1)
                column = first + lax.broadcasted_iota(jnp.int32, (BLOCK, 1), 0)
                banned = jnp.where(openings(lens_ref, column), -1, place) == other
                scores = [jnp.where(banned, HIDE, s) for s in scores]
            out = []
            for h in (0, 1):
                peak, acc = carry[h]
                new = jnp.maximum(peak, jnp.max(scores[h], axis=1, keepdims=True))
                p = jnp.exp(scores[h] - new).astype(jnp.bfloat16)
                acc = acc * jnp.exp(peak - new) + dot(p, values[h], 1, 0)
                out.append((new, acc))
            return tuple(out)

        empty = (jnp.full((BLOCK, 1), NEGATIVE, jnp.float32), jnp.zeros((BLOCK, 128), jnp.float32))
        (peak0, acc0), (peak1, acc1) = over_blocks(low, high, first, WIDE, step, (empty, empty), ranked)
        total = jnp.where(half, acc1, acc0)
        mixed = jnp.where(half, acc0, acc1)
        o_ref[pl.ds(start, BLOCK), :] = mixed / pltpu.roll(total, 64, 1)
        lse_ref[pl.ds(start, BLOCK), :] = jnp.where(half, peak1, peak0) + jnp.log(total)
        return 0

    lax.fori_loop(0, rows // BLOCK, one_block, 0)


def attend_forward(ranked, lens, own, q, qm, k, v, km):
    rows = q.shape[0]
    whole = pl.BlockSpec(memory_space=pltpu.VMEM)
    smem = pl.BlockSpec(memory_space=pltpu.SMEM)
    return pl.pallas_call(
        functools.partial(forward_kernel, ranked),
        out_shape=(jax.ShapeDtypeStruct((rows, 128), jnp.float32),) * 2,
        in_specs=[smem, smem] + [whole] * 5,
        out_specs=(whole, whole),
        compiler_params=pltpu.CompilerParams(vmem_limit_bytes=56 << 20),
    )(lens, own, q, qm, k, v, km)


def with_stat(marks, stat, lane, at):
    high = stat.astype(jnp.bfloat16)
    rest = stat - high.astype(jnp.float32)
    middle = rest.astype(jnp.bfloat16)
    tail = (rest - middle.astype(jnp.float32)).astype(jnp.bfloat16)
    side = jnp.where(lane == at, high, jnp.where(lane == at + 1, middle, jnp.where(lane == at + 2, tail, marks)))
    return side


def backward_kernel(ranked, lens_ref, own_ref, q_ref, qm_ref, k_ref, v_ref, km_ref, o_ref, lse_ref, do_ref,
                    dq_ref, dk_ref, dv_ref):
    rows = q_ref.shape[0]
    base = own_ref[0] * rows
    half = left_half((BLOCK, 128))
    lane = lax.broadcasted_iota(jnp.int32, (BLOCK, 128), 1)
    one = jnp.ones((BLOCK, 128), jnp.bfloat16)
    zero = jnp.zeros((BLOCK, 128), jnp.bfloat16)

    def clear(index, _):
        at = pl.multiple_of(index * BLOCK, BLOCK)
        dk_ref[pl.ds(at, BLOCK), :] = jnp.zeros((BLOCK, 128), jnp.float32)
        dv_ref[pl.ds(at, BLOCK), :] = jnp.zeros((BLOCK, 128), jnp.float32)
        return 0

    lax.fori_loop(0, k_ref.shape[0] // BLOCK, clear, 0)

    def one_block(block, _):
        start = pl.multiple_of(block * BLOCK, BLOCK)
        first = base + start
        low, high = spans(lens_ref, first, BLOCK)
        here = pl.ds(start, BLOCK)
        q, qm, do, lse = q_ref[here, :], qm_ref[here, :], do_ref[here, :], lse_ref[here, :]
        shared = do.astype(jnp.float32) * o_ref[here, :]
        delta0 = jnp.sum(jnp.where(half, shared, 0.0), axis=1, keepdims=True)
        delta1 = jnp.sum(jnp.where(half, 0.0, shared), axis=1, keepdims=True)
        side = with_stat(qm, lse, lane % 64, STAT)
        queries = (jnp.where(half, q, side), jnp.where(half, side, q))
        side = with_stat(zero, -jnp.where(half, delta1, delta0), lane % 64, STAT)
        grads = (jnp.where(half, do, side), jnp.where(half, side, do))

        def step(at, carry, diagonal=False):
            there = pl.ds(at, BLOCK)
            k, v, km = k_ref[there, :], v_ref[there, :], km_ref[there, :]
            keys = (jnp.where(half, k, km), jnp.where(half, km, k))
            values = (jnp.where(half, v, one), jnp.where(half, one, v))
            scores = [dot(keys[h], queries[h], 1, 1) for h in (0, 1)]
            if diagonal:
                other = first + lax.broadcasted_iota(jnp.int32, (BLOCK, BLOCK), 0)
                row = first + lax.broadcasted_iota(jnp.int32, (1, BLOCK), 1)
                banned = other == jnp.where(openings(lens_ref, row), -1, row)
                scores = [jnp.where(banned, HIDE, s) for s in scores]
            dvs, dks, dqs = [], [], []
            for h in (0, 1):
                p = jnp.exp(scores[h])
                dp = dot(values[h], grads[h], 1, 1)
                ds = (p * dp).astype(jnp.bfloat16)
                dvs.append(dot(p.astype(jnp.bfloat16), do, 1, 0))
                dks.append(dot(ds, q, 1, 0))
                dqs.append(dot(ds, k, 0, 0))
            dv_ref[there, :] += jnp.where(half, dvs[0], dvs[1])
            dk_ref[there, :] += jnp.where(half, dks[0], dks[1])
            return carry + jnp.where(half, dqs[0], dqs[1])

        dq = over_blocks(low, high, first, BLOCK, step, jnp.zeros((BLOCK, 128), jnp.float32), ranked)
        dq_ref[here, :] = (dq * 0.125).astype(dq_ref.dtype)
        return 0

    lax.fori_loop(0, rows // BLOCK, one_block, 0)


def attend_backward(ranked, lens, own, q, qm, k, v, km, o, lse, do):
    rows, keys = q.shape[0], k.shape[0]
    whole = pl.BlockSpec(memory_space=pltpu.VMEM)
    smem = pl.BlockSpec(memory_space=pltpu.SMEM)
    return pl.pallas_call(
        functools.partial(backward_kernel, ranked),
        out_shape=(jax.ShapeDtypeStruct((rows, 128), jnp.bfloat16),) + (jax.ShapeDtypeStruct((keys, 128), jnp.float32),) * 2,
        in_specs=[smem, smem] + [whole] * 8,
        out_specs=(whole, whole, whole),
        compiler_params=pltpu.CompilerParams(vmem_limit_bytes=56 << 20),
    )(lens, own, q, qm, k, v, km, o, lse, do)


def mark_tables(lengths, ranks, limits, offset, rows, ranked):
    total = ranks.shape[0]
    docs = lengths.shape[0]
    ends = jnp.stack([jnp.sum(lengths[: d + 1]) for d in range(docs)])
    begins = jnp.stack([jnp.sum(lengths[:d]) for d in range(docs)])
    place = lax.broadcasted_iota(jnp.int32, (total, 64), 0)
    lane = lax.broadcasted_iota(jnp.int32, (total, 64), 1)
    doc = jnp.zeros((total, 1), jnp.int32)
    is_open = jnp.zeros((total, 1), bool)
    for d in range(docs):
        doc = doc + (place[:, :1] >= ends[d]).astype(jnp.int32)
        is_open = jnp.logical_or(is_open, place[:, :1] == begins[d])
    rank = jnp.where(is_open, 0, ranks[:, None] + 1)
    key_marks = jnp.where(lane == doc, 1.0, 0.0)
    if ranked:
        key_marks = key_marks + jnp.where(lane == rank + 16, 1.0, 0.0)
    key_marks = key_marks - jnp.where(jnp.logical_and(lane >= STAT, lane < STAT + 3), 1.0, 0.0)
    hide = jnp.where(jnp.logical_and(lane < docs, lane != doc), HIDE, 0.0)
    if ranked:
        hide = hide + jnp.where(jnp.logical_and(lane >= 16, jnp.logical_and(lane < 33, lane - 17 >= limits[:, None])), HIDE, 0.0)
    query_marks = lax.dynamic_slice_in_dim(hide, offset, rows, 0)
    both = lambda m: jnp.concatenate([m, m], axis=1).astype(jnp.bfloat16)
    return both(key_marks), both(query_marks)


def matmul(left, right):
    return jnp.dot(left, right, preferred_element_type=jnp.float32)


def left_product(left, right):
    return jnp.einsum("ta,tb->ab", left, right, preferred_element_type=jnp.float32)


def right_product(left, right):
    return jnp.einsum("ta,ba->tb", left, right, preferred_element_type=jnp.float32)


def column_sum(value):
    return jnp.sum(value.astype(jnp.float32), axis=0)


def gelu_slope(value):
    cumulative = 0.5 * (1.0 + lax.erf(value * ROOT_HALF))
    return cumulative + value * jnp.exp(-0.5 * value * value) * INV_ROOT_TWO_PI


def norm_forward(value, gain_row, shift_row):
    middle = jnp.mean(value, axis=-1, keepdims=True)
    centred = value - middle
    spread = jnp.mean(centred * centred, axis=-1, keepdims=True)
    inverse = lax.rsqrt(spread + EPSILON)
    normed = centred * inverse
    return (normed * gain_row + shift_row, normed, inverse)


def norm_backward(incoming, normed, inverse, gain_row):
    scaled = incoming * gain_row
    centred = (
        scaled
        - jnp.mean(scaled, axis=-1, keepdims=True)
        - normed * jnp.mean(scaled * normed, axis=-1, keepdims=True)
    )
    return (inverse * centred, jnp.sum(incoming * normed, axis=0), jnp.sum(incoming, axis=0))


MESH = pl.DeviceIdType.MESH
ANY = pl.BlockSpec(memory_space=pltpu.HBM)
VMEM = pl.BlockSpec(memory_space=pltpu.VMEM)
SMEM = pl.BlockSpec(memory_space=pltpu.SMEM)
DMA = pltpu.SemaphoreType.DMA


def across(place, offset):
    if offset == 1:
        return place + 1 - 2 * lax.rem(place, 2)
    if offset == 2:
        return lax.rem(place + 2, 4)
    return 3 - place


def remote(src, dst, sends, recvs, where):
    return pltpu.make_async_remote_copy(
        src_ref=src, dst_ref=dst, send_sem=sends, recv_sem=recvs, device_id=where, device_id_type=MESH)


def greet(grp_count, wa_count, plane=True, groups=True, rows=True):
    barrier = pltpu.get_barrier_semaphore()
    grp, pln, wa = lax.axis_index("grp"), lax.axis_index("pln"), lax.axis_index("wa")

    def hello(where):
        pl.semaphore_signal(barrier, inc=1, device_id=where, device_id_type=MESH)

    count = 0
    if plane:
        for offset in (1, 2, 3):
            hello({"pln": across(pln, offset)})
        count += 3
    if rows:
        for offset in range(1, wa_count):
            hello({"wa": lax.rem(wa + offset, wa_count)})
        count += wa_count - 1
    if groups:
        @pl.when(grp > 0)
        def _():
            hello({"grp": grp - 1})

        @pl.when(grp < grp_count - 1)
        def _():
            hello({"grp": grp + 1})

        count = count + jnp.where(grp > 0, 1, 0) + jnp.where(grp < grp_count - 1, 1, 0)
    pl.semaphore_wait(barrier, count)


class Rows:
    def __init__(self, shard, full, sems, index, wa_count):
        self.shard, self.full, self.sems, self.index, self.wa_count = shard, full, sems, index, wa_count
        self.size = shard.shape[0]
        self.half = self.size // 2
        self.wa, self.pln = lax.axis_index("wa"), lax.axis_index("pln")
        self.core = lax.rem(self.pln, 2)

    def part(self, owner, core):
        return pl.ds(pl.multiple_of(owner * self.size + core * self.half, 16), self.half)

    def keep(self):
        own = pl.ds(pl.multiple_of(self.wa * self.size, 16), self.size)
        return pltpu.make_async_copy(self.shard, self.full.at[own], self.sems.at[0, self.index, 0])

    def push(self, offset):
        mine = pl.ds(pl.multiple_of(self.core * self.half, 16), self.half)
        return remote(self.shard.at[mine], self.full.at[self.part(self.wa, self.core)],
                      self.sems.at[1, self.index, offset - 1], self.sems.at[2, self.index, offset - 1],
                      {"wa": lax.rem(self.wa + offset, self.wa_count)})

    def hand(self, offset):
        owner = lax.rem(self.wa + self.wa_count - offset, self.wa_count)
        spot = self.full.at[self.part(owner, self.core)]
        return remote(spot, spot, self.sems.at[3, self.index, offset - 1], self.sems.at[4, self.index, offset - 1],
                      {"pln": across(self.pln, 1)})

    def begin(self):
        self.keep().start()
        for offset in range(1, self.wa_count):
            self.push(offset).start()

    def pass_on(self):
        for offset in range(1, self.wa_count):
            self.push(offset).wait_recv()
            self.hand(offset).start()

    def arrived(self):
        self.keep().wait()
        for offset in range(1, self.wa_count):
            self.hand(offset).wait_recv()

    def finish(self):
        for offset in range(1, self.wa_count):
            self.push(offset).wait_send()
            self.hand(offset).wait_send()


class Line:
    def __init__(self, full, sems, grp_count, reach, block):
        self.full, self.sems, self.count, self.reach, self.block = full, sems, grp_count, reach, block
        self.grp = lax.axis_index("grp")

    def rows(self, owner, block):
        return pl.ds(pl.multiple_of((owner * PLANE + block) * self.block, 16), self.block)

    def copy(self, side, step, block, source=None):
        toward = 1 if side == 0 else -1
        owner = self.grp - toward * (step - 1)
        spot = self.full.at[self.rows(owner, block)]
        return remote(spot if source is None else source, spot, self.sems.at[0, side, step - 1, block],
                      self.sems.at[1, side, step - 1, block], {"grp": self.grp + toward})

    def sends(self, side, step):
        if side == 0:
            return jnp.logical_and(self.grp - step + 1 >= 0, self.grp + 1 < self.count)
        return jnp.logical_and(self.grp + step - 1 < self.count, self.grp - 1 >= 0)

    def receives(self, side, step):
        return self.grp - step >= 0 if side == 0 else self.grp + step < self.count

    def send(self, step, block, source=None):
        for side in (0, 1):
            @pl.when(self.sends(side, step))
            def _():
                self.copy(side, step, block, source).start()

    def arrival(self, side, step, block):
        toward = 1 if side == 0 else -1
        spot = self.full.at[self.rows(self.grp - toward * step, block)]
        return remote(spot, spot, self.sems.at[0, side, step - 1, block], self.sems.at[1, side, step - 1, block],
                      {"grp": self.grp - toward})

    def forward(self, step):
        for block in range(PLANE):
            for side in (0, 1):
                @pl.when(self.receives(side, step))
                def _():
                    self.arrival(side, step, block).wait_recv()

                    if step < self.reach:
                        @pl.when(self.sends(side, step + 1))
                        def _():
                            self.copy(side, step + 1, block).start()

    def finish(self, source=None):
        for step in range(1, self.reach + 1):
            for block in range(PLANE):
                for side in (0, 1):
                    @pl.when(self.sends(side, step))
                    def _():
                        self.copy(side, step, block, source[block] if source and step == 1 else None).wait_send()


class Swap:
    def __init__(self, src, dst, sems):
        self.src, self.dst, self.sems = src, dst, sems
        self.pln = lax.axis_index("pln")

    def copy(self, offset):
        peer = across(self.pln, offset)
        return remote(self.src(peer), self.dst(self.pln), self.sems.at[0, offset], self.sems.at[1, offset], {"pln": peer})

    def keep(self):
        return pltpu.make_async_copy(self.src(self.pln), self.dst(self.pln), self.sems.at[0, 0])

    def begin(self):
        for offset in (2, 3, 1):
            self.copy(offset).start()
        self.keep().start()

    def arrived(self, offset):
        self.keep().wait() if offset == 0 else self.copy(offset).wait_recv()

    def finish(self):
        for offset in (1, 2, 3):
            self.copy(offset).wait_send()


VEC_ORDER = ("self_query_bias", "self_value_bias", "cross_value_bias", "self_out_bias", "norm_one_gain", "norm_one_shift",
             "cross_query_bias", "cross_out_bias", "norm_two_gain", "norm_two_shift", "expand_bias", "shrink_bias",
             "norm_three_gain", "norm_three_shift")


def pack_vectors(vecs):
    parts = []
    for v in vecs:
        width = min(128, v.shape[0])
        rows = v.reshape(-1, width)
        parts.append(jnp.pad(rows, ((0, 0), (0, 128 - width))))
    pack = jnp.concatenate(parts)
    return jnp.pad(pack, ((0, -pack.shape[0] % 16), (0, 0)))


def vector_row(pack_ref, wa_count, start, length):
    width = min(128, length)
    pieces = []
    for wa in range(wa_count):
        for row in range(length // width):
            pieces.append(pack_ref[wa, start + row : start + row + 1, :width].astype(jnp.float32))
    return jnp.concatenate(pieces, axis=1)


def split_pairs(value, buffer, column):
    for pair in range(PLANE):
        buffer[pair, :, column : column + 128] = value[:, pair * 128 : pair * 128 + 128]


def opening_kernel(grp_count, wa_count, reach, count, vec_at, content_ref, query_ref, encoder_ref, vec_ref, *refs):
    shards = refs[:count]
    fulls = refs[count : 2 * count]
    vec_out, q_out, kv_out, kv2_out = refs[2 * count : 2 * count + 4]
    held, vec_all, kvbuf, kvbuf2, qbuf, row_sems, vec_sems, line_sems, swap_sems, out_sems = refs[2 * count + 4 :]
    grp, pln, wa = lax.axis_index("grp"), lax.axis_index("pln"), lax.axis_index("wa")
    tok = content_ref.shape[0]
    gathers = [Rows(shards[i], held.at[i] if i < 5 else fulls[i], row_sems, i, wa_count) for i in range(count)]
    greet(grp_count, wa_count)
    vec_keep = pltpu.make_async_copy(vec_ref, vec_all.at[wa], vec_sems.at[0, 0])
    vec_keep.start()
    pushes = [remote(vec_ref, vec_all.at[wa], vec_sems.at[0, o], vec_sems.at[1, o], {"wa": lax.rem(wa + o, wa_count)})
              for o in range(1, wa_count)]
    for g in gathers[:2]:
        g.begin()
    for p in pushes:
        p.start()
    for g in gathers[:2]:
        g.pass_on()
    for g in gathers[2:5]:
        g.begin()
    vec_keep.wait()
    for p in pushes:
        p.wait_recv()
    for g in gathers[:2]:
        g.arrived()
    content = content_ref[...]
    split_pairs(matmul(content, held[0]).astype(jnp.bfloat16), kvbuf, 0)
    row = lambda i: vector_row(vec_all, wa_count, *vec_at[i])
    split_pairs((matmul(content, held[1]) + row(1)).astype(jnp.bfloat16), kvbuf, 128)
    line = Line(kv_out, line_sems, grp_count, reach, tok)
    spot = lambda ref: lambda p: ref.at[pl.ds(pl.multiple_of((grp * PLANE + p) * tok, 16), tok)]
    swap = Swap(lambda p: kvbuf.at[p], spot(kv_out), swap_sems.at[0])
    swap.begin()
    line.send(1, pln, kvbuf.at[pln])
    swap.arrived(1)
    line.send(1, across(pln, 1))
    for g in gathers[2:5]:
        g.pass_on()
    for g in gathers[5:]:
        g.begin()
    for offset in (2, 3):
        swap.arrived(offset)
        line.send(1, across(pln, offset))
    for g in gathers[2:5]:
        g.arrived()
    outs = [pltpu.make_async_copy(held.at[i], fulls[i], out_sems.at[i]) for i in range(5)]
    for o in outs:
        o.start()
    vec_save = pltpu.make_async_copy(vec_all, vec_out, out_sems.at[5])
    vec_save.start()
    query = (matmul(query_ref[...], held[2]) + row(0)).astype(jnp.bfloat16)
    query = query * 0.125
    for pair in range(PLANE):
        qbuf[pair] = query[:, pair * 128 : pair * 128 + 128]
    place = lambda p: q_out.at[pl.ds(pl.multiple_of(p * tok, 16), tok)]
    swap_q = Swap(lambda p: qbuf.at[p], place, swap_sems.at[1])
    swap_q.begin()
    encoder = encoder_ref[...]
    split_pairs(matmul(encoder, held[3]).astype(jnp.bfloat16), kvbuf2, 0)
    split_pairs((matmul(encoder, held[4]) + row(2)).astype(jnp.bfloat16), kvbuf2, 128)
    place2 = lambda p: kv2_out.at[pl.ds(pl.multiple_of(p * tok, 16), tok)]
    swap_2 = Swap(lambda p: kvbuf2.at[p], place2, swap_sems.at[2])
    swap_2.begin()
    for step in range(1, reach + 1):
        line.forward(step)
    swap.arrived(0)
    for s in (swap_q, swap_2):
        for offset in range(4):
            s.arrived(offset)
    for g in gathers[5:]:
        g.pass_on()
    for g in gathers[5:]:
        g.arrived()
    for g in gathers:
        g.finish()
    for p in pushes:
        p.wait_send()
    for o in outs:
        o.wait()
    vec_save.wait()
    line.finish()
    for s in (swap, swap_q, swap_2):
        s.finish()


def run_opening(grp_count, wa_count, content, query, encoder, vecs, mats, vec_at):
    tok = content.shape[0]
    reach = min(grp_count - 1, (DOCLEN + PLANE * tok - 2) // (PLANE * tok))
    count = len(mats)
    low = jnp.bfloat16
    shape = lambda *s: jax.ShapeDtypeStruct(s, low)
    out_shape = [shape(m.shape[0] * wa_count, m.shape[1]) for m in mats]
    out_shape += [shape(wa_count, *vecs.shape), shape(PLANE * tok, 128), shape(grp_count * PLANE * tok, 256),
                  shape(PLANE * tok, 256)]
    return pl.pallas_call(
        functools.partial(opening_kernel, grp_count, wa_count, reach, count, vec_at),
        out_shape=tuple(out_shape),
        in_specs=[VMEM] * 4 + [ANY] * count,
        out_specs=tuple([ANY] * len(out_shape)),
        scratch_shapes=[
            pltpu.VMEM((5, 512, 512), low), pltpu.VMEM((wa_count,) + vecs.shape, low), pltpu.VMEM((PLANE, tok, 256), low),
            pltpu.VMEM((PLANE, tok, 256), low), pltpu.VMEM((PLANE, tok, 128), low),
            DMA((5, count, max(1, wa_count - 1))), DMA((2, wa_count)), DMA((2, 2, reach, PLANE)), DMA((3, 2, 4)), DMA((6,))],
        compiler_params=pltpu.CompilerParams(collective_id=1, has_side_effects=True, vmem_limit_bytes=40 << 20),
    )(content, query, encoder, vecs, *mats)


def to_pairs(value):
    return lax.all_to_all(value, "pln", 1, 0, tiled=True)


def to_tokens(value):
    return lax.all_to_all(value, "pln", 0, 1, tiled=True)


def return_pairs(keys, values):
    both = jnp.concatenate([keys, values], axis=1).astype(jnp.bfloat16)
    mine = lax.psum_scatter(both, "grp", scatter_dimension=0, tiled=True).astype(jnp.bfloat16)
    return to_tokens(mine[:, :128]), to_tokens(mine[:, 128:])


def reduce_grads(grads):
    wa = lax.axis_size("wa")
    mats = [g.astype(jnp.bfloat16).reshape(wa, -1, 512) for g in grads if g.ndim == 2]
    vecs = [g.reshape(wa, -1) for g in grads if g.ndim == 1]
    pack = jnp.concatenate(mats, axis=1)
    mine = lax.psum_scatter(pack, "wa", scatter_dimension=0, tiled=False)
    total = lax.psum(mine, ("grp", "pln")).astype(jnp.float32)
    line = lax.psum(jnp.concatenate(vecs, axis=1).astype(jnp.bfloat16), ("grp", "pln", "wa")).astype(jnp.float32)
    line = lax.dynamic_index_in_dim(line, lax.axis_index("wa"), 0, False)
    out, at, vat = [], 0, 0
    for g in grads:
        if g.ndim == 2:
            n = g.size // wa // 512
            out.append(total[at : at + n].reshape(g.shape[0] // wa, g.shape[1]))
            at += n
        else:
            n = g.size // wa
            out.append(line[vat : vat + n])
            vat += n
    return tuple(out)


def shards(
    query_in,
    content_in,
    encoder_in,
    out_grad,
    document_lengths,
    key_ranks,
    query_limits,
    self_query_weight,
    self_query_bias,
    self_key_weight,
    self_value_weight,
    self_value_bias,
    self_out_weight,
    self_out_bias,
    norm_one_gain,
    norm_one_shift,
    cross_query_weight,
    cross_query_bias,
    cross_key_weight,
    cross_value_weight,
    cross_value_bias,
    cross_out_weight,
    cross_out_bias,
    norm_two_gain,
    norm_two_shift,
    expand_weight,
    expand_bias,
    shrink_weight,
    shrink_bias,
    norm_three_gain,
    norm_three_shift,
):
    grp_count = lax.axis_size("grp")
    own = lax.axis_index("grp")[None].astype(jnp.int32)
    lens = document_lengths
    tok = query_in.shape[1]
    rows = tok * PLANE
    row_at = lax.axis_index("grp") * rows
    cross_keys, cross_marks = mark_tables(lens[0], key_ranks[0], query_limits[0], row_at, rows, False)
    self_keys, self_marks = mark_tables(lens[0], key_ranks[0], query_limits[0], row_at, rows, True)
    wa_count = lax.axis_size("wa")
    vectors = (self_query_bias, self_value_bias, cross_value_bias, self_out_bias, norm_one_gain, norm_one_shift,
        cross_query_bias, cross_out_bias, norm_two_gain, norm_two_shift, expand_bias, shrink_bias, norm_three_gain,
        norm_three_shift)
    vec_at, at = [], 0
    for v in vectors:
        vec_at.append((at, v.shape[0]))
        at += v.shape[0] // min(128, v.shape[0])
    vec_at = tuple(vec_at)
    mats = (self_key_weight, self_value_weight, self_query_weight, cross_key_weight, cross_value_weight, self_out_weight,
        cross_query_weight, cross_out_weight, expand_weight, shrink_weight)
    (self_key_matrix, self_value_mat, self_query_mat, cross_key_matrix, cross_value_mat, self_out_mat, cross_query_mat,
        cross_out_mat, expand_mat, shrink_mat, vec_all, pair_one, kv_one, kv_two) = run_opening(
        grp_count, wa_count, content_in[0], query_in[0], encoder_in[0], pack_vectors(vectors), mats, vec_at)
    lines = [jnp.concatenate([vec_all[w, s : s + n // min(n, 128), : min(n, 128)].reshape(-1) for w in range(wa_count)])
        .astype(jnp.float32) for s, n in vec_at]
    (self_query_vec, self_value_vec, cross_value_vec, self_out_vec, gain_one, shift_one, cross_query_vec, cross_out_vec,
        gain_two, shift_two, expand_vec, shrink_vec, gain_three, shift_three) = lines
    source = query_in[0]
    content_states = content_in[0]
    encoder_output = encoder_in[0]
    cotangent = out_grad[0].astype(jnp.float32)
    kv_two = lax.all_gather(kv_two, "grp", axis=0, tiled=True)
    keys_one, values_one = kv_one[:, :128], kv_one[:, 128:]
    keys_two, values_two = kv_two[:, :128], kv_two[:, 128:]
    attended_one, total_one = attend_forward(True, lens, own, pair_one, self_marks, keys_one, values_one, self_keys)
    mixed_one = to_tokens(attended_one.astype(jnp.bfloat16))
    hidden_one, normed_one, inverse_one = norm_forward(
        source.astype(jnp.float32) + matmul(mixed_one, self_out_mat) + self_out_vec, gain_one, shift_one)
    hidden_one_low = hidden_one.astype(jnp.bfloat16)
    query_two = (matmul(hidden_one_low, cross_query_mat) + cross_query_vec).astype(jnp.bfloat16)
    pair_two = to_pairs(query_two * jnp.bfloat16(0.125))
    attended_two, total_two = attend_forward(False, lens, own, pair_two, cross_marks, keys_two, values_two, cross_keys)
    mixed_two = to_tokens(attended_two.astype(jnp.bfloat16))
    hidden_two, normed_two, inverse_two = norm_forward(
        hidden_one + matmul(mixed_two, cross_out_mat) + cross_out_vec, gain_two, shift_two)
    hidden_two_low = hidden_two.astype(jnp.bfloat16)
    expanded = matmul(hidden_two_low, expand_mat) + expand_vec
    activated = jax.nn.gelu(expanded, approximate=False).astype(jnp.bfloat16)
    layer_out, normed_three, inverse_three = norm_forward(
        hidden_two + matmul(activated, shrink_mat) + shrink_vec, gain_three, shift_three)
    back_three, grad_gain_three, grad_shift_three = norm_backward(cotangent, normed_three, inverse_three, gain_three)
    shrink_in_grad = back_three.astype(jnp.bfloat16)
    grad_shrink_mat = left_product(activated, shrink_in_grad)
    grad_shrink_vec = column_sum(shrink_in_grad)
    activated_grad = right_product(shrink_in_grad, shrink_mat)
    expand_grad = (activated_grad * gelu_slope(expanded)).astype(jnp.bfloat16)
    grad_expand_mat = left_product(hidden_two_low, expand_grad)
    grad_expand_vec = column_sum(expand_grad)
    hidden_two_grad = back_three + right_product(expand_grad, expand_mat)
    back_two, grad_gain_two, grad_shift_two = norm_backward(hidden_two_grad, normed_two, inverse_two, gain_two)
    branch_two = back_two.astype(jnp.bfloat16)
    grad_cross_out_mat = left_product(mixed_two, branch_two)
    grad_cross_out_vec = column_sum(branch_two)
    mixed_two_grad = right_product(branch_two, cross_out_mat).astype(jnp.bfloat16)
    dq_two, dk_two, dv_two = attend_backward(False, lens, own, pair_two, cross_marks, keys_two, values_two, cross_keys,
        attended_two, total_two, to_pairs(mixed_two_grad))
    key_two_low, value_two_low = return_pairs(dk_two, dv_two)
    query_two_low = to_tokens(dq_two)
    grad_cross_query_mat = left_product(hidden_one_low, query_two_low)
    grad_cross_query_vec = column_sum(query_two_low)
    grad_cross_key_mat = left_product(encoder_output, key_two_low)
    grad_cross_value_mat = left_product(encoder_output, value_two_low)
    grad_cross_value_vec = column_sum(value_two_low)
    encoder_grad = right_product(key_two_low, cross_key_matrix) + right_product(value_two_low, cross_value_mat)
    hidden_one_grad = back_two + right_product(query_two_low, cross_query_mat)
    back_one, grad_gain_one, grad_shift_one = norm_backward(hidden_one_grad, normed_one, inverse_one, gain_one)
    branch_one = back_one.astype(jnp.bfloat16)
    grad_self_out_mat = left_product(mixed_one, branch_one)
    grad_self_out_vec = column_sum(branch_one)
    mixed_one_grad = right_product(branch_one, self_out_mat).astype(jnp.bfloat16)
    dq_one, dk_one, dv_one = attend_backward(True, lens, own, pair_one, self_marks, keys_one, values_one, self_keys,
        attended_one, total_one, to_pairs(mixed_one_grad))
    key_one_low, value_one_low = return_pairs(dk_one, dv_one)
    query_one_low = to_tokens(dq_one)
    grad_self_query_mat = left_product(source, query_one_low)
    grad_self_query_vec = column_sum(query_one_low)
    grad_self_key_mat = left_product(content_states, key_one_low)
    grad_self_value_mat = left_product(content_states, value_one_low)
    grad_self_value_vec = column_sum(value_one_low)
    query_grad = back_one + right_product(query_one_low, self_query_mat)
    content_grad = right_product(key_one_low, self_key_matrix) + right_product(value_one_low, self_value_mat)
    grads = reduce_grads((
        grad_self_query_mat, grad_self_query_vec, grad_self_key_mat, grad_self_value_mat, grad_self_value_vec, grad_self_out_mat, grad_self_out_vec, grad_gain_one, grad_shift_one, grad_cross_query_mat, grad_cross_query_vec, grad_cross_key_mat, grad_cross_value_mat, grad_cross_value_vec, grad_cross_out_mat, grad_cross_out_vec, grad_gain_two, grad_shift_two, grad_expand_mat, grad_expand_vec, grad_shrink_mat, grad_shrink_vec, grad_gain_three, grad_shift_three))
    return (layer_out[None], query_grad[None], content_grad[None], encoder_grad[None]) + grads


def solution(mesh):
    ctx, wa = mesh.devices.shape
    mesh = Mesh(mesh.devices.reshape(ctx // PLANE, PLANE, wa), ("grp", "pln", "wa"))
    in_specs = (
        P("wa", ("grp", "pln"), None),
        P("wa", ("grp", "pln"), None),
        P("wa", ("grp", "pln"), None),
        P("wa", ("grp", "pln"), None),
        P("wa", None),
        P("wa", None),
        P("wa", None),
        P("wa", None),
        P("wa"),
        P("wa", None),
        P("wa", None),
        P("wa"),
        P("wa", None),
        P("wa"),
        P("wa"),
        P("wa"),
        P("wa", None),
        P("wa"),
        P("wa", None),
        P("wa", None),
        P("wa"),
        P("wa", None),
        P("wa"),
        P("wa"),
        P("wa"),
        P("wa", None),
        P("wa"),
        P("wa", None),
        P("wa"),
        P("wa"),
        P("wa"),
    )
    out_specs = (
        P("wa", ("grp", "pln"), None),
        P("wa", ("grp", "pln"), None),
        P("wa", ("grp", "pln"), None),
        P("wa", ("grp", "pln"), None),
        P("wa", None),
        P("wa"),
        P("wa", None),
        P("wa", None),
        P("wa"),
        P("wa", None),
        P("wa"),
        P("wa"),
        P("wa"),
        P("wa", None),
        P("wa"),
        P("wa", None),
        P("wa", None),
        P("wa"),
        P("wa", None),
        P("wa"),
        P("wa"),
        P("wa"),
        P("wa", None),
        P("wa"),
        P("wa", None),
        P("wa"),
        P("wa"),
        P("wa"),
    )
    return jax.shard_map(shards, mesh=mesh, in_specs=in_specs, out_specs=out_specs, check_vma=False)
```

```python
import functools
import jax
import jax.numpy as jnp
from jax import lax
from jax.experimental import pallas as pl
from jax.experimental.pallas import tpu as pltpu
from jax.sharding import Mesh
from jax.sharding import PartitionSpec as P

PLANE = 4
DOCLEN = 2048
EPSILON = 1e-05
ROOT_HALF = 0.7071067811865476
INV_ROOT_TWO_PI = 0.3989422804014327

NEGATIVE = -1e29
HIDE = -(2.0 ** 100)
BLOCK = 256
WIDE = 512
STAT = 40


def dot(a, b, ca, cb):
    return lax.dot_general(a, b, (((ca,), (cb,)), ((), ())), preferred_element_type=jnp.float32)


def left_half(shape):
    return lax.broadcasted_iota(jnp.int32, shape, 1) < 64


def spans(lens_ref, first, count):
    low, high, total = 0, 0, 0
    for d in range(lens_ref.shape[1]):
        begin = total
        total = total + lens_ref[0, d]
        low = jnp.where(begin <= first, begin, low)
        high = jnp.where(begin <= first + count - 1, total, high)
    return low, high


def openings(lens_ref, places):
    total, found = 0, places == 0
    for d in range(lens_ref.shape[1] - 1):
        total = total + lens_ref[0, d]
        found = jnp.logical_or(found, places == total)
    return found


def over_blocks(low, high, first, size, step, carry, ranked):
    begin, end = low // size, (high + size - 1) // size
    own = first // size
    skip = 1 if ranked else 0

    def body(index, carry):
        if ranked:
            index = index + jnp.where(index >= own, 1, 0)
        return step(pl.multiple_of(index * size, size), carry)

    carry = lax.fori_loop(begin, end - skip, body, carry)
    if ranked:
        carry = step(pl.multiple_of(own * size, size), carry, True)
    return carry


def forward_kernel(ranked, lens_ref, own_ref, q_ref, qm_ref, k_ref, v_ref, km_ref, o_ref, lse_ref):
    rows = q_ref.shape[0]
    base = own_ref[0] * rows
    half = left_half((BLOCK, 128))
    khalf = left_half((WIDE, 128))
    one = jnp.ones((WIDE, 128), jnp.bfloat16)

    def one_block(block, _):
        start = pl.multiple_of(block * BLOCK, BLOCK)
        first = base + start
        low, high = spans(lens_ref, first, BLOCK)
        q = q_ref[pl.ds(start, BLOCK), :]
        qm = qm_ref[pl.ds(start, BLOCK), :]
        queries = (jnp.where(half, q, qm), jnp.where(half, qm, q))

        def step(at, carry, diagonal=False):
            k = k_ref[pl.ds(at, WIDE), :]
            v = v_ref[pl.ds(at, WIDE), :]
            km = km_ref[pl.ds(at, WIDE), :]
            keys = (jnp.where(khalf, k, km), jnp.where(khalf, km, k))
            values = (jnp.where(khalf, v, one), jnp.where(khalf, one, v))
            scores = [dot(queries[h], keys[h], 1, 1) for h in (0, 1)]
            if diagonal:
                place = first + lax.broadcasted_iota(jnp.int32, (BLOCK, WIDE), 0)
                other = at + lax.broadcasted_iota(jnp.int32, (BLOCK, WIDE), 1)
                column = first + lax.broadcasted_iota(jnp.int32, (BLOCK, 1), 0)
                banned = jnp.where(openings(lens_ref, column), -1, place) == other
                scores = [jnp.where(banned, HIDE, s) for s in scores]
            out = []
            for h in (0, 1):
                peak, acc = carry[h]
                new = jnp.maximum(peak, jnp.max(scores[h], axis=1, keepdims=True))
                p = jnp.exp(scores[h] - new).astype(jnp.bfloat16)
                acc = acc * jnp.exp(peak - new) + dot(p, values[h], 1, 0)
                out.append((new, acc))
            return tuple(out)

        empty = (jnp.full((BLOCK, 1), NEGATIVE, jnp.float32), jnp.zeros((BLOCK, 128), jnp.float32))
        (peak0, acc0), (peak1, acc1) = over_blocks(low, high, first, WIDE, step, (empty, empty), ranked)
        total = jnp.where(half, acc1, acc0)
        mixed = jnp.where(half, acc0, acc1)
        o_ref[pl.ds(start, BLOCK), :] = mixed / pltpu.roll(total, 64, 1)
        lse_ref[pl.ds(start, BLOCK), :] = jnp.where(half, peak1, peak0) + jnp.log(total)
        return 0

    lax.fori_loop(0, rows // BLOCK, one_block, 0)


def attend_forward(ranked, lens, own, q, qm, k, v, km):
    rows = q.shape[0]
    whole = pl.BlockSpec(memory_space=pltpu.VMEM)
    smem = pl.BlockSpec(memory_space=pltpu.SMEM)
    return pl.pallas_call(
        functools.partial(forward_kernel, ranked),
        out_shape=(jax.ShapeDtypeStruct((rows, 128), jnp.float32),) * 2,
        in_specs=[smem, smem] + [whole] * 5,
        out_specs=(whole, whole),
        compiler_params=pltpu.CompilerParams(vmem_limit_bytes=60 << 20),
    )(lens, own, q, qm, k, v, km)


def with_stat(marks, stat, lane, at):
    high = stat.astype(jnp.bfloat16)
    rest = stat - high.astype(jnp.float32)
    middle = rest.astype(jnp.bfloat16)
    tail = (rest - middle.astype(jnp.float32)).astype(jnp.bfloat16)
    side = jnp.where(lane == at, high, jnp.where(lane == at + 1, middle, jnp.where(lane == at + 2, tail, marks)))
    return side


def backward_kernel(ranked, lens_ref, own_ref, q_ref, qm_ref, k_ref, v_ref, km_ref, o_ref, lse_ref, do_ref,
                    dq_ref, dk_ref, dv_ref):
    rows = q_ref.shape[0]
    base = own_ref[0] * rows
    half = left_half((BLOCK, 128))
    lane = lax.broadcasted_iota(jnp.int32, (BLOCK, 128), 1)
    one = jnp.ones((BLOCK, 128), jnp.bfloat16)
    zero = jnp.zeros((BLOCK, 128), jnp.bfloat16)

    def clear(index, _):
        at = pl.multiple_of(index * BLOCK, BLOCK)
        dk_ref[pl.ds(at, BLOCK), :] = jnp.zeros((BLOCK, 128), jnp.float32)
        dv_ref[pl.ds(at, BLOCK), :] = jnp.zeros((BLOCK, 128), jnp.float32)
        return 0

    lax.fori_loop(0, k_ref.shape[0] // BLOCK, clear, 0)

    def one_block(block, _):
        start = pl.multiple_of(block * BLOCK, BLOCK)
        first = base + start
        low, high = spans(lens_ref, first, BLOCK)
        here = pl.ds(start, BLOCK)
        q, qm, do, lse = q_ref[here, :], qm_ref[here, :], do_ref[here, :], lse_ref[here, :]
        shared = do.astype(jnp.float32) * o_ref[here, :]
        delta0 = jnp.sum(jnp.where(half, shared, 0.0), axis=1, keepdims=True)
        delta1 = jnp.sum(jnp.where(half, 0.0, shared), axis=1, keepdims=True)
        side = with_stat(qm, lse, lane % 64, STAT)
        queries = (jnp.where(half, q, side), jnp.where(half, side, q))
        side = with_stat(zero, -jnp.where(half, delta1, delta0), lane % 64, STAT)
        grads = (jnp.where(half, do, side), jnp.where(half, side, do))

        def step(at, carry, diagonal=False):
            there = pl.ds(at, BLOCK)
            k, v, km = k_ref[there, :], v_ref[there, :], km_ref[there, :]
            keys = (jnp.where(half, k, km), jnp.where(half, km, k))
            values = (jnp.where(half, v, one), jnp.where(half, one, v))
            scores = [dot(keys[h], queries[h], 1, 1) for h in (0, 1)]
            if diagonal:
                other = first + lax.broadcasted_iota(jnp.int32, (BLOCK, BLOCK), 0)
                row = first + lax.broadcasted_iota(jnp.int32, (1, BLOCK), 1)
                banned = other == jnp.where(openings(lens_ref, row), -1, row)
                scores = [jnp.where(banned, HIDE, s) for s in scores]
            dvs, dks, dqs = [], [], []
            for h in (0, 1):
                p = jnp.exp(scores[h])
                dp = dot(values[h], grads[h], 1, 1)
                ds = (p * dp).astype(jnp.bfloat16)
                dvs.append(dot(p.astype(jnp.bfloat16), do, 1, 0))
                dks.append(dot(ds, q, 1, 0))
                dqs.append(dot(ds, k, 0, 0))
            dv_ref[there, :] += jnp.where(half, dvs[0], dvs[1])
            dk_ref[there, :] += jnp.where(half, dks[0], dks[1])
            return carry + jnp.where(half, dqs[0], dqs[1])

        dq = over_blocks(low, high, first, BLOCK, step, jnp.zeros((BLOCK, 128), jnp.float32), ranked)
        dq_ref[here, :] = (dq * 0.125).astype(dq_ref.dtype)
        return 0

    lax.fori_loop(0, rows // BLOCK, one_block, 0)


def attend_backward(ranked, lens, own, q, qm, k, v, km, o, lse, do):
    rows, keys = q.shape[0], k.shape[0]
    whole = pl.BlockSpec(memory_space=pltpu.VMEM)
    smem = pl.BlockSpec(memory_space=pltpu.SMEM)
    return pl.pallas_call(
        functools.partial(backward_kernel, ranked),
        out_shape=(jax.ShapeDtypeStruct((rows, 128), jnp.bfloat16),) + (jax.ShapeDtypeStruct((keys, 128), jnp.float32),) * 2,
        in_specs=[smem, smem] + [whole] * 8,
        out_specs=(whole, whole, whole),
        compiler_params=pltpu.CompilerParams(vmem_limit_bytes=60 << 20),
    )(lens, own, q, qm, k, v, km, o, lse, do)


def mark_tables(lengths, ranks, limits, offset, rows, ranked):
    total = ranks.shape[0]
    docs = lengths.shape[0]
    ends = jnp.stack([jnp.sum(lengths[: d + 1]) for d in range(docs)])
    begins = jnp.stack([jnp.sum(lengths[:d]) for d in range(docs)])
    place = lax.broadcasted_iota(jnp.int32, (total, 64), 0)
    lane = lax.broadcasted_iota(jnp.int32, (total, 64), 1)
    doc = jnp.zeros((total, 1), jnp.int32)
    is_open = jnp.zeros((total, 1), bool)
    for d in range(docs):
        doc = doc + (place[:, :1] >= ends[d]).astype(jnp.int32)
        is_open = jnp.logical_or(is_open, place[:, :1] == begins[d])
    rank = jnp.where(is_open, 0, ranks[:, None] + 1)
    key_marks = jnp.where(lane == doc, 1.0, 0.0)
    if ranked:
        key_marks = key_marks + jnp.where(lane == rank + 16, 1.0, 0.0)
    key_marks = key_marks - jnp.where(jnp.logical_and(lane >= STAT, lane < STAT + 3), 1.0, 0.0)
    hide = jnp.where(jnp.logical_and(lane < docs, lane != doc), HIDE, 0.0)
    if ranked:
        hide = hide + jnp.where(jnp.logical_and(lane >= 16, jnp.logical_and(lane < 33, lane - 17 >= limits[:, None])), HIDE, 0.0)
    query_marks = lax.dynamic_slice_in_dim(hide, offset, rows, 0)
    both = lambda m: jnp.concatenate([m, m], axis=1).astype(jnp.bfloat16)
    return both(key_marks), both(query_marks)


def matmul(left, right):
    return jnp.dot(left, right, preferred_element_type=jnp.float32)


def left_product(left, right):
    return jnp.einsum("ta,tb->ab", left, right, preferred_element_type=jnp.float32)


def right_product(left, right):
    return jnp.einsum("ta,ba->tb", left, right, preferred_element_type=jnp.float32)


def column_sum(value):
    return jnp.sum(value.astype(jnp.float32), axis=0)


def gelu_slope(value):
    cumulative = 0.5 * (1.0 + lax.erf(value * ROOT_HALF))
    return cumulative + value * jnp.exp(-0.5 * value * value) * INV_ROOT_TWO_PI


def norm_forward(value, gain_row, shift_row):
    middle = jnp.mean(value, axis=-1, keepdims=True)
    centred = value - middle
    spread = jnp.mean(centred * centred, axis=-1, keepdims=True)
    inverse = lax.rsqrt(spread + EPSILON)
    normed = centred * inverse
    return (normed * gain_row + shift_row, normed, inverse)


def norm_backward(incoming, normed, inverse, gain_row):
    scaled = incoming * gain_row
    centred = (
        scaled
        - jnp.mean(scaled, axis=-1, keepdims=True)
        - normed * jnp.mean(scaled * normed, axis=-1, keepdims=True)
    )
    return (inverse * centred, jnp.sum(incoming * normed, axis=0), jnp.sum(incoming, axis=0))


MESH = pl.DeviceIdType.MESH
ANY = pl.BlockSpec(memory_space=pltpu.HBM)
VMEM = pl.BlockSpec(memory_space=pltpu.VMEM)
SMEM = pl.BlockSpec(memory_space=pltpu.SMEM)
DMA = pltpu.SemaphoreType.DMA


def across(place, offset):
    if offset == 1:
        return place + 1 - 2 * lax.rem(place, 2)
    if offset == 2:
        return lax.rem(place + 2, 4)
    return 3 - place


def remote(src, dst, sends, recvs, where):
    return pltpu.make_async_remote_copy(
        src_ref=src, dst_ref=dst, send_sem=sends, recv_sem=recvs, device_id=where, device_id_type=MESH)


def greet(grp_count, wa_count, plane=True, groups=True, rows=True):
    barrier = pltpu.get_barrier_semaphore()
    grp, pln, wa = lax.axis_index("grp"), lax.axis_index("pln"), lax.axis_index("wa")

    def hello(where):
        pl.semaphore_signal(barrier, inc=1, device_id=where, device_id_type=MESH)

    count = 0
    if plane:
        for offset in (1, 2, 3):
            hello({"pln": across(pln, offset)})
        count += 3
    if rows:
        for offset in range(1, wa_count):
            hello({"wa": lax.rem(wa + offset, wa_count)})
        count += wa_count - 1
    if groups:
        @pl.when(grp > 0)
        def _():
            hello({"grp": grp - 1})

        @pl.when(grp < grp_count - 1)
        def _():
            hello({"grp": grp + 1})

        count = count + jnp.where(grp > 0, 1, 0) + jnp.where(grp < grp_count - 1, 1, 0)
    pl.semaphore_wait(barrier, count)


class Rows:
    def __init__(self, shard, full, sems, index, wa_count):
        self.shard, self.full, self.sems, self.index, self.wa_count = shard, full, sems, index, wa_count
        self.size = shard.shape[0]
        self.half = self.size // 2
        self.wa, self.pln = lax.axis_index("wa"), lax.axis_index("pln")
        self.core = lax.rem(self.pln, 2)

    def part(self, owner, core):
        return pl.ds(pl.multiple_of(owner * self.size + core * self.half, 16), self.half)

    def keep(self):
        own = pl.ds(pl.multiple_of(self.wa * self.size, 16), self.size)
        return pltpu.make_async_copy(self.shard, self.full.at[own], self.sems.at[0, self.index, 0])

    def push(self, offset):
        mine = pl.ds(pl.multiple_of(self.core * self.half, 16), self.half)
        return remote(self.shard.at[mine], self.full.at[self.part(self.wa, self.core)],
                      self.sems.at[1, self.index, offset - 1], self.sems.at[2, self.index, offset - 1],
                      {"wa": lax.rem(self.wa + offset, self.wa_count)})

    def hand(self, offset):
        owner = lax.rem(self.wa + self.wa_count - offset, self.wa_count)
        spot = self.full.at[self.part(owner, self.core)]
        return remote(spot, spot, self.sems.at[3, self.index, offset - 1], self.sems.at[4, self.index, offset - 1],
                      {"pln": across(self.pln, 1)})

    def begin(self):
        self.keep().start()
        for offset in range(1, self.wa_count):
            self.push(offset).start()

    def pass_on(self):
        for offset in range(1, self.wa_count):
            self.push(offset).wait_recv()
            self.hand(offset).start()

    def arrived(self):
        self.keep().wait()
        for offset in range(1, self.wa_count):
            self.hand(offset).wait_recv()

    def finish(self):
        for offset in range(1, self.wa_count):
            self.push(offset).wait_send()
            self.hand(offset).wait_send()


class Line:
    def __init__(self, full, sems, grp_count, reach, block):
        self.full, self.sems, self.count, self.reach, self.block = full, sems, grp_count, reach, block
        self.grp = lax.axis_index("grp")

    def rows(self, owner, block):
        return pl.ds(pl.multiple_of((owner * PLANE + block) * self.block, 16), self.block)

    def copy(self, side, step, block, source=None):
        toward = 1 if side == 0 else -1
        owner = self.grp - toward * (step - 1)
        spot = self.full.at[self.rows(owner, block)]
        return remote(spot if source is None else source, spot, self.sems.at[0, side, step - 1, block],
                      self.sems.at[1, side, step - 1, block], {"grp": self.grp + toward})

    def sends(self, side, step):
        if side == 0:
            return jnp.logical_and(self.grp - step + 1 >= 0, self.grp + 1 < self.count)
        return jnp.logical_and(self.grp + step - 1 < self.count, self.grp - 1 >= 0)

    def receives(self, side, step):
        return self.grp - step >= 0 if side == 0 else self.grp + step < self.count

    def send(self, step, block, source=None):
        for side in (0, 1):
            @pl.when(self.sends(side, step))
            def _():
                self.copy(side, step, block, source).start()

    def arrival(self, side, step, block):
        toward = 1 if side == 0 else -1
        spot = self.full.at[self.rows(self.grp - toward * step, block)]
        return remote(spot, spot, self.sems.at[0, side, step - 1, block], self.sems.at[1, side, step - 1, block],
                      {"grp": self.grp - toward})

    def forward(self, step):
        for block in range(PLANE):
            for side in (0, 1):
                @pl.when(self.receives(side, step))
                def _():
                    self.arrival(side, step, block).wait_recv()

                    if step < self.reach:
                        @pl.when(self.sends(side, step + 1))
                        def _():
                            self.copy(side, step + 1, block).start()

    def finish(self, source=None):
        for step in range(1, self.reach + 1):
            for block in range(PLANE):
                for side in (0, 1):
                    @pl.when(self.sends(side, step))
                    def _():
                        self.copy(side, step, block, source[block] if source and step == 1 else None).wait_send()


class Swap:
    def __init__(self, src, dst, sems):
        self.src, self.dst, self.sems = src, dst, sems
        self.pln = lax.axis_index("pln")

    def copy(self, offset):
        peer = across(self.pln, offset)
        return remote(self.src(peer), self.dst(self.pln), self.sems.at[0, offset], self.sems.at[1, offset], {"pln": peer})

    def keep(self):
        return pltpu.make_async_copy(self.src(self.pln), self.dst(self.pln), self.sems.at[0, 0])

    def begin(self):
        for offset in (2, 3, 1):
            self.copy(offset).start()
        self.keep().start()

    def arrived(self, offset):
        self.keep().wait() if offset == 0 else self.copy(offset).wait_recv()

    def finish(self):
        for offset in (1, 2, 3):
            self.copy(offset).wait_send()


VEC_ORDER = ("self_query_bias", "self_value_bias", "cross_value_bias", "self_out_bias", "norm_one_gain", "norm_one_shift",
             "cross_query_bias", "cross_out_bias", "norm_two_gain", "norm_two_shift", "expand_bias", "shrink_bias",
             "norm_three_gain", "norm_three_shift")


def pack_vectors(vecs):
    parts = []
    for v in vecs:
        width = min(128, v.shape[0])
        rows = v.reshape(-1, width)
        parts.append(jnp.pad(rows, ((0, 0), (0, 128 - width))))
    pack = jnp.concatenate(parts)
    return jnp.pad(pack, ((0, -pack.shape[0] % 16), (0, 0)))


def vector_row(pack_ref, wa_count, start, length):
    width = min(128, length)
    pieces = []
    for wa in range(wa_count):
        for row in range(length // width):
            pieces.append(pack_ref[wa, start + row : start + row + 1, :width].astype(jnp.float32))
    return jnp.concatenate(pieces, axis=1)


def split_pairs(value, buffer, column):
    for pair in range(PLANE):
        buffer[pair, :, column : column + 128] = value[:, pair * 128 : pair * 128 + 128]


def opening_kernel(grp_count, wa_count, reach, count, vec_at, content_ref, query_ref, encoder_ref, vec_ref, *refs):
    shards = refs[:count]
    fulls = refs[count : 2 * count]
    vec_out, q_out, kv_out, kv2_out = refs[2 * count : 2 * count + 4]
    held, vec_all, kvbuf, kvbuf2, qbuf, row_sems, vec_sems, line_sems, swap_sems, out_sems = refs[2 * count + 4 :]
    grp, pln, wa = lax.axis_index("grp"), lax.axis_index("pln"), lax.axis_index("wa")
    tok = content_ref.shape[0]
    gathers = [Rows(shards[i], held.at[i] if i < 5 else fulls[i], row_sems, i, wa_count) for i in range(count)]
    greet(grp_count, wa_count)
    vec_keep = pltpu.make_async_copy(vec_ref, vec_all.at[wa], vec_sems.at[0, 0])
    vec_keep.start()
    pushes = [remote(vec_ref, vec_all.at[wa], vec_sems.at[0, o], vec_sems.at[1, o], {"wa": lax.rem(wa + o, wa_count)})
              for o in range(1, wa_count)]
    for g in gathers[:2]:
        g.begin()
    for p in pushes:
        p.start()
    for g in gathers[:2]:
        g.pass_on()
    for g in gathers[2:5]:
        g.begin()
    vec_keep.wait()
    for p in pushes:
        p.wait_recv()
    for g in gathers[:2]:
        g.arrived()
    content = content_ref[...]
    split_pairs(matmul(content, held[0]).astype(jnp.bfloat16), kvbuf, 0)
    row = lambda i: vector_row(vec_all, wa_count, *vec_at[i])
    split_pairs((matmul(content, held[1]) + row(1)).astype(jnp.bfloat16), kvbuf, 128)
    line = Line(kv_out, line_sems, grp_count, reach, tok)
    spot = lambda ref: lambda p: ref.at[pl.ds(pl.multiple_of((grp * PLANE + p) * tok, 16), tok)]
    swap = Swap(lambda p: kvbuf.at[p], spot(kv_out), swap_sems.at[0])
    swap.begin()
    line.send(1, pln, kvbuf.at[pln])
    swap.arrived(1)
    line.send(1, across(pln, 1))
    for g in gathers[2:5]:
        g.pass_on()
    for g in gathers[5:]:
        g.begin()
    for offset in (2, 3):
        swap.arrived(offset)
        line.send(1, across(pln, offset))
    for g in gathers[2:5]:
        g.arrived()
    outs = [pltpu.make_async_copy(held.at[i], fulls[i], out_sems.at[i]) for i in range(5)]
    for o in outs:
        o.start()
    vec_save = pltpu.make_async_copy(vec_all, vec_out, out_sems.at[5])
    vec_save.start()
    query = (matmul(query_ref[...], held[2]) + row(0)).astype(jnp.bfloat16)
    query = query * 0.125
    for pair in range(PLANE):
        qbuf[pair] = query[:, pair * 128 : pair * 128 + 128]
    place = lambda p: q_out.at[pl.ds(pl.multiple_of(p * tok, 16), tok)]
    swap_q = Swap(lambda p: qbuf.at[p], place, swap_sems.at[1])
    swap_q.begin()
    encoder = encoder_ref[...]
    split_pairs(matmul(encoder, held[3]).astype(jnp.bfloat16), kvbuf2, 0)
    split_pairs((matmul(encoder, held[4]) + row(2)).astype(jnp.bfloat16), kvbuf2, 128)
    place2 = lambda p: kv2_out.at[pl.ds(pl.multiple_of(p * tok, 16), tok)]
    swap_2 = Swap(lambda p: kvbuf2.at[p], place2, swap_sems.at[2])
    swap_2.begin()
    for step in range(1, reach + 1):
        line.forward(step)
    swap.arrived(0)
    for s in (swap_q, swap_2):
        for offset in range(4):
            s.arrived(offset)
    for g in gathers[5:]:
        g.pass_on()
    for g in gathers[5:]:
        g.arrived()
    for g in gathers:
        g.finish()
    for p in pushes:
        p.wait_send()
    for o in outs:
        o.wait()
    vec_save.wait()
    line.finish()
    for s in (swap, swap_q, swap_2):
        s.finish()


def run_opening(grp_count, wa_count, content, query, encoder, vecs, mats, vec_at):
    tok = content.shape[0]
    reach = min(grp_count - 1, (DOCLEN + PLANE * tok - 2) // (PLANE * tok))
    count = len(mats)
    low = jnp.bfloat16
    shape = lambda *s: jax.ShapeDtypeStruct(s, low)
    out_shape = [shape(m.shape[0] * wa_count, m.shape[1]) for m in mats]
    out_shape += [shape(wa_count, *vecs.shape), shape(PLANE * tok, 128), shape(grp_count * PLANE * tok, 256),
                  shape(PLANE * tok, 256)]
    return pl.pallas_call(
        functools.partial(opening_kernel, grp_count, wa_count, reach, count, vec_at),
        out_shape=tuple(out_shape),
        in_specs=[VMEM] * 4 + [ANY] * count,
        out_specs=tuple([ANY] * len(out_shape)),
        scratch_shapes=[
            pltpu.VMEM((5, 512, 512), low), pltpu.VMEM((wa_count,) + vecs.shape, low), pltpu.VMEM((PLANE, tok, 256), low),
            pltpu.VMEM((PLANE, tok, 256), low), pltpu.VMEM((PLANE, tok, 128), low),
            DMA((5, count, max(1, wa_count - 1))), DMA((2, wa_count)), DMA((2, 2, reach, PLANE)), DMA((3, 2, 4)), DMA((6,))],
        compiler_params=pltpu.CompilerParams(collective_id=1, has_side_effects=True, vmem_limit_bytes=60 << 20),
    )(content, query, encoder, vecs, *mats)


def flat_pairs(buffer):
    return jnp.concatenate([buffer[p] for p in range(PLANE)], axis=1)


def middle_kernel(grp_count, wa_count, reach, vec_at, attended_ref, query_ref, out_mat_ref, query_mat_ref, vec_ref,
                  kv_own_ref, expand_ref, shrink_ref,
                  hidden_ref, normed_ref, inverse_ref, mixed_ref, q_out, kv_out, expand_full, shrink_full,
                  sendbuf, mixbuf, qbuf, row_sems, line_sems, swap_sems, keep_sem):
    grp, pln = lax.axis_index("grp"), lax.axis_index("pln")
    tok = query_ref.shape[0]
    gathers = [Rows(expand_ref, expand_full, row_sems, 0, wa_count), Rows(shrink_ref, shrink_full, row_sems, 1, wa_count)]
    for p in range(PLANE):
        sendbuf[p] = attended_ref[p * tok : p * tok + tok, :].astype(jnp.bfloat16)
    greet(grp_count, wa_count)
    swap = Swap(lambda p: sendbuf.at[p], lambda p: mixbuf.at[p], swap_sems.at[0])
    swap.begin()
    line = Line(kv_out, line_sems, grp_count, reach, tok)
    sources = [kv_own_ref.at[pl.ds(b * tok, tok)] for b in range(PLANE)]
    for b in range(PLANE):
        line.send(1, b, sources[b])
    for g in gathers:
        g.begin()
    whole = pl.ds(pl.multiple_of(grp * PLANE * tok, 16), PLANE * tok)
    keep = pltpu.make_async_copy(kv_own_ref, kv_out.at[whole], keep_sem)
    keep.start()
    row = lambda i: vector_row(vec_ref, wa_count, *vec_at[i])
    for offset in range(4):
        swap.arrived(offset)
    mixed = flat_pairs(mixbuf)
    mixed_ref[...] = mixed
    value = query_ref[...].astype(jnp.float32) + matmul(mixed, out_mat_ref[...]) + row(3)
    hidden, normed, inverse = norm_forward(value, row(4), row(5))
    hidden_ref[...] = hidden
    normed_ref[...] = normed
    inverse_ref[...] = jnp.broadcast_to(inverse, inverse_ref.shape)
    query = (matmul(hidden.astype(jnp.bfloat16), query_mat_ref[...]) + row(6)).astype(jnp.bfloat16) * 0.125
    for pair in range(PLANE):
        qbuf[pair] = query[:, pair * 128 : pair * 128 + 128]
    place = lambda p: q_out.at[pl.ds(pl.multiple_of(p * tok, 16), tok)]
    swap_q = Swap(lambda p: qbuf.at[p], place, swap_sems.at[1])
    swap_q.begin()
    line.forward(1)
    for g in gathers:
        g.pass_on()
    for step in range(2, reach + 1):
        line.forward(step)
    for offset in range(4):
        swap_q.arrived(offset)
    for g in gathers:
        g.arrived()
    for g in gathers:
        g.finish()
    line.finish(sources)
    keep.wait()
    swap.finish()
    swap_q.finish()


def run_middle(grp_count, wa_count, attended, query, out_mat, query_mat, vecs, vec_at, kv_own, expand, shrink):
    tok = query.shape[0]
    reach = min(grp_count - 1, (DOCLEN + PLANE * tok - 2) // (PLANE * tok))
    low, full = jnp.bfloat16, jnp.float32
    shape = jax.ShapeDtypeStruct
    return pl.pallas_call(
        functools.partial(middle_kernel, grp_count, wa_count, reach, vec_at),
        out_shape=(shape((tok, 512), full), shape((tok, 512), full), shape((tok, 128), full), shape((tok, 512), low),
                   shape((PLANE * tok, 128), low), shape((grp_count * PLANE * tok, 256), low),
                   shape((expand.shape[0] * wa_count, expand.shape[1]), low),
                   shape((shrink.shape[0] * wa_count, shrink.shape[1]), low)),
        in_specs=[VMEM] * 5 + [ANY] * 3,
        out_specs=tuple([VMEM] * 4 + [ANY] * 4),
        scratch_shapes=[
            pltpu.VMEM((PLANE, tok, 128), low), pltpu.VMEM((PLANE, tok, 128), low), pltpu.VMEM((PLANE, tok, 128), low),
            DMA((5, 2, max(1, wa_count - 1))), DMA((2, 2, reach, PLANE)), DMA((2, 2, 4)), DMA],
        compiler_params=pltpu.CompilerParams(collective_id=2, has_side_effects=True, vmem_limit_bytes=60 << 20),
    )(attended, query, out_mat, query_mat, vecs, kv_own, expand, shrink)


def swap_kernel(inverse, in_ref, out_ref, sendbuf, getbuf, swap_sems):
    tok = getbuf.shape[1]
    for p in range(PLANE):
        if inverse:
            sendbuf[p] = in_ref[p * tok : p * tok + tok, :].astype(jnp.bfloat16)
        else:
            sendbuf[p] = in_ref[:, p * 128 : p * 128 + 128].astype(jnp.bfloat16)
    greet(1, 1, groups=False, rows=False)
    swap = Swap(lambda p: sendbuf.at[p], lambda p: getbuf.at[p], swap_sems)
    swap.begin()
    for offset in range(4):
        swap.arrived(offset)
    for p in range(PLANE):
        if inverse:
            out_ref[:, p * 128 : p * 128 + 128] = getbuf[p]
        else:
            out_ref[p * tok : p * tok + tok, :] = getbuf[p]
    swap.finish()


def run_swap(inverse, value, ident):
    tok = value.shape[0] // PLANE if inverse else value.shape[0]
    low = jnp.bfloat16
    return pl.pallas_call(
        functools.partial(swap_kernel, inverse),
        out_shape=jax.ShapeDtypeStruct((tok, 512) if inverse else (PLANE * tok, 128), low),
        in_specs=[VMEM], out_specs=VMEM,
        scratch_shapes=[pltpu.VMEM((PLANE, tok, 128), low), pltpu.VMEM((PLANE, tok, 128), low), DMA((2, 4))],
        compiler_params=pltpu.CompilerParams(collective_id=ident, has_side_effects=True, vmem_limit_bytes=60 << 20),
    )(value)


def to_pairs(value):
    return lax.all_to_all(value, "pln", 1, 0, tiled=True)


def to_tokens(value):
    return lax.all_to_all(value, "pln", 0, 1, tiled=True)


def return_pairs(keys, values):
    both = jnp.concatenate([keys, values], axis=1).astype(jnp.bfloat16)
    mine = lax.psum_scatter(both, "grp", scatter_dimension=0, tiled=True).astype(jnp.bfloat16)
    return to_tokens(mine[:, :128]), to_tokens(mine[:, 128:])


def reduce_grads(grads):
    wa = lax.axis_size("wa")
    mats = [g.astype(jnp.bfloat16).reshape(wa, -1, 512) for g in grads if g.ndim == 2]
    vecs = [g.reshape(wa, -1) for g in grads if g.ndim == 1]
    pack = jnp.concatenate(mats, axis=1)
    mine = lax.psum_scatter(pack, "wa", scatter_dimension=0, tiled=False)
    total = lax.psum(mine, ("grp", "pln")).astype(jnp.float32)
    line = lax.psum(jnp.concatenate(vecs, axis=1).astype(jnp.bfloat16), ("grp", "pln", "wa")).astype(jnp.float32)
    line = lax.dynamic_index_in_dim(line, lax.axis_index("wa"), 0, False)
    out, at, vat = [], 0, 0
    for g in grads:
        if g.ndim == 2:
            n = g.size // wa // 512
            out.append(total[at : at + n].reshape(g.shape[0] // wa, g.shape[1]))
            at += n
        else:
            n = g.size // wa
            out.append(line[vat : vat + n])
            vat += n
    return tuple(out)


def shards(
    query_in,
    content_in,
    encoder_in,
    out_grad,
    document_lengths,
    key_ranks,
    query_limits,
    self_query_weight,
    self_query_bias,
    self_key_weight,
    self_value_weight,
    self_value_bias,
    self_out_weight,
    self_out_bias,
    norm_one_gain,
    norm_one_shift,
    cross_query_weight,
    cross_query_bias,
    cross_key_weight,
    cross_value_weight,
    cross_value_bias,
    cross_out_weight,
    cross_out_bias,
    norm_two_gain,
    norm_two_shift,
    expand_weight,
    expand_bias,
    shrink_weight,
    shrink_bias,
    norm_three_gain,
    norm_three_shift,
):
    grp_count = lax.axis_size("grp")
    own = lax.axis_index("grp")[None].astype(jnp.int32)
    lens = document_lengths
    tok = query_in.shape[1]
    rows = tok * PLANE
    row_at = lax.axis_index("grp") * rows
    cross_keys, cross_marks = mark_tables(lens[0], key_ranks[0], query_limits[0], row_at, rows, False)
    self_keys, self_marks = mark_tables(lens[0], key_ranks[0], query_limits[0], row_at, rows, True)
    wa_count = lax.axis_size("wa")
    vectors = (self_query_bias, self_value_bias, cross_value_bias, self_out_bias, norm_one_gain, norm_one_shift,
        cross_query_bias, cross_out_bias, norm_two_gain, norm_two_shift, expand_bias, shrink_bias, norm_three_gain,
        norm_three_shift)
    vec_at, at = [], 0
    for v in vectors:
        vec_at.append((at, v.shape[0]))
        at += v.shape[0] // min(128, v.shape[0])
    vec_at = tuple(vec_at)
    mats = (self_key_weight, self_value_weight, self_query_weight, cross_key_weight, cross_value_weight, self_out_weight,
        cross_query_weight, cross_out_weight)
    (self_key_matrix, self_value_mat, self_query_mat, cross_key_matrix, cross_value_mat, self_out_mat, cross_query_mat,
        cross_out_mat, vec_all, pair_one, kv_one, kv_two_own) = run_opening(
        grp_count, wa_count, content_in[0], query_in[0], encoder_in[0], pack_vectors(vectors), mats, vec_at)
    lines = [jnp.concatenate([vec_all[w, s : s + n // min(n, 128), : min(n, 128)].reshape(-1) for w in range(wa_count)])
        .astype(jnp.float32) for s, n in vec_at]
    (self_query_vec, self_value_vec, cross_value_vec, self_out_vec, gain_one, shift_one, cross_query_vec, cross_out_vec,
        gain_two, shift_two, expand_vec, shrink_vec, gain_three, shift_three) = lines
    source = query_in[0]
    content_states = content_in[0]
    encoder_output = encoder_in[0]
    cotangent = out_grad[0].astype(jnp.float32)
    keys_one, values_one = kv_one[:, :128], kv_one[:, 128:]
    attended_one, total_one = attend_forward(True, lens, own, pair_one, self_marks, keys_one, values_one, self_keys)
    hidden_one, normed_one, inverse_one, mixed_one, pair_two, kv_two, expand_mat, shrink_mat = run_middle(
        grp_count, wa_count, attended_one, source, self_out_mat, cross_query_mat, vec_all, vec_at, kv_two_own,
        expand_weight, shrink_weight)
    inverse_one = inverse_one[:, :1]
    hidden_one_low = hidden_one.astype(jnp.bfloat16)
    keys_two, values_two = kv_two[:, :128], kv_two[:, 128:]
    attended_two, total_two = attend_forward(False, lens, own, pair_two, cross_marks, keys_two, values_two, cross_keys)
    mixed_two = run_swap(True, attended_two, 3)
    hidden_two, normed_two, inverse_two = norm_forward(
        hidden_one + matmul(mixed_two, cross_out_mat) + cross_out_vec, gain_two, shift_two)
    hidden_two_low = hidden_two.astype(jnp.bfloat16)
    expanded = matmul(hidden_two_low, expand_mat) + expand_vec
    activated = jax.nn.gelu(expanded, approximate=False).astype(jnp.bfloat16)
    layer_out, normed_three, inverse_three = norm_forward(
        hidden_two + matmul(activated, shrink_mat) + shrink_vec, gain_three, shift_three)
    back_three, grad_gain_three, grad_shift_three = norm_backward(cotangent, normed_three, inverse_three, gain_three)
    shrink_in_grad = back_three.astype(jnp.bfloat16)
    grad_shrink_mat = left_product(activated, shrink_in_grad)
    grad_shrink_vec = column_sum(shrink_in_grad)
    activated_grad = right_product(shrink_in_grad, shrink_mat)
    expand_grad = (activated_grad * gelu_slope(expanded)).astype(jnp.bfloat16)
    grad_expand_mat = left_product(hidden_two_low, expand_grad)
    grad_expand_vec = column_sum(expand_grad)
    hidden_two_grad = back_three + right_product(expand_grad, expand_mat)
    back_two, grad_gain_two, grad_shift_two = norm_backward(hidden_two_grad, normed_two, inverse_two, gain_two)
    branch_two = back_two.astype(jnp.bfloat16)
    grad_cross_out_mat = left_product(mixed_two, branch_two)
    grad_cross_out_vec = column_sum(branch_two)
    mixed_two_grad = right_product(branch_two, cross_out_mat).astype(jnp.bfloat16)
    dq_two, dk_two, dv_two = attend_backward(False, lens, own, pair_two, cross_marks, keys_two, values_two, cross_keys,
        attended_two, total_two, run_swap(False, mixed_two_grad, 4))
    key_two_low, value_two_low = return_pairs(dk_two, dv_two)
    query_two_low = run_swap(True, dq_two, 6)
    grad_cross_query_mat = left_product(hidden_one_low, query_two_low)
    grad_cross_query_vec = column_sum(query_two_low)
    grad_cross_key_mat = left_product(encoder_output, key_two_low)
    grad_cross_value_mat = left_product(encoder_output, value_two_low)
    grad_cross_value_vec = column_sum(value_two_low)
    encoder_grad = right_product(key_two_low, cross_key_matrix) + right_product(value_two_low, cross_value_mat)
    hidden_one_grad = back_two + right_product(query_two_low, cross_query_mat)
    back_one, grad_gain_one, grad_shift_one = norm_backward(hidden_one_grad, normed_one, inverse_one, gain_one)
    branch_one = back_one.astype(jnp.bfloat16)
    grad_self_out_mat = left_product(mixed_one, branch_one)
    grad_self_out_vec = column_sum(branch_one)
    mixed_one_grad = right_product(branch_one, self_out_mat).astype(jnp.bfloat16)
    dq_one, dk_one, dv_one = attend_backward(True, lens, own, pair_one, self_marks, keys_one, values_one, self_keys,
        attended_one, total_one, run_swap(False, mixed_one_grad, 5))
    key_one_low, value_one_low = return_pairs(dk_one, dv_one)
    query_one_low = run_swap(True, dq_one, 7)
    grad_self_query_mat = left_product(source, query_one_low)
    grad_self_query_vec = column_sum(query_one_low)
    grad_self_key_mat = left_product(content_states, key_one_low)
    grad_self_value_mat = left_product(content_states, value_one_low)
    grad_self_value_vec = column_sum(value_one_low)
    query_grad = back_one + right_product(query_one_low, self_query_mat)
    content_grad = right_product(key_one_low, self_key_matrix) + right_product(value_one_low, self_value_mat)
    grads = reduce_grads((
        grad_self_query_mat, grad_self_query_vec, grad_self_key_mat, grad_self_value_mat, grad_self_value_vec, grad_self_out_mat, grad_self_out_vec, grad_gain_one, grad_shift_one, grad_cross_query_mat, grad_cross_query_vec, grad_cross_key_mat, grad_cross_value_mat, grad_cross_value_vec, grad_cross_out_mat, grad_cross_out_vec, grad_gain_two, grad_shift_two, grad_expand_mat, grad_expand_vec, grad_shrink_mat, grad_shrink_vec, grad_gain_three, grad_shift_three))
    return (layer_out[None], query_grad[None], content_grad[None], encoder_grad[None]) + grads


def solution(mesh):
    ctx, wa = mesh.devices.shape
    mesh = Mesh(mesh.devices.reshape(ctx // PLANE, PLANE, wa), ("grp", "pln", "wa"))
    in_specs = (
        P("wa", ("grp", "pln"), None),
        P("wa", ("grp", "pln"), None),
        P("wa", ("grp", "pln"), None),
        P("wa", ("grp", "pln"), None),
        P("wa", None),
        P("wa", None),
        P("wa", None),
        P("wa", None),
        P("wa"),
        P("wa", None),
        P("wa", None),
        P("wa"),
        P("wa", None),
        P("wa"),
        P("wa"),
        P("wa"),
        P("wa", None),
        P("wa"),
        P("wa", None),
        P("wa", None),
        P("wa"),
        P("wa", None),
        P("wa"),
        P("wa"),
        P("wa"),
        P("wa", None),
        P("wa"),
        P("wa", None),
        P("wa"),
        P("wa"),
        P("wa"),
    )
    out_specs = (
        P("wa", ("grp", "pln"), None),
        P("wa", ("grp", "pln"), None),
        P("wa", ("grp", "pln"), None),
        P("wa", ("grp", "pln"), None),
        P("wa", None),
        P("wa"),
        P("wa", None),
        P("wa", None),
        P("wa"),
        P("wa", None),
        P("wa"),
        P("wa"),
        P("wa"),
        P("wa", None),
        P("wa"),
        P("wa", None),
        P("wa", None),
        P("wa"),
        P("wa", None),
        P("wa"),
        P("wa"),
        P("wa"),
        P("wa", None),
        P("wa"),
        P("wa", None),
        P("wa"),
        P("wa"),
        P("wa"),
    )
    return jax.shard_map(shards, mesh=mesh, in_specs=in_specs, out_specs=out_specs, check_vma=False)
```

```python
import functools
import jax
import jax.numpy as jnp
from jax import lax
from jax.experimental import pallas as pl
from jax.experimental.pallas import tpu as pltpu
from jax.sharding import Mesh
from jax.sharding import PartitionSpec as P

PLANE = 4
DOCLEN = 2048
EPSILON = 1e-05
ROOT_HALF = 0.7071067811865476
INV_ROOT_TWO_PI = 0.3989422804014327
NEGATIVE = -1e29
HIDE = -(2.0 ** 100)
BLOCK = 256
WIDE = 512
STAT = 40


def dot(a, b, ca, cb):
    return lax.dot_general(a, b, (((ca,), (cb,)), ((), ())), preferred_element_type=jnp.float32)


def left_half(shape):
    return lax.broadcasted_iota(jnp.int32, shape, 1) < 64


def spans(lens_ref, first, count):
    low, high, total = 0, 0, 0
    for d in range(lens_ref.shape[1]):
        begin = total
        total = total + lens_ref[0, d]
        low = jnp.where(begin <= first, begin, low)
        high = jnp.where(begin <= first + count - 1, total, high)
    return low, high


def openings(lens_ref, places):
    total, found = 0, places == 0
    for d in range(lens_ref.shape[1] - 1):
        total = total + lens_ref[0, d]
        found = jnp.logical_or(found, places == total)
    return found


def over_blocks(low, high, first, size, step, carry, ranked):
    begin, end = low // size, (high + size - 1) // size
    own = first // size
    skip = 1 if ranked else 0

    def body(index, carry):
        if ranked:
            index = index + jnp.where(index >= own, 1, 0)
        return step(pl.multiple_of(index * size, size), carry)

    carry = lax.fori_loop(begin, end - skip, body, carry)
    if ranked:
        carry = step(pl.multiple_of(own * size, size), carry, True)
    return carry


def forward_kernel(ranked, lens_ref, own_ref, q_ref, qm_ref, k_ref, v_ref, km_ref, o_ref, lse_ref):
    rows = q_ref.shape[0]
    base = own_ref[0] * rows
    half = left_half((BLOCK, 128))
    khalf = left_half((WIDE, 128))
    one = jnp.ones((WIDE, 128), jnp.bfloat16)

    def one_block(block, _):
        start = pl.multiple_of(block * BLOCK, BLOCK)
        first = base + start
        low, high = spans(lens_ref, first, BLOCK)
        q = q_ref[pl.ds(start, BLOCK), :]
        qm = qm_ref[pl.ds(start, BLOCK), :]
        queries = (jnp.where(half, q, qm), jnp.where(half, qm, q))

        def step(at, carry, diagonal=False):
            k = k_ref[pl.ds(at, WIDE), :]
            v = v_ref[pl.ds(at, WIDE), :]
            km = km_ref[pl.ds(at, WIDE), :]
            keys = (jnp.where(khalf, k, km), jnp.where(khalf, km, k))
            values = (jnp.where(khalf, v, one), jnp.where(khalf, one, v))
            scores = [dot(queries[h], keys[h], 1, 1) for h in (0, 1)]
            if diagonal:
                place = first + lax.broadcasted_iota(jnp.int32, (BLOCK, WIDE), 0)
                other = at + lax.broadcasted_iota(jnp.int32, (BLOCK, WIDE), 1)
                column = first + lax.broadcasted_iota(jnp.int32, (BLOCK, 1), 0)
                banned = jnp.where(openings(lens_ref, column), -1, place) == other
                scores = [jnp.where(banned, HIDE, s) for s in scores]
            out = []
            for h in (0, 1):
                peak, acc = carry[h]
                new = jnp.maximum(peak, jnp.max(scores[h], axis=1, keepdims=True))
                p = jnp.exp(scores[h] - new).astype(jnp.bfloat16)
                acc = acc * jnp.exp(peak - new) + dot(p, values[h], 1, 0)
                out.append((new, acc))
            return tuple(out)

        empty = (jnp.full((BLOCK, 1), NEGATIVE, jnp.float32), jnp.zeros((BLOCK, 128), jnp.float32))
        (peak0, acc0), (peak1, acc1) = over_blocks(low, high, first, WIDE, step, (empty, empty), ranked)
        total = jnp.where(half, acc1, acc0)
        mixed = jnp.where(half, acc0, acc1)
        o_ref[pl.ds(start, BLOCK), :] = mixed / pltpu.roll(total, 64, 1)
        lse_ref[pl.ds(start, BLOCK), :] = jnp.where(half, peak1, peak0) + jnp.log(total)
        return 0

    lax.fori_loop(0, rows // BLOCK, one_block, 0)


def attend_forward(ranked, lens, own, q, qm, k, v, km):
    rows = q.shape[0]
    whole = pl.BlockSpec(memory_space=pltpu.VMEM)
    smem = pl.BlockSpec(memory_space=pltpu.SMEM)
    return pl.pallas_call(
        functools.partial(forward_kernel, ranked),
        out_shape=(jax.ShapeDtypeStruct((rows, 128), jnp.float32),) * 2,
        in_specs=[smem, smem] + [whole] * 5,
        out_specs=(whole, whole),
        compiler_params=pltpu.CompilerParams(vmem_limit_bytes=60 << 20),
    )(lens, own, q, qm, k, v, km)


def with_stat(marks, stat, lane, at):
    high = stat.astype(jnp.bfloat16)
    rest = stat - high.astype(jnp.float32)
    middle = rest.astype(jnp.bfloat16)
    tail = (rest - middle.astype(jnp.float32)).astype(jnp.bfloat16)
    side = jnp.where(lane == at, high, jnp.where(lane == at + 1, middle, jnp.where(lane == at + 2, tail, marks)))
    return side


def backward_kernel(ranked, lens_ref, own_ref, q_ref, qm_ref, k_ref, v_ref, km_ref, o_ref, lse_ref, do_ref,
                    dq_ref, dkv_ref, own_dkv_ref, dk_ref, dv_ref):
    rows = q_ref.shape[0]
    base = own_ref[0] * rows
    half = left_half((BLOCK, 128))
    lane = lax.broadcasted_iota(jnp.int32, (BLOCK, 128), 1)
    one = jnp.ones((BLOCK, 128), jnp.bfloat16)
    zero = jnp.zeros((BLOCK, 128), jnp.bfloat16)

    def clear(index, _):
        at = pl.multiple_of(index * BLOCK, BLOCK)
        dk_ref[pl.ds(at, BLOCK), :] = jnp.zeros((BLOCK, 128), jnp.float32)
        dv_ref[pl.ds(at, BLOCK), :] = jnp.zeros((BLOCK, 128), jnp.float32)
        return 0

    lax.fori_loop(0, k_ref.shape[0] // BLOCK, clear, 0)

    def one_block(block, _):
        start = pl.multiple_of(block * BLOCK, BLOCK)
        first = base + start
        low, high = spans(lens_ref, first, BLOCK)
        here = pl.ds(start, BLOCK)
        q, qm, do, lse = q_ref[here, :], qm_ref[here, :], do_ref[here, :], lse_ref[here, :]
        shared = do.astype(jnp.float32) * o_ref[here, :]
        delta0 = jnp.sum(jnp.where(half, shared, 0.0), axis=1, keepdims=True)
        delta1 = jnp.sum(jnp.where(half, 0.0, shared), axis=1, keepdims=True)
        side = with_stat(qm, lse, lane % 64, STAT)
        queries = (jnp.where(half, q, side), jnp.where(half, side, q))
        side = with_stat(zero, -jnp.where(half, delta1, delta0), lane % 64, STAT)
        grads = (jnp.where(half, do, side), jnp.where(half, side, do))

        def step(at, carry, diagonal=False):
            there = pl.ds(at, BLOCK)
            k, v, km = k_ref[there, :], v_ref[there, :], km_ref[there, :]
            keys = (jnp.where(half, k, km), jnp.where(half, km, k))
            values = (jnp.where(half, v, one), jnp.where(half, one, v))
            scores = [dot(keys[h], queries[h], 1, 1) for h in (0, 1)]
            if diagonal:
                other = first + lax.broadcasted_iota(jnp.int32, (BLOCK, BLOCK), 0)
                row = first + lax.broadcasted_iota(jnp.int32, (1, BLOCK), 1)
                banned = other == jnp.where(openings(lens_ref, row), -1, row)
                scores = [jnp.where(banned, HIDE, s) for s in scores]
            dvs, dks, dqs = [], [], []
            for h in (0, 1):
                p = jnp.exp(scores[h])
                dp = dot(values[h], grads[h], 1, 1)
                ds = (p * dp).astype(jnp.bfloat16)
                dvs.append(dot(p.astype(jnp.bfloat16), do, 1, 0))
                dks.append(dot(ds, q, 1, 0))
                dqs.append(dot(ds, k, 0, 0))
            dv_ref[there, :] += jnp.where(half, dvs[0], dvs[1])
            dk_ref[there, :] += jnp.where(half, dks[0], dks[1])
            return carry + jnp.where(half, dqs[0], dqs[1])

        dq = over_blocks(low, high, first, BLOCK, step, jnp.zeros((BLOCK, 128), jnp.float32), ranked)
        dq_ref[here, :] = (dq * 0.125).astype(dq_ref.dtype)
        return 0

    lax.fori_loop(0, rows // BLOCK, one_block, 0)

    def save(index, _):
        there = pl.ds(pl.multiple_of(index * BLOCK, BLOCK), BLOCK)
        dkv_ref[there, :128] = dk_ref[there, :].astype(jnp.bfloat16)
        dkv_ref[there, 128:] = dv_ref[there, :].astype(jnp.bfloat16)
        return 0

    lax.fori_loop(0, k_ref.shape[0] // BLOCK, save, 0)
    mine = pl.ds(pl.multiple_of(base, BLOCK), rows)
    own_dkv_ref[:, :128] = dk_ref[mine, :]
    own_dkv_ref[:, 128:] = dv_ref[mine, :]


def attend_backward(ranked, lens, own, q, qm, k, v, km, o, lse, do):
    rows, keys = q.shape[0], k.shape[0]
    whole = pl.BlockSpec(memory_space=pltpu.VMEM)
    smem = pl.BlockSpec(memory_space=pltpu.SMEM)
    return pl.pallas_call(
        functools.partial(backward_kernel, ranked),
        out_shape=(jax.ShapeDtypeStruct((rows, 128), jnp.bfloat16),) + (
            jax.ShapeDtypeStruct((keys, 256), jnp.bfloat16), jax.ShapeDtypeStruct((rows, 256), jnp.float32)),
        in_specs=[smem, smem] + [whole] * 8,
        out_specs=(whole, whole, whole),
        scratch_shapes=[pltpu.VMEM((keys, 128), jnp.float32)] * 2,
        compiler_params=pltpu.CompilerParams(vmem_limit_bytes=60 << 20),
    )(lens, own, q, qm, k, v, km, o, lse, do)


def mark_tables(lengths, ranks, limits, offset, rows, ranked):
    total = ranks.shape[0]
    docs = lengths.shape[0]
    ends = jnp.stack([jnp.sum(lengths[: d + 1]) for d in range(docs)])
    begins = jnp.stack([jnp.sum(lengths[:d]) for d in range(docs)])
    place = lax.broadcasted_iota(jnp.int32, (total, 64), 0)
    lane = lax.broadcasted_iota(jnp.int32, (total, 64), 1)
    doc = jnp.zeros((total, 1), jnp.int32)
    is_open = jnp.zeros((total, 1), bool)
    for d in range(docs):
        doc = doc + (place[:, :1] >= ends[d]).astype(jnp.int32)
        is_open = jnp.logical_or(is_open, place[:, :1] == begins[d])
    rank = jnp.where(is_open, 0, ranks[:, None] + 1)
    key_marks = jnp.where(lane == doc, 1.0, 0.0)
    if ranked:
        key_marks = key_marks + jnp.where(lane == rank + 16, 1.0, 0.0)
    key_marks = key_marks - jnp.where(jnp.logical_and(lane >= STAT, lane < STAT + 3), 1.0, 0.0)
    hide = jnp.where(jnp.logical_and(lane < docs, lane != doc), HIDE, 0.0)
    if ranked:
        hide = hide + jnp.where(jnp.logical_and(lane >= 16, jnp.logical_and(lane < 33, lane - 17 >= limits[:, None])), HIDE, 0.0)
    query_marks = lax.dynamic_slice_in_dim(hide, offset, rows, 0)
    both = lambda m: jnp.concatenate([m, m], axis=1).astype(jnp.bfloat16)
    return both(key_marks), both(query_marks)


def matmul(left, right):
    return jnp.dot(left, right, preferred_element_type=jnp.float32)


def left_product(left, right):
    return jnp.einsum("ta,tb->ab", left, right, preferred_element_type=jnp.float32)


def right_product(left, right):
    return jnp.einsum("ta,ba->tb", left, right, preferred_element_type=jnp.float32)


def column_sum(value):
    return jnp.sum(value.astype(jnp.float32), axis=0)


def gelu_slope(value):
    cumulative = 0.5 * (1.0 + lax.erf(value * ROOT_HALF))
    return cumulative + value * jnp.exp(-0.5 * value * value) * INV_ROOT_TWO_PI


def norm_forward(value, gain_row, shift_row):
    middle = jnp.mean(value, axis=-1, keepdims=True)
    centred = value - middle
    spread = jnp.mean(centred * centred, axis=-1, keepdims=True)
    inverse = lax.rsqrt(spread + EPSILON)
    normed = centred * inverse
    return (normed * gain_row + shift_row, normed, inverse)


def norm_backward(incoming, normed, inverse, gain_row):
    scaled = incoming * gain_row
    centred = (
        scaled
        - jnp.mean(scaled, axis=-1, keepdims=True)
        - normed * jnp.mean(scaled * normed, axis=-1, keepdims=True)
    )
    return (inverse * centred, jnp.sum(incoming * normed, axis=0), jnp.sum(incoming, axis=0))


MESH = pl.DeviceIdType.MESH
ANY = pl.BlockSpec(memory_space=pltpu.HBM)
VMEM = pl.BlockSpec(memory_space=pltpu.VMEM)
SMEM = pl.BlockSpec(memory_space=pltpu.SMEM)
DMA = pltpu.SemaphoreType.DMA


def across(place, offset):
    if offset == 1:
        return place + 1 - 2 * lax.rem(place, 2)
    if offset == 2:
        return lax.rem(place + 2, 4)
    return 3 - place


def remote(src, dst, sends, recvs, where):
    return pltpu.make_async_remote_copy(
        src_ref=src, dst_ref=dst, send_sem=sends, recv_sem=recvs, device_id=where, device_id_type=MESH)


def greet(grp_count, wa_count, plane=True, groups=True, rows=True):
    barrier = pltpu.get_barrier_semaphore()
    grp, pln, wa = lax.axis_index("grp"), lax.axis_index("pln"), lax.axis_index("wa")

    def hello(where):
        pl.semaphore_signal(barrier, inc=1, device_id=where, device_id_type=MESH)

    count = 0
    if plane:
        for offset in (1, 2, 3):
            hello({"pln": across(pln, offset)})
        count += 3
    if rows:
        for offset in range(1, wa_count):
            hello({"wa": lax.rem(wa + offset, wa_count)})
        count += wa_count - 1
    if groups:
        @pl.when(grp > 0)
        def _():
            hello({"grp": grp - 1})

        @pl.when(grp < grp_count - 1)
        def _():
            hello({"grp": grp + 1})

        count = count + jnp.where(grp > 0, 1, 0) + jnp.where(grp < grp_count - 1, 1, 0)
    pl.semaphore_wait(barrier, count)


class Rows:
    def __init__(self, shard, full, sems, index, wa_count, stage=None):
        self.shard, self.full, self.sems, self.index, self.wa_count = shard, full, sems, index, wa_count
        self.stage = stage
        self.size = shard.shape[0]
        self.half = self.size // 2
        self.wa, self.pln = lax.axis_index("wa"), lax.axis_index("pln")
        self.core = lax.rem(self.pln, 2)

    def part(self, owner, core):
        return pl.ds(pl.multiple_of(owner * self.size + core * self.half, 16), self.half)

    def keep(self):
        own = pl.ds(pl.multiple_of(self.wa * self.size, 16), self.size)
        source = self.shard if self.stage is None else self.stage
        return pltpu.make_async_copy(source, self.full.at[own], self.sems.at[0, self.index, 0])

    def load(self):
        return pltpu.make_async_copy(self.shard, self.stage, self.sems.at[0, self.index, 0])

    def push(self, offset):
        mine = pl.ds(pl.multiple_of(self.core * self.half, 16), self.half)
        return remote(self.shard.at[mine], self.full.at[self.part(self.wa, self.core)],
                      self.sems.at[1, self.index, offset - 1], self.sems.at[2, self.index, offset - 1],
                      {"wa": lax.rem(self.wa + offset, self.wa_count)})

    def hand(self, offset):
        owner = lax.rem(self.wa + self.wa_count - offset, self.wa_count)
        spot = self.full.at[self.part(owner, self.core)]
        return remote(spot, spot, self.sems.at[3, self.index, offset - 1], self.sems.at[4, self.index, offset - 1],
                      {"pln": across(self.pln, 1)})

    def begin(self):
        if self.stage is None:
            self.keep().start()
        else:
            self.load().start()
        for offset in range(1, self.wa_count):
            self.push(offset).start()

    def staged(self):
        self.load().wait()
        self.keep().start()

    def pass_on(self):
        for offset in range(1, self.wa_count):
            self.push(offset).wait_recv()
            self.hand(offset).start()

    def arrived(self):
        self.keep().wait()
        for offset in range(1, self.wa_count):
            self.hand(offset).wait_recv()

    def finish(self):
        for offset in range(1, self.wa_count):
            self.push(offset).wait_send()
            self.hand(offset).wait_send()


class Line:
    def __init__(self, full, sems, grp_count, reach, block):
        self.full, self.sems, self.count, self.reach, self.block = full, sems, grp_count, reach, block
        self.grp = lax.axis_index("grp")

    def rows(self, owner, block):
        return pl.ds(pl.multiple_of((owner * PLANE + block) * self.block, 16), self.block)

    def copy(self, side, step, block, source=None):
        toward = 1 if side == 0 else -1
        owner = self.grp - toward * (step - 1)
        spot = self.full.at[self.rows(owner, block)]
        return remote(spot if source is None else source, spot, self.sems.at[0, side, step - 1, block],
                      self.sems.at[1, side, step - 1, block], {"grp": self.grp + toward})

    def sends(self, side, step):
        if side == 0:
            return jnp.logical_and(self.grp - step + 1 >= 0, self.grp + 1 < self.count)
        return jnp.logical_and(self.grp + step - 1 < self.count, self.grp - 1 >= 0)

    def receives(self, side, step):
        return self.grp - step >= 0 if side == 0 else self.grp + step < self.count

    def send(self, step, block, source=None):
        for side in (0, 1):
            @pl.when(self.sends(side, step))
            def _():
                self.copy(side, step, block, source).start()

    def arrival(self, side, step, block):
        toward = 1 if side == 0 else -1
        spot = self.full.at[self.rows(self.grp - toward * step, block)]
        return remote(spot, spot, self.sems.at[0, side, step - 1, block], self.sems.at[1, side, step - 1, block],
                      {"grp": self.grp - toward})

    def forward(self, step):
        for block in range(PLANE):
            for side in (0, 1):
                @pl.when(self.receives(side, step))
                def _():
                    self.arrival(side, step, block).wait_recv()

                    if step < self.reach:
                        @pl.when(self.sends(side, step + 1))
                        def _():
                            self.copy(side, step + 1, block).start()

    def finish(self, source=None):
        for step in range(1, self.reach + 1):
            for block in range(PLANE):
                for side in (0, 1):
                    @pl.when(self.sends(side, step))
                    def _():
                        self.copy(side, step, block, source[block] if source and step == 1 else None).wait_send()


class Swap:
    def __init__(self, src, dst, sems):
        self.src, self.dst, self.sems = src, dst, sems
        self.pln = lax.axis_index("pln")

    def copy(self, offset):
        peer = across(self.pln, offset)
        return remote(self.src(peer), self.dst(self.pln), self.sems.at[0, offset], self.sems.at[1, offset], {"pln": peer})

    def keep(self):
        return pltpu.make_async_copy(self.src(self.pln), self.dst(self.pln), self.sems.at[0, 0])

    def begin(self):
        for offset in (2, 3, 1):
            self.copy(offset).start()
        self.keep().start()

    def arrived(self, offset):
        self.keep().wait() if offset == 0 else self.copy(offset).wait_recv()

    def finish(self):
        for offset in (1, 2, 3):
            self.copy(offset).wait_send()


VEC_ORDER = ("self_query_bias", "self_value_bias", "cross_value_bias", "self_out_bias", "norm_one_gain", "norm_one_shift",
             "cross_query_bias", "cross_out_bias", "norm_two_gain", "norm_two_shift", "expand_bias", "shrink_bias",
             "norm_three_gain", "norm_three_shift")


def pack_vectors(vecs):
    parts = []
    for v in vecs:
        width = min(128, v.shape[0])
        rows = v.reshape(-1, width)
        parts.append(jnp.pad(rows, ((0, 0), (0, 128 - width))))
    pack = jnp.concatenate(parts)
    return jnp.pad(pack, ((0, -pack.shape[0] % 16), (0, 0)))


def vector_row(pack_ref, wa_count, start, length):
    width = min(128, length)
    pieces = []
    for wa in range(wa_count):
        for row in range(length // width):
            pieces.append(pack_ref[wa, start + row : start + row + 1, :width].astype(jnp.float32))
    return jnp.concatenate(pieces, axis=1)


def split_pairs(value, buffer, column):
    for pair in range(PLANE):
        buffer[pair, :, column : column + 128] = value[:, pair * 128 : pair * 128 + 128]


def opening_kernel(grp_count, wa_count, reach, count, vec_at, content_ref, query_ref, encoder_ref, vec_ref, *refs):
    shards = refs[:count]
    fulls = refs[count : 2 * count]
    vec_out, q_out, kv_out, kv2_out = refs[2 * count : 2 * count + 4]
    held, vec_all, kvbuf, kvbuf2, qbuf, row_sems, vec_sems, line_sems, swap_sems, out_sems = refs[2 * count + 4 :]
    grp, pln, wa = lax.axis_index("grp"), lax.axis_index("pln"), lax.axis_index("wa")
    tok = content_ref.shape[0]
    gathers = [Rows(shards[i], held.at[i], row_sems, i, wa_count) for i in range(count)]
    greet(grp_count, wa_count)
    vec_keep = pltpu.make_async_copy(vec_ref, vec_all.at[wa], vec_sems.at[0, 0])
    vec_keep.start()
    pushes = [remote(vec_ref, vec_all.at[wa], vec_sems.at[0, o], vec_sems.at[1, o], {"wa": lax.rem(wa + o, wa_count)})
              for o in range(1, wa_count)]
    for g in gathers[:2]:
        g.begin()
    for p in pushes:
        p.start()
    for g in gathers[:2]:
        g.pass_on()
    for g in gathers[2:5]:
        g.begin()
    vec_keep.wait()
    for p in pushes:
        p.wait_recv()
    for g in gathers[:2]:
        g.arrived()
    content = content_ref[...]
    split_pairs(matmul(content, held[0]).astype(jnp.bfloat16), kvbuf, 0)
    row = lambda i: vector_row(vec_all, wa_count, *vec_at[i])
    split_pairs((matmul(content, held[1]) + row(1)).astype(jnp.bfloat16), kvbuf, 128)
    line = Line(kv_out, line_sems, grp_count, reach, tok)
    spot = lambda ref: lambda p: ref.at[pl.ds(pl.multiple_of((grp * PLANE + p) * tok, 16), tok)]
    swap = Swap(lambda p: kvbuf.at[p], spot(kv_out), swap_sems.at[0])
    swap.begin()
    line.send(1, pln, kvbuf.at[pln])
    swap.arrived(1)
    line.send(1, across(pln, 1))
    for g in gathers[2:5]:
        g.pass_on()
    for g in gathers[5:]:
        g.begin()
    for offset in (2, 3):
        swap.arrived(offset)
        line.send(1, across(pln, offset))
    for g in gathers[2:5]:
        g.arrived()
    outs = [pltpu.make_async_copy(held.at[i], fulls[i], out_sems.at[i]) for i in range(count)]
    for o in outs[:5]:
        o.start()
    vec_save = pltpu.make_async_copy(vec_all, vec_out, out_sems.at[count])
    vec_save.start()
    query = (matmul(query_ref[...], held[2]) + row(0)).astype(jnp.bfloat16)
    query = query * 0.125
    for pair in range(PLANE):
        qbuf[pair] = query[:, pair * 128 : pair * 128 + 128]
    place = lambda p: q_out.at[pl.ds(pl.multiple_of(p * tok, 16), tok)]
    swap_q = Swap(lambda p: qbuf.at[p], place, swap_sems.at[1])
    swap_q.begin()
    encoder = encoder_ref[...]
    split_pairs(matmul(encoder, held[3]).astype(jnp.bfloat16), kvbuf2, 0)
    split_pairs((matmul(encoder, held[4]) + row(2)).astype(jnp.bfloat16), kvbuf2, 128)
    place2 = lambda p: kv2_out.at[pl.ds(pl.multiple_of(p * tok, 16), tok)]
    swap_2 = Swap(lambda p: kvbuf2.at[p], place2, swap_sems.at[2])
    swap_2.begin()
    for step in range(1, reach + 1):
        line.forward(step)
    swap.arrived(0)
    for s in (swap_q, swap_2):
        for offset in range(4):
            s.arrived(offset)
    for g in gathers[5:]:
        g.pass_on()
    for g in gathers[5:]:
        g.arrived()
    for o in outs[5:]:
        o.start()
    for g in gathers:
        g.finish()
    for p in pushes:
        p.wait_send()
    for o in outs:
        o.wait()
    vec_save.wait()
    line.finish()
    for s in (swap, swap_q, swap_2):
        s.finish()


def run_opening(grp_count, wa_count, content, query, encoder, vecs, mats, vec_at):
    tok = content.shape[0]
    reach = min(grp_count - 1, (DOCLEN + PLANE * tok - 2) // (PLANE * tok))
    count = len(mats)
    low = jnp.bfloat16
    shape = lambda *s: jax.ShapeDtypeStruct(s, low)
    out_shape = [shape(m.shape[0] * wa_count, m.shape[1]) for m in mats]
    out_shape += [shape(wa_count, *vecs.shape), shape(PLANE * tok, 128), shape(grp_count * PLANE * tok, 256),
                  shape(PLANE * tok, 256)]
    return pl.pallas_call(
        functools.partial(opening_kernel, grp_count, wa_count, reach, count, vec_at),
        out_shape=tuple(out_shape),
        in_specs=[VMEM] * 4 + [ANY] * count,
        out_specs=tuple([ANY] * len(out_shape)),
        scratch_shapes=[
            pltpu.VMEM((count, 512, 512), low), pltpu.VMEM((wa_count,) + vecs.shape, low), pltpu.VMEM((PLANE, tok, 256), low),
            pltpu.VMEM((PLANE, tok, 256), low), pltpu.VMEM((PLANE, tok, 128), low),
            DMA((5, count, max(1, wa_count - 1))), DMA((2, wa_count)), DMA((2, 2, reach, PLANE)), DMA((3, 2, 4)), DMA((count + 1,))],
        compiler_params=pltpu.CompilerParams(collective_id=1, has_side_effects=True, vmem_limit_bytes=60 << 20),
    )(content, query, encoder, vecs, *mats)


def flat_pairs(buffer):
    return jnp.concatenate([buffer[p] for p in range(PLANE)], axis=1)


def middle_kernel(grp_count, wa_count, reach, vec_at, attended_ref, query_ref, out_mat_ref, query_mat_ref, vec_ref,
                  kv_own_ref, expand_ref, shrink_ref,
                  hidden_ref, normed_ref, inverse_ref, mixed_ref, q_out, kv_out, expand_full, shrink_full,
                  sendbuf, mixbuf, qbuf, expand_stage, shrink_stage, kv_stage, row_sems, line_sems, swap_sems, keep_sem):
    grp, pln = lax.axis_index("grp"), lax.axis_index("pln")
    tok = query_ref.shape[0]
    gathers = [Rows(expand_ref, expand_full, row_sems, 0, wa_count, expand_stage),
               Rows(shrink_ref, shrink_full, row_sems, 1, wa_count, shrink_stage)]
    load = pltpu.make_async_copy(kv_own_ref, kv_stage, keep_sem)
    load.start()
    for p in range(PLANE):
        sendbuf[p] = attended_ref[p * tok : p * tok + tok, :].astype(jnp.bfloat16)
    greet(grp_count, wa_count)
    swap = Swap(lambda p: sendbuf.at[p], lambda p: mixbuf.at[p], swap_sems.at[0])
    swap.begin()
    line = Line(kv_out, line_sems, grp_count, reach, tok)
    sources = [kv_own_ref.at[pl.ds(b * tok, tok)] for b in range(PLANE)]
    for b in range(PLANE):
        line.send(1, b, sources[b])
    for g in gathers:
        g.begin()
    whole = pl.ds(pl.multiple_of(grp * PLANE * tok, 16), PLANE * tok)
    load.wait()
    keep = pltpu.make_async_copy(kv_stage, kv_out.at[whole], keep_sem)
    keep.start()
    row = lambda i: vector_row(vec_ref, wa_count, *vec_at[i])
    for offset in range(4):
        swap.arrived(offset)
    mixed = flat_pairs(mixbuf)
    mixed_ref[...] = mixed
    value = query_ref[...].astype(jnp.float32) + matmul(mixed, out_mat_ref[...]) + row(3)
    hidden, normed, inverse = norm_forward(value, row(4), row(5))
    hidden_ref[...] = hidden
    normed_ref[...] = normed
    inverse_ref[...] = jnp.broadcast_to(inverse, inverse_ref.shape)
    query = (matmul(hidden.astype(jnp.bfloat16), query_mat_ref[...]) + row(6)).astype(jnp.bfloat16) * 0.125
    for pair in range(PLANE):
        qbuf[pair] = query[:, pair * 128 : pair * 128 + 128]
    place = lambda p: q_out.at[pl.ds(pl.multiple_of(p * tok, 16), tok)]
    swap_q = Swap(lambda p: qbuf.at[p], place, swap_sems.at[1])
    swap_q.begin()
    for g in gathers:
        g.staged()
    line.forward(1)
    for g in gathers:
        g.pass_on()
    for step in range(2, reach + 1):
        line.forward(step)
    for offset in range(4):
        swap_q.arrived(offset)
    for g in gathers:
        g.arrived()
    for g in gathers:
        g.finish()
    line.finish(sources)
    keep.wait()
    swap.finish()
    swap_q.finish()


def run_middle(grp_count, wa_count, attended, query, out_mat, query_mat, vecs, vec_at, kv_own, expand, shrink):
    tok = query.shape[0]
    reach = min(grp_count - 1, (DOCLEN + PLANE * tok - 2) // (PLANE * tok))
    low, full = jnp.bfloat16, jnp.float32
    shape = jax.ShapeDtypeStruct
    return pl.pallas_call(
        functools.partial(middle_kernel, grp_count, wa_count, reach, vec_at),
        out_shape=(shape((tok, 512), full), shape((tok, 512), full), shape((tok, 128), full), shape((tok, 512), low),
                   shape((PLANE * tok, 128), low), shape((grp_count * PLANE * tok, 256), low),
                   shape((expand.shape[0] * wa_count, expand.shape[1]), low),
                   shape((shrink.shape[0] * wa_count, shrink.shape[1]), low)),
        in_specs=[VMEM] * 5 + [ANY] * 3,
        out_specs=tuple([VMEM] * 4 + [ANY] * 4),
        scratch_shapes=[
            pltpu.VMEM((PLANE, tok, 128), low), pltpu.VMEM((PLANE, tok, 128), low), pltpu.VMEM((PLANE, tok, 128), low),
            pltpu.VMEM(expand.shape, low), pltpu.VMEM(shrink.shape, low), pltpu.VMEM((PLANE * tok, 256), low),
            DMA((5, 2, max(1, wa_count - 1))), DMA((2, 2, reach, PLANE)), DMA((2, 2, 4)), DMA],
        compiler_params=pltpu.CompilerParams(collective_id=2, has_side_effects=True, vmem_limit_bytes=60 << 20),
    )(attended, query, out_mat, query_mat, vecs, kv_own, expand, shrink)


def swap_kernel(inverse, in_ref, out_ref, sendbuf, getbuf, swap_sems):
    tok = getbuf.shape[1]
    for p in range(PLANE):
        if inverse:
            sendbuf[p] = in_ref[p * tok : p * tok + tok, :].astype(jnp.bfloat16)
        else:
            sendbuf[p] = in_ref[:, p * 128 : p * 128 + 128].astype(jnp.bfloat16)
    greet(1, 1, groups=False, rows=False)
    swap = Swap(lambda p: sendbuf.at[p], lambda p: getbuf.at[p], swap_sems)
    swap.begin()
    for offset in range(4):
        swap.arrived(offset)
    for p in range(PLANE):
        if inverse:
            out_ref[:, p * 128 : p * 128 + 128] = getbuf[p]
        else:
            out_ref[p * tok : p * tok + tok, :] = getbuf[p]
    swap.finish()


def run_swap(inverse, value, ident):
    tok = value.shape[0] // PLANE if inverse else value.shape[0]
    low = jnp.bfloat16
    return pl.pallas_call(
        functools.partial(swap_kernel, inverse),
        out_shape=jax.ShapeDtypeStruct((tok, 512) if inverse else (PLANE * tok, 128), low),
        in_specs=[VMEM], out_specs=VMEM,
        scratch_shapes=[pltpu.VMEM((PLANE, tok, 128), low), pltpu.VMEM((PLANE, tok, 128), low), DMA((2, 4))],
        compiler_params=pltpu.CompilerParams(collective_id=ident, has_side_effects=True, vmem_limit_bytes=60 << 20),
    )(value)


class Fold:
    def __init__(self, partial, mine, sendbuf, getbuf, sems, load_sems, grp_count, reach, block):
        self.partial, self.mine, self.sendbuf, self.getbuf = partial, mine, sendbuf, getbuf
        self.sems, self.load_sems = sems, load_sems
        self.count, self.reach, self.block = grp_count, reach, block
        self.grp = lax.axis_index("grp")

    def toward(self, side):
        return 1 if side == 0 else -1

    def rows(self, owner, block):
        return pl.ds(pl.multiple_of((owner * PLANE + block) * self.block, 16), self.block)

    def part(self, block):
        return pl.ds(block * self.block, self.block)

    def sends(self, side, stage):
        return self.grp + stage < self.count if side == 0 else self.grp - stage >= 0

    def receives(self, side, stage):
        if side == 0:
            return jnp.logical_and(self.grp >= 1, self.grp - 1 + stage < self.count)
        return jnp.logical_and(self.grp + 1 < self.count, self.grp + 1 - stage >= 0)

    def copy(self, side, stage, block, back=False):
        source = self.sendbuf.at[side, stage - 1, self.part(block)]
        if stage == self.reach and not back:
            source = self.partial.at[self.rows(self.grp + self.toward(side) * stage, block)]
        peer = self.grp + (-self.toward(side) if back else self.toward(side))
        return remote(source, self.getbuf.at[side, stage - 1, self.part(block)], self.sems.at[0, side, stage - 1, block],
                      self.sems.at[1, side, stage - 1, block], {"grp": peer})

    def load(self, side, stage):
        size = PLANE * self.block
        rows = pl.ds(pl.multiple_of((self.grp + self.toward(side) * stage) * size, 16), size)
        return pltpu.make_async_copy(self.partial.at[rows], self.mine.at[side, stage - 1], self.load_sems.at[side, stage - 1])

    def begin(self):
        for block in range(PLANE):
            for side in (0, 1):
                @pl.when(self.sends(side, self.reach))
                def _():
                    self.copy(side, self.reach, block).start()
        for stage in range(1, self.reach):
            for side in (0, 1):
                @pl.when(self.sends(side, stage))
                def _():
                    self.load(side, stage).start()

    def grow(self, stage):
        for side in (0, 1):
            @pl.when(self.sends(side, stage))
            def _():
                self.load(side, stage).wait()
        for block in range(PLANE):
            part = self.part(block)
            for side in (0, 1):
                @pl.when(self.sends(side, stage))
                def _():
                    self.sendbuf[side, stage - 1, part, :] = self.mine[side, stage - 1, part, :]

                    @pl.when(self.receives(side, stage + 1))
                    def _():
                        self.copy(side, stage + 1, block, True).wait_recv()
                        total = self.mine[side, stage - 1, part, :].astype(jnp.float32)
                        total = total + self.getbuf[side, stage, part, :].astype(jnp.float32)
                        self.sendbuf[side, stage - 1, part, :] = total.astype(jnp.bfloat16)

                    self.copy(side, stage, block).start()

    def total(self, own, out):
        for block in range(PLANE):
            part = self.part(block)
            for side in (0, 1):
                @pl.when(self.receives(side, 1))
                def _():
                    self.copy(side, 1, block, True).wait_recv()
                    own[part, :] = own[part, :] + self.getbuf[side, 0, part, :].astype(jnp.float32)
            out[block] = own[part, :].astype(jnp.bfloat16)

    def finish(self):
        for stage in range(1, self.reach + 1):
            for block in range(PLANE):
                for side in (0, 1):
                    @pl.when(self.sends(side, stage))
                    def _():
                        self.copy(side, stage, block, True).wait_send()


def store_blocks(buffer, value):
    for c in range(PLANE):
        buffer[c] = value[:, c * 128 : c * 128 + 128].astype(jnp.bfloat16)


def halves(buffer):
    keys = jnp.concatenate([buffer[p, :, :128] for p in range(PLANE)], axis=1)
    values = jnp.concatenate([buffer[p, :, 128:] for p in range(PLANE)], axis=1)
    return keys, values


def turn_kernel(grp_count, wa_count, reach, vec_at, dq_ref, dkv_ref, own_ref, back_ref, normed_ref, inverse_ref, hidden_ref,
                mixed_one_ref, mixed_two_ref, branch_two_ref, encoder_ref, query_mat_ref, out_mat_ref, vec_ref, vg_ref,
                do_out, back_out, kv_out, grads_out, vg_out,
                dqsend, dqget, dosend, doget, kvsend, kvget, total, mine, foldsend, foldget, grads, fold_sems, load_sems,
                swap_sems, out_sems):
    tok = back_ref.shape[0]
    for p in range(PLANE):
        dqsend[p] = dq_ref[p * tok : p * tok + tok, :]
    greet(grp_count, wa_count, rows=False)
    swap_dq = Swap(lambda p: dqsend.at[p], lambda p: dqget.at[p], swap_sems.at[0])
    swap_dq.begin()
    fold = Fold(dkv_ref, mine, foldsend, foldget, fold_sems, load_sems, grp_count, reach, tok)
    fold.begin()
    row = lambda i: vector_row(vec_ref, wa_count, *vec_at[i])
    vg_out[...] = vg_ref[...]
    saves = [pltpu.make_async_copy(grads.at[i], grads_out.at[i], out_sems.at[i]) for i in range(5)]
    total[...] = own_ref[...]
    store_blocks(grads.at[0], dot(mixed_two_ref[...], branch_two_ref[...], 0, 0))
    saves[0].start()
    for offset in range(4):
        swap_dq.arrived(offset)
    dq = flat_pairs(dqget)
    incoming = back_ref[...] + dot(dq, query_mat_ref[...], 1, 1)
    back, gain_grad, shift_grad = norm_backward(incoming, normed_ref[...], inverse_ref[:, :1], row(4))
    back_out[...] = back
    branch = back.astype(jnp.bfloat16)
    do = dot(branch, out_mat_ref[...], 1, 1).astype(jnp.bfloat16)
    for p in range(PLANE):
        dosend[p] = do[:, p * 128 : p * 128 + 128]
    swap_do = Swap(lambda p: dosend.at[p], lambda p: doget.at[p], swap_sems.at[1])
    swap_do.begin()
    vg_out[10:11, :] = gain_grad.reshape(1, 512)
    vg_out[11:12, :] = shift_grad.reshape(1, 512)
    vg_out[12:13, :] = column_sum(branch).reshape(1, 512)
    vg_out[13:14, :] = column_sum(dq).reshape(1, 512)
    store_blocks(grads.at[1], dot(hidden_ref[...].astype(jnp.bfloat16), dq, 0, 0))
    saves[1].start()
    store_blocks(grads.at[2], dot(mixed_one_ref[...], branch, 0, 0))
    saves[2].start()
    for stage in range(reach - 1, 0, -1):
        fold.grow(stage)
    for offset in range(4):
        swap_do.arrived(offset)
    for p in range(PLANE):
        do_out[p * tok : p * tok + tok, :] = doget[p]
    fold.total(total, kvsend)
    swap_kv = Swap(lambda p: kvsend.at[p], lambda p: kvget.at[p], swap_sems.at[2])
    swap_kv.begin()
    for offset in range(4):
        swap_kv.arrived(offset)
    keys, values = halves(kvget)
    kv_out[:, :512] = keys
    kv_out[:, 512:] = values
    encoder = encoder_ref[...]
    store_blocks(grads.at[3], dot(encoder, keys, 0, 0))
    saves[3].start()
    store_blocks(grads.at[4], dot(encoder, values, 0, 0))
    saves[4].start()
    vg_out[14:15, :] = column_sum(values).reshape(1, 512)
    for s in saves:
        s.wait()
    fold.finish()
    for s in (swap_dq, swap_do, swap_kv):
        s.finish()


def fold_scratch(tok, reach):
    low = jnp.bfloat16
    size = PLANE * tok
    return [pltpu.VMEM((PLANE, tok, 256), low), pltpu.VMEM((PLANE, tok, 256), low), pltpu.VMEM((size, 256), jnp.float32),
            pltpu.VMEM((2, max(1, reach - 1), size, 256), low), pltpu.VMEM((2, reach, size, 256), low),
            pltpu.VMEM((2, reach, size, 256), low)]


def run_turn(grp_count, wa_count, vec_at, dq, dkv, own, back, normed, inverse, hidden, mixed_one, mixed_two, branch_two,
             encoder, query_mat, out_mat, vecs, vg):
    tok = back.shape[0]
    reach = min(grp_count - 1, (DOCLEN + PLANE * tok - 2) // (PLANE * tok))
    low, full = jnp.bfloat16, jnp.float32
    shape = jax.ShapeDtypeStruct
    pairs = pltpu.VMEM((PLANE, tok, 128), low)
    return pl.pallas_call(
        functools.partial(turn_kernel, grp_count, wa_count, reach, vec_at),
        out_shape=(shape((PLANE * tok, 128), low), shape((tok, 512), full), shape((tok, 1024), low),
                   shape((5, PLANE, 512, 128), low), shape(vg.shape, full)),
        in_specs=[VMEM, ANY] + [VMEM] * 13,
        out_specs=(VMEM, VMEM, VMEM, ANY, VMEM),
        scratch_shapes=[pairs] * 4 + fold_scratch(tok, reach) + [
            pltpu.VMEM((5, PLANE, 512, 128), low), DMA((2, 2, reach, PLANE)), DMA((2, max(1, reach - 1))), DMA((3, 2, 4)),
            DMA((5,))],
        compiler_params=pltpu.CompilerParams(collective_id=8, has_side_effects=True, vmem_limit_bytes=60 << 20),
    )(dq, dkv, own, back, normed, inverse, hidden, mixed_one, mixed_two, branch_two, encoder, query_mat, out_mat, vecs, vg)


class Reduce:
    def __init__(self, index, source, parts, got, kept, sems, wa_count):
        self.index, self.source, self.sems, self.wa_count = index, source, sems, wa_count
        self.parts, (self.got_core, self.got_wa, self.got_row) = parts, got
        self.by_core, self.by_wa, self.by_row = kept
        self.wa, self.pln = lax.axis_index("wa"), lax.axis_index("pln")
        self.core = lax.rem(self.pln, 2)
        self.row = self.pln // 2
        self.size = 512 // wa_count

    def core_copy(self, row):
        return remote(self.source.at[row * 2 + 1 - self.core], self.got_core.at[self.index, row],
                      self.sems.at[0, self.index, row], self.sems.at[1, self.index, row], {"pln": across(self.pln, 1)})

    def rows_of(self, wa):
        return pl.ds(pl.multiple_of(wa * self.size, 16), self.size)

    def wa_copy(self, offset):
        peer = lax.rem(self.wa + offset, self.wa_count)
        return remote(self.by_core.at[self.index, :, self.rows_of(peer)], self.got_wa.at[offset - 1, self.index],
                      self.sems.at[0, self.index, 1 + offset], self.sems.at[1, self.index, 1 + offset], {"wa": peer})

    def row_copy(self):
        return remote(self.by_wa.at[self.index, 1 - self.row], self.got_row.at[self.index],
                      self.sems.at[0, self.index, 1 + self.wa_count], self.sems.at[1, self.index, 1 + self.wa_count],
                      {"pln": across(self.pln, 2)})

    def begin(self):
        for row in (0, 1):
            self.core_copy(row).start()

    def after_core(self):
        for row in (0, 1):
            self.core_copy(row).wait_recv()
            mine = self.parts[row * 2 + self.core].astype(jnp.float32)
            total = mine + self.got_core[self.index, row].astype(jnp.float32)
            self.by_core[self.index, row] = total.astype(jnp.bfloat16)
        for offset in range(1, self.wa_count):
            self.wa_copy(offset).start()

    def after_wa(self):
        for offset in range(1, self.wa_count):
            self.wa_copy(offset).wait_recv()
        for row in (0, 1):
            total = self.by_core[self.index, row, self.rows_of(self.wa), :].astype(jnp.float32)
            for offset in range(1, self.wa_count):
                total = total + self.got_wa[offset - 1, self.index, row].astype(jnp.float32)
            self.by_wa[self.index, row] = total.astype(jnp.bfloat16)
        self.row_copy().start()

    def after_row(self):
        self.row_copy().wait_recv()
        total = self.by_wa[self.index, self.row].astype(jnp.float32) + self.got_row[self.index].astype(jnp.float32)
        self.by_row[self.index] = total.astype(jnp.bfloat16)

    def finish(self):
        for row in (0, 1):
            self.core_copy(row).wait_send()
        for offset in range(1, self.wa_count):
            self.wa_copy(offset).wait_send()
        self.row_copy().wait_send()


def greet_all(grp_count, wa_count):
    barrier = pltpu.get_barrier_semaphore()
    grp, pln, wa = lax.axis_index("grp"), lax.axis_index("pln"), lax.axis_index("wa")
    peers = [{"pln": across(pln, o)} for o in (1, 2, 3)]
    peers += [{"wa": lax.rem(wa + o, wa_count)} for o in range(1, wa_count)]
    peers += [{"grp": lax.rem(grp + o, grp_count)} for o in range(1, grp_count)]
    for where in peers:
        pl.semaphore_signal(barrier, inc=1, device_id=where, device_id_type=MESH)
    pl.semaphore_wait(barrier, len(peers))


def closing_kernel(grp_count, wa_count, reach, count, dq_ref, dkv_ref, own_ref, query_ref, content_ref, early_ref, vg_ref,
                   dq_out, kv_out, out_ref, vg_out,
                   dqsend, dqget, kvsend, kvget, total, mine, foldsend, foldget, parts, got_core, got_wa, got_row,
                   by_core, by_wa, by_row, got_grp, final, vsum, vgot, vall,
                   fold_sems, load_sems, swap_sems, part_sems, red_sems, vec_sems, grp_sems, share_sems):
    grp, pln, wa = lax.axis_index("grp"), lax.axis_index("pln"), lax.axis_index("wa")
    tok = query_ref.shape[0]
    early = early_ref.shape[0]
    size = 512 // wa_count
    slab = size // grp_count
    for p in range(PLANE):
        dqsend[p] = dq_ref[p * tok : p * tok + tok, :]
    greet_all(grp_count, wa_count)
    swap_dq = Swap(lambda p: dqsend.at[p], lambda p: dqget.at[p], swap_sems.at[0])
    swap_dq.begin()
    fold = Fold(dkv_ref, mine, foldsend, foldget, fold_sems, load_sems, grp_count, reach, tok)
    fold.begin()
    loads = [pltpu.make_async_copy(early_ref.at[i], parts.at[i], part_sems.at[i]) for i in range(early)]
    for l in loads:
        l.start()
    got, kept = (got_core, got_wa, got_row), (by_core, by_wa, by_row)
    reds = [Reduce(i, early_ref.at[i] if i < early else parts.at[i], parts.at[i], got, kept, red_sems, wa_count)
            for i in range(count)]
    for r in reds[:early]:
        r.begin()
    total[...] = own_ref[...]
    vsum[0] = vg_ref[...]
    for offset in range(4):
        swap_dq.arrived(offset)
    dq = flat_pairs(dqget)
    dq_out[...] = dq
    store_blocks(parts.at[early], dot(query_ref[...], dq, 0, 0))
    vsum[0, 15:16, :] = column_sum(dq).reshape(1, 512)
    reds[early].begin()
    for l in loads:
        l.wait()
    for r in reds[: early + 1]:
        r.after_core()
    for stage in range(reach - 1, 0, -1):
        fold.grow(stage)
    for r in reds[: early + 1]:
        r.after_wa()
    fold.total(total, kvsend)
    swap_kv = Swap(lambda p: kvsend.at[p], lambda p: kvget.at[p], swap_sems.at[1])
    swap_kv.begin()
    for r in reds[: early + 1]:
        r.after_row()
    for offset in range(4):
        swap_kv.arrived(offset)
    keys, values = halves(kvget)
    content = content_ref[...]
    store_blocks(parts.at[early + 1], dot(content, keys, 0, 0))
    reds[early + 1].begin()
    store_blocks(parts.at[early + 2], dot(content, values, 0, 0))
    reds[early + 2].begin()
    vsum[0, 16:17, :] = column_sum(values).reshape(1, 512)
    vec_core = remote(vsum.at[0], vgot.at[0], vec_sems.at[0, 0], vec_sems.at[1, 0], {"pln": across(pln, 1)})
    vec_core.start()
    kv_out[:, :512] = keys
    kv_out[:, 512:] = values

    def grp_copy(set_at, offset):
        start, length = ((0, early + 1), (early + 1, count - early - 1))[set_at]
        peer = lax.rem(grp + offset, grp_count)
        some = pl.ds(start, length)
        rows = pl.ds(pl.multiple_of(peer * slab, 8), slab)
        return remote(by_row.at[some, rows], got_grp.at[offset - 1, some], grp_sems.at[0, set_at, offset - 1],
                      grp_sems.at[1, set_at, offset - 1], {"grp": peer})

    offsets = range(1, grp_count)
    for o in offsets:
        grp_copy(0, o).start()
    for r in reds[early + 1 :]:
        r.after_core()
    vec_core.wait_recv()
    vsum[1] = vsum[0] + vgot[0]
    vec_wa = [remote(vsum.at[1], vgot.at[o], vec_sems.at[0, o], vec_sems.at[1, o], {"wa": lax.rem(wa + o, wa_count)})
              for o in range(1, wa_count)]
    for v in vec_wa:
        v.start()
    for r in reds[early + 1 :]:
        r.after_wa()
    for v in vec_wa:
        v.wait_recv()
    vall[wa] = vsum[1]
    for o in range(1, wa_count):
        vall[lax.rem(wa + wa_count - o, wa_count)] = vgot[o]
    joined = vall[0]
    for o in range(1, wa_count):
        joined = joined + vall[o]
    vsum[2] = joined
    vec_row = remote(vsum.at[2], vgot.at[wa_count], vec_sems.at[0, wa_count], vec_sems.at[1, wa_count],
                     {"pln": across(pln, 2)})
    vec_row.start()
    own_rows = pl.ds(pl.multiple_of(grp * slab, 8), slab)

    def settle(set_at):
        start, length = ((0, early + 1), (early + 1, count - early - 1))[set_at]
        some = pl.ds(start, length)
        for o in offsets:
            grp_copy(set_at, o).wait_recv()
        value = by_row[some, own_rows, :].astype(jnp.float32)
        for o in offsets:
            value = value + got_grp[o - 1, some].astype(jnp.float32)
        final[some] = value.astype(jnp.bfloat16)

    def spot(column, source, some):
        return out_ref.at[column, some, pl.ds(pl.multiple_of(source * slab, 8), slab)]

    def spread(set_at, offset):
        start, length = ((0, early + 1), (early + 1, count - early - 1))[set_at]
        some = pl.ds(start, length)
        return remote(final.at[some], spot(pln, grp, some), share_sems.at[0, set_at, 0, offset],
                      share_sems.at[1, set_at, 0, offset], {"grp": lax.rem(grp + offset, grp_count)})

    def keep(set_at):
        start, length = ((0, early + 1), (early + 1, count - early - 1))[set_at]
        some = pl.ds(start, length)
        return pltpu.make_async_copy(final.at[some], spot(pln, grp, some), share_sems.at[0, set_at, 0, 0])

    def give(set_at, kind, offset):
        start, length = ((0, early + 1), (early + 1, count - early - 1))[set_at]
        some = pl.ds(start, length)
        source = lax.rem(grp + grp_count - offset, grp_count)
        column = pln if kind < 3 else across(pln, 2)
        there = spot(column, source, some)
        return remote(there, there, share_sems.at[0, set_at, kind, offset], share_sems.at[1, set_at, kind, offset],
                      {"pln": across(pln, 2 if kind == 1 else 1)})

    settle(0)
    keep(0).start()
    for o in offsets:
        spread(0, o).start()
    for r in reds[early + 1 :]:
        r.after_row()
    for o in offsets:
        grp_copy(1, o).start()
    vec_row.wait_recv()
    vsum[3] = vsum[2] + vgot[wa_count]
    vec_grp = [remote(vsum.at[3], vall.at[wa_count + o], vec_sems.at[0, wa_count + o], vec_sems.at[1, wa_count + o],
                      {"grp": lax.rem(grp + o, grp_count)}) for o in offsets]
    for v in vec_grp:
        v.start()
    everyone = range(grp_count)

    def hand_out(set_at, offset):
        if offset == 0:
            keep(set_at).wait()
        else:
            spread(set_at, offset).wait_recv()
        give(set_at, 1, offset).start()
        give(set_at, 2, offset).start()

    for o in everyone:
        hand_out(0, o)
    settle(1)
    keep(1).start()
    for o in offsets:
        spread(1, o).start()
    for o in everyone:
        give(0, 1, o).wait_recv()
        give(0, 3, o).start()
    for o in everyone:
        hand_out(1, o)
    for v in vec_grp:
        v.wait_recv()
    ordered = jnp.zeros_like(vsum[3])
    for g in everyone:
        piece = jnp.where(grp == g, vsum[3], 0.0)
        for o in offsets:
            piece = piece + jnp.where(lax.rem(grp + grp_count - o, grp_count) == g, vall[wa_count + o], 0.0)
        ordered = ordered + piece
    vg_out[...] = ordered
    for o in everyone:
        give(1, 1, o).wait_recv()
        give(1, 3, o).start()
    for set_at in (0, 1):
        for o in everyone:
            give(set_at, 2, o).wait_recv()
            give(set_at, 3, o).wait_recv()
    for set_at in (0, 1):
        for o in everyone:
            for kind in (1, 2, 3):
                give(set_at, kind, o).wait_send()
        for o in offsets:
            spread(set_at, o).wait_send()
            grp_copy(set_at, o).wait_send()
    for v in [vec_core, vec_row] + vec_wa + vec_grp:
        v.wait_send()
    for r in reds:
        r.finish()
    fold.finish()
    swap_dq.finish()
    swap_kv.finish()


def run_closing(grp_count, wa_count, dq, dkv, own, query, content, early, vg):
    tok = query.shape[0]
    count = early.shape[0] + 3
    reach = min(grp_count - 1, (DOCLEN + PLANE * tok - 2) // (PLANE * tok))
    size = 512 // wa_count
    slab = size // grp_count
    low, full = jnp.bfloat16, jnp.float32
    shape = jax.ShapeDtypeStruct
    pairs = pltpu.VMEM((PLANE, tok, 128), low)
    steps = wa_count + 2
    return pl.pallas_call(
        functools.partial(closing_kernel, grp_count, wa_count, reach, count),
        out_shape=(shape((tok, 512), low), shape((tok, 1024), low), shape((PLANE, count, size, 128), low),
                   shape(vg.shape, full)),
        in_specs=[VMEM, ANY, VMEM, VMEM, VMEM, ANY, VMEM],
        out_specs=(VMEM, VMEM, ANY, VMEM),
        scratch_shapes=[pairs] * 2 + fold_scratch(tok, reach) + [
            pltpu.VMEM((count, PLANE, 512, 128), low), pltpu.VMEM((count, 2, 512, 128), low),
            pltpu.VMEM((max(1, wa_count - 1), count, 2, size, 128), low), pltpu.VMEM((count, size, 128), low),
            pltpu.VMEM((count, 2, 512, 128), low), pltpu.VMEM((count, 2, size, 128), low), pltpu.VMEM((count, size, 128), low),
            pltpu.VMEM((grp_count - 1, count, slab, 128), low), pltpu.VMEM((count, slab, 128), low),
            pltpu.VMEM((4,) + vg.shape, full), pltpu.VMEM((wa_count + 1,) + vg.shape, full),
            pltpu.VMEM((wa_count + grp_count,) + vg.shape, full),
            DMA((2, 2, reach, PLANE)), DMA((2, max(1, reach - 1))), DMA((2, 2, 4)), DMA((early.shape[0],)),
            DMA((2, count, steps)), DMA((2, wa_count + grp_count)), DMA((2, 2, grp_count - 1)), DMA((2, 2, 4, grp_count))],
        compiler_params=pltpu.CompilerParams(collective_id=9, has_side_effects=True, vmem_limit_bytes=60 << 20),
    )(dq, dkv, own, query, content, early, vg)


def reduce_wide(grad):
    mine = lax.psum_scatter(grad.astype(jnp.bfloat16), "wa", scatter_dimension=0, tiled=True)
    return lax.psum(mine, ("grp", "pln")).astype(jnp.float32)


def shards(
    query_in,
    content_in,
    encoder_in,
    out_grad,
    document_lengths,
    key_ranks,
    query_limits,
    self_query_weight,
    self_query_bias,
    self_key_weight,
    self_value_weight,
    self_value_bias,
    self_out_weight,
    self_out_bias,
    norm_one_gain,
    norm_one_shift,
    cross_query_weight,
    cross_query_bias,
    cross_key_weight,
    cross_value_weight,
    cross_value_bias,
    cross_out_weight,
    cross_out_bias,
    norm_two_gain,
    norm_two_shift,
    expand_weight,
    expand_bias,
    shrink_weight,
    shrink_bias,
    norm_three_gain,
    norm_three_shift,
):
    grp_count = lax.axis_size("grp")
    own = lax.axis_index("grp")[None].astype(jnp.int32)
    lens = document_lengths
    tok = query_in.shape[1]
    rows = tok * PLANE
    row_at = lax.axis_index("grp") * rows
    cross_keys, cross_marks = mark_tables(lens[0], key_ranks[0], query_limits[0], row_at, rows, False)
    self_keys, self_marks = mark_tables(lens[0], key_ranks[0], query_limits[0], row_at, rows, True)
    wa_count = lax.axis_size("wa")
    vectors = (self_query_bias, self_value_bias, cross_value_bias, self_out_bias, norm_one_gain, norm_one_shift,
        cross_query_bias, cross_out_bias, norm_two_gain, norm_two_shift, expand_bias, shrink_bias, norm_three_gain,
        norm_three_shift)
    vec_at, at = [], 0
    for v in vectors:
        vec_at.append((at, v.shape[0]))
        at += v.shape[0] // min(128, v.shape[0])
    vec_at = tuple(vec_at)
    mats = (self_key_weight, self_value_weight, self_query_weight, cross_key_weight, cross_value_weight, self_out_weight,
        cross_query_weight, cross_out_weight)
    (self_key_matrix, self_value_mat, self_query_mat, cross_key_matrix, cross_value_mat, self_out_mat, cross_query_mat,
        cross_out_mat, vec_all, pair_one, kv_one, kv_two_own) = run_opening(
        grp_count, wa_count, content_in[0], query_in[0], encoder_in[0], pack_vectors(vectors), mats, vec_at)
    lines = [jnp.concatenate([vec_all[w, s : s + n // min(n, 128), : min(n, 128)].reshape(-1) for w in range(wa_count)])
        .astype(jnp.float32) for s, n in vec_at]
    (self_query_vec, self_value_vec, cross_value_vec, self_out_vec, gain_one, shift_one, cross_query_vec, cross_out_vec,
        gain_two, shift_two, expand_vec, shrink_vec, gain_three, shift_three) = lines
    source = query_in[0]
    content_states = content_in[0]
    encoder_output = encoder_in[0]
    cotangent = out_grad[0].astype(jnp.float32)
    keys_one, values_one = kv_one[:, :128], kv_one[:, 128:]
    attended_one, total_one = attend_forward(True, lens, own, pair_one, self_marks, keys_one, values_one, self_keys)
    hidden_one, normed_one, inverse_one, mixed_one, pair_two, kv_two, expand_mat, shrink_mat = run_middle(
        grp_count, wa_count, attended_one, source, self_out_mat, cross_query_mat, vec_all, vec_at, kv_two_own,
        expand_weight, shrink_weight)
    hidden_one_low = hidden_one.astype(jnp.bfloat16)
    keys_two, values_two = kv_two[:, :128], kv_two[:, 128:]
    attended_two, total_two = attend_forward(False, lens, own, pair_two, cross_marks, keys_two, values_two, cross_keys)
    mixed_two = run_swap(True, attended_two, 3)
    hidden_two, normed_two, inverse_two = norm_forward(
        hidden_one + matmul(mixed_two, cross_out_mat) + cross_out_vec, gain_two, shift_two)
    hidden_two_low = hidden_two.astype(jnp.bfloat16)
    expanded = matmul(hidden_two_low, expand_mat) + expand_vec
    activated = jax.nn.gelu(expanded, approximate=False).astype(jnp.bfloat16)
    layer_out, normed_three, inverse_three = norm_forward(
        hidden_two + matmul(activated, shrink_mat) + shrink_vec, gain_three, shift_three)
    back_three, grad_gain_three, grad_shift_three = norm_backward(cotangent, normed_three, inverse_three, gain_three)
    shrink_in_grad = back_three.astype(jnp.bfloat16)
    grad_shrink_mat = left_product(activated, shrink_in_grad)
    grad_shrink_mat = reduce_wide(grad_shrink_mat)
    grad_shrink_vec = column_sum(shrink_in_grad)
    activated_grad = right_product(shrink_in_grad, shrink_mat)
    expand_grad = (activated_grad * gelu_slope(expanded)).astype(jnp.bfloat16)
    grad_expand_mat = left_product(hidden_two_low, expand_grad)
    grad_expand_mat = reduce_wide(grad_expand_mat)
    grad_expand_vec = column_sum(expand_grad)
    hidden_two_grad = back_three + right_product(expand_grad, expand_mat)
    back_two, grad_gain_two, grad_shift_two = norm_backward(hidden_two_grad, normed_two, inverse_two, gain_two)
    branch_two = back_two.astype(jnp.bfloat16)
    grad_cross_out_vec = column_sum(branch_two)
    mixed_two_grad = right_product(branch_two, cross_out_mat).astype(jnp.bfloat16)
    dq_two, dkv_two, own_two = attend_backward(False, lens, own, pair_two, cross_marks, keys_two, values_two, cross_keys,
        attended_two, total_two, run_swap(False, mixed_two_grad, 4))
    marks = (grad_gain_three, grad_shift_three, grad_shrink_vec, grad_expand_vec, grad_gain_two, grad_shift_two,
        grad_cross_out_vec, jnp.zeros((14 * 512,), jnp.float32))
    do_one, back_one, kv_two_grad, early, lines = run_turn(grp_count, wa_count, vec_at, dq_two, dkv_two, own_two, back_two,
        normed_one, inverse_one, hidden_one, mixed_one, mixed_two, branch_two, encoder_output, cross_query_mat, self_out_mat,
        vec_all, jnp.concatenate(marks).reshape(24, 512))
    key_two_low, value_two_low = kv_two_grad[:, :512], kv_two_grad[:, 512:]
    encoder_grad = right_product(key_two_low, cross_key_matrix) + right_product(value_two_low, cross_value_mat)
    dq_one, dkv_one, own_one = attend_backward(True, lens, own, pair_one, self_marks, keys_one, values_one, self_keys,
        attended_one, total_one, do_one)
    query_one_low, kv_one_grad, late, sums = run_closing(grp_count, wa_count, dq_one, dkv_one, own_one, source,
        content_states, early, lines)
    query_grad = back_one + right_product(query_one_low, self_query_mat)
    content_grad = right_product(kv_one_grad[:, :512], self_key_matrix) + right_product(kv_one_grad[:, 512:], self_value_mat)
    names = ("cross_out", "cross_query", "self_out", "cross_key", "cross_value", "self_query", "self_key", "self_value")
    mat = {n: jnp.concatenate([late[c, i] for c in range(PLANE)], axis=1).astype(jnp.float32) for i, n in enumerate(names)}
    names = ("gain_three", "shift_three", "shrink", "expand", "gain_two", "shift_two", "cross_out", "gain_one", "shift_one",
        "self_out", "cross_query", "cross_value", "self_query", "self_value")
    vec, at = {}, 0
    for n in names:
        rows_used = 4 if n == "expand" else 1
        line = sums[at : at + rows_used].reshape(-1)
        share = line.shape[0] // wa_count
        vec[n] = lax.dynamic_slice_in_dim(line, lax.axis_index("wa") * share, share, 0)
        at += rows_used
    grads = (mat["self_query"], vec["self_query"], mat["self_key"], mat["self_value"], vec["self_value"], mat["self_out"],
        vec["self_out"], vec["gain_one"], vec["shift_one"], mat["cross_query"], vec["cross_query"], mat["cross_key"],
        mat["cross_value"], vec["cross_value"], mat["cross_out"], vec["cross_out"], vec["gain_two"], vec["shift_two"],
        grad_expand_mat, vec["expand"], grad_shrink_mat, vec["shrink"], vec["gain_three"], vec["shift_three"])
    return (layer_out[None], query_grad[None], content_grad[None], encoder_grad[None]) + grads


def solution(mesh):
    ctx, wa = mesh.devices.shape
    mesh = Mesh(mesh.devices.reshape(ctx // PLANE, PLANE, wa), ("grp", "pln", "wa"))
    in_specs = (
        P("wa", ("grp", "pln"), None),
        P("wa", ("grp", "pln"), None),
        P("wa", ("grp", "pln"), None),
        P("wa", ("grp", "pln"), None),
        P("wa", None),
        P("wa", None),
        P("wa", None),
        P("wa", None),
        P("wa"),
        P("wa", None),
        P("wa", None),
        P("wa"),
        P("wa", None),
        P("wa"),
        P("wa"),
        P("wa"),
        P("wa", None),
        P("wa"),
        P("wa", None),
        P("wa", None),
        P("wa"),
        P("wa", None),
        P("wa"),
        P("wa"),
        P("wa"),
        P("wa", None),
        P("wa"),
        P("wa", None),
        P("wa"),
        P("wa"),
        P("wa"),
    )
    out_specs = (
        P("wa", ("grp", "pln"), None),
        P("wa", ("grp", "pln"), None),
        P("wa", ("grp", "pln"), None),
        P("wa", ("grp", "pln"), None),
        P("wa", None),
        P("wa"),
        P("wa", None),
        P("wa", None),
        P("wa"),
        P("wa", None),
        P("wa"),
        P("wa"),
        P("wa"),
        P("wa", None),
        P("wa"),
        P("wa", None),
        P("wa", None),
        P("wa"),
        P("wa", None),
        P("wa"),
        P("wa"),
        P("wa"),
        P("wa", None),
        P("wa"),
        P("wa", None),
        P("wa"),
        P("wa"),
        P("wa"),
    )
    return jax.shard_map(shards, mesh=mesh, in_specs=in_specs, out_specs=out_specs, check_vma=False)
```

```python
import functools
import jax
import jax.numpy as jnp
from jax import lax
from jax.experimental import pallas as pl
from jax.experimental.pallas import tpu as pltpu
from jax.sharding import Mesh
from jax.sharding import PartitionSpec as P

PLANE = 4
DOCLEN = 2048
EPSILON = 1e-05
ROOT_HALF = 0.7071067811865476
INV_ROOT_TWO_PI = 0.3989422804014327
NEGATIVE = -1e29
HIDE = -(2.0 ** 100)
BLOCK = 256
WIDE = 512
STAT = 40


def dot(a, b, ca, cb):
    return lax.dot_general(a, b, (((ca,), (cb,)), ((), ())), preferred_element_type=jnp.float32)


def left_half(shape):
    return lax.broadcasted_iota(jnp.int32, shape, 1) < 64


def spans(lens_ref, first, count):
    low, high, total = 0, 0, 0
    for d in range(lens_ref.shape[1]):
        begin = total
        total = total + lens_ref[0, d]
        low = jnp.where(begin <= first, begin, low)
        high = jnp.where(begin <= first + count - 1, total, high)
    return low, high


def openings(lens_ref, places):
    total, found = 0, places == 0
    for d in range(lens_ref.shape[1] - 1):
        total = total + lens_ref[0, d]
        found = jnp.logical_or(found, places == total)
    return found


def over_blocks(low, high, first, size, step, carry, ranked):
    begin, end = low // size, (high + size - 1) // size
    own = first // size
    skip = 1 if ranked else 0

    def body(index, carry):
        if ranked:
            index = index + jnp.where(index >= own, 1, 0)
        return step(pl.multiple_of(index * size, size), carry)

    carry = lax.fori_loop(begin, end - skip, body, carry)
    if ranked:
        carry = step(pl.multiple_of(own * size, size), carry, True)
    return carry


def forward_kernel(ranked, lens_ref, own_ref, q_ref, qm_ref, kv_ref, km_ref, o_ref, lse_ref):
    rows = q_ref.shape[0]
    base = own_ref[0] * rows
    half = left_half((BLOCK, 128))
    khalf = left_half((WIDE, 128))
    one = jnp.ones((WIDE, 128), jnp.bfloat16)

    def one_block(block, _):
        start = pl.multiple_of(block * BLOCK, BLOCK)
        first = base + start
        low, high = spans(lens_ref, first, BLOCK)
        q = q_ref[pl.ds(start, BLOCK), :]
        qm = qm_ref[pl.ds(start, BLOCK), :]
        queries = (jnp.where(half, q, qm), jnp.where(half, qm, q))

        def step(at, carry, diagonal=False):
            k = kv_ref[pl.ds(at, WIDE), :128]
            v = kv_ref[pl.ds(at, WIDE), 128:]
            km = km_ref[pl.ds(at, WIDE), :]
            keys = (jnp.where(khalf, k, km), jnp.where(khalf, km, k))
            values = (jnp.where(khalf, v, one), jnp.where(khalf, one, v))
            scores = [dot(queries[h], keys[h], 1, 1) for h in (0, 1)]
            if diagonal:
                place = first + lax.broadcasted_iota(jnp.int32, (BLOCK, WIDE), 0)
                other = at + lax.broadcasted_iota(jnp.int32, (BLOCK, WIDE), 1)
                column = first + lax.broadcasted_iota(jnp.int32, (BLOCK, 1), 0)
                banned = jnp.where(openings(lens_ref, column), -1, place) == other
                scores = [jnp.where(banned, HIDE, s) for s in scores]
            out = []
            for h in (0, 1):
                peak, acc = carry[h]
                new = jnp.maximum(peak, jnp.max(scores[h], axis=1, keepdims=True))
                p = jnp.exp(scores[h] - new).astype(jnp.bfloat16)
                acc = acc * jnp.exp(peak - new) + dot(p, values[h], 1, 0)
                out.append((new, acc))
            return tuple(out)

        empty = (jnp.full((BLOCK, 1), NEGATIVE, jnp.float32), jnp.zeros((BLOCK, 128), jnp.float32))
        (peak0, acc0), (peak1, acc1) = over_blocks(low, high, first, WIDE, step, (empty, empty), ranked)
        total = jnp.where(half, acc1, acc0)
        mixed = jnp.where(half, acc0, acc1)
        o_ref[pl.ds(start, BLOCK), :] = mixed / pltpu.roll(total, 64, 1)
        lse_ref[pl.ds(start, BLOCK), :] = jnp.where(half, peak1, peak0) + jnp.log(total)
        return 0

    lax.fori_loop(0, rows // BLOCK, one_block, 0)


def attend_forward(ranked, lens, own, q, qm, kv, km):
    rows = q.shape[0]
    whole = pl.BlockSpec(memory_space=pltpu.VMEM)
    smem = pl.BlockSpec(memory_space=pltpu.SMEM)
    return pl.pallas_call(
        functools.partial(forward_kernel, ranked),
        out_shape=(jax.ShapeDtypeStruct((rows, 128), jnp.float32),) * 2,
        in_specs=[smem, smem] + [whole] * 4,
        out_specs=(whole, whole),
        cost_estimate=pl.CostEstimate(flops=12000000000, bytes_accessed=0, transcendentals=0),
        compiler_params=pltpu.CompilerParams(vmem_limit_bytes=60 << 20),
    )(lens, own, q, qm, kv, km)


def with_stat(marks, stat, lane, at):
    high = stat.astype(jnp.bfloat16)
    rest = stat - high.astype(jnp.float32)
    middle = rest.astype(jnp.bfloat16)
    tail = (rest - middle.astype(jnp.float32)).astype(jnp.bfloat16)
    side = jnp.where(lane == at, high, jnp.where(lane == at + 1, middle, jnp.where(lane == at + 2, tail, marks)))
    return side


def backward_kernel(ranked, lens_ref, own_ref, q_ref, qm_ref, kv_ref, km_ref, o_ref, lse_ref, do_ref,
                    dq_ref, dkv_ref, own_dkv_ref, dk_ref, dv_ref):
    rows = q_ref.shape[0]
    base = own_ref[0] * rows
    half = left_half((BLOCK, 128))
    lane = lax.broadcasted_iota(jnp.int32, (BLOCK, 128), 1)
    one = jnp.ones((BLOCK, 128), jnp.bfloat16)
    zero = jnp.zeros((BLOCK, 128), jnp.bfloat16)

    def clear(index, _):
        at = pl.multiple_of(index * BLOCK, BLOCK)
        dk_ref[pl.ds(at, BLOCK), :] = jnp.zeros((BLOCK, 128), jnp.float32)
        dv_ref[pl.ds(at, BLOCK), :] = jnp.zeros((BLOCK, 128), jnp.float32)
        return 0

    lax.fori_loop(0, kv_ref.shape[0] // BLOCK, clear, 0)

    def one_block(block, _):
        start = pl.multiple_of(block * BLOCK, BLOCK)
        first = base + start
        low, high = spans(lens_ref, first, BLOCK)
        here = pl.ds(start, BLOCK)
        q, qm, do, lse = q_ref[here, :], qm_ref[here, :], do_ref[here, :], lse_ref[here, :]
        shared = do.astype(jnp.float32) * o_ref[here, :]
        delta0 = jnp.sum(jnp.where(half, shared, 0.0), axis=1, keepdims=True)
        delta1 = jnp.sum(jnp.where(half, 0.0, shared), axis=1, keepdims=True)
        side = with_stat(qm, lse, lane % 64, STAT)
        queries = (jnp.where(half, q, side), jnp.where(half, side, q))
        side = with_stat(zero, -jnp.where(half, delta1, delta0), lane % 64, STAT)
        grads = (jnp.where(half, do, side), jnp.where(half, side, do))

        def step(at, carry, diagonal=False):
            there = pl.ds(at, BLOCK)
            k, v, km = kv_ref[there, :128], kv_ref[there, 128:], km_ref[there, :]
            keys = (jnp.where(half, k, km), jnp.where(half, km, k))
            values = (jnp.where(half, v, one), jnp.where(half, one, v))
            scores = [dot(keys[h], queries[h], 1, 1) for h in (0, 1)]
            if diagonal:
                other = first + lax.broadcasted_iota(jnp.int32, (BLOCK, BLOCK), 0)
                row = first + lax.broadcasted_iota(jnp.int32, (1, BLOCK), 1)
                banned = other == jnp.where(openings(lens_ref, row), -1, row)
                scores = [jnp.where(banned, HIDE, s) for s in scores]
            dvs, dks, dqs = [], [], []
            for h in (0, 1):
                p = jnp.exp(scores[h])
                dp = dot(values[h], grads[h], 1, 1)
                ds = (p * dp).astype(jnp.bfloat16)
                dvs.append(dot(p.astype(jnp.bfloat16), do, 1, 0))
                dks.append(dot(ds, q, 1, 0))
                dqs.append(dot(ds, k, 0, 0))
            dv_ref[there, :] += jnp.where(half, dvs[0], dvs[1])
            dk_ref[there, :] += jnp.where(half, dks[0], dks[1])
            return carry + jnp.where(half, dqs[0], dqs[1])

        dq = over_blocks(low, high, first, BLOCK, step, jnp.zeros((BLOCK, 128), jnp.float32), ranked)
        dq_ref[here, :] = (dq * 0.125).astype(dq_ref.dtype)
        return 0

    lax.fori_loop(0, rows // BLOCK, one_block, 0)

    def save(index, _):
        there = pl.ds(pl.multiple_of(index * BLOCK, BLOCK), BLOCK)
        dkv_ref[there, :128] = dk_ref[there, :].astype(jnp.bfloat16)
        dkv_ref[there, 128:] = dv_ref[there, :].astype(jnp.bfloat16)
        return 0

    lax.fori_loop(0, kv_ref.shape[0] // BLOCK, save, 0)
    mine = pl.ds(pl.multiple_of(base, BLOCK), rows)
    own_dkv_ref[:, :128] = dk_ref[mine, :]
    own_dkv_ref[:, 128:] = dv_ref[mine, :]


def attend_backward(ranked, lens, own, q, qm, kv, km, o, lse, do):
    rows, keys = q.shape[0], kv.shape[0]
    whole = pl.BlockSpec(memory_space=pltpu.VMEM)
    smem = pl.BlockSpec(memory_space=pltpu.SMEM)
    return pl.pallas_call(
        functools.partial(backward_kernel, ranked),
        out_shape=(jax.ShapeDtypeStruct((rows, 128), jnp.bfloat16),) + (
            jax.ShapeDtypeStruct((keys, 256), jnp.bfloat16), jax.ShapeDtypeStruct((rows, 256), jnp.float32)),
        in_specs=[smem, smem] + [whole] * 7,
        out_specs=(whole, whole, whole),
        scratch_shapes=[pltpu.VMEM((keys, 128), jnp.float32)] * 2,
        cost_estimate=pl.CostEstimate(flops=26000000000, bytes_accessed=0, transcendentals=0),
        compiler_params=pltpu.CompilerParams(vmem_limit_bytes=60 << 20),
    )(lens, own, q, qm, kv, km, o, lse, do)


def matmul(left, right):
    return jnp.dot(left, right, preferred_element_type=jnp.float32)


def left_product(left, right):
    return jnp.einsum("ta,tb->ab", left, right, preferred_element_type=jnp.float32)


def right_product(left, right):
    return jnp.einsum("ta,ba->tb", left, right, preferred_element_type=jnp.float32)


def column_sum(value):
    return jnp.sum(value.astype(jnp.float32), axis=0)


def gelu_slope(value):
    cumulative = 0.5 * (1.0 + lax.erf(value * ROOT_HALF))
    return cumulative + value * jnp.exp(-0.5 * value * value) * INV_ROOT_TWO_PI


def norm_forward(value, gain_row, shift_row):
    middle = jnp.mean(value, axis=-1, keepdims=True)
    centred = value - middle
    spread = jnp.mean(centred * centred, axis=-1, keepdims=True)
    inverse = lax.rsqrt(spread + EPSILON)
    normed = centred * inverse
    return (normed * gain_row + shift_row, normed, inverse)


def norm_backward(incoming, normed, inverse, gain_row):
    scaled = incoming * gain_row
    centred = (
        scaled
        - jnp.mean(scaled, axis=-1, keepdims=True)
        - normed * jnp.mean(scaled * normed, axis=-1, keepdims=True)
    )
    return (inverse * centred, jnp.sum(incoming * normed, axis=0), jnp.sum(incoming, axis=0))


MESH = pl.DeviceIdType.MESH
ANY = pl.BlockSpec(memory_space=pltpu.HBM)
VMEM = pl.BlockSpec(memory_space=pltpu.VMEM)
SMEM = pl.BlockSpec(memory_space=pltpu.SMEM)
DMA = pltpu.SemaphoreType.DMA


def across(place, offset):
    if offset == 1:
        return place + 1 - 2 * lax.rem(place, 2)
    if offset == 2:
        return lax.rem(place + 2, 4)
    return 3 - place


def remote(src, dst, sends, recvs, where):
    return pltpu.make_async_remote_copy(
        src_ref=src, dst_ref=dst, send_sem=sends, recv_sem=recvs, device_id=where, device_id_type=MESH)


def greet(grp_count, wa_count, plane=True, groups=True, rows=True):
    barrier = pltpu.get_barrier_semaphore()
    grp, pln, wa = lax.axis_index("grp"), lax.axis_index("pln"), lax.axis_index("wa")

    def hello(where):
        pl.semaphore_signal(barrier, inc=1, device_id=where, device_id_type=MESH)

    count = 0
    if plane:
        for offset in (1, 2, 3):
            hello({"pln": across(pln, offset)})
        count += 3
    if rows:
        for offset in range(1, wa_count):
            hello({"wa": lax.rem(wa + offset, wa_count)})
        count += wa_count - 1
    if groups:
        @pl.when(grp > 0)
        def _():
            hello({"grp": grp - 1})

        @pl.when(grp < grp_count - 1)
        def _():
            hello({"grp": grp + 1})

        count = count + jnp.where(grp > 0, 1, 0) + jnp.where(grp < grp_count - 1, 1, 0)
    pl.semaphore_wait(barrier, count)


class Rows:
    def __init__(self, shard, full, sems, index, wa_count, stage=None):
        self.shard, self.full, self.sems, self.index, self.wa_count = shard, full, sems, index, wa_count
        self.stage = stage
        self.size = shard.shape[0]
        self.half = self.size // 2
        self.wa, self.pln = lax.axis_index("wa"), lax.axis_index("pln")
        self.core = lax.rem(self.pln, 2)

    def part(self, owner, core):
        return pl.ds(pl.multiple_of(owner * self.size + core * self.half, 16), self.half)

    def keep(self):
        own = pl.ds(pl.multiple_of(self.wa * self.size, 16), self.size)
        source = self.shard if self.stage is None else self.stage
        return pltpu.make_async_copy(source, self.full.at[own], self.sems.at[0, self.index, 0])

    def load(self):
        return pltpu.make_async_copy(self.shard, self.stage, self.sems.at[0, self.index, 0])

    def push(self, offset):
        mine = pl.ds(pl.multiple_of(self.core * self.half, 16), self.half)
        return remote(self.shard.at[mine], self.full.at[self.part(self.wa, self.core)],
                      self.sems.at[1, self.index, offset - 1], self.sems.at[2, self.index, offset - 1],
                      {"wa": lax.rem(self.wa + offset, self.wa_count)})

    def hand(self, offset):
        owner = lax.rem(self.wa + self.wa_count - offset, self.wa_count)
        spot = self.full.at[self.part(owner, self.core)]
        return remote(spot, spot, self.sems.at[3, self.index, offset - 1], self.sems.at[4, self.index, offset - 1],
                      {"pln": across(self.pln, 1)})

    def begin(self):
        if self.stage is None:
            self.keep().start()
        else:
            self.load().start()
        for offset in range(1, self.wa_count):
            self.push(offset).start()

    def staged(self):
        self.load().wait()
        self.keep().start()

    def pass_on(self):
        for offset in range(1, self.wa_count):
            self.push(offset).wait_recv()
            self.hand(offset).start()

    def arrived(self):
        self.keep().wait()
        for offset in range(1, self.wa_count):
            self.hand(offset).wait_recv()

    def finish(self):
        for offset in range(1, self.wa_count):
            self.push(offset).wait_send()
            self.hand(offset).wait_send()


class Line:
    def __init__(self, full, sems, grp_count, reach, block):
        self.full, self.sems, self.count, self.reach, self.block = full, sems, grp_count, reach, block
        self.grp = lax.axis_index("grp")

    def rows(self, owner, block):
        return pl.ds(pl.multiple_of((owner * PLANE + block) * self.block, 16), self.block)

    def copy(self, side, step, block, source=None):
        toward = 1 if side == 0 else -1
        owner = self.grp - toward * (step - 1)
        spot = self.full.at[self.rows(owner, block)]
        return remote(spot if source is None else source, spot, self.sems.at[0, side, step - 1, block],
                      self.sems.at[1, side, step - 1, block], {"grp": self.grp + toward})

    def sends(self, side, step):
        if side == 0:
            return jnp.logical_and(self.grp - step + 1 >= 0, self.grp + 1 < self.count)
        return jnp.logical_and(self.grp + step - 1 < self.count, self.grp - 1 >= 0)

    def receives(self, side, step):
        return self.grp - step >= 0 if side == 0 else self.grp + step < self.count

    def send(self, step, block, source=None):
        for side in (0, 1):
            @pl.when(self.sends(side, step))
            def _():
                self.copy(side, step, block, source).start()

    def arrival(self, side, step, block):
        toward = 1 if side == 0 else -1
        spot = self.full.at[self.rows(self.grp - toward * step, block)]
        return remote(spot, spot, self.sems.at[0, side, step - 1, block], self.sems.at[1, side, step - 1, block],
                      {"grp": self.grp - toward})

    def forward(self, step):
        for block in range(PLANE):
            for side in (0, 1):
                @pl.when(self.receives(side, step))
                def _():
                    self.arrival(side, step, block).wait_recv()

                    if step < self.reach:
                        @pl.when(self.sends(side, step + 1))
                        def _():
                            self.copy(side, step + 1, block).start()

    def finish(self, source=None):
        for step in range(1, self.reach + 1):
            for block in range(PLANE):
                for side in (0, 1):
                    @pl.when(self.sends(side, step))
                    def _():
                        self.copy(side, step, block, source[block] if source and step == 1 else None).wait_send()


class Swap:
    def __init__(self, src, dst, sems):
        self.src, self.dst, self.sems = src, dst, sems
        self.pln = lax.axis_index("pln")

    def copy(self, offset):
        peer = across(self.pln, offset)
        return remote(self.src(peer), self.dst(self.pln), self.sems.at[0, offset], self.sems.at[1, offset], {"pln": peer})

    def keep(self):
        return pltpu.make_async_copy(self.src(self.pln), self.dst(self.pln), self.sems.at[0, 0])

    def begin(self):
        for offset in (2, 3, 1):
            self.copy(offset).start()
        self.keep().start()

    def arrived(self, offset):
        self.keep().wait() if offset == 0 else self.copy(offset).wait_recv()

    def finish(self):
        for offset in (1, 2, 3):
            self.copy(offset).wait_send()


def pack_vectors(refs, pack):
    pack[...] = jnp.zeros_like(pack)
    at = 0
    for ref in refs:
        length = ref.shape[0]
        width = min(128, length)
        line = ref[...].astype(jnp.float32).reshape(1, length)
        for start in range(0, length, width):
            pack[at : at + 1, :width] = line[:, start : start + width]
            at += 1


def columns_of(ref, block):
    at = pl.multiple_of(block * 128, 128)
    line = ref[0:1, pl.ds(at, 128)].astype(jnp.float32)
    return jnp.transpose(jnp.broadcast_to(line, (128, 128)))


def make_marks(lens_ref, ranks_ref, limits_ref, base, self_keys, cross_keys, self_queries, cross_queries):
    docs = lens_ref.shape[1]
    lane = lax.rem(lax.broadcasted_iota(jnp.int32, (128, 128), 1), 64)
    stat = jnp.where(jnp.logical_and(lane >= STAT, lane < STAT + 3), -1.0, 0.0)

    def document(place):
        doc, opened, total = jnp.zeros((128, 128), jnp.int32), place == 0, 0
        for d in range(docs):
            total = total + lens_ref[0, d]
            doc = doc + jnp.where(place >= total, 1, 0)
            if d < docs - 1:
                opened = jnp.logical_or(opened, place == total)
        return doc, opened

    def keys(block, _):
        place = block * 128 + lax.broadcasted_iota(jnp.int32, (128, 128), 0)
        doc, opened = document(place)
        rank = jnp.where(opened, 0, columns_of(ranks_ref, block).astype(jnp.int32) + 1)
        marks = jnp.where(lane == doc, 1.0, stat)
        there = pl.ds(pl.multiple_of(block * 128, 128), 128)
        cross_keys[there, :] = marks.astype(jnp.bfloat16)
        self_keys[there, :] = jnp.where(lane == rank + 16, 1.0, marks).astype(jnp.bfloat16)
        return 0

    def queries(block, _):
        place = base + block * 128 + lax.broadcasted_iota(jnp.int32, (128, 128), 0)
        doc, _ = document(place)
        limit = columns_of(limits_ref, base // 128 + block).astype(jnp.int32)
        marks = jnp.where(jnp.logical_and(lane < docs, lane != doc), HIDE, 0.0)
        ranks = jnp.logical_and(lane >= 16, jnp.logical_and(lane < 33, lane - 17 >= limit))
        there = pl.ds(pl.multiple_of(block * 128, 128), 128)
        cross_queries[there, :] = marks.astype(jnp.bfloat16)
        self_queries[there, :] = jnp.where(ranks, HIDE, marks).astype(jnp.bfloat16)
        return 0

    lax.fori_loop(0, self_keys.shape[0] // 128, keys, 0)
    lax.fori_loop(0, self_queries.shape[0] // 128, queries, 0)


def vector_row(pack_ref, wa_count, start, length):
    width = min(128, length)
    pieces = []
    for wa in range(wa_count):
        for row in range(length // width):
            pieces.append(pack_ref[wa, start + row : start + row + 1, :width])
    return jnp.concatenate(pieces, axis=1)


def split_pairs(value, buffer, column):
    for pair in range(PLANE):
        buffer[pair, :, column : column + 128] = value[:, pair * 128 : pair * 128 + 128]


def opening_kernel(grp_count, wa_count, reach, count, vec_at, lens_ref, ranks_ref, limits_ref, content_ref, query_ref,
                   encoder_ref, *refs):
    vecs, refs = refs[: len(vec_at)], refs[len(vec_at) :]
    shards = refs[:count]
    fulls = refs[count : 2 * count]
    vec_out, q_out, kv_out, kv2_out = refs[2 * count : 2 * count + 4]
    mark_outs = refs[2 * count + 4 : 2 * count + 8]
    marks = refs[2 * count + 8 : 2 * count + 12]
    vec_ref, held, vec_all, kvbuf, kvbuf2, qbuf, row_sems, vec_sems, line_sems, swap_sems, out_sems = refs[2 * count + 12 :]
    grp, pln, wa = lax.axis_index("grp"), lax.axis_index("pln"), lax.axis_index("wa")
    tok = content_ref.shape[0]
    gathers = [Rows(shards[i], held.at[i], row_sems, i, wa_count) for i in range(count)]
    pack_vectors(vecs, vec_ref)
    greet(grp_count, wa_count)
    vec_keep = pltpu.make_async_copy(vec_ref, vec_all.at[wa], vec_sems.at[0, 0])
    vec_keep.start()
    pushes = [remote(vec_ref, vec_all.at[wa], vec_sems.at[0, o], vec_sems.at[1, o], {"wa": lax.rem(wa + o, wa_count)})
              for o in range(1, wa_count)]
    for g in gathers[:2]:
        g.begin()
    for p in pushes:
        p.start()
    for g in gathers[:2]:
        g.pass_on()
    for g in gathers[2:5]:
        g.begin()
    vec_keep.wait()
    for p in pushes:
        p.wait_recv()
    for g in gathers[:2]:
        g.arrived()
    content = content_ref[...]
    split_pairs(matmul(content, held[0]).astype(jnp.bfloat16), kvbuf, 0)
    row = lambda i: vector_row(vec_all, wa_count, *vec_at[i])
    split_pairs((matmul(content, held[1]) + row(1)).astype(jnp.bfloat16), kvbuf, 128)
    line = Line(kv_out, line_sems, grp_count, reach, tok)
    spot = lambda ref: lambda p: ref.at[pl.ds(pl.multiple_of((grp * PLANE + p) * tok, 16), tok)]
    swap = Swap(lambda p: kvbuf.at[p], spot(kv_out), swap_sems.at[0])
    swap.begin()
    line.send(1, pln, kvbuf.at[pln])
    swap.arrived(1)
    line.send(1, across(pln, 1))
    for g in gathers[2:5]:
        g.pass_on()
    for g in gathers[5:]:
        g.begin()
    for offset in (2, 3):
        swap.arrived(offset)
        line.send(1, across(pln, offset))
    for g in gathers[2:5]:
        g.arrived()
    outs = [pltpu.make_async_copy(held.at[i], fulls[i], out_sems.at[i]) for i in range(count)]
    for o in outs[:5]:
        o.start()
    vec_save = pltpu.make_async_copy(vec_all, vec_out, out_sems.at[count])
    vec_save.start()
    query = (matmul(query_ref[...], held[2]) + row(0)).astype(jnp.bfloat16)
    query = query * 0.125
    for pair in range(PLANE):
        qbuf[pair] = query[:, pair * 128 : pair * 128 + 128]
    place = lambda p: q_out.at[pl.ds(pl.multiple_of(p * tok, 16), tok)]
    swap_q = Swap(lambda p: qbuf.at[p], place, swap_sems.at[1])
    swap_q.begin()
    encoder = encoder_ref[...]
    split_pairs(matmul(encoder, held[3]).astype(jnp.bfloat16), kvbuf2, 0)
    split_pairs((matmul(encoder, held[4]) + row(2)).astype(jnp.bfloat16), kvbuf2, 128)
    place2 = lambda p: kv2_out.at[pl.ds(pl.multiple_of(p * tok, 16), tok)]
    swap_2 = Swap(lambda p: kvbuf2.at[p], place2, swap_sems.at[2])
    swap_2.begin()
    make_marks(lens_ref, ranks_ref, limits_ref, grp * PLANE * tok, *marks)
    mark_saves = [pltpu.make_async_copy(m, o, out_sems.at[count + 1 + i]) for i, (m, o) in enumerate(zip(marks, mark_outs))]
    for m in mark_saves:
        m.start()
    for step in range(1, reach + 1):
        line.forward(step)
    swap.arrived(0)
    for s in (swap_q, swap_2):
        for offset in range(4):
            s.arrived(offset)
    for g in gathers[5:]:
        g.pass_on()
    for g in gathers[5:]:
        g.arrived()
    for o in outs[5:]:
        o.start()
    for g in gathers:
        g.finish()
    for p in pushes:
        p.wait_send()
    for o in outs:
        o.wait()
    vec_save.wait()
    for m in mark_saves:
        m.wait()
    line.finish()
    for s in (swap, swap_q, swap_2):
        s.finish()


def run_opening(grp_count, wa_count, lens, ranks, limits, content, query, encoder, vecs, mats, vec_at):
    tok = content.shape[0]
    reach = min(grp_count - 1, (DOCLEN + PLANE * tok - 2) // (PLANE * tok))
    count = len(mats)
    low = jnp.bfloat16
    shape = lambda *s: jax.ShapeDtypeStruct(s, low)
    out_shape = [shape(m.shape[0] * wa_count, m.shape[1]) for m in mats]
    rows, keys = PLANE * tok, grp_count * PLANE * tok
    used = sum(length // min(128, length) for _, length in vec_at)
    pack = (used + -used % 16, 128)
    marks = [(keys, 128), (keys, 128), (rows, 128), (rows, 128)]
    out_shape += [jax.ShapeDtypeStruct((wa_count,) + pack, jnp.float32), shape(rows, 128), shape(keys, 256), shape(rows, 256)]
    out_shape += [shape(*m) for m in marks]
    return pl.pallas_call(
        functools.partial(opening_kernel, grp_count, wa_count, reach, count, vec_at),
        out_shape=tuple(out_shape),
        in_specs=[SMEM] + [VMEM] * (5 + len(vecs)) + [ANY] * count,
        out_specs=tuple([ANY] * len(out_shape)),
        scratch_shapes=[pltpu.VMEM(m, low) for m in marks] + [
            pltpu.VMEM(pack, jnp.float32), pltpu.VMEM((count, 512, 512), low), pltpu.VMEM((wa_count,) + pack, jnp.float32),
            pltpu.VMEM((PLANE, tok, 256), low), pltpu.VMEM((PLANE, tok, 256), low), pltpu.VMEM((PLANE, tok, 128), low),
            DMA((5, count, max(1, wa_count - 1))), DMA((2, wa_count)), DMA((2, 2, reach, PLANE)), DMA((3, 2, 4)),
            DMA((count + 5,))],
        cost_estimate=pl.CostEstimate(flops=38000000000, bytes_accessed=0, transcendentals=0),
        compiler_params=pltpu.CompilerParams(collective_id=1, has_side_effects=True, vmem_limit_bytes=60 << 20),
    )(lens, ranks, limits, content, query, encoder, *vecs, *mats)


def flat_pairs(buffer):
    return jnp.concatenate([buffer[p] for p in range(PLANE)], axis=1)


def middle_kernel(grp_count, wa_count, reach, vec_at, attended_ref, query_ref, out_mat_ref, query_mat_ref, vec_ref,
                  kv_own_ref, expand_ref, shrink_ref,
                  hidden_ref, normed_ref, inverse_ref, mixed_ref, q_out, kv_out, expand_full, shrink_full,
                  sendbuf, mixbuf, qbuf, expand_stage, shrink_stage, kv_stage, row_sems, line_sems, swap_sems, keep_sem):
    grp, pln = lax.axis_index("grp"), lax.axis_index("pln")
    tok = query_ref.shape[0]
    gathers = [Rows(expand_ref, expand_full, row_sems, 0, wa_count, expand_stage),
               Rows(shrink_ref, shrink_full, row_sems, 1, wa_count, shrink_stage)]
    load = pltpu.make_async_copy(kv_own_ref, kv_stage, keep_sem)
    load.start()
    for p in range(PLANE):
        sendbuf[p] = attended_ref[p * tok : p * tok + tok, :].astype(jnp.bfloat16)
    greet(grp_count, wa_count)
    swap = Swap(lambda p: sendbuf.at[p], lambda p: mixbuf.at[p], swap_sems.at[0])
    swap.begin()
    line = Line(kv_out, line_sems, grp_count, reach, tok)
    sources = [kv_own_ref.at[pl.ds(b * tok, tok)] for b in range(PLANE)]
    for b in range(PLANE):
        line.send(1, b, sources[b])
    for g in gathers:
        g.begin()
    whole = pl.ds(pl.multiple_of(grp * PLANE * tok, 16), PLANE * tok)
    load.wait()
    keep = pltpu.make_async_copy(kv_stage, kv_out.at[whole], keep_sem)
    keep.start()
    row = lambda i: vector_row(vec_ref, wa_count, *vec_at[i])
    for offset in range(4):
        swap.arrived(offset)
    mixed = flat_pairs(mixbuf)
    mixed_ref[...] = mixed
    value = query_ref[...].astype(jnp.float32) + matmul(mixed, out_mat_ref[...]) + row(3)
    hidden, normed, inverse = norm_forward(value, row(4), row(5))
    hidden_ref[...] = hidden
    normed_ref[...] = normed
    inverse_ref[...] = jnp.broadcast_to(inverse, inverse_ref.shape)
    query = (matmul(hidden.astype(jnp.bfloat16), query_mat_ref[...]) + row(6)).astype(jnp.bfloat16) * 0.125
    for pair in range(PLANE):
        qbuf[pair] = query[:, pair * 128 : pair * 128 + 128]
    place = lambda p: q_out.at[pl.ds(pl.multiple_of(p * tok, 16), tok)]
    swap_q = Swap(lambda p: qbuf.at[p], place, swap_sems.at[1])
    swap_q.begin()
    for g in gathers:
        g.staged()
    line.forward(1)
    for g in gathers:
        g.pass_on()
    for step in range(2, reach + 1):
        line.forward(step)
    for offset in range(4):
        swap_q.arrived(offset)
    for g in gathers:
        g.arrived()
    for g in gathers:
        g.finish()
    line.finish(sources)
    keep.wait()
    swap.finish()
    swap_q.finish()


def run_middle(grp_count, wa_count, attended, query, out_mat, query_mat, vecs, vec_at, kv_own, expand, shrink):
    tok = query.shape[0]
    reach = min(grp_count - 1, (DOCLEN + PLANE * tok - 2) // (PLANE * tok))
    low, full = jnp.bfloat16, jnp.float32
    shape = jax.ShapeDtypeStruct
    return pl.pallas_call(
        functools.partial(middle_kernel, grp_count, wa_count, reach, vec_at),
        out_shape=(shape((tok, 512), full), shape((tok, 512), full), shape((tok, 128), full), shape((tok, 512), low),
                   shape((PLANE * tok, 128), low), shape((grp_count * PLANE * tok, 256), low),
                   shape((expand.shape[0] * wa_count, expand.shape[1]), low),
                   shape((shrink.shape[0] * wa_count, shrink.shape[1]), low)),
        in_specs=[VMEM] * 5 + [ANY] * 3,
        out_specs=tuple([VMEM] * 4 + [ANY] * 4),
        scratch_shapes=[
            pltpu.VMEM((PLANE, tok, 128), low), pltpu.VMEM((PLANE, tok, 128), low), pltpu.VMEM((PLANE, tok, 128), low),
            pltpu.VMEM(expand.shape, low), pltpu.VMEM(shrink.shape, low), pltpu.VMEM((PLANE * tok, 256), low),
            DMA((5, 2, max(1, wa_count - 1))), DMA((2, 2, reach, PLANE)), DMA((2, 2, 4)), DMA],
        cost_estimate=pl.CostEstimate(flops=30000000000, bytes_accessed=0, transcendentals=0),
        compiler_params=pltpu.CompilerParams(collective_id=2, has_side_effects=True, vmem_limit_bytes=60 << 20),
    )(attended, query, out_mat, query_mat, vecs, kv_own, expand, shrink)


def swap_kernel(inverse, in_ref, out_ref, sendbuf, getbuf, swap_sems):
    tok = getbuf.shape[1]
    for p in range(PLANE):
        if inverse:
            sendbuf[p] = in_ref[p * tok : p * tok + tok, :].astype(jnp.bfloat16)
        else:
            sendbuf[p] = in_ref[:, p * 128 : p * 128 + 128].astype(jnp.bfloat16)
    greet(1, 1, groups=False, rows=False)
    swap = Swap(lambda p: sendbuf.at[p], lambda p: getbuf.at[p], swap_sems)
    swap.begin()
    for offset in range(4):
        swap.arrived(offset)
    for p in range(PLANE):
        if inverse:
            out_ref[:, p * 128 : p * 128 + 128] = getbuf[p]
        else:
            out_ref[p * tok : p * tok + tok, :] = getbuf[p]
    swap.finish()


def run_swap(inverse, value, ident):
    tok = value.shape[0] // PLANE if inverse else value.shape[0]
    low = jnp.bfloat16
    return pl.pallas_call(
        functools.partial(swap_kernel, inverse),
        out_shape=jax.ShapeDtypeStruct((tok, 512) if inverse else (PLANE * tok, 128), low),
        in_specs=[VMEM], out_specs=VMEM,
        scratch_shapes=[pltpu.VMEM((PLANE, tok, 128), low), pltpu.VMEM((PLANE, tok, 128), low), DMA((2, 4))],
        cost_estimate=pl.CostEstimate(flops=6000000000, bytes_accessed=0, transcendentals=0),
        compiler_params=pltpu.CompilerParams(collective_id=ident, has_side_effects=True, vmem_limit_bytes=60 << 20),
    )(value)


class Fold:
    def __init__(self, partial, mine, sendbuf, getbuf, sems, load_sems, grp_count, reach, block):
        self.partial, self.mine, self.sendbuf, self.getbuf = partial, mine, sendbuf, getbuf
        self.sems, self.load_sems = sems, load_sems
        self.count, self.reach, self.block = grp_count, reach, block
        self.grp = lax.axis_index("grp")

    def toward(self, side):
        return 1 if side == 0 else -1

    def rows(self, owner, block):
        return pl.ds(pl.multiple_of((owner * PLANE + block) * self.block, 16), self.block)

    def part(self, block):
        return pl.ds(block * self.block, self.block)

    def sends(self, side, stage):
        return self.grp + stage < self.count if side == 0 else self.grp - stage >= 0

    def receives(self, side, stage):
        if side == 0:
            return jnp.logical_and(self.grp >= 1, self.grp - 1 + stage < self.count)
        return jnp.logical_and(self.grp + 1 < self.count, self.grp + 1 - stage >= 0)

    def copy(self, side, stage, block, back=False):
        source = self.sendbuf.at[side, stage - 1, self.part(block)]
        if stage == self.reach and not back:
            source = self.partial.at[self.rows(self.grp + self.toward(side) * stage, block)]
        peer = self.grp + (-self.toward(side) if back else self.toward(side))
        return remote(source, self.getbuf.at[side, stage - 1, self.part(block)], self.sems.at[0, side, stage - 1, block],
                      self.sems.at[1, side, stage - 1, block], {"grp": peer})

    def load(self, side, stage):
        size = PLANE * self.block
        rows = pl.ds(pl.multiple_of((self.grp + self.toward(side) * stage) * size, 16), size)
        return pltpu.make_async_copy(self.partial.at[rows], self.mine.at[side, stage - 1], self.load_sems.at[side, stage - 1])

    def begin(self):
        for block in range(PLANE):
            for side in (0, 1):
                @pl.when(self.sends(side, self.reach))
                def _():
                    self.copy(side, self.reach, block).start()
        for stage in range(1, self.reach):
            for side in (0, 1):
                @pl.when(self.sends(side, stage))
                def _():
                    self.load(side, stage).start()

    def grow(self, stage):
        for side in (0, 1):
            @pl.when(self.sends(side, stage))
            def _():
                self.load(side, stage).wait()
        for block in range(PLANE):
            part = self.part(block)
            for side in (0, 1):
                @pl.when(self.sends(side, stage))
                def _():
                    self.sendbuf[side, stage - 1, part, :] = self.mine[side, stage - 1, part, :]

                    @pl.when(self.receives(side, stage + 1))
                    def _():
                        self.copy(side, stage + 1, block, True).wait_recv()
                        total = self.mine[side, stage - 1, part, :].astype(jnp.float32)
                        total = total + self.getbuf[side, stage, part, :].astype(jnp.float32)
                        self.sendbuf[side, stage - 1, part, :] = total.astype(jnp.bfloat16)

                    self.copy(side, stage, block).start()

    def total(self, own, out):
        for block in range(PLANE):
            part = self.part(block)
            for side in (0, 1):
                @pl.when(self.receives(side, 1))
                def _():
                    self.copy(side, 1, block, True).wait_recv()
                    own[part, :] = own[part, :] + self.getbuf[side, 0, part, :].astype(jnp.float32)
            out[block] = own[part, :].astype(jnp.bfloat16)

    def finish(self):
        for stage in range(1, self.reach + 1):
            for block in range(PLANE):
                for side in (0, 1):
                    @pl.when(self.sends(side, stage))
                    def _():
                        self.copy(side, stage, block, True).wait_send()


def store_blocks(buffer, value):
    for c in range(PLANE):
        buffer[c] = value[:, c * 128 : c * 128 + 128].astype(jnp.bfloat16)


def halves(buffer):
    keys = jnp.concatenate([buffer[p, :, :128] for p in range(PLANE)], axis=1)
    values = jnp.concatenate([buffer[p, :, 128:] for p in range(PLANE)], axis=1)
    return keys, values


def turn_kernel(grp_count, wa_count, reach, vec_at, dq_ref, dkv_ref, own_ref, back_ref, normed_ref, inverse_ref, hidden_ref,
                mixed_one_ref, mixed_two_ref, branch_two_ref, encoder_ref, query_mat_ref, out_mat_ref, vec_ref, vg_ref,
                do_out, back_out, kv_out, grads_out, vg_out,
                dqsend, dqget, dosend, doget, kvsend, kvget, total, mine, foldsend, foldget, grads, fold_sems, load_sems,
                swap_sems, out_sems):
    tok = back_ref.shape[0]
    for p in range(PLANE):
        dqsend[p] = dq_ref[p * tok : p * tok + tok, :]
    greet(grp_count, wa_count, rows=False)
    swap_dq = Swap(lambda p: dqsend.at[p], lambda p: dqget.at[p], swap_sems.at[0])
    swap_dq.begin()
    fold = Fold(dkv_ref, mine, foldsend, foldget, fold_sems, load_sems, grp_count, reach, tok)
    fold.begin()
    row = lambda i: vector_row(vec_ref, wa_count, *vec_at[i])
    vg_out[...] = vg_ref[...]
    saves = [pltpu.make_async_copy(grads.at[i], grads_out.at[i], out_sems.at[i]) for i in range(5)]
    total[...] = own_ref[...]
    store_blocks(grads.at[0], dot(mixed_two_ref[...], branch_two_ref[...], 0, 0))
    saves[0].start()
    for offset in range(4):
        swap_dq.arrived(offset)
    dq = flat_pairs(dqget)
    incoming = back_ref[...] + dot(dq, query_mat_ref[...], 1, 1)
    back, gain_grad, shift_grad = norm_backward(incoming, normed_ref[...], inverse_ref[:, :1], row(4))
    back_out[...] = back
    branch = back.astype(jnp.bfloat16)
    do = dot(branch, out_mat_ref[...], 1, 1).astype(jnp.bfloat16)
    for p in range(PLANE):
        dosend[p] = do[:, p * 128 : p * 128 + 128]
    swap_do = Swap(lambda p: dosend.at[p], lambda p: doget.at[p], swap_sems.at[1])
    swap_do.begin()
    vg_out[10:11, :] = gain_grad.reshape(1, 512)
    vg_out[11:12, :] = shift_grad.reshape(1, 512)
    vg_out[12:13, :] = column_sum(branch).reshape(1, 512)
    vg_out[13:14, :] = column_sum(dq).reshape(1, 512)
    store_blocks(grads.at[1], dot(hidden_ref[...].astype(jnp.bfloat16), dq, 0, 0))
    saves[1].start()
    store_blocks(grads.at[2], dot(mixed_one_ref[...], branch, 0, 0))
    saves[2].start()
    for stage in range(reach - 1, 0, -1):
        fold.grow(stage)
    for offset in range(4):
        swap_do.arrived(offset)
    for p in range(PLANE):
        do_out[p * tok : p * tok + tok, :] = doget[p]
    fold.total(total, kvsend)
    swap_kv = Swap(lambda p: kvsend.at[p], lambda p: kvget.at[p], swap_sems.at[2])
    swap_kv.begin()
    for offset in range(4):
        swap_kv.arrived(offset)
    keys, values = halves(kvget)
    kv_out[:, :512] = keys
    kv_out[:, 512:] = values
    encoder = encoder_ref[...]
    store_blocks(grads.at[3], dot(encoder, keys, 0, 0))
    saves[3].start()
    store_blocks(grads.at[4], dot(encoder, values, 0, 0))
    saves[4].start()
    vg_out[14:15, :] = column_sum(values).reshape(1, 512)
    for s in saves:
        s.wait()
    fold.finish()
    for s in (swap_dq, swap_do, swap_kv):
        s.finish()


def fold_scratch(tok, reach):
    low = jnp.bfloat16
    size = PLANE * tok
    return [pltpu.VMEM((PLANE, tok, 256), low), pltpu.VMEM((PLANE, tok, 256), low), pltpu.VMEM((size, 256), jnp.float32),
            pltpu.VMEM((2, max(1, reach - 1), size, 256), low), pltpu.VMEM((2, reach, size, 256), low),
            pltpu.VMEM((2, reach, size, 256), low)]


def run_turn(grp_count, wa_count, vec_at, dq, dkv, own, back, normed, inverse, hidden, mixed_one, mixed_two, branch_two,
             encoder, query_mat, out_mat, vecs, vg):
    tok = back.shape[0]
    reach = min(grp_count - 1, (DOCLEN + PLANE * tok - 2) // (PLANE * tok))
    low, full = jnp.bfloat16, jnp.float32
    shape = jax.ShapeDtypeStruct
    pairs = pltpu.VMEM((PLANE, tok, 128), low)
    return pl.pallas_call(
        functools.partial(turn_kernel, grp_count, wa_count, reach, vec_at),
        out_shape=(shape((PLANE * tok, 128), low), shape((tok, 512), full), shape((tok, 1024), low),
                   shape((5, PLANE, 512, 128), low), shape(vg.shape, full)),
        in_specs=[VMEM, ANY] + [VMEM] * 13,
        out_specs=(VMEM, VMEM, VMEM, ANY, VMEM),
        scratch_shapes=[pairs] * 4 + fold_scratch(tok, reach) + [
            pltpu.VMEM((5, PLANE, 512, 128), low), DMA((2, 2, reach, PLANE)), DMA((2, max(1, reach - 1))), DMA((3, 2, 4)),
            DMA((5,))],
        cost_estimate=pl.CostEstimate(flops=32000000000, bytes_accessed=0, transcendentals=0),
        compiler_params=pltpu.CompilerParams(collective_id=8, has_side_effects=True, vmem_limit_bytes=60 << 20),
    )(dq, dkv, own, back, normed, inverse, hidden, mixed_one, mixed_two, branch_two, encoder, query_mat, out_mat, vecs, vg)


class Reduce:
    def __init__(self, index, source, parts, got, kept, sems, wa_count):
        self.index, self.source, self.sems, self.wa_count = index, source, sems, wa_count
        self.parts, (self.got_core, self.got_wa, self.got_row) = parts, got
        self.by_core, self.by_wa, self.by_row = kept
        self.wa, self.pln = lax.axis_index("wa"), lax.axis_index("pln")
        self.core = lax.rem(self.pln, 2)
        self.row = self.pln // 2
        self.size = 512 // wa_count

    def core_copy(self, row):
        return remote(self.source.at[row * 2 + 1 - self.core], self.got_core.at[self.index, row],
                      self.sems.at[0, self.index, row], self.sems.at[1, self.index, row], {"pln": across(self.pln, 1)})

    def rows_of(self, wa):
        return pl.ds(pl.multiple_of(wa * self.size, 16), self.size)

    def wa_copy(self, offset):
        peer = lax.rem(self.wa + offset, self.wa_count)
        return remote(self.by_core.at[self.index, :, self.rows_of(peer)], self.got_wa.at[offset - 1, self.index],
                      self.sems.at[0, self.index, 1 + offset], self.sems.at[1, self.index, 1 + offset], {"wa": peer})

    def row_copy(self):
        return remote(self.by_wa.at[self.index, 1 - self.row], self.got_row.at[self.index],
                      self.sems.at[0, self.index, 1 + self.wa_count], self.sems.at[1, self.index, 1 + self.wa_count],
                      {"pln": across(self.pln, 2)})

    def begin(self):
        for row in (0, 1):
            self.core_copy(row).start()

    def after_core(self):
        for row in (0, 1):
            self.core_copy(row).wait_recv()
            mine = self.parts[row * 2 + self.core].astype(jnp.float32)
            total = mine + self.got_core[self.index, row].astype(jnp.float32)
            self.by_core[self.index, row] = total.astype(jnp.bfloat16)
        for offset in range(1, self.wa_count):
            self.wa_copy(offset).start()

    def after_wa(self):
        for offset in range(1, self.wa_count):
            self.wa_copy(offset).wait_recv()
        for row in (0, 1):
            total = self.by_core[self.index, row, self.rows_of(self.wa), :].astype(jnp.float32)
            for offset in range(1, self.wa_count):
                total = total + self.got_wa[offset - 1, self.index, row].astype(jnp.float32)
            self.by_wa[self.index, row] = total.astype(jnp.bfloat16)
        self.row_copy().start()

    def after_row(self):
        self.row_copy().wait_recv()
        total = self.by_wa[self.index, self.row].astype(jnp.float32) + self.got_row[self.index].astype(jnp.float32)
        self.by_row[self.index] = total.astype(jnp.bfloat16)

    def finish(self):
        for row in (0, 1):
            self.core_copy(row).wait_send()
        for offset in range(1, self.wa_count):
            self.wa_copy(offset).wait_send()
        self.row_copy().wait_send()


def greet_all(grp_count, wa_count):
    barrier = pltpu.get_barrier_semaphore()
    grp, pln, wa = lax.axis_index("grp"), lax.axis_index("pln"), lax.axis_index("wa")
    peers = [{"pln": across(pln, o)} for o in (1, 2, 3)]
    peers += [{"wa": lax.rem(wa + o, wa_count)} for o in range(1, wa_count)]
    peers += [{"grp": lax.rem(grp + o, grp_count)} for o in range(1, grp_count)]
    for where in peers:
        pl.semaphore_signal(barrier, inc=1, device_id=where, device_id_type=MESH)
    pl.semaphore_wait(barrier, len(peers))


def closing_kernel(grp_count, wa_count, reach, count, dq_ref, dkv_ref, own_ref, query_ref, content_ref, early_ref, vg_ref,
                   dq_out, kv_out, out_ref, vg_out,
                   dqsend, dqget, kvsend, kvget, total, mine, foldsend, foldget, parts, got_core, got_wa, got_row,
                   by_core, by_wa, by_row, got_grp, final, vsum, vgot, vall,
                   fold_sems, load_sems, swap_sems, part_sems, red_sems, vec_sems, grp_sems, share_sems):
    grp, pln, wa = lax.axis_index("grp"), lax.axis_index("pln"), lax.axis_index("wa")
    tok = query_ref.shape[0]
    early = early_ref.shape[0]
    size = 512 // wa_count
    slab = size // grp_count
    for p in range(PLANE):
        dqsend[p] = dq_ref[p * tok : p * tok + tok, :]
    greet_all(grp_count, wa_count)
    swap_dq = Swap(lambda p: dqsend.at[p], lambda p: dqget.at[p], swap_sems.at[0])
    swap_dq.begin()
    fold = Fold(dkv_ref, mine, foldsend, foldget, fold_sems, load_sems, grp_count, reach, tok)
    fold.begin()
    loads = [pltpu.make_async_copy(early_ref.at[i], parts.at[i], part_sems.at[i]) for i in range(early)]
    for l in loads:
        l.start()
    got, kept = (got_core, got_wa, got_row), (by_core, by_wa, by_row)
    reds = [Reduce(i, early_ref.at[i] if i < early else parts.at[i], parts.at[i], got, kept, red_sems, wa_count)
            for i in range(count)]
    for r in reds[:early]:
        r.begin()
    total[...] = own_ref[...]
    vsum[0] = vg_ref[...]
    for offset in range(4):
        swap_dq.arrived(offset)
    dq = flat_pairs(dqget)
    dq_out[...] = dq
    store_blocks(parts.at[early], dot(query_ref[...], dq, 0, 0))
    vsum[0, 15:16, :] = column_sum(dq).reshape(1, 512)
    reds[early].begin()
    for l in loads:
        l.wait()
    for r in reds[: early + 1]:
        r.after_core()
    for stage in range(reach - 1, 0, -1):
        fold.grow(stage)
    for r in reds[: early + 1]:
        r.after_wa()
    fold.total(total, kvsend)
    swap_kv = Swap(lambda p: kvsend.at[p], lambda p: kvget.at[p], swap_sems.at[1])
    swap_kv.begin()
    for r in reds[: early + 1]:
        r.after_row()
    for offset in range(4):
        swap_kv.arrived(offset)
    keys, values = halves(kvget)
    content = content_ref[...]
    store_blocks(parts.at[early + 1], dot(content, keys, 0, 0))
    reds[early + 1].begin()
    store_blocks(parts.at[early + 2], dot(content, values, 0, 0))
    reds[early + 2].begin()
    vsum[0, 16:17, :] = column_sum(values).reshape(1, 512)
    vec_core = remote(vsum.at[0], vgot.at[0], vec_sems.at[0, 0], vec_sems.at[1, 0], {"pln": across(pln, 1)})
    vec_core.start()
    kv_out[:, :512] = keys
    kv_out[:, 512:] = values

    def grp_copy(set_at, offset):
        start, length = ((0, early + 1), (early + 1, count - early - 1))[set_at]
        peer = lax.rem(grp + offset, grp_count)
        some = pl.ds(start, length)
        rows = pl.ds(pl.multiple_of(peer * slab, 8), slab)
        return remote(by_row.at[some, rows], got_grp.at[offset - 1, some], grp_sems.at[0, set_at, offset - 1],
                      grp_sems.at[1, set_at, offset - 1], {"grp": peer})

    offsets = range(1, grp_count)
    for o in offsets:
        grp_copy(0, o).start()
    for r in reds[early + 1 :]:
        r.after_core()
    vec_core.wait_recv()
    vsum[1] = vsum[0] + vgot[0]
    vec_wa = [remote(vsum.at[1], vgot.at[o], vec_sems.at[0, o], vec_sems.at[1, o], {"wa": lax.rem(wa + o, wa_count)})
              for o in range(1, wa_count)]
    for v in vec_wa:
        v.start()
    for r in reds[early + 1 :]:
        r.after_wa()
    for v in vec_wa:
        v.wait_recv()
    vall[wa] = vsum[1]
    for o in range(1, wa_count):
        vall[lax.rem(wa + wa_count - o, wa_count)] = vgot[o]
    joined = vall[0]
    for o in range(1, wa_count):
        joined = joined + vall[o]
    vsum[2] = joined
    vec_row = remote(vsum.at[2], vgot.at[wa_count], vec_sems.at[0, wa_count], vec_sems.at[1, wa_count],
                     {"pln": across(pln, 2)})
    vec_row.start()
    own_rows = pl.ds(pl.multiple_of(grp * slab, 8), slab)

    def settle(set_at):
        start, length = ((0, early + 1), (early + 1, count - early - 1))[set_at]
        some = pl.ds(start, length)
        for o in offsets:
            grp_copy(set_at, o).wait_recv()
        value = by_row[some, own_rows, :].astype(jnp.float32)
        for o in offsets:
            value = value + got_grp[o - 1, some].astype(jnp.float32)
        final[some] = value.astype(jnp.bfloat16)

    def spot(column, source, some):
        return out_ref.at[column, some, pl.ds(pl.multiple_of(source * slab, 8), slab)]

    def spread(set_at, offset):
        start, length = ((0, early + 1), (early + 1, count - early - 1))[set_at]
        some = pl.ds(start, length)
        return remote(final.at[some], spot(pln, grp, some), share_sems.at[0, set_at, 0, offset],
                      share_sems.at[1, set_at, 0, offset], {"grp": lax.rem(grp + offset, grp_count)})

    def keep(set_at):
        start, length = ((0, early + 1), (early + 1, count - early - 1))[set_at]
        some = pl.ds(start, length)
        return pltpu.make_async_copy(final.at[some], spot(pln, grp, some), share_sems.at[0, set_at, 0, 0])

    def give(set_at, kind, offset):
        start, length = ((0, early + 1), (early + 1, count - early - 1))[set_at]
        some = pl.ds(start, length)
        source = lax.rem(grp + grp_count - offset, grp_count)
        column = pln if kind < 3 else across(pln, 2)
        there = spot(column, source, some)
        return remote(there, there, share_sems.at[0, set_at, kind, offset], share_sems.at[1, set_at, kind, offset],
                      {"pln": across(pln, 2 if kind == 1 else 1)})

    settle(0)
    keep(0).start()
    for o in offsets:
        spread(0, o).start()
    for r in reds[early + 1 :]:
        r.after_row()
    for o in offsets:
        grp_copy(1, o).start()
    vec_row.wait_recv()
    vsum[3] = vsum[2] + vgot[wa_count]
    vec_grp = [remote(vsum.at[3], vall.at[wa_count + o], vec_sems.at[0, wa_count + o], vec_sems.at[1, wa_count + o],
                      {"grp": lax.rem(grp + o, grp_count)}) for o in offsets]
    for v in vec_grp:
        v.start()
    everyone = range(grp_count)

    def hand_out(set_at, offset):
        if offset == 0:
            keep(set_at).wait()
        else:
            spread(set_at, offset).wait_recv()
        give(set_at, 1, offset).start()
        give(set_at, 2, offset).start()

    for o in everyone:
        hand_out(0, o)
    settle(1)
    keep(1).start()
    for o in offsets:
        spread(1, o).start()
    for o in everyone:
        give(0, 1, o).wait_recv()
        give(0, 3, o).start()
    for o in everyone:
        hand_out(1, o)
    for v in vec_grp:
        v.wait_recv()
    ordered = jnp.zeros_like(vsum[3])
    for g in everyone:
        piece = jnp.where(grp == g, vsum[3], 0.0)
        for o in offsets:
            piece = piece + jnp.where(lax.rem(grp + grp_count - o, grp_count) == g, vall[wa_count + o], 0.0)
        ordered = ordered + piece
    vg_out[...] = ordered
    for o in everyone:
        give(1, 1, o).wait_recv()
        give(1, 3, o).start()
    for set_at in (0, 1):
        for o in everyone:
            give(set_at, 2, o).wait_recv()
            give(set_at, 3, o).wait_recv()
    for set_at in (0, 1):
        for o in everyone:
            for kind in (1, 2, 3):
                give(set_at, kind, o).wait_send()
        for o in offsets:
            spread(set_at, o).wait_send()
            grp_copy(set_at, o).wait_send()
    for v in [vec_core, vec_row] + vec_wa + vec_grp:
        v.wait_send()
    for r in reds:
        r.finish()
    fold.finish()
    swap_dq.finish()
    swap_kv.finish()


def run_closing(grp_count, wa_count, dq, dkv, own, query, content, early, vg):
    tok = query.shape[0]
    count = early.shape[0] + 3
    reach = min(grp_count - 1, (DOCLEN + PLANE * tok - 2) // (PLANE * tok))
    size = 512 // wa_count
    slab = size // grp_count
    low, full = jnp.bfloat16, jnp.float32
    shape = jax.ShapeDtypeStruct
    pairs = pltpu.VMEM((PLANE, tok, 128), low)
    steps = wa_count + 2
    return pl.pallas_call(
        functools.partial(closing_kernel, grp_count, wa_count, reach, count),
        out_shape=(shape((tok, 512), low), shape((tok, 1024), low), shape((PLANE, count, size, 128), low),
                   shape(vg.shape, full)),
        in_specs=[VMEM, ANY, VMEM, VMEM, VMEM, ANY, VMEM],
        out_specs=(VMEM, VMEM, ANY, VMEM),
        scratch_shapes=[pairs] * 2 + fold_scratch(tok, reach) + [
            pltpu.VMEM((count, PLANE, 512, 128), low), pltpu.VMEM((count, 2, 512, 128), low),
            pltpu.VMEM((max(1, wa_count - 1), count, 2, size, 128), low), pltpu.VMEM((count, size, 128), low),
            pltpu.VMEM((count, 2, 512, 128), low), pltpu.VMEM((count, 2, size, 128), low), pltpu.VMEM((count, size, 128), low),
            pltpu.VMEM((grp_count - 1, count, slab, 128), low), pltpu.VMEM((count, slab, 128), low),
            pltpu.VMEM((4,) + vg.shape, full), pltpu.VMEM((wa_count + 1,) + vg.shape, full),
            pltpu.VMEM((wa_count + grp_count,) + vg.shape, full),
            DMA((2, 2, reach, PLANE)), DMA((2, max(1, reach - 1))), DMA((2, 2, 4)), DMA((early.shape[0],)),
            DMA((2, count, steps)), DMA((2, wa_count + grp_count)), DMA((2, 2, grp_count - 1)), DMA((2, 2, 4, grp_count))],
        cost_estimate=pl.CostEstimate(flops=75000000000, bytes_accessed=0, transcendentals=0),
        compiler_params=pltpu.CompilerParams(collective_id=9, has_side_effects=True, vmem_limit_bytes=60 << 20),
    )(dq, dkv, own, query, content, early, vg)


def centre_kernel(wa_count, vec_at, attended_ref, hidden_ref, cotangent_ref, out_mat_ref, expand_ref, shrink_ref, vec_ref,
                  layer_out, mixed_out, back_out, branch_out, do_out, grad_shrink, grad_expand, vg_out,
                  sendbuf, getbuf, dosend, doget, slopes, actives, swap_sems):
    tok = hidden_ref.shape[0]
    for p in range(PLANE):
        sendbuf[p] = attended_ref[p * tok : p * tok + tok, :].astype(jnp.bfloat16)
    greet(1, 1, groups=False, rows=False)
    swap = Swap(lambda p: sendbuf.at[p], lambda p: getbuf.at[p], swap_sems.at[0])
    swap.begin()
    row = lambda i: vector_row(vec_ref, wa_count, *vec_at[i])
    vg_out[...] = jnp.zeros_like(vg_out)
    for offset in range(4):
        swap.arrived(offset)
    mixed = flat_pairs(getbuf)
    mixed_out[...] = mixed
    value = hidden_ref[...] + matmul(mixed, out_mat_ref[...]) + row(7)
    hidden, normed_two, inverse_two = norm_forward(value, row(8), row(9))
    low = hidden.astype(jnp.bfloat16)
    expand_row = row(10)
    total = hidden + row(11)
    width = 512
    chunks = expand_ref.shape[1] // width
    for c in range(chunks):
        span = slice(c * width, c * width + width)
        u = matmul(low, expand_ref[:, span]) + expand_row[:, span]
        cumulative = 0.5 * (1.0 + lax.erf(u * ROOT_HALF))
        active = (u * cumulative).astype(jnp.bfloat16)
        actives[:, span] = active
        slopes[:, span] = cumulative + u * jnp.exp(-0.5 * u * u) * INV_ROOT_TWO_PI
        total = total + matmul(active, shrink_ref[span, :])
    out, normed_three, inverse_three = norm_forward(total, row(12), row(13))
    layer_out[...] = out
    cotangent = cotangent_ref[...].astype(jnp.float32)
    back, gain_grad, shift_grad = norm_backward(cotangent, normed_three, inverse_three, row(12))
    vg_out[0:1, :] = gain_grad.reshape(1, 512)
    vg_out[1:2, :] = shift_grad.reshape(1, 512)
    grad = back.astype(jnp.bfloat16)
    vg_out[2:3, :] = column_sum(grad).reshape(1, 512)
    incoming = back
    steps = []
    for c in range(chunks):
        span = slice(c * width, c * width + width)
        du = (dot(grad, shrink_ref[span, :], 1, 1) * slopes[:, span]).astype(jnp.bfloat16)
        vg_out[3 + c : 4 + c, :] = column_sum(du).reshape(1, 512)
        incoming = incoming + dot(du, expand_ref[:, span], 1, 1)
        steps.append(du)
    back, gain_grad, shift_grad = norm_backward(incoming, normed_two, inverse_two, row(8))
    back_out[...] = back
    branch = back.astype(jnp.bfloat16)
    branch_out[...] = branch
    do = dot(branch, out_mat_ref[...], 1, 1).astype(jnp.bfloat16)
    for p in range(PLANE):
        dosend[p] = do[:, p * 128 : p * 128 + 128]
    swap_do = Swap(lambda p: dosend.at[p], lambda p: doget.at[p], swap_sems.at[1])
    swap_do.begin()
    vg_out[7:8, :] = gain_grad.reshape(1, 512)
    vg_out[8:9, :] = shift_grad.reshape(1, 512)
    vg_out[9:10, :] = column_sum(branch).reshape(1, 512)
    for c in range(chunks):
        span = slice(c * width, c * width + width)
        grad_shrink[span, :] = dot(actives[:, span], grad, 0, 0).astype(jnp.bfloat16)
        grad_expand[:, span] = dot(low, steps[c], 0, 0).astype(jnp.bfloat16)
    for offset in range(4):
        swap_do.arrived(offset)
    for p in range(PLANE):
        do_out[p * tok : p * tok + tok, :] = doget[p]
    swap.finish()
    swap_do.finish()


def run_centre(wa_count, vec_at, attended, hidden, cotangent, out_mat, expand, shrink, vecs):
    tok = hidden.shape[0]
    low, full = jnp.bfloat16, jnp.float32
    shape = jax.ShapeDtypeStruct
    pairs = pltpu.VMEM((PLANE, tok, 128), low)
    wide = expand.shape[1]
    return pl.pallas_call(
        functools.partial(centre_kernel, wa_count, vec_at),
        out_shape=(shape((tok, 512), full), shape((tok, 512), low), shape((tok, 512), full), shape((tok, 512), low),
                   shape((PLANE * tok, 128), low), shape(shrink.shape, low), shape(expand.shape, low), shape((24, 512), full)),
        in_specs=[VMEM] * 7,
        out_specs=(VMEM,) * 8,
        scratch_shapes=[pairs] * 4 + [pltpu.VMEM((tok, wide), full), pltpu.VMEM((tok, wide), low), DMA((2, 2, 4))],
        compiler_params=pltpu.CompilerParams(collective_id=3, has_side_effects=True, vmem_limit_bytes=60 << 20),
    )(attended, hidden, cotangent, out_mat, expand, shrink, vecs)


def last_kernel(wa_count, shares, at_ref, late_ref, sums_ref, dq_ref, dkv_ref, back_ref, query_mat, key_mat, value_mat,
                expand_ref, shrink_ref, query_out, content_out, expand_out, shrink_out, *outs):
    count = late_ref.shape[1]
    for i in range(count):
        for c in range(PLANE):
            outs[i][:, c * 128 : c * 128 + 128] = late_ref[c, i].astype(jnp.float32)
    query_out[...] = back_ref[...] + dot(dq_ref[...], query_mat[...], 1, 1)
    content_out[...] = dot(dkv_ref[:, :512], key_mat[...], 1, 1) + dot(dkv_ref[:, 512:], value_mat[...], 1, 1)
    expand_out[...] = expand_ref[...].astype(jnp.float32)
    shrink_out[...] = shrink_ref[...].astype(jnp.float32)
    at = 0
    for i, share in enumerate(shares):
        used = share * wa_count // 512
        line = jnp.concatenate([sums_ref[at + r : at + r + 1, :] for r in range(used)], axis=1)
        at += used
        mine = line[:, :share]
        for w in range(1, wa_count):
            mine = jnp.where(at_ref[0] == w, line[:, w * share : w * share + share], mine)
        outs[count + i][...] = mine.reshape(share)


def run_last(wa_count, shares, at, late, sums, dq, dkv, back, query_mat, key_mat, value_mat, expand, shrink):
    full = jnp.float32
    shape = jax.ShapeDtypeStruct
    tok = dq.shape[0]
    out_shape = [shape((tok, 512), full), shape((tok, 512), full), shape(expand.shape, full), shape(shrink.shape, full)]
    out_shape += [shape((late.shape[2], 512), full)] * late.shape[1] + [shape((s,), full) for s in shares]
    return pl.pallas_call(
        functools.partial(last_kernel, wa_count, shares),
        out_shape=tuple(out_shape),
        in_specs=[SMEM] + [VMEM] * 10,
        out_specs=tuple([VMEM] * len(out_shape)),
        compiler_params=pltpu.CompilerParams(vmem_limit_bytes=60 << 20),
    )(at, late, sums, dq, dkv, back, query_mat, key_mat, value_mat, expand, shrink)


def scatter_wide(grad):
    return lax.psum_scatter(grad.astype(jnp.bfloat16), "wa", scatter_dimension=0, tiled=True)


def sum_wide(share):
    return lax.psum(share, ("grp", "pln"))


def shards(
    query_in,
    content_in,
    encoder_in,
    out_grad,
    document_lengths,
    key_ranks,
    query_limits,
    self_query_weight,
    self_query_bias,
    self_key_weight,
    self_value_weight,
    self_value_bias,
    self_out_weight,
    self_out_bias,
    norm_one_gain,
    norm_one_shift,
    cross_query_weight,
    cross_query_bias,
    cross_key_weight,
    cross_value_weight,
    cross_value_bias,
    cross_out_weight,
    cross_out_bias,
    norm_two_gain,
    norm_two_shift,
    expand_weight,
    expand_bias,
    shrink_weight,
    shrink_bias,
    norm_three_gain,
    norm_three_shift,
):
    grp_count = lax.axis_size("grp")
    own = lax.axis_index("grp")[None].astype(jnp.int32)
    lens = document_lengths


    wa_count = lax.axis_size("wa")
    vectors = (self_query_bias, self_value_bias, cross_value_bias, self_out_bias, norm_one_gain, norm_one_shift,
        cross_query_bias, cross_out_bias, norm_two_gain, norm_two_shift, expand_bias, shrink_bias, norm_three_gain,
        norm_three_shift)
    vec_at, at = [], 0
    for v in vectors:
        vec_at.append((at, v.shape[0]))
        at += v.shape[0] // min(128, v.shape[0])
    vec_at = tuple(vec_at)
    mats = (self_key_weight, self_value_weight, self_query_weight, cross_key_weight, cross_value_weight, self_out_weight,
        cross_query_weight, cross_out_weight)
    (self_key_matrix, self_value_mat, self_query_mat, cross_key_matrix, cross_value_mat, self_out_mat, cross_query_mat,
        cross_out_mat, vec_all, pair_one, kv_one, kv_two_own, self_keys, cross_keys, self_marks, cross_marks) = run_opening(
        grp_count, wa_count, lens, key_ranks, query_limits, content_in[0], query_in[0],
        encoder_in[0], vectors, mats, vec_at)
    source = query_in[0]
    content_states = content_in[0]
    encoder_output = encoder_in[0]
    attended_one, total_one = attend_forward(True, lens, own, pair_one, self_marks, kv_one, self_keys)
    hidden_one, normed_one, inverse_one, mixed_one, pair_two, kv_two, expand_mat, shrink_mat = run_middle(
        grp_count, wa_count, attended_one, source, self_out_mat, cross_query_mat, vec_all, vec_at, kv_two_own,
        expand_weight, shrink_weight)
    attended_two, total_two = attend_forward(False, lens, own, pair_two, cross_marks, kv_two, cross_keys)
    layer_out, mixed_two, back_two, branch_two, do_two, grad_shrink_mat, grad_expand_mat, lines = run_centre(
        wa_count, vec_at, attended_two, hidden_one, out_grad[0], cross_out_mat, expand_mat, shrink_mat, vec_all)
    grad_shrink_mat = scatter_wide(grad_shrink_mat)
    grad_expand_mat = scatter_wide(grad_expand_mat)
    dq_two, dkv_two, own_two = attend_backward(False, lens, own, pair_two, cross_marks, kv_two, cross_keys,
        attended_two, total_two, do_two)
    do_one, back_one, kv_two_grad, early, lines = run_turn(grp_count, wa_count, vec_at, dq_two, dkv_two, own_two, back_two,
        normed_one, inverse_one, hidden_one, mixed_one, mixed_two, branch_two, encoder_output, cross_query_mat, self_out_mat,
        vec_all, lines)
    do_one, grad_shrink_mat, grad_expand_mat = lax.optimization_barrier((do_one, grad_shrink_mat, grad_expand_mat))
    grad_shrink_mat = sum_wide(grad_shrink_mat)
    grad_expand_mat = sum_wide(grad_expand_mat)
    key_two_low, value_two_low = kv_two_grad[:, :512], kv_two_grad[:, 512:]
    encoder_grad = right_product(key_two_low, cross_key_matrix) + right_product(value_two_low, cross_value_mat)
    dq_one, dkv_one, own_one = attend_backward(True, lens, own, pair_one, self_marks, kv_one, self_keys,
        attended_one, total_one, do_one)
    query_one_low, kv_one_grad, late, sums = run_closing(grp_count, wa_count, dq_one, dkv_one, own_one, source,
        content_states, early, lines)
    shares = tuple(v.shape[0] for v in (norm_three_gain, norm_three_shift, shrink_bias, expand_bias, norm_two_gain,
        norm_two_shift, cross_out_bias, norm_one_gain, norm_one_shift, self_out_bias, cross_query_bias, cross_value_bias,
        self_query_bias, self_value_bias))
    query_grad, content_grad, expand_grad, shrink_grad, *rest = run_last(wa_count, shares,
        lax.axis_index("wa")[None].astype(jnp.int32), late, sums, query_one_low, kv_one_grad, back_one, self_query_mat,
        self_key_matrix, self_value_mat, grad_expand_mat, grad_shrink_mat)
    names = ("cross_out", "cross_query", "self_out", "cross_key", "cross_value", "self_query", "self_key", "self_value")
    mat = dict(zip(names, rest))
    names = ("gain_three", "shift_three", "shrink", "expand", "gain_two", "shift_two", "cross_out", "gain_one", "shift_one",
        "self_out", "cross_query", "cross_value", "self_query", "self_value")
    vec = dict(zip(names, rest[len(mat):]))
    grads = (mat["self_query"], vec["self_query"], mat["self_key"], mat["self_value"], vec["self_value"], mat["self_out"],
        vec["self_out"], vec["gain_one"], vec["shift_one"], mat["cross_query"], vec["cross_query"], mat["cross_key"],
        mat["cross_value"], vec["cross_value"], mat["cross_out"], vec["cross_out"], vec["gain_two"], vec["shift_two"],
        expand_grad, vec["expand"], shrink_grad, vec["shrink"], vec["gain_three"], vec["shift_three"])
    return (layer_out[None], query_grad[None], content_grad[None], encoder_grad[None]) + grads


def solution(mesh):
    ctx, wa = mesh.devices.shape
    mesh = Mesh(mesh.devices.reshape(ctx // PLANE, PLANE, wa), ("grp", "pln", "wa"))
    in_specs = (
        P("wa", ("grp", "pln"), None),
        P("wa", ("grp", "pln"), None),
        P("wa", ("grp", "pln"), None),
        P("wa", ("grp", "pln"), None),
        P("wa", None),
        P("wa", None),
        P("wa", None),
        P("wa", None),
        P("wa"),
        P("wa", None),
        P("wa", None),
        P("wa"),
        P("wa", None),
        P("wa"),
        P("wa"),
        P("wa"),
        P("wa", None),
        P("wa"),
        P("wa", None),
        P("wa", None),
        P("wa"),
        P("wa", None),
        P("wa"),
        P("wa"),
        P("wa"),
        P("wa", None),
        P("wa"),
        P("wa", None),
        P("wa"),
        P("wa"),
        P("wa"),
    )
    out_specs = (
        P("wa", ("grp", "pln"), None),
        P("wa", ("grp", "pln"), None),
        P("wa", ("grp", "pln"), None),
        P("wa", ("grp", "pln"), None),
        P("wa", None),
        P("wa"),
        P("wa", None),
        P("wa", None),
        P("wa"),
        P("wa", None),
        P("wa"),
        P("wa"),
        P("wa"),
        P("wa", None),
        P("wa"),
        P("wa", None),
        P("wa", None),
        P("wa"),
        P("wa", None),
        P("wa"),
        P("wa"),
        P("wa"),
        P("wa", None),
        P("wa"),
        P("wa", None),
        P("wa"),
        P("wa"),
        P("wa"),
    )
    return jax.shard_map(shards, mesh=mesh, in_specs=in_specs, out_specs=out_specs, check_vma=False)
```

```python
import functools
import jax
import jax.numpy as jnp
from jax import lax
from jax.experimental import pallas as pl
from jax.experimental.pallas import tpu as pltpu
from jax.sharding import Mesh
from jax.sharding import PartitionSpec as P

PLANE = 4
DOCLEN = 2048
EPSILON = 1e-05
ROOT_HALF = 0.7071067811865476
INV_ROOT_TWO_PI = 0.3989422804014327
NEGATIVE = -1e29
HIDE = -(2.0 ** 100)
BLOCK = 512
WIDE = 1024
QUERIES = 512
KEYS = 512
STAT = 40


def dot(a, b, ca, cb):
    return lax.dot_general(a, b, (((ca,), (cb,)), ((), ())), preferred_element_type=jnp.float32)


def left_half(shape):
    return lax.broadcasted_iota(jnp.int32, shape, 1) < 64


def spans(lens_ref, first, count):
    low, high, total = 0, 0, 0
    for d in range(lens_ref.shape[1]):
        begin = total
        total = total + lens_ref[0, d]
        low = jnp.where(begin <= first, begin, low)
        high = jnp.where(begin <= first + count - 1, total, high)
    return low, high


def openings(lens_ref, places):
    total, found = 0, places == 0
    for d in range(lens_ref.shape[1] - 1):
        total = total + lens_ref[0, d]
        found = jnp.logical_or(found, places == total)
    return found


def over_blocks(low, high, first, size, step, carry, ranked):
    begin, end = low // size, (high + size - 1) // size
    own = first // size
    skip = 1 if ranked else 0

    def body(index, carry):
        if ranked:
            index = index + jnp.where(index >= own, 1, 0)
        return step(pl.multiple_of(index * size, size), carry)

    carry = lax.fori_loop(begin, end - skip, body, carry)
    if ranked:
        carry = step(pl.multiple_of(own * size, size), carry, True)
    return carry


def turned(value, eye):
    return dot(eye, value, 1, 1).astype(jnp.bfloat16)


def unit_matrix():
    row = lax.broadcasted_iota(jnp.int32, (128, 128), 0)
    lane = lax.broadcasted_iota(jnp.int32, (128, 128), 1)
    return jnp.where(row == lane, 1.0, 0.0).astype(jnp.bfloat16)


def forward_kernel(ranked, lens_ref, own_ref, q_ref, qm_ref, kv_ref, km_ref, o_ref, lse_ref):
    rows = q_ref.shape[0]
    base = own_ref[0] * rows
    half = left_half((QUERIES, 128))
    khalf = left_half((WIDE, 128))
    one = jnp.ones((WIDE, 128), jnp.bfloat16)

    def one_block(block, _):
        start = pl.multiple_of(block * QUERIES, QUERIES)
        first = base + start
        low, high = spans(lens_ref, first, QUERIES)
        q = q_ref[pl.ds(start, QUERIES), :]
        qm = qm_ref[pl.ds(start, QUERIES), :]
        queries = (jnp.where(half, q, qm), jnp.where(half, qm, q))

        def step(at, carry, diagonal=False):
            k = kv_ref[pl.ds(at, WIDE), :128]
            v = kv_ref[pl.ds(at, WIDE), 128:]
            km = km_ref[pl.ds(at, WIDE), :]
            keys = (jnp.where(khalf, k, km), jnp.where(khalf, km, k))
            values = (jnp.where(khalf, v, one), jnp.where(khalf, one, v))
            scores = [dot(queries[h], keys[h], 1, 1) for h in (0, 1)]
            if diagonal:
                place = first + lax.broadcasted_iota(jnp.int32, (QUERIES, WIDE), 0)
                other = at + lax.broadcasted_iota(jnp.int32, (QUERIES, WIDE), 1)
                column = first + lax.broadcasted_iota(jnp.int32, (QUERIES, 1), 0)
                banned = jnp.where(openings(lens_ref, column), -1, place) == other
                scores = [jnp.where(banned, HIDE, s) for s in scores]
            out = []
            for h in (0, 1):
                peak, acc = carry[h]
                new = jnp.maximum(peak, jnp.max(scores[h], axis=1, keepdims=True))
                p = jnp.exp(scores[h] - new).astype(jnp.bfloat16)
                acc = acc * jnp.exp(peak - new) + dot(p, values[h], 1, 0)
                out.append((new, acc))
            return tuple(out)

        empty = (jnp.full((QUERIES, 1), NEGATIVE, jnp.float32), jnp.zeros((QUERIES, 128), jnp.float32))
        (peak0, acc0), (peak1, acc1) = over_blocks(low, high, first, WIDE, step, (empty, empty), ranked)
        total = jnp.where(half, acc1, acc0)
        mixed = jnp.where(half, acc0, acc1)
        o_ref[pl.ds(start, QUERIES), :] = mixed / pltpu.roll(total, 64, 1)
        lse_ref[pl.ds(start, QUERIES), :] = jnp.where(half, peak1, peak0) + jnp.log(total)
        return 0

    lax.fori_loop(0, rows // QUERIES, one_block, 0)


def attend_forward(ranked, lens, own, q, qm, kv, km):
    rows = q.shape[0]
    whole = pl.BlockSpec(memory_space=pltpu.VMEM)
    smem = pl.BlockSpec(memory_space=pltpu.SMEM)
    return pl.pallas_call(
        functools.partial(forward_kernel, ranked),
        out_shape=(jax.ShapeDtypeStruct((rows, 128), jnp.float32),) * 2,
        in_specs=[smem, smem] + [whole] * 4,
        out_specs=(whole, whole),
        cost_estimate=pl.CostEstimate(flops=12000000000, bytes_accessed=0, transcendentals=0),
        compiler_params=pltpu.CompilerParams(vmem_limit_bytes=60 << 20),
    )(lens, own, q, qm, kv, km)


def with_stat(marks, stat, lane, at):
    high = stat.astype(jnp.bfloat16)
    rest = stat - high.astype(jnp.float32)
    middle = rest.astype(jnp.bfloat16)
    tail = (rest - middle.astype(jnp.float32)).astype(jnp.bfloat16)
    side = jnp.where(lane == at, high, jnp.where(lane == at + 1, middle, jnp.where(lane == at + 2, tail, marks)))
    return side


def backward_kernel(ranked, lens_ref, own_ref, q_ref, qm_ref, kv_ref, km_ref, o_ref, lse_ref, do_ref,
                    dq_ref, dkv_ref, own_dkv_ref, dk_ref, dv_ref, kt0_ref, kt1_ref):
    rows = q_ref.shape[0]
    base = own_ref[0] * rows
    half = left_half((BLOCK, 128))
    khalf = left_half((KEYS, 128))
    lane = lax.broadcasted_iota(jnp.int32, (BLOCK, 128), 1)
    one = jnp.ones((KEYS, 128), jnp.bfloat16)
    zero = jnp.zeros((BLOCK, 128), jnp.bfloat16)

    def clear(index, _):
        at = pl.multiple_of(index * BLOCK, BLOCK)
        dk_ref[pl.ds(at, BLOCK), :] = jnp.zeros((BLOCK, 128), jnp.float32)
        dv_ref[pl.ds(at, BLOCK), :] = jnp.zeros((BLOCK, 128), jnp.float32)
        return 0

    lax.fori_loop(0, kv_ref.shape[0] // BLOCK, clear, 0)
    eye = unit_matrix()
    tops = lax.broadcasted_iota(jnp.int32, (128, KEYS), 0) < 64
    low_all, high_all = spans(lens_ref, base, rows)

    def prepare(block, _):
        there = pl.ds(pl.multiple_of(block * KEYS, KEYS), KEYS)
        kt = turned(kv_ref[there, :128], eye)
        none = jnp.zeros((128, KEYS), jnp.bfloat16)
        kt0_ref[:, there] = jnp.where(tops, kt, none)
        kt1_ref[:, there] = jnp.where(tops, none, kt)
        return 0

    lax.fori_loop(low_all // KEYS, (high_all + KEYS - 1) // KEYS, prepare, 0)

    def one_block(block, _):
        start = pl.multiple_of(block * BLOCK, BLOCK)
        first = base + start
        low, high = spans(lens_ref, first, BLOCK)
        here = pl.ds(start, BLOCK)
        q, qm, do, lse = q_ref[here, :], qm_ref[here, :], do_ref[here, :], lse_ref[here, :]
        shared = do.astype(jnp.float32) * o_ref[here, :]
        delta0 = jnp.sum(jnp.where(half, shared, 0.0), axis=1, keepdims=True)
        delta1 = jnp.sum(jnp.where(half, 0.0, shared), axis=1, keepdims=True)
        side = with_stat(qm, lse, lane % 64, STAT)
        queries = (jnp.where(half, q, side), jnp.where(half, side, q))
        side = with_stat(zero, -jnp.where(half, delta1, delta0), lane % 64, STAT)
        grads = (jnp.where(half, do, side), jnp.where(half, side, do))

        both_q = jnp.concatenate([jnp.where(half, q, zero), jnp.where(half, zero, q)], axis=0)
        both_do = jnp.concatenate([jnp.where(half, do, zero), jnp.where(half, zero, do)], axis=0)

        def step(at, carry, diagonal=False):
            there = pl.ds(at, KEYS)
            k, v, km = kv_ref[there, :128], kv_ref[there, 128:], km_ref[there, :]
            keys = (jnp.where(khalf, k, km), jnp.where(khalf, km, k))
            values = (jnp.where(khalf, v, one), jnp.where(khalf, one, v))
            scores = [dot(keys[h], queries[h], 1, 1) for h in (0, 1)]
            if diagonal:
                other = at + lax.broadcasted_iota(jnp.int32, (KEYS, BLOCK), 0)
                row = first + lax.broadcasted_iota(jnp.int32, (1, BLOCK), 1)
                banned = other == jnp.where(openings(lens_ref, row), -1, row)
                scores = [jnp.where(banned, HIDE, s) for s in scores]
            ps = [jnp.exp(scores[h]) for h in (0, 1)]
            ds = [(ps[h] * dot(values[h], grads[h], 1, 1)).astype(jnp.bfloat16) for h in (0, 1)]
            ps = [p.astype(jnp.bfloat16) for p in ps]
            dv_ref[there, :] += dot(jnp.concatenate(ps, axis=1), both_do, 1, 0)
            dk_ref[there, :] += dot(jnp.concatenate(ds, axis=1), both_q, 1, 0)
            return carry + dot(kt0_ref[:, there], ds[0], 1, 0) + dot(kt1_ref[:, there], ds[1], 1, 0)

        dq = over_blocks(low, high, first, KEYS, step, jnp.zeros((128, BLOCK), jnp.float32), ranked)
        dq_ref[here, :] = jnp.transpose(dq * 0.125).astype(dq_ref.dtype)
        return 0

    lax.fori_loop(0, rows // BLOCK, one_block, 0)

    def save(index, _):
        there = pl.ds(pl.multiple_of(index * BLOCK, BLOCK), BLOCK)
        dkv_ref[there, :128] = dk_ref[there, :].astype(jnp.bfloat16)
        dkv_ref[there, 128:] = dv_ref[there, :].astype(jnp.bfloat16)
        return 0

    lax.fori_loop(0, kv_ref.shape[0] // BLOCK, save, 0)
    mine = pl.ds(pl.multiple_of(base, BLOCK), rows)
    own_dkv_ref[:, :128] = dk_ref[mine, :]
    own_dkv_ref[:, 128:] = dv_ref[mine, :]


def attend_backward(ranked, lens, own, q, qm, kv, km, o, lse, do):
    rows, keys = q.shape[0], kv.shape[0]
    whole = pl.BlockSpec(memory_space=pltpu.VMEM)
    smem = pl.BlockSpec(memory_space=pltpu.SMEM)
    return pl.pallas_call(
        functools.partial(backward_kernel, ranked),
        out_shape=(jax.ShapeDtypeStruct((rows, 128), jnp.bfloat16),) + (
            jax.ShapeDtypeStruct((keys, 256), jnp.bfloat16), jax.ShapeDtypeStruct((rows, 256), jnp.float32)),
        in_specs=[smem, smem] + [whole] * 7,
        out_specs=(whole, whole, whole),
        scratch_shapes=[pltpu.VMEM((keys, 128), jnp.float32)] * 2 + [pltpu.VMEM((128, keys), jnp.bfloat16)] * 2,
        cost_estimate=pl.CostEstimate(flops=26000000000, bytes_accessed=0, transcendentals=0),
        compiler_params=pltpu.CompilerParams(vmem_limit_bytes=60 << 20),
    )(lens, own, q, qm, kv, km, o, lse, do)


def matmul(left, right):
    return jnp.dot(left, right, preferred_element_type=jnp.float32)


def left_product(left, right):
    return jnp.einsum("ta,tb->ab", left, right, preferred_element_type=jnp.float32)


def right_product(left, right):
    return jnp.einsum("ta,ba->tb", left, right, preferred_element_type=jnp.float32)


def column_sum(value):
    return jnp.sum(value.astype(jnp.float32), axis=0)


def gelu_slope(value):
    cumulative = 0.5 * (1.0 + lax.erf(value * ROOT_HALF))
    return cumulative + value * jnp.exp(-0.5 * value * value) * INV_ROOT_TWO_PI


def norm_forward(value, gain_row, shift_row):
    middle = jnp.mean(value, axis=-1, keepdims=True)
    centred = value - middle
    spread = jnp.mean(centred * centred, axis=-1, keepdims=True)
    inverse = lax.rsqrt(spread + EPSILON)
    normed = centred * inverse
    return (normed * gain_row + shift_row, normed, inverse)


def norm_backward(incoming, normed, inverse, gain_row):
    scaled = incoming * gain_row
    centred = (
        scaled
        - jnp.mean(scaled, axis=-1, keepdims=True)
        - normed * jnp.mean(scaled * normed, axis=-1, keepdims=True)
    )
    return (inverse * centred, jnp.sum(incoming * normed, axis=0), jnp.sum(incoming, axis=0))


MESH = pl.DeviceIdType.MESH
ANY = pl.BlockSpec(memory_space=pltpu.HBM)
VMEM = pl.BlockSpec(memory_space=pltpu.VMEM)
SMEM = pl.BlockSpec(memory_space=pltpu.SMEM)
DMA = pltpu.SemaphoreType.DMA


def across(place, offset):
    if offset == 1:
        return place + 1 - 2 * lax.rem(place, 2)
    if offset == 2:
        return lax.rem(place + 2, 4)
    return 3 - place


def remote(src, dst, sends, recvs, where):
    return pltpu.make_async_remote_copy(
        src_ref=src, dst_ref=dst, send_sem=sends, recv_sem=recvs, device_id=where, device_id_type=MESH)


def greet(grp_count, wa_count, plane=True, groups=True, rows=True):
    barrier = pltpu.get_barrier_semaphore()
    grp, pln, wa = lax.axis_index("grp"), lax.axis_index("pln"), lax.axis_index("wa")

    def hello(where):
        pl.semaphore_signal(barrier, inc=1, device_id=where, device_id_type=MESH)

    count = 0
    if plane:
        for offset in (1, 2, 3):
            hello({"pln": across(pln, offset)})
        count += 3
    if rows:
        for offset in range(1, wa_count):
            hello({"wa": lax.rem(wa + offset, wa_count)})
        count += wa_count - 1
    if groups:
        @pl.when(grp > 0)
        def _():
            hello({"grp": grp - 1})

        @pl.when(grp < grp_count - 1)
        def _():
            hello({"grp": grp + 1})

        count = count + jnp.where(grp > 0, 1, 0) + jnp.where(grp < grp_count - 1, 1, 0)
    pl.semaphore_wait(barrier, count)


class Rows:
    def __init__(self, shard, full, sems, index, wa_count, stage=None):
        self.shard, self.full, self.sems, self.index, self.wa_count = shard, full, sems, index, wa_count
        self.stage = stage
        self.size = shard.shape[0]
        self.half = self.size // 2
        self.wa, self.pln = lax.axis_index("wa"), lax.axis_index("pln")
        self.core = lax.rem(self.pln, 2)

    def part(self, owner, core):
        return pl.ds(pl.multiple_of(owner * self.size + core * self.half, 16), self.half)

    def keep(self):
        own = pl.ds(pl.multiple_of(self.wa * self.size, 16), self.size)
        source = self.shard if self.stage is None else self.stage
        return pltpu.make_async_copy(source, self.full.at[own], self.sems.at[0, self.index, 0])

    def load(self):
        return pltpu.make_async_copy(self.shard, self.stage, self.sems.at[0, self.index, 0])

    def push(self, offset):
        mine = pl.ds(pl.multiple_of(self.core * self.half, 16), self.half)
        return remote(self.shard.at[mine], self.full.at[self.part(self.wa, self.core)],
                      self.sems.at[1, self.index, offset - 1], self.sems.at[2, self.index, offset - 1],
                      {"wa": lax.rem(self.wa + offset, self.wa_count)})

    def hand(self, offset):
        owner = lax.rem(self.wa + self.wa_count - offset, self.wa_count)
        spot = self.full.at[self.part(owner, self.core)]
        return remote(spot, spot, self.sems.at[3, self.index, offset - 1], self.sems.at[4, self.index, offset - 1],
                      {"pln": across(self.pln, 1)})

    def begin(self):
        if self.stage is None:
            self.keep().start()
        else:
            self.load().start()
        for offset in range(1, self.wa_count):
            self.push(offset).start()

    def staged(self):
        self.load().wait()
        self.keep().start()

    def pass_on(self):
        for offset in range(1, self.wa_count):
            self.push(offset).wait_recv()
            self.hand(offset).start()

    def arrived(self):
        self.keep().wait()
        for offset in range(1, self.wa_count):
            self.hand(offset).wait_recv()

    def finish(self):
        for offset in range(1, self.wa_count):
            self.push(offset).wait_send()
            self.hand(offset).wait_send()


class Line:
    def __init__(self, full, sems, grp_count, reach, block):
        self.full, self.sems, self.count, self.reach, self.block = full, sems, grp_count, reach, block
        self.grp = lax.axis_index("grp")

    def rows(self, owner, block):
        return pl.ds(pl.multiple_of((owner * PLANE + block) * self.block, 16), self.block)

    def copy(self, side, step, block, source=None):
        toward = 1 if side == 0 else -1
        owner = self.grp - toward * (step - 1)
        spot = self.full.at[self.rows(owner, block)]
        return remote(spot if source is None else source, spot, self.sems.at[0, side, step - 1, block],
                      self.sems.at[1, side, step - 1, block], {"grp": self.grp + toward})

    def sends(self, side, step):
        if side == 0:
            return jnp.logical_and(self.grp - step + 1 >= 0, self.grp + 1 < self.count)
        return jnp.logical_and(self.grp + step - 1 < self.count, self.grp - 1 >= 0)

    def receives(self, side, step):
        return self.grp - step >= 0 if side == 0 else self.grp + step < self.count

    def send(self, step, block, source=None):
        for side in (0, 1):
            @pl.when(self.sends(side, step))
            def _():
                self.copy(side, step, block, source).start()

    def arrival(self, side, step, block):
        toward = 1 if side == 0 else -1
        spot = self.full.at[self.rows(self.grp - toward * step, block)]
        return remote(spot, spot, self.sems.at[0, side, step - 1, block], self.sems.at[1, side, step - 1, block],
                      {"grp": self.grp - toward})

    def forward(self, step):
        for block in range(PLANE):
            for side in (0, 1):
                @pl.when(self.receives(side, step))
                def _():
                    self.arrival(side, step, block).wait_recv()

                    if step < self.reach:
                        @pl.when(self.sends(side, step + 1))
                        def _():
                            self.copy(side, step + 1, block).start()

    def finish(self, source=None):
        for step in range(1, self.reach + 1):
            for block in range(PLANE):
                for side in (0, 1):
                    @pl.when(self.sends(side, step))
                    def _():
                        self.copy(side, step, block, source[block] if source and step == 1 else None).wait_send()


class Swap:
    def __init__(self, src, dst, sems):
        self.src, self.dst, self.sems = src, dst, sems
        self.pln = lax.axis_index("pln")

    def copy(self, offset):
        peer = across(self.pln, offset)
        return remote(self.src(peer), self.dst(self.pln), self.sems.at[0, offset], self.sems.at[1, offset], {"pln": peer})

    def keep(self):
        return pltpu.make_async_copy(self.src(self.pln), self.dst(self.pln), self.sems.at[0, 0])

    def begin(self):
        for offset in (2, 3, 1):
            self.copy(offset).start()
        self.keep().start()

    def arrived(self, offset):
        self.keep().wait() if offset == 0 else self.copy(offset).wait_recv()

    def finish(self):
        for offset in (1, 2, 3):
            self.copy(offset).wait_send()


def pack_vectors(refs, pack):
    pack[...] = jnp.zeros_like(pack)
    at = 0
    for ref in refs:
        length = ref.shape[0]
        width = min(128, length)
        line = ref[...].astype(jnp.float32).reshape(1, length)
        for start in range(0, length, width):
            pack[at : at + 1, :width] = line[:, start : start + width]
            at += 1


def columns_of(ref, block):
    at = pl.multiple_of(block * 128, 128)
    line = ref[0:1, pl.ds(at, 128)].astype(jnp.float32)
    return jnp.transpose(jnp.broadcast_to(line, (128, 128)))


def make_marks(lens_ref, ranks_ref, limits_ref, base, self_keys, cross_keys, self_queries, cross_queries):
    docs = lens_ref.shape[1]
    lane = lax.rem(lax.broadcasted_iota(jnp.int32, (128, 128), 1), 64)
    stat = jnp.where(jnp.logical_and(lane >= STAT, lane < STAT + 3), -1.0, 0.0)

    def document(place):
        doc, opened, total = jnp.zeros((128, 128), jnp.int32), place == 0, 0
        for d in range(docs):
            total = total + lens_ref[0, d]
            doc = doc + jnp.where(place >= total, 1, 0)
            if d < docs - 1:
                opened = jnp.logical_or(opened, place == total)
        return doc, opened

    def keys(block, _):
        place = block * 128 + lax.broadcasted_iota(jnp.int32, (128, 128), 0)
        doc, opened = document(place)
        rank = jnp.where(opened, 0, columns_of(ranks_ref, block).astype(jnp.int32) + 1)
        marks = jnp.where(lane == doc, 1.0, stat)
        there = pl.ds(pl.multiple_of(block * 128, 128), 128)
        cross_keys[there, :] = marks.astype(jnp.bfloat16)
        self_keys[there, :] = jnp.where(lane == rank + 16, 1.0, marks).astype(jnp.bfloat16)
        return 0

    def queries(block, _):
        place = base + block * 128 + lax.broadcasted_iota(jnp.int32, (128, 128), 0)
        doc, _ = document(place)
        limit = columns_of(limits_ref, base // 128 + block).astype(jnp.int32)
        marks = jnp.where(jnp.logical_and(lane < docs, lane != doc), HIDE, 0.0)
        ranks = jnp.logical_and(lane >= 16, jnp.logical_and(lane < 33, lane - 17 >= limit))
        there = pl.ds(pl.multiple_of(block * 128, 128), 128)
        cross_queries[there, :] = marks.astype(jnp.bfloat16)
        self_queries[there, :] = jnp.where(ranks, HIDE, marks).astype(jnp.bfloat16)
        return 0

    lax.fori_loop(0, self_keys.shape[0] // 128, keys, 0)
    lax.fori_loop(0, self_queries.shape[0] // 128, queries, 0)


def vector_row(pack_ref, wa_count, start, length):
    width = min(128, length)
    pieces = []
    for wa in range(wa_count):
        for row in range(length // width):
            pieces.append(pack_ref[wa, start + row : start + row + 1, :width])
    return jnp.concatenate(pieces, axis=1)


def split_pairs(value, buffer, column):
    for pair in range(PLANE):
        buffer[pair, :, column : column + 128] = value[:, pair * 128 : pair * 128 + 128]


def opening_kernel(grp_count, wa_count, reach, count, vec_at, lens_ref, ranks_ref, limits_ref, content_ref, query_ref,
                   encoder_ref, *refs):
    vecs, refs = refs[: len(vec_at)], refs[len(vec_at) :]
    shards = refs[:count]
    fulls = refs[count : 2 * count]
    vec_out, q_out, kv_out, kv2_out = refs[2 * count : 2 * count + 4]
    mark_outs = refs[2 * count + 4 : 2 * count + 8]
    marks = refs[2 * count + 8 : 2 * count + 12]
    vec_ref, held, vec_all, kvbuf, kvbuf2, qbuf, row_sems, vec_sems, line_sems, swap_sems, out_sems = refs[2 * count + 12 :]
    grp, pln, wa = lax.axis_index("grp"), lax.axis_index("pln"), lax.axis_index("wa")
    tok = content_ref.shape[0]
    gathers = [Rows(shards[i], held.at[i], row_sems, i, wa_count) for i in range(count)]
    pack_vectors(vecs, vec_ref)
    greet(grp_count, wa_count)
    vec_keep = pltpu.make_async_copy(vec_ref, vec_all.at[wa], vec_sems.at[0, 0])
    vec_keep.start()
    pushes = [remote(vec_ref, vec_all.at[wa], vec_sems.at[0, o], vec_sems.at[1, o], {"wa": lax.rem(wa + o, wa_count)})
              for o in range(1, wa_count)]
    for g in gathers[:2]:
        g.begin()
    for p in pushes:
        p.start()
    for g in gathers[:2]:
        g.pass_on()
    for g in gathers[2:5]:
        g.begin()
    vec_keep.wait()
    for p in pushes:
        p.wait_recv()
    for g in gathers[:2]:
        g.arrived()
    content = content_ref[...]
    split_pairs(matmul(content, held[0]).astype(jnp.bfloat16), kvbuf, 0)
    row = lambda i: vector_row(vec_all, wa_count, *vec_at[i])
    split_pairs((matmul(content, held[1]) + row(1)).astype(jnp.bfloat16), kvbuf, 128)
    line = Line(kv_out, line_sems, grp_count, reach, tok)
    spot = lambda ref: lambda p: ref.at[pl.ds(pl.multiple_of((grp * PLANE + p) * tok, 16), tok)]
    swap = Swap(lambda p: kvbuf.at[p], spot(kv_out), swap_sems.at[0])
    swap.begin()
    line.send(1, pln, kvbuf.at[pln])
    swap.arrived(1)
    line.send(1, across(pln, 1))
    for g in gathers[2:5]:
        g.pass_on()
    for g in gathers[5:]:
        g.begin()
    for offset in (2, 3):
        swap.arrived(offset)
        line.send(1, across(pln, offset))
    for g in gathers[2:5]:
        g.arrived()
    outs = [pltpu.make_async_copy(held.at[i], fulls[i], out_sems.at[i]) for i in range(count)]
    for o in outs[:5]:
        o.start()
    vec_save = pltpu.make_async_copy(vec_all, vec_out, out_sems.at[count])
    vec_save.start()
    query = (matmul(query_ref[...], held[2]) + row(0)).astype(jnp.bfloat16)
    query = query * 0.125
    for pair in range(PLANE):
        qbuf[pair] = query[:, pair * 128 : pair * 128 + 128]
    place = lambda p: q_out.at[pl.ds(pl.multiple_of(p * tok, 16), tok)]
    swap_q = Swap(lambda p: qbuf.at[p], place, swap_sems.at[1])
    swap_q.begin()
    encoder = encoder_ref[...]
    split_pairs(matmul(encoder, held[3]).astype(jnp.bfloat16), kvbuf2, 0)
    split_pairs((matmul(encoder, held[4]) + row(2)).astype(jnp.bfloat16), kvbuf2, 128)
    place2 = lambda p: kv2_out.at[pl.ds(pl.multiple_of(p * tok, 16), tok)]
    swap_2 = Swap(lambda p: kvbuf2.at[p], place2, swap_sems.at[2])
    swap_2.begin()
    make_marks(lens_ref, ranks_ref, limits_ref, grp * PLANE * tok, *marks)
    mark_saves = [pltpu.make_async_copy(m, o, out_sems.at[count + 1 + i]) for i, (m, o) in enumerate(zip(marks, mark_outs))]
    for m in mark_saves:
        m.start()
    for step in range(1, reach + 1):
        line.forward(step)
    swap.arrived(0)
    for s in (swap_q, swap_2):
        for offset in range(4):
            s.arrived(offset)
    for g in gathers[5:]:
        g.pass_on()
    for g in gathers[5:]:
        g.arrived()
    for o in outs[5:]:
        o.start()
    for g in gathers:
        g.finish()
    for p in pushes:
        p.wait_send()
    for o in outs:
        o.wait()
    vec_save.wait()
    for m in mark_saves:
        m.wait()
    line.finish()
    for s in (swap, swap_q, swap_2):
        s.finish()


def run_opening(grp_count, wa_count, lens, ranks, limits, content, query, encoder, vecs, mats, vec_at):
    tok = content.shape[0]
    reach = min(grp_count - 1, (DOCLEN + PLANE * tok - 2) // (PLANE * tok))
    count = len(mats)
    low = jnp.bfloat16
    shape = lambda *s: jax.ShapeDtypeStruct(s, low)
    out_shape = [shape(m.shape[0] * wa_count, m.shape[1]) for m in mats]
    rows, keys = PLANE * tok, grp_count * PLANE * tok
    used = sum(length // min(128, length) for _, length in vec_at)
    pack = (used + -used % 16, 128)
    marks = [(keys, 128), (keys, 128), (rows, 128), (rows, 128)]
    out_shape += [jax.ShapeDtypeStruct((wa_count,) + pack, jnp.float32), shape(rows, 128), shape(keys, 256), shape(rows, 256)]
    out_shape += [shape(*m) for m in marks]
    return pl.pallas_call(
        functools.partial(opening_kernel, grp_count, wa_count, reach, count, vec_at),
        out_shape=tuple(out_shape),
        in_specs=[SMEM] + [VMEM] * (5 + len(vecs)) + [ANY] * count,
        out_specs=tuple([ANY] * len(out_shape)),
        scratch_shapes=[pltpu.VMEM(m, low) for m in marks] + [
            pltpu.VMEM(pack, jnp.float32), pltpu.VMEM((count, 512, 512), low), pltpu.VMEM((wa_count,) + pack, jnp.float32),
            pltpu.VMEM((PLANE, tok, 256), low), pltpu.VMEM((PLANE, tok, 256), low), pltpu.VMEM((PLANE, tok, 128), low),
            DMA((5, count, max(1, wa_count - 1))), DMA((2, wa_count)), DMA((2, 2, reach, PLANE)), DMA((3, 2, 4)),
            DMA((count + 5,))],
        cost_estimate=pl.CostEstimate(flops=38000000000, bytes_accessed=0, transcendentals=0),
        compiler_params=pltpu.CompilerParams(collective_id=1, has_side_effects=True, vmem_limit_bytes=60 << 20),
    )(lens, ranks, limits, content, query, encoder, *vecs, *mats)


def flat_pairs(buffer):
    return jnp.concatenate([buffer[p] for p in range(PLANE)], axis=1)


def middle_kernel(grp_count, wa_count, reach, vec_at, attended_ref, query_ref, out_mat_ref, query_mat_ref, vec_ref,
                  kv_own_ref, expand_ref, shrink_ref,
                  hidden_ref, normed_ref, inverse_ref, mixed_ref, q_out, kv_out, expand_full, shrink_full,
                  sendbuf, mixbuf, qbuf, expand_stage, shrink_stage, kv_stage, row_sems, line_sems, swap_sems, keep_sem):
    grp, pln = lax.axis_index("grp"), lax.axis_index("pln")
    tok = query_ref.shape[0]
    gathers = [Rows(expand_ref, expand_full, row_sems, 0, wa_count, expand_stage),
               Rows(shrink_ref, shrink_full, row_sems, 1, wa_count, shrink_stage)]
    load = pltpu.make_async_copy(kv_own_ref, kv_stage, keep_sem)
    load.start()
    for p in range(PLANE):
        sendbuf[p] = attended_ref[p * tok : p * tok + tok, :].astype(jnp.bfloat16)
    greet(grp_count, wa_count)
    swap = Swap(lambda p: sendbuf.at[p], lambda p: mixbuf.at[p], swap_sems.at[0])
    swap.begin()
    line = Line(kv_out, line_sems, grp_count, reach, tok)
    sources = [kv_own_ref.at[pl.ds(b * tok, tok)] for b in range(PLANE)]
    for b in range(PLANE):
        line.send(1, b, sources[b])
    for g in gathers:
        g.begin()
    whole = pl.ds(pl.multiple_of(grp * PLANE * tok, 16), PLANE * tok)
    load.wait()
    keep = pltpu.make_async_copy(kv_stage, kv_out.at[whole], keep_sem)
    keep.start()
    row = lambda i: vector_row(vec_ref, wa_count, *vec_at[i])
    for offset in range(4):
        swap.arrived(offset)
    mixed = flat_pairs(mixbuf)
    mixed_ref[...] = mixed
    value = query_ref[...].astype(jnp.float32) + matmul(mixed, out_mat_ref[...]) + row(3)
    hidden, normed, inverse = norm_forward(value, row(4), row(5))
    hidden_ref[...] = hidden
    normed_ref[...] = normed
    inverse_ref[...] = jnp.broadcast_to(inverse, inverse_ref.shape)
    query = (matmul(hidden.astype(jnp.bfloat16), query_mat_ref[...]) + row(6)).astype(jnp.bfloat16) * 0.125
    for pair in range(PLANE):
        qbuf[pair] = query[:, pair * 128 : pair * 128 + 128]
    place = lambda p: q_out.at[pl.ds(pl.multiple_of(p * tok, 16), tok)]
    swap_q = Swap(lambda p: qbuf.at[p], place, swap_sems.at[1])
    swap_q.begin()
    for g in gathers:
        g.staged()
    line.forward(1)
    for g in gathers:
        g.pass_on()
    for step in range(2, reach + 1):
        line.forward(step)
    for offset in range(4):
        swap_q.arrived(offset)
    for g in gathers:
        g.arrived()
    for g in gathers:
        g.finish()
    line.finish(sources)
    keep.wait()
    swap.finish()
    swap_q.finish()


def run_middle(grp_count, wa_count, attended, query, out_mat, query_mat, vecs, vec_at, kv_own, expand, shrink):
    tok = query.shape[0]
    reach = min(grp_count - 1, (DOCLEN + PLANE * tok - 2) // (PLANE * tok))
    low, full = jnp.bfloat16, jnp.float32
    shape = jax.ShapeDtypeStruct
    return pl.pallas_call(
        functools.partial(middle_kernel, grp_count, wa_count, reach, vec_at),
        out_shape=(shape((tok, 512), full), shape((tok, 512), full), shape((tok, 128), full), shape((tok, 512), low),
                   shape((PLANE * tok, 128), low), shape((grp_count * PLANE * tok, 256), low),
                   shape((expand.shape[0] * wa_count, expand.shape[1]), low),
                   shape((shrink.shape[0] * wa_count, shrink.shape[1]), low)),
        in_specs=[VMEM] * 5 + [ANY] * 3,
        out_specs=tuple([VMEM] * 4 + [ANY] * 4),
        scratch_shapes=[
            pltpu.VMEM((PLANE, tok, 128), low), pltpu.VMEM((PLANE, tok, 128), low), pltpu.VMEM((PLANE, tok, 128), low),
            pltpu.VMEM(expand.shape, low), pltpu.VMEM(shrink.shape, low), pltpu.VMEM((PLANE * tok, 256), low),
            DMA((5, 2, max(1, wa_count - 1))), DMA((2, 2, reach, PLANE)), DMA((2, 2, 4)), DMA],
        cost_estimate=pl.CostEstimate(flops=30000000000, bytes_accessed=0, transcendentals=0),
        compiler_params=pltpu.CompilerParams(collective_id=2, has_side_effects=True, vmem_limit_bytes=60 << 20),
    )(attended, query, out_mat, query_mat, vecs, kv_own, expand, shrink)


def swap_kernel(inverse, in_ref, out_ref, sendbuf, getbuf, swap_sems):
    tok = getbuf.shape[1]
    for p in range(PLANE):
        if inverse:
            sendbuf[p] = in_ref[p * tok : p * tok + tok, :].astype(jnp.bfloat16)
        else:
            sendbuf[p] = in_ref[:, p * 128 : p * 128 + 128].astype(jnp.bfloat16)
    greet(1, 1, groups=False, rows=False)
    swap = Swap(lambda p: sendbuf.at[p], lambda p: getbuf.at[p], swap_sems)
    swap.begin()
    for offset in range(4):
        swap.arrived(offset)
    for p in range(PLANE):
        if inverse:
            out_ref[:, p * 128 : p * 128 + 128] = getbuf[p]
        else:
            out_ref[p * tok : p * tok + tok, :] = getbuf[p]
    swap.finish()


def run_swap(inverse, value, ident):
    tok = value.shape[0] // PLANE if inverse else value.shape[0]
    low = jnp.bfloat16
    return pl.pallas_call(
        functools.partial(swap_kernel, inverse),
        out_shape=jax.ShapeDtypeStruct((tok, 512) if inverse else (PLANE * tok, 128), low),
        in_specs=[VMEM], out_specs=VMEM,
        scratch_shapes=[pltpu.VMEM((PLANE, tok, 128), low), pltpu.VMEM((PLANE, tok, 128), low), DMA((2, 4))],
        cost_estimate=pl.CostEstimate(flops=6000000000, bytes_accessed=0, transcendentals=0),
        compiler_params=pltpu.CompilerParams(collective_id=ident, has_side_effects=True, vmem_limit_bytes=60 << 20),
    )(value)


class Fold:
    def __init__(self, partial, mine, sendbuf, getbuf, sems, load_sems, grp_count, reach, block):
        self.partial, self.mine, self.sendbuf, self.getbuf = partial, mine, sendbuf, getbuf
        self.sems, self.load_sems = sems, load_sems
        self.count, self.reach, self.block = grp_count, reach, block
        self.grp = lax.axis_index("grp")

    def toward(self, side):
        return 1 if side == 0 else -1

    def rows(self, owner, block):
        return pl.ds(pl.multiple_of((owner * PLANE + block) * self.block, 16), self.block)

    def part(self, block):
        return pl.ds(block * self.block, self.block)

    def sends(self, side, stage):
        return self.grp + stage < self.count if side == 0 else self.grp - stage >= 0

    def receives(self, side, stage):
        if side == 0:
            return jnp.logical_and(self.grp >= 1, self.grp - 1 + stage < self.count)
        return jnp.logical_and(self.grp + 1 < self.count, self.grp + 1 - stage >= 0)

    def copy(self, side, stage, block, back=False):
        source = self.sendbuf.at[side, stage - 1, self.part(block)]
        if stage == self.reach and not back:
            source = self.partial.at[self.rows(self.grp + self.toward(side) * stage, block)]
        peer = self.grp + (-self.toward(side) if back else self.toward(side))
        return remote(source, self.getbuf.at[side, stage - 1, self.part(block)], self.sems.at[0, side, stage - 1, block],
                      self.sems.at[1, side, stage - 1, block], {"grp": peer})

    def load(self, side, stage):
        size = PLANE * self.block
        rows = pl.ds(pl.multiple_of((self.grp + self.toward(side) * stage) * size, 16), size)
        return pltpu.make_async_copy(self.partial.at[rows], self.mine.at[side, stage - 1], self.load_sems.at[side, stage - 1])

    def begin(self):
        for block in range(PLANE):
            for side in (0, 1):
                @pl.when(self.sends(side, self.reach))
                def _():
                    self.copy(side, self.reach, block).start()
        for stage in range(1, self.reach):
            for side in (0, 1):
                @pl.when(self.sends(side, stage))
                def _():
                    self.load(side, stage).start()

    def grow(self, stage):
        for side in (0, 1):
            @pl.when(self.sends(side, stage))
            def _():
                self.load(side, stage).wait()
        for block in range(PLANE):
            part = self.part(block)
            for side in (0, 1):
                @pl.when(self.sends(side, stage))
                def _():
                    self.sendbuf[side, stage - 1, part, :] = self.mine[side, stage - 1, part, :]

                    @pl.when(self.receives(side, stage + 1))
                    def _():
                        self.copy(side, stage + 1, block, True).wait_recv()
                        total = self.mine[side, stage - 1, part, :].astype(jnp.float32)
                        total = total + self.getbuf[side, stage, part, :].astype(jnp.float32)
                        self.sendbuf[side, stage - 1, part, :] = total.astype(jnp.bfloat16)

                    self.copy(side, stage, block).start()

    def total(self, own, out):
        for block in range(PLANE):
            part = self.part(block)
            for side in (0, 1):
                @pl.when(self.receives(side, 1))
                def _():
                    self.copy(side, 1, block, True).wait_recv()
                    own[part, :] = own[part, :] + self.getbuf[side, 0, part, :].astype(jnp.float32)
            out[block] = own[part, :].astype(jnp.bfloat16)

    def finish(self):
        for stage in range(1, self.reach + 1):
            for block in range(PLANE):
                for side in (0, 1):
                    @pl.when(self.sends(side, stage))
                    def _():
                        self.copy(side, stage, block, True).wait_send()


def store_blocks(buffer, value):
    for c in range(PLANE):
        buffer[c] = value[:, c * 128 : c * 128 + 128].astype(jnp.bfloat16)


def halves(buffer):
    keys = jnp.concatenate([buffer[p, :, :128] for p in range(PLANE)], axis=1)
    values = jnp.concatenate([buffer[p, :, 128:] for p in range(PLANE)], axis=1)
    return keys, values


class Reduce:
    def __init__(self, index, source, parts, got, kept, sems, wa_count, place=None):
        self.index, self.source, self.sems, self.wa_count = index, source, sems, wa_count
        self.parts, (self.got_core, self.got_wa, self.got_row) = parts, got
        self.by_core, self.by_wa, self.by_row = kept
        self.place = index if place is None else place
        self.wa, self.pln = lax.axis_index("wa"), lax.axis_index("pln")
        self.core = lax.rem(self.pln, 2)
        self.row = self.pln // 2
        self.size = 512 // wa_count

    def core_copy(self, row):
        return remote(self.source.at[row * 2 + 1 - self.core], self.got_core.at[self.index, row],
                      self.sems.at[0, self.index, row], self.sems.at[1, self.index, row], {"pln": across(self.pln, 1)})

    def rows_of(self, wa):
        return pl.ds(pl.multiple_of(wa * self.size, 16), self.size)

    def wa_copy(self, offset):
        peer = lax.rem(self.wa + offset, self.wa_count)
        return remote(self.by_core.at[self.index, :, self.rows_of(peer)], self.got_wa.at[offset - 1, self.index],
                      self.sems.at[0, self.index, 1 + offset], self.sems.at[1, self.index, 1 + offset], {"wa": peer})

    def row_copy(self):
        return remote(self.by_wa.at[self.index, 1 - self.row], self.got_row.at[self.index],
                      self.sems.at[0, self.index, 1 + self.wa_count], self.sems.at[1, self.index, 1 + self.wa_count],
                      {"pln": across(self.pln, 2)})

    def begin(self):
        for row in (0, 1):
            self.core_copy(row).start()

    def after_core(self):
        for row in (0, 1):
            self.core_copy(row).wait_recv()
            mine = self.parts[row * 2 + self.core].astype(jnp.float32)
            total = mine + self.got_core[self.index, row].astype(jnp.float32)
            self.by_core[self.index, row] = total.astype(jnp.bfloat16)
        for offset in range(1, self.wa_count):
            self.wa_copy(offset).start()

    def after_wa(self):
        for offset in range(1, self.wa_count):
            self.wa_copy(offset).wait_recv()
        for row in (0, 1):
            total = self.by_core[self.index, row, self.rows_of(self.wa), :].astype(jnp.float32)
            for offset in range(1, self.wa_count):
                total = total + self.got_wa[offset - 1, self.index, row].astype(jnp.float32)
            self.by_wa[self.index, row] = total.astype(jnp.bfloat16)
        self.row_copy().start()

    def after_row(self):
        self.row_copy().wait_recv()
        total = self.by_wa[self.index, self.row].astype(jnp.float32) + self.got_row[self.index].astype(jnp.float32)
        self.by_row[self.place] = total.astype(jnp.bfloat16)

    def finish(self):
        for row in (0, 1):
            self.core_copy(row).wait_send()
        for offset in range(1, self.wa_count):
            self.wa_copy(offset).wait_send()
        self.row_copy().wait_send()


def turn_kernel(grp_count, wa_count, reach, vec_at, dq_ref, dkv_ref, own_ref, back_ref, normed_ref, inverse_ref, hidden_ref,
                mixed_one_ref, mixed_two_ref, branch_two_ref, encoder_ref, query_mat_ref, out_mat_ref, vec_ref, vg_ref, wide_ref,
                do_out, back_out, kv_out, grads_out, vg_out, wide_out,
                dqsend, dqget, dosend, doget, kvsend, kvget, total, mine, foldsend, foldget, grads, parts, got_core, got_wa,
                got_row, by_core, by_wa, by_row, fold_sems, load_sems, swap_sems, out_sems, part_sems, red_sems):
    tok = back_ref.shape[0]
    for p in range(PLANE):
        dqsend[p] = dq_ref[p * tok : p * tok + tok, :]
    wide = wide_ref.shape[0]
    loads = [pltpu.make_async_copy(wide_ref.at[i], parts.at[i], part_sems.at[i]) for i in range(wide)]
    for l in loads:
        l.start()
    greet(grp_count, wa_count)
    swap_dq = Swap(lambda p: dqsend.at[p], lambda p: dqget.at[p], swap_sems.at[0])
    swap_dq.begin()
    fold = Fold(dkv_ref, mine, foldsend, foldget, fold_sems, load_sems, grp_count, reach, tok)
    fold.begin()
    reds = [Reduce(i, wide_ref.at[i], parts.at[i], (got_core, got_wa, got_row), (by_core, by_wa, by_row), red_sems, wa_count)
            for i in range(wide)]
    for r in reds:
        r.begin()
    row = lambda i: vector_row(vec_ref, wa_count, *vec_at[i])
    vg_out[...] = vg_ref[...]
    saves = [pltpu.make_async_copy(grads.at[i], grads_out.at[i], out_sems.at[i]) for i in range(5)]
    total[...] = own_ref[...]
    store_blocks(grads.at[0], dot(mixed_two_ref[...], branch_two_ref[...], 0, 0))
    saves[0].start()
    for l in loads:
        l.wait()
    for r in reds:
        r.after_core()
    for offset in range(4):
        swap_dq.arrived(offset)
    dq = flat_pairs(dqget)
    incoming = back_ref[...] + dot(dq, query_mat_ref[...], 1, 1)
    back, gain_grad, shift_grad = norm_backward(incoming, normed_ref[...], inverse_ref[:, :1], row(4))
    back_out[...] = back
    branch = back.astype(jnp.bfloat16)
    do = dot(branch, out_mat_ref[...], 1, 1).astype(jnp.bfloat16)
    for p in range(PLANE):
        dosend[p] = do[:, p * 128 : p * 128 + 128]
    swap_do = Swap(lambda p: dosend.at[p], lambda p: doget.at[p], swap_sems.at[1])
    swap_do.begin()
    vg_out[10:11, :] = gain_grad.reshape(1, 512)
    vg_out[11:12, :] = shift_grad.reshape(1, 512)
    vg_out[12:13, :] = column_sum(branch).reshape(1, 512)
    vg_out[13:14, :] = column_sum(dq).reshape(1, 512)
    store_blocks(grads.at[1], dot(hidden_ref[...].astype(jnp.bfloat16), dq, 0, 0))
    saves[1].start()
    store_blocks(grads.at[2], dot(mixed_one_ref[...], branch, 0, 0))
    saves[2].start()
    for stage in range(reach - 1, 0, -1):
        fold.grow(stage)
    for offset in range(4):
        swap_do.arrived(offset)
    for p in range(PLANE):
        do_out[p * tok : p * tok + tok, :] = doget[p]
    for r in reds:
        r.after_wa()
    fold.total(total, kvsend)
    swap_kv = Swap(lambda p: kvsend.at[p], lambda p: kvget.at[p], swap_sems.at[2])
    swap_kv.begin()
    for offset in range(4):
        swap_kv.arrived(offset)
    keys, values = halves(kvget)
    kv_out[:, :512] = keys
    kv_out[:, 512:] = values
    encoder = encoder_ref[...]
    store_blocks(grads.at[3], dot(encoder, keys, 0, 0))
    saves[3].start()
    store_blocks(grads.at[4], dot(encoder, values, 0, 0))
    saves[4].start()
    vg_out[14:15, :] = column_sum(values).reshape(1, 512)
    for r in reds:
        r.after_row()
    wide_save = pltpu.make_async_copy(by_row, wide_out, part_sems.at[0])
    wide_save.start()
    for s in saves:
        s.wait()
    for r in reds:
        r.finish()
    wide_save.wait()
    fold.finish()
    for s in (swap_dq, swap_do, swap_kv):
        s.finish()


def fold_scratch(tok, reach):
    low = jnp.bfloat16
    size = PLANE * tok
    return [pltpu.VMEM((PLANE, tok, 256), low), pltpu.VMEM((PLANE, tok, 256), low), pltpu.VMEM((size, 256), jnp.float32),
            pltpu.VMEM((2, max(1, reach - 1), size, 256), low), pltpu.VMEM((2, reach, size, 256), low),
            pltpu.VMEM((2, reach, size, 256), low)]


def run_turn(grp_count, wa_count, vec_at, dq, dkv, own, back, normed, inverse, hidden, mixed_one, mixed_two, branch_two,
             encoder, query_mat, out_mat, vecs, vg, wide):
    tok = back.shape[0]
    reach = min(grp_count - 1, (DOCLEN + PLANE * tok - 2) // (PLANE * tok))
    low, full = jnp.bfloat16, jnp.float32
    shape = jax.ShapeDtypeStruct
    pairs = pltpu.VMEM((PLANE, tok, 128), low)
    count, size = wide.shape[0], 512 // wa_count
    return pl.pallas_call(
        functools.partial(turn_kernel, grp_count, wa_count, reach, vec_at),
        out_shape=(shape((PLANE * tok, 128), low), shape((tok, 512), full), shape((tok, 1024), low),
                   shape((5, PLANE, 512, 128), low), shape(vg.shape, full), shape((count, size, 128), low)),
        in_specs=[VMEM, ANY] + [VMEM] * 13 + [ANY],
        out_specs=(VMEM, VMEM, VMEM, ANY, VMEM, ANY),
        scratch_shapes=[pairs] * 4 + fold_scratch(tok, reach) + [
            pltpu.VMEM((5, PLANE, 512, 128), low), pltpu.VMEM((count, PLANE, 512, 128), low),
            pltpu.VMEM((count, 2, 512, 128), low), pltpu.VMEM((max(1, wa_count - 1), count, 2, size, 128), low),
            pltpu.VMEM((count, size, 128), low), pltpu.VMEM((count, 2, 512, 128), low), pltpu.VMEM((count, 2, size, 128), low),
            pltpu.VMEM((count, size, 128), low), DMA((2, 2, reach, PLANE)), DMA((2, max(1, reach - 1))), DMA((3, 2, 4)),
            DMA((5,)), DMA((count,)), DMA((2, count, wa_count + 2))],
        cost_estimate=pl.CostEstimate(flops=32000000000, bytes_accessed=0, transcendentals=0),
        compiler_params=pltpu.CompilerParams(collective_id=8, has_side_effects=True, vmem_limit_bytes=60 << 20),
    )(dq, dkv, own, back, normed, inverse, hidden, mixed_one, mixed_two, branch_two, encoder, query_mat, out_mat, vecs, vg,
      wide)


def greet_all(grp_count, wa_count):
    barrier = pltpu.get_barrier_semaphore()
    grp, pln, wa = lax.axis_index("grp"), lax.axis_index("pln"), lax.axis_index("wa")
    peers = [{"pln": across(pln, o)} for o in (1, 2, 3)]
    peers += [{"wa": lax.rem(wa + o, wa_count)} for o in range(1, wa_count)]
    peers += [{"grp": lax.rem(grp + o, grp_count)} for o in range(1, grp_count)]
    for where in peers:
        pl.semaphore_signal(barrier, inc=1, device_id=where, device_id_type=MESH)
    pl.semaphore_wait(barrier, len(peers))


def closing_kernel(grp_count, wa_count, reach, count, dq_ref, dkv_ref, own_ref, query_ref, content_ref, early_ref, wide_ref, vg_ref,
                   dq_out, kv_out, out_ref, vg_out,
                   dqsend, dqget, kvsend, kvget, total, mine, foldsend, foldget, parts, got_core, got_wa, got_row,
                   by_core, by_wa, by_row, got_grp, final, vsum, vgot, vall,
                   fold_sems, load_sems, swap_sems, part_sems, wide_sem, red_sems, vec_sems, grp_sems, share_sems):
    grp, pln, wa = lax.axis_index("grp"), lax.axis_index("pln"), lax.axis_index("wa")
    tok = query_ref.shape[0]
    early = early_ref.shape[0]
    wide = wide_ref.shape[0]
    sets = ((0, wide), (wide, early + 1), (wide + early + 1, count - early - 1))
    size = 512 // wa_count
    slab = size // grp_count
    for p in range(PLANE):
        dqsend[p] = dq_ref[p * tok : p * tok + tok, :]
    greet_all(grp_count, wa_count)
    swap_dq = Swap(lambda p: dqsend.at[p], lambda p: dqget.at[p], swap_sems.at[0])
    swap_dq.begin()
    fold = Fold(dkv_ref, mine, foldsend, foldget, fold_sems, load_sems, grp_count, reach, tok)
    fold.begin()
    loads = [pltpu.make_async_copy(early_ref.at[i], parts.at[i], part_sems.at[i]) for i in range(early)]
    for l in loads:
        l.start()
    wide_load = pltpu.make_async_copy(wide_ref, by_row.at[pl.ds(0, wide)], wide_sem)
    wide_load.start()
    got, kept = (got_core, got_wa, got_row), (by_core, by_wa, by_row)
    reds = [Reduce(i, early_ref.at[i] if i < early else parts.at[i], parts.at[i], got, kept, red_sems, wa_count,
                   wide + i) for i in range(count)]
    for r in reds[:early]:
        r.begin()
    total[...] = own_ref[...]
    vsum[0] = vg_ref[...]
    for offset in range(4):
        swap_dq.arrived(offset)
    dq = flat_pairs(dqget)
    dq_out[...] = dq
    store_blocks(parts.at[early], dot(query_ref[...], dq, 0, 0))
    vsum[0, 15:16, :] = column_sum(dq).reshape(1, 512)
    reds[early].begin()
    for l in loads:
        l.wait()
    for r in reds[: early + 1]:
        r.after_core()
    for stage in range(reach - 1, 0, -1):
        fold.grow(stage)
    wide_load.wait()

    def grp_copy(set_at, offset):
        start, length = sets[set_at]
        peer = lax.rem(grp + offset, grp_count)
        some = pl.ds(start, length)
        rows = pl.ds(pl.multiple_of(peer * slab, 8), slab)
        return remote(by_row.at[some, rows], got_grp.at[offset - 1, some], grp_sems.at[0, set_at, offset - 1],
                      grp_sems.at[1, set_at, offset - 1], {"grp": peer})

    offsets = range(1, grp_count)
    for o in offsets:
        grp_copy(0, o).start()
    for r in reds[: early + 1]:
        r.after_wa()
    fold.total(total, kvsend)
    swap_kv = Swap(lambda p: kvsend.at[p], lambda p: kvget.at[p], swap_sems.at[1])
    swap_kv.begin()
    for r in reds[: early + 1]:
        r.after_row()
    for o in offsets:
        grp_copy(1, o).start()
    for offset in range(4):
        swap_kv.arrived(offset)
    keys, values = halves(kvget)
    content = content_ref[...]
    store_blocks(parts.at[early + 1], dot(content, keys, 0, 0))
    reds[early + 1].begin()
    store_blocks(parts.at[early + 2], dot(content, values, 0, 0))
    reds[early + 2].begin()
    vsum[0, 16:17, :] = column_sum(values).reshape(1, 512)
    vec_core = remote(vsum.at[0], vgot.at[0], vec_sems.at[0, 0], vec_sems.at[1, 0], {"pln": across(pln, 1)})
    vec_core.start()
    kv_out[:, :512] = keys
    kv_out[:, 512:] = values

    for r in reds[early + 1 :]:
        r.after_core()
    vec_core.wait_recv()
    vsum[1] = vsum[0] + vgot[0]
    vec_wa = [remote(vsum.at[1], vgot.at[o], vec_sems.at[0, o], vec_sems.at[1, o], {"wa": lax.rem(wa + o, wa_count)})
              for o in range(1, wa_count)]
    for v in vec_wa:
        v.start()
    for r in reds[early + 1 :]:
        r.after_wa()
    for v in vec_wa:
        v.wait_recv()
    vall[wa] = vsum[1]
    for o in range(1, wa_count):
        vall[lax.rem(wa + wa_count - o, wa_count)] = vgot[o]
    joined = vall[0]
    for o in range(1, wa_count):
        joined = joined + vall[o]
    vsum[2] = joined
    vec_row = remote(vsum.at[2], vgot.at[wa_count], vec_sems.at[0, wa_count], vec_sems.at[1, wa_count],
                     {"pln": across(pln, 2)})
    vec_row.start()
    own_rows = pl.ds(pl.multiple_of(grp * slab, 8), slab)

    def settle(set_at):
        start, length = sets[set_at]
        some = pl.ds(start, length)
        for o in offsets:
            grp_copy(set_at, o).wait_recv()
        value = by_row[some, own_rows, :].astype(jnp.float32)
        for o in offsets:
            value = value + got_grp[o - 1, some].astype(jnp.float32)
        final[some] = value.astype(jnp.bfloat16)

    def spot(column, source, some):
        return out_ref.at[column, some, pl.ds(pl.multiple_of(source * slab, 8), slab)]

    def spread(set_at, offset):
        start, length = sets[set_at]
        some = pl.ds(start, length)
        return remote(final.at[some], spot(pln, grp, some), share_sems.at[0, set_at, 0, offset],
                      share_sems.at[1, set_at, 0, offset], {"grp": lax.rem(grp + offset, grp_count)})

    def keep(set_at):
        start, length = sets[set_at]
        some = pl.ds(start, length)
        return pltpu.make_async_copy(final.at[some], spot(pln, grp, some), share_sems.at[0, set_at, 0, 0])

    def give(set_at, kind, offset):
        start, length = sets[set_at]
        some = pl.ds(start, length)
        source = lax.rem(grp + grp_count - offset, grp_count)
        column = pln if kind < 3 else across(pln, 2)
        there = spot(column, source, some)
        return remote(there, there, share_sems.at[0, set_at, kind, offset], share_sems.at[1, set_at, kind, offset],
                      {"pln": across(pln, 2 if kind == 1 else 1)})

    def share(set_at):
        settle(set_at)
        keep(set_at).start()
        for o in offsets:
            spread(set_at, o).start()

    share(0)
    share(1)
    for r in reds[early + 1 :]:
        r.after_row()
    for o in offsets:
        grp_copy(2, o).start()
    vec_row.wait_recv()
    vsum[3] = vsum[2] + vgot[wa_count]
    vec_grp = [remote(vsum.at[3], vall.at[wa_count + o], vec_sems.at[0, wa_count + o], vec_sems.at[1, wa_count + o],
                      {"grp": lax.rem(grp + o, grp_count)}) for o in offsets]
    for v in vec_grp:
        v.start()
    everyone = range(grp_count)

    def hand_out(set_at, offset):
        if offset == 0:
            keep(set_at).wait()
        else:
            spread(set_at, offset).wait_recv()
        give(set_at, 1, offset).start()
        give(set_at, 2, offset).start()

    def cross_over(set_at):
        for o in everyone:
            give(set_at, 1, o).wait_recv()
            give(set_at, 3, o).start()

    for o in everyone:
        hand_out(0, o)
    for o in everyone:
        hand_out(1, o)
    share(2)
    cross_over(0)
    cross_over(1)
    for o in everyone:
        hand_out(2, o)
    for v in vec_grp:
        v.wait_recv()
    ordered = jnp.zeros_like(vsum[3])
    for g in everyone:
        piece = jnp.where(grp == g, vsum[3], 0.0)
        for o in offsets:
            piece = piece + jnp.where(lax.rem(grp + grp_count - o, grp_count) == g, vall[wa_count + o], 0.0)
        ordered = ordered + piece
    vg_out[...] = ordered
    cross_over(2)
    for set_at in range(3):
        for o in everyone:
            give(set_at, 2, o).wait_recv()
            give(set_at, 3, o).wait_recv()
    for set_at in range(3):
        for o in everyone:
            for kind in (1, 2, 3):
                give(set_at, kind, o).wait_send()
        for o in offsets:
            spread(set_at, o).wait_send()
            grp_copy(set_at, o).wait_send()
    for v in [vec_core, vec_row] + vec_wa + vec_grp:
        v.wait_send()
    for r in reds:
        r.finish()
    fold.finish()
    swap_dq.finish()
    swap_kv.finish()


def run_closing(grp_count, wa_count, dq, dkv, own, query, content, early, wide, vg):
    tok = query.shape[0]
    count = early.shape[0] + 3
    every = count + wide.shape[0]
    reach = min(grp_count - 1, (DOCLEN + PLANE * tok - 2) // (PLANE * tok))
    size = 512 // wa_count
    slab = size // grp_count
    low, full = jnp.bfloat16, jnp.float32
    shape = jax.ShapeDtypeStruct
    pairs = pltpu.VMEM((PLANE, tok, 128), low)
    steps = wa_count + 2
    return pl.pallas_call(
        functools.partial(closing_kernel, grp_count, wa_count, reach, count),
        out_shape=(shape((tok, 512), low), shape((tok, 1024), low), shape((PLANE, every, size, 128), low),
                   shape(vg.shape, full)),
        in_specs=[VMEM, ANY, VMEM, VMEM, VMEM, ANY, ANY, VMEM],
        out_specs=(VMEM, VMEM, ANY, VMEM),
        scratch_shapes=[pairs] * 2 + fold_scratch(tok, reach) + [
            pltpu.VMEM((count, PLANE, 512, 128), low), pltpu.VMEM((count, 2, 512, 128), low),
            pltpu.VMEM((max(1, wa_count - 1), count, 2, size, 128), low), pltpu.VMEM((count, size, 128), low),
            pltpu.VMEM((count, 2, 512, 128), low), pltpu.VMEM((count, 2, size, 128), low), pltpu.VMEM((every, size, 128), low),
            pltpu.VMEM((grp_count - 1, every, slab, 128), low), pltpu.VMEM((every, slab, 128), low),
            pltpu.VMEM((4,) + vg.shape, full), pltpu.VMEM((wa_count + 1,) + vg.shape, full),
            pltpu.VMEM((wa_count + grp_count,) + vg.shape, full),
            DMA((2, 2, reach, PLANE)), DMA((2, max(1, reach - 1))), DMA((2, 2, 4)), DMA((early.shape[0],)), DMA,
            DMA((2, count, steps)), DMA((2, wa_count + grp_count)), DMA((2, 3, grp_count - 1)), DMA((2, 3, 4, grp_count))],
        cost_estimate=pl.CostEstimate(flops=75000000000, bytes_accessed=0, transcendentals=0),
        compiler_params=pltpu.CompilerParams(collective_id=9, has_side_effects=True, vmem_limit_bytes=60 << 20),
    )(dq, dkv, own, query, content, early, wide, vg)


def centre_kernel(wa_count, vec_at, attended_ref, hidden_ref, cotangent_ref, out_mat_ref, expand_ref, shrink_ref, vec_ref,
                  layer_out, mixed_out, back_out, branch_out, do_out, grads_out, vg_out,
                  sendbuf, getbuf, dosend, doget, slopes, actives, grads, swap_sems, out_sems):
    tok = hidden_ref.shape[0]
    for p in range(PLANE):
        sendbuf[p] = attended_ref[p * tok : p * tok + tok, :].astype(jnp.bfloat16)
    greet(1, 1, groups=False, rows=False)
    swap = Swap(lambda p: sendbuf.at[p], lambda p: getbuf.at[p], swap_sems.at[0])
    swap.begin()
    row = lambda i: vector_row(vec_ref, wa_count, *vec_at[i])
    vg_out[...] = jnp.zeros_like(vg_out)
    for offset in range(4):
        swap.arrived(offset)
    mixed = flat_pairs(getbuf)
    mixed_out[...] = mixed
    value = hidden_ref[...] + matmul(mixed, out_mat_ref[...]) + row(7)
    hidden, normed_two, inverse_two = norm_forward(value, row(8), row(9))
    low = hidden.astype(jnp.bfloat16)
    expand_row = row(10)
    total = hidden + row(11)
    width = 512
    chunks = expand_ref.shape[1] // width
    for c in range(chunks):
        span = slice(c * width, c * width + width)
        u = matmul(low, expand_ref[:, span]) + expand_row[:, span]
        cumulative = 0.5 * (1.0 + lax.erf(u * ROOT_HALF))
        active = (u * cumulative).astype(jnp.bfloat16)
        actives[:, span] = active
        slopes[:, span] = cumulative + u * jnp.exp(-0.5 * u * u) * INV_ROOT_TWO_PI
        total = total + matmul(active, shrink_ref[span, :])
    out, normed_three, inverse_three = norm_forward(total, row(12), row(13))
    layer_out[...] = out
    cotangent = cotangent_ref[...].astype(jnp.float32)
    back, gain_grad, shift_grad = norm_backward(cotangent, normed_three, inverse_three, row(12))
    vg_out[0:1, :] = gain_grad.reshape(1, 512)
    vg_out[1:2, :] = shift_grad.reshape(1, 512)
    grad = back.astype(jnp.bfloat16)
    vg_out[2:3, :] = column_sum(grad).reshape(1, 512)
    incoming = back
    steps = []
    for c in range(chunks):
        span = slice(c * width, c * width + width)
        du = (dot(grad, shrink_ref[span, :], 1, 1) * slopes[:, span]).astype(jnp.bfloat16)
        vg_out[3 + c : 4 + c, :] = column_sum(du).reshape(1, 512)
        incoming = incoming + dot(du, expand_ref[:, span], 1, 1)
        steps.append(du)
    back, gain_grad, shift_grad = norm_backward(incoming, normed_two, inverse_two, row(8))
    back_out[...] = back
    branch = back.astype(jnp.bfloat16)
    branch_out[...] = branch
    do = dot(branch, out_mat_ref[...], 1, 1).astype(jnp.bfloat16)
    for p in range(PLANE):
        dosend[p] = do[:, p * 128 : p * 128 + 128]
    swap_do = Swap(lambda p: dosend.at[p], lambda p: doget.at[p], swap_sems.at[1])
    swap_do.begin()
    vg_out[7:8, :] = gain_grad.reshape(1, 512)
    vg_out[8:9, :] = shift_grad.reshape(1, 512)
    vg_out[9:10, :] = column_sum(branch).reshape(1, 512)
    size = 512 // wa_count
    saves = [pltpu.make_async_copy(grads.at[i], grads_out.at[i], out_sems.at[i]) for i in range(2 * chunks)]
    for c in range(chunks):
        span = slice(c * width, c * width + width)
        store_blocks(grads.at[c], dot(low, steps[c], 0, 0))
        saves[c].start()
        value = dot(actives[:, span], grad, 0, 0).astype(jnp.bfloat16)
        for piece in range(width // size):
            owner, index = divmod(c * (width // size) + piece, chunks)
            for column in range(PLANE):
                grads[chunks + index, column, owner * size : owner * size + size, :] = value[
                    piece * size : piece * size + size, column * 128 : column * 128 + 128]
    for c in range(chunks):
        saves[chunks + c].start()
    for offset in range(4):
        swap_do.arrived(offset)
    for p in range(PLANE):
        do_out[p * tok : p * tok + tok, :] = doget[p]
    for save in saves:
        save.wait()
    swap.finish()
    swap_do.finish()


def run_centre(wa_count, vec_at, attended, hidden, cotangent, out_mat, expand, shrink, vecs):
    tok = hidden.shape[0]
    low, full = jnp.bfloat16, jnp.float32
    shape = jax.ShapeDtypeStruct
    pairs = pltpu.VMEM((PLANE, tok, 128), low)
    wide = expand.shape[1]
    return pl.pallas_call(
        functools.partial(centre_kernel, wa_count, vec_at),
        out_shape=(shape((tok, 512), full), shape((tok, 512), low), shape((tok, 512), full), shape((tok, 512), low),
                   shape((PLANE * tok, 128), low), shape((2 * wide // 512, PLANE, 512, 128), low), shape((24, 512), full)),
        in_specs=[VMEM] * 7,
        out_specs=(VMEM,) * 5 + (ANY, VMEM),
        scratch_shapes=[pairs] * 4 + [pltpu.VMEM((tok, wide), full), pltpu.VMEM((tok, wide), low),
            pltpu.VMEM((2 * wide // 512, PLANE, 512, 128), low), DMA((2, 2, 4)), DMA((2 * wide // 512,))],
        compiler_params=pltpu.CompilerParams(collective_id=3, has_side_effects=True, vmem_limit_bytes=60 << 20),
    )(attended, hidden, cotangent, out_mat, expand, shrink, vecs)


def last_kernel(wa_count, shares, at_ref, late_ref, sums_ref, dq_ref, dkv_ref, back_ref, query_mat, key_mat, value_mat,
                query_out, content_out, expand_out, shrink_out, *outs):
    wide = expand_out.shape[1] // 512
    size = late_ref.shape[2]
    count = late_ref.shape[1] - 2 * wide
    for c in range(PLANE):
        span = slice(c * 128, c * 128 + 128)
        for i in range(count):
            outs[i][:, span] = late_ref[c, 2 * wide + i].astype(jnp.float32)
        for i in range(wide):
            expand_out[:, i * 512 + c * 128 : i * 512 + c * 128 + 128] = late_ref[c, i].astype(jnp.float32)
            shrink_out[i * size : i * size + size, span] = late_ref[c, wide + i].astype(jnp.float32)
    query_out[...] = back_ref[...] + dot(dq_ref[...], query_mat[...], 1, 1)
    content_out[...] = dot(dkv_ref[:, :512], key_mat[...], 1, 1) + dot(dkv_ref[:, 512:], value_mat[...], 1, 1)
    at = 0
    for i, share in enumerate(shares):
        used = share * wa_count // 512
        line = jnp.concatenate([sums_ref[at + r : at + r + 1, :] for r in range(used)], axis=1)
        at += used
        mine = line[:, :share]
        for w in range(1, wa_count):
            mine = jnp.where(at_ref[0] == w, line[:, w * share : w * share + share], mine)
        outs[count + i][...] = mine.reshape(share)


def run_last(wa_count, wide, shares, at, late, sums, dq, dkv, back, query_mat, key_mat, value_mat):
    full = jnp.float32
    shape = jax.ShapeDtypeStruct
    tok = dq.shape[0]
    out_shape = [shape((tok, 512), full), shape((tok, 512), full), shape((late.shape[2], wide), full),
                 shape((wide // wa_count, 512), full)]
    out_shape += [shape((late.shape[2], 512), full)] * (late.shape[1] - wide // 256) + [shape((s,), full) for s in shares]
    return pl.pallas_call(
        functools.partial(last_kernel, wa_count, shares),
        out_shape=tuple(out_shape),
        in_specs=[SMEM] + [VMEM] * 8,
        out_specs=tuple([VMEM] * len(out_shape)),
        compiler_params=pltpu.CompilerParams(vmem_limit_bytes=60 << 20),
    )(at, late, sums, dq, dkv, back, query_mat, key_mat, value_mat)


def shards(
    query_in,
    content_in,
    encoder_in,
    out_grad,
    document_lengths,
    key_ranks,
    query_limits,
    self_query_weight,
    self_query_bias,
    self_key_weight,
    self_value_weight,
    self_value_bias,
    self_out_weight,
    self_out_bias,
    norm_one_gain,
    norm_one_shift,
    cross_query_weight,
    cross_query_bias,
    cross_key_weight,
    cross_value_weight,
    cross_value_bias,
    cross_out_weight,
    cross_out_bias,
    norm_two_gain,
    norm_two_shift,
    expand_weight,
    expand_bias,
    shrink_weight,
    shrink_bias,
    norm_three_gain,
    norm_three_shift,
):
    grp_count = lax.axis_size("grp")
    own = lax.axis_index("grp")[None].astype(jnp.int32)
    lens = document_lengths


    wa_count = lax.axis_size("wa")
    vectors = (self_query_bias, self_value_bias, cross_value_bias, self_out_bias, norm_one_gain, norm_one_shift,
        cross_query_bias, cross_out_bias, norm_two_gain, norm_two_shift, expand_bias, shrink_bias, norm_three_gain,
        norm_three_shift)
    vec_at, at = [], 0
    for v in vectors:
        vec_at.append((at, v.shape[0]))
        at += v.shape[0] // min(128, v.shape[0])
    vec_at = tuple(vec_at)
    mats = (self_key_weight, self_value_weight, self_query_weight, cross_key_weight, cross_value_weight, self_out_weight,
        cross_query_weight, cross_out_weight)
    (self_key_matrix, self_value_mat, self_query_mat, cross_key_matrix, cross_value_mat, self_out_mat, cross_query_mat,
        cross_out_mat, vec_all, pair_one, kv_one, kv_two_own, self_keys, cross_keys, self_marks, cross_marks) = run_opening(
        grp_count, wa_count, lens, key_ranks, query_limits, content_in[0], query_in[0],
        encoder_in[0], vectors, mats, vec_at)
    source = query_in[0]
    content_states = content_in[0]
    encoder_output = encoder_in[0]
    attended_one, total_one = attend_forward(True, lens, own, pair_one, self_marks, kv_one, self_keys)
    hidden_one, normed_one, inverse_one, mixed_one, pair_two, kv_two, expand_mat, shrink_mat = run_middle(
        grp_count, wa_count, attended_one, source, self_out_mat, cross_query_mat, vec_all, vec_at, kv_two_own,
        expand_weight, shrink_weight)
    attended_two, total_two = attend_forward(False, lens, own, pair_two, cross_marks, kv_two, cross_keys)
    layer_out, mixed_two, back_two, branch_two, do_two, wide, lines = run_centre(
        wa_count, vec_at, attended_two, hidden_one, out_grad[0], cross_out_mat, expand_mat, shrink_mat, vec_all)
    dq_two, dkv_two, own_two = attend_backward(False, lens, own, pair_two, cross_marks, kv_two, cross_keys,
        attended_two, total_two, do_two)
    do_one, back_one, kv_two_grad, early, lines, wide = run_turn(grp_count, wa_count, vec_at, dq_two, dkv_two, own_two, back_two,
        normed_one, inverse_one, hidden_one, mixed_one, mixed_two, branch_two, encoder_output, cross_query_mat, self_out_mat,
        vec_all, lines, wide)
    key_two_low, value_two_low = kv_two_grad[:, :512], kv_two_grad[:, 512:]
    encoder_grad = right_product(key_two_low, cross_key_matrix) + right_product(value_two_low, cross_value_mat)
    dq_one, dkv_one, own_one = attend_backward(True, lens, own, pair_one, self_marks, kv_one, self_keys,
        attended_one, total_one, do_one)
    query_one_low, kv_one_grad, late, sums = run_closing(grp_count, wa_count, dq_one, dkv_one, own_one, source,
        content_states, early, wide, lines)
    shares = tuple(v.shape[0] for v in (norm_three_gain, norm_three_shift, shrink_bias, expand_bias, norm_two_gain,
        norm_two_shift, cross_out_bias, norm_one_gain, norm_one_shift, self_out_bias, cross_query_bias, cross_value_bias,
        self_query_bias, self_value_bias))
    query_grad, content_grad, expand_grad, shrink_grad, *rest = run_last(wa_count, expand_weight.shape[1], shares,
        lax.axis_index("wa")[None].astype(jnp.int32), late, sums, query_one_low, kv_one_grad, back_one, self_query_mat,
        self_key_matrix, self_value_mat)
    names = ("cross_out", "cross_query", "self_out", "cross_key", "cross_value", "self_query", "self_key", "self_value")
    mat = dict(zip(names, rest))
    names = ("gain_three", "shift_three", "shrink", "expand", "gain_two", "shift_two", "cross_out", "gain_one", "shift_one",
        "self_out", "cross_query", "cross_value", "self_query", "self_value")
    vec = dict(zip(names, rest[len(mat):]))
    grads = (mat["self_query"], vec["self_query"], mat["self_key"], mat["self_value"], vec["self_value"], mat["self_out"],
        vec["self_out"], vec["gain_one"], vec["shift_one"], mat["cross_query"], vec["cross_query"], mat["cross_key"],
        mat["cross_value"], vec["cross_value"], mat["cross_out"], vec["cross_out"], vec["gain_two"], vec["shift_two"],
        expand_grad, vec["expand"], shrink_grad, vec["shrink"], vec["gain_three"], vec["shift_three"])
    return (layer_out[None], query_grad[None], content_grad[None], encoder_grad[None]) + grads


def solution(mesh):
    ctx, wa = mesh.devices.shape
    mesh = Mesh(mesh.devices.reshape(ctx // PLANE, PLANE, wa), ("grp", "pln", "wa"))
    in_specs = (
        P("wa", ("grp", "pln"), None),
        P("wa", ("grp", "pln"), None),
        P("wa", ("grp", "pln"), None),
        P("wa", ("grp", "pln"), None),
        P("wa", None),
        P("wa", None),
        P("wa", None),
        P("wa", None),
        P("wa"),
        P("wa", None),
        P("wa", None),
        P("wa"),
        P("wa", None),
        P("wa"),
        P("wa"),
        P("wa"),
        P("wa", None),
        P("wa"),
        P("wa", None),
        P("wa", None),
        P("wa"),
        P("wa", None),
        P("wa"),
        P("wa"),
        P("wa"),
        P("wa", None),
        P("wa"),
        P("wa", None),
        P("wa"),
        P("wa"),
        P("wa"),
    )
    out_specs = (
        P("wa", ("grp", "pln"), None),
        P("wa", ("grp", "pln"), None),
        P("wa", ("grp", "pln"), None),
        P("wa", ("grp", "pln"), None),
        P("wa", None),
        P("wa"),
        P("wa", None),
        P("wa", None),
        P("wa"),
        P("wa", None),
        P("wa"),
        P("wa"),
        P("wa"),
        P("wa", None),
        P("wa"),
        P("wa", None),
        P("wa", None),
        P("wa"),
        P("wa", None),
        P("wa"),
        P("wa"),
        P("wa"),
        P("wa", None),
        P("wa"),
        P("wa", None),
        P("wa"),
        P("wa"),
        P("wa"),
    )
    return jax.shard_map(shards, mesh=mesh, in_specs=in_specs, out_specs=out_specs, check_vma=False)
```

```python
import functools
import jax
import jax.numpy as jnp
from jax import lax
from jax.experimental import pallas as pl
from jax.experimental.pallas import tpu as pltpu
from jax.sharding import Mesh
from jax.sharding import PartitionSpec as P

PLANE = 4
DOCLEN = 2048
EPSILON = 1e-05
ROOT_HALF = 0.7071067811865476
INV_ROOT_TWO_PI = 0.3989422804014327
NEGATIVE = -1e29
HIDE = -(2.0 ** 100)
BLOCK = 512
WIDE = 1024
QUERIES = 512
KEYS = 512
STAT = 40


def dot(a, b, ca, cb):
    return lax.dot_general(a, b, (((ca,), (cb,)), ((), ())), preferred_element_type=jnp.float32)


def left_half(shape):
    return lax.broadcasted_iota(jnp.int32, shape, 1) < 64


def spans(lens_ref, first, count):
    low, high, total = 0, 0, 0
    for d in range(lens_ref.shape[1]):
        begin = total
        total = total + lens_ref[0, d]
        low = jnp.where(begin <= first, begin, low)
        high = jnp.where(begin <= first + count - 1, total, high)
    return low, high


def openings(lens_ref, places):
    total, found = 0, places == 0
    for d in range(lens_ref.shape[1] - 1):
        total = total + lens_ref[0, d]
        found = jnp.logical_or(found, places == total)
    return found


def over_blocks(low, high, first, size, step, carry, ranked):
    begin, end = low // size, (high + size - 1) // size
    own = first // size
    skip = 1 if ranked else 0

    def body(index, carry):
        if ranked:
            index = index + jnp.where(index >= own, 1, 0)
        return step(pl.multiple_of(index * size, size), carry)

    carry = lax.fori_loop(begin, end - skip, body, carry)
    if ranked:
        carry = step(pl.multiple_of(own * size, size), carry, True)
    return carry


def turned(value, eye):
    return dot(eye, value, 1, 1).astype(jnp.bfloat16)


def unit_matrix():
    row = lax.broadcasted_iota(jnp.int32, (128, 128), 0)
    lane = lax.broadcasted_iota(jnp.int32, (128, 128), 1)
    return jnp.where(row == lane, 1.0, 0.0).astype(jnp.bfloat16)


def with_stat(marks, stat, lane, at):
    high = stat.astype(jnp.bfloat16)
    rest = stat - high.astype(jnp.float32)
    middle = rest.astype(jnp.bfloat16)
    tail = (rest - middle.astype(jnp.float32)).astype(jnp.bfloat16)
    side = jnp.where(lane == at, high, jnp.where(lane == at + 1, middle, jnp.where(lane == at + 2, tail, marks)))
    return side


def backward_kernel(ranked, lens_ref, own_ref, q_ref, qm_ref, kv_ref, km_ref, o_ref, lse_ref, do_ref,
                    dq_ref, dkv_ref, own_dkv_ref, dk_ref, dv_ref, kt0_ref, kt1_ref):
    rows = q_ref.shape[0]
    base = own_ref[0] * rows
    half = left_half((BLOCK, 128))
    khalf = left_half((KEYS, 128))
    lane = lax.broadcasted_iota(jnp.int32, (BLOCK, 128), 1)
    one = jnp.ones((KEYS, 128), jnp.bfloat16)
    zero = jnp.zeros((BLOCK, 128), jnp.bfloat16)

    def clear(index, _):
        at = pl.multiple_of(index * BLOCK, BLOCK)
        dk_ref[pl.ds(at, BLOCK), :] = jnp.zeros((BLOCK, 128), jnp.float32)
        dv_ref[pl.ds(at, BLOCK), :] = jnp.zeros((BLOCK, 128), jnp.float32)
        return 0

    lax.fori_loop(0, kv_ref.shape[0] // BLOCK, clear, 0)
    eye = unit_matrix()
    tops = lax.broadcasted_iota(jnp.int32, (128, KEYS), 0) < 64
    low_all, high_all = spans(lens_ref, base, rows)

    def prepare(block, _):
        there = pl.ds(pl.multiple_of(block * KEYS, KEYS), KEYS)
        kt = turned(kv_ref[there, :128], eye)
        none = jnp.zeros((128, KEYS), jnp.bfloat16)
        kt0_ref[:, there] = jnp.where(tops, kt, none)
        kt1_ref[:, there] = jnp.where(tops, none, kt)
        return 0

    lax.fori_loop(low_all // KEYS, (high_all + KEYS - 1) // KEYS, prepare, 0)

    def one_block(block, _):
        start = pl.multiple_of(block * BLOCK, BLOCK)
        first = base + start
        low, high = spans(lens_ref, first, BLOCK)
        here = pl.ds(start, BLOCK)
        q, qm, do, lse = q_ref[here, :], qm_ref[here, :], do_ref[here, :], lse_ref[here, :]
        shared = do.astype(jnp.float32) * o_ref[here, :]
        delta0 = jnp.sum(jnp.where(half, shared, 0.0), axis=1, keepdims=True)
        delta1 = jnp.sum(jnp.where(half, 0.0, shared), axis=1, keepdims=True)
        side = with_stat(qm, lse, lane % 64, STAT)
        queries = (jnp.where(half, q, side), jnp.where(half, side, q))
        side = with_stat(zero, -jnp.where(half, delta1, delta0), lane % 64, STAT)
        grads = (jnp.where(half, do, side), jnp.where(half, side, do))

        both_q = jnp.concatenate([jnp.where(half, q, zero), jnp.where(half, zero, q)], axis=0)
        both_do = jnp.concatenate([jnp.where(half, do, zero), jnp.where(half, zero, do)], axis=0)

        def step(at, carry, diagonal=False):
            there = pl.ds(at, KEYS)
            k, v, km = kv_ref[there, :128], kv_ref[there, 128:], km_ref[there, :]
            keys = (jnp.where(khalf, k, km), jnp.where(khalf, km, k))
            values = (jnp.where(khalf, v, one), jnp.where(khalf, one, v))
            scores = [dot(keys[h], queries[h], 1, 1) for h in (0, 1)]
            if diagonal:
                other = at + lax.broadcasted_iota(jnp.int32, (KEYS, BLOCK), 0)
                row = first + lax.broadcasted_iota(jnp.int32, (1, BLOCK), 1)
                banned = other == jnp.where(openings(lens_ref, row), -1, row)
                scores = [jnp.where(banned, HIDE, s) for s in scores]
            ps = [jnp.exp(scores[h]) for h in (0, 1)]
            ds = [(ps[h] * dot(values[h], grads[h], 1, 1)).astype(jnp.bfloat16) for h in (0, 1)]
            ps = [p.astype(jnp.bfloat16) for p in ps]
            dv_ref[there, :] += dot(jnp.concatenate(ps, axis=1), both_do, 1, 0)
            dk_ref[there, :] += dot(jnp.concatenate(ds, axis=1), both_q, 1, 0)
            return carry + dot(kt0_ref[:, there], ds[0], 1, 0) + dot(kt1_ref[:, there], ds[1], 1, 0)

        dq = over_blocks(low, high, first, KEYS, step, jnp.zeros((128, BLOCK), jnp.float32), ranked)
        dq_ref[here, :] = jnp.transpose(dq * 0.125).astype(dq_ref.dtype)
        return 0

    lax.fori_loop(0, rows // BLOCK, one_block, 0)

    def save(index, _):
        there = pl.ds(pl.multiple_of(index * BLOCK, BLOCK), BLOCK)
        dkv_ref[there, :128] = dk_ref[there, :].astype(jnp.bfloat16)
        dkv_ref[there, 128:] = dv_ref[there, :].astype(jnp.bfloat16)
        return 0

    lax.fori_loop(0, kv_ref.shape[0] // BLOCK, save, 0)
    mine = pl.ds(pl.multiple_of(base, BLOCK), rows)
    own_dkv_ref[:, :128] = dk_ref[mine, :]
    own_dkv_ref[:, 128:] = dv_ref[mine, :]


def attend_backward(ranked, lens, own, q, qm, kv, km, o, lse, do):
    rows, keys = q.shape[0], kv.shape[0]
    whole = pl.BlockSpec(memory_space=pltpu.VMEM)
    smem = pl.BlockSpec(memory_space=pltpu.SMEM)
    return pl.pallas_call(
        functools.partial(backward_kernel, ranked),
        out_shape=(jax.ShapeDtypeStruct((rows, 128), jnp.bfloat16),) + (
            jax.ShapeDtypeStruct((keys, 256), jnp.bfloat16), jax.ShapeDtypeStruct((rows, 256), jnp.float32)),
        in_specs=[smem, smem] + [whole] * 7,
        out_specs=(whole, whole, whole),
        scratch_shapes=[pltpu.VMEM((keys, 128), jnp.float32)] * 2 + [pltpu.VMEM((128, keys), jnp.bfloat16)] * 2,
        cost_estimate=pl.CostEstimate(flops=26000000000, bytes_accessed=0, transcendentals=0),
        compiler_params=pltpu.CompilerParams(vmem_limit_bytes=60 << 20),
    )(lens, own, q, qm, kv, km, o, lse, do)


def matmul(left, right):
    return jnp.dot(left, right, preferred_element_type=jnp.float32)


def left_product(left, right):
    return jnp.einsum("ta,tb->ab", left, right, preferred_element_type=jnp.float32)


def right_product(left, right):
    return jnp.einsum("ta,ba->tb", left, right, preferred_element_type=jnp.float32)


def column_sum(value):
    return jnp.sum(value.astype(jnp.float32), axis=0)


def gelu_slope(value):
    cumulative = 0.5 * (1.0 + lax.erf(value * ROOT_HALF))
    return cumulative + value * jnp.exp(-0.5 * value * value) * INV_ROOT_TWO_PI


def norm_forward(value, gain_row, shift_row):
    middle = jnp.mean(value, axis=-1, keepdims=True)
    centred = value - middle
    spread = jnp.mean(centred * centred, axis=-1, keepdims=True)
    inverse = lax.rsqrt(spread + EPSILON)
    normed = centred * inverse
    return (normed * gain_row + shift_row, normed, inverse)


def norm_backward(incoming, normed, inverse, gain_row):
    scaled = incoming * gain_row
    centred = (
        scaled
        - jnp.mean(scaled, axis=-1, keepdims=True)
        - normed * jnp.mean(scaled * normed, axis=-1, keepdims=True)
    )
    return (inverse * centred, jnp.sum(incoming * normed, axis=0), jnp.sum(incoming, axis=0))


MESH = pl.DeviceIdType.MESH
ANY = pl.BlockSpec(memory_space=pltpu.HBM)
VMEM = pl.BlockSpec(memory_space=pltpu.VMEM)
SMEM = pl.BlockSpec(memory_space=pltpu.SMEM)
DMA = pltpu.SemaphoreType.DMA


def across(place, offset):
    if offset == 1:
        return place + 1 - 2 * lax.rem(place, 2)
    if offset == 2:
        return lax.rem(place + 2, 4)
    return 3 - place


def remote(src, dst, sends, recvs, where):
    return pltpu.make_async_remote_copy(
        src_ref=src, dst_ref=dst, send_sem=sends, recv_sem=recvs, device_id=where, device_id_type=MESH)


def greet(grp_count, wa_count, plane=True, groups=True, rows=True):
    barrier = pltpu.get_barrier_semaphore()
    grp, pln, wa = lax.axis_index("grp"), lax.axis_index("pln"), lax.axis_index("wa")

    def hello(where):
        pl.semaphore_signal(barrier, inc=1, device_id=where, device_id_type=MESH)

    count = 0
    if plane:
        for offset in (1, 2, 3):
            hello({"pln": across(pln, offset)})
        count += 3
    if rows:
        for offset in range(1, wa_count):
            hello({"wa": lax.rem(wa + offset, wa_count)})
        count += wa_count - 1
    if groups:
        @pl.when(grp > 0)
        def _():
            hello({"grp": grp - 1})

        @pl.when(grp < grp_count - 1)
        def _():
            hello({"grp": grp + 1})

        count = count + jnp.where(grp > 0, 1, 0) + jnp.where(grp < grp_count - 1, 1, 0)
    pl.semaphore_wait(barrier, count)


class Rows:
    def __init__(self, shard, full, sems, index, wa_count, stage=None):
        self.shard, self.full, self.sems, self.index, self.wa_count = shard, full, sems, index, wa_count
        self.stage = stage
        self.size = shard.shape[0]
        self.half = self.size // 2
        self.wa, self.pln = lax.axis_index("wa"), lax.axis_index("pln")
        self.core = lax.rem(self.pln, 2)

    def part(self, owner, core):
        return pl.ds(pl.multiple_of(owner * self.size + core * self.half, 16), self.half)

    def keep(self):
        own = pl.ds(pl.multiple_of(self.wa * self.size, 16), self.size)
        source = self.shard if self.stage is None else self.stage
        return pltpu.make_async_copy(source, self.full.at[own], self.sems.at[0, self.index, 0])

    def load(self):
        return pltpu.make_async_copy(self.shard, self.stage, self.sems.at[0, self.index, 0])

    def push(self, offset):
        mine = pl.ds(pl.multiple_of(self.core * self.half, 16), self.half)
        return remote(self.shard.at[mine], self.full.at[self.part(self.wa, self.core)],
                      self.sems.at[1, self.index, offset - 1], self.sems.at[2, self.index, offset - 1],
                      {"wa": lax.rem(self.wa + offset, self.wa_count)})

    def hand(self, offset):
        owner = lax.rem(self.wa + self.wa_count - offset, self.wa_count)
        spot = self.full.at[self.part(owner, self.core)]
        return remote(spot, spot, self.sems.at[3, self.index, offset - 1], self.sems.at[4, self.index, offset - 1],
                      {"pln": across(self.pln, 1)})

    def begin(self):
        if self.stage is None:
            self.keep().start()
        else:
            self.load().start()
        for offset in range(1, self.wa_count):
            self.push(offset).start()

    def staged(self):
        self.load().wait()
        self.keep().start()

    def pass_on(self):
        for offset in range(1, self.wa_count):
            self.push(offset).wait_recv()
            self.hand(offset).start()

    def arrived(self):
        self.keep().wait()
        for offset in range(1, self.wa_count):
            self.hand(offset).wait_recv()

    def finish(self):
        for offset in range(1, self.wa_count):
            self.push(offset).wait_send()
            self.hand(offset).wait_send()


class Line:
    def __init__(self, full, sems, grp_count, reach, block):
        self.full, self.sems, self.count, self.reach, self.block = full, sems, grp_count, reach, block
        self.grp = lax.axis_index("grp")

    def rows(self, owner, block):
        return pl.ds(pl.multiple_of((owner * PLANE + block) * self.block, 16), self.block)

    def copy(self, side, step, block, source=None):
        toward = 1 if side == 0 else -1
        owner = self.grp - toward * (step - 1)
        spot = self.full.at[self.rows(owner, block)]
        return remote(spot if source is None else source, spot, self.sems.at[0, side, step - 1, block],
                      self.sems.at[1, side, step - 1, block], {"grp": self.grp + toward})

    def sends(self, side, step):
        if side == 0:
            return jnp.logical_and(self.grp - step + 1 >= 0, self.grp + 1 < self.count)
        return jnp.logical_and(self.grp + step - 1 < self.count, self.grp - 1 >= 0)

    def receives(self, side, step):
        return self.grp - step >= 0 if side == 0 else self.grp + step < self.count

    def send(self, step, block, source=None):
        for side in (0, 1):
            @pl.when(self.sends(side, step))
            def _():
                self.copy(side, step, block, source).start()

    def arrival(self, side, step, block):
        toward = 1 if side == 0 else -1
        spot = self.full.at[self.rows(self.grp - toward * step, block)]
        return remote(spot, spot, self.sems.at[0, side, step - 1, block], self.sems.at[1, side, step - 1, block],
                      {"grp": self.grp - toward})

    def forward(self, step):
        for block in range(PLANE):
            for side in (0, 1):
                @pl.when(self.receives(side, step))
                def _():
                    self.arrival(side, step, block).wait_recv()

                    if step < self.reach:
                        @pl.when(self.sends(side, step + 1))
                        def _():
                            self.copy(side, step + 1, block).start()

    def finish(self, source=None):
        for step in range(1, self.reach + 1):
            for block in range(PLANE):
                for side in (0, 1):
                    @pl.when(self.sends(side, step))
                    def _():
                        self.copy(side, step, block, source[block] if source and step == 1 else None).wait_send()


class Swap:
    def __init__(self, src, dst, sems):
        self.src, self.dst, self.sems = src, dst, sems
        self.pln = lax.axis_index("pln")

    def copy(self, offset):
        peer = across(self.pln, offset)
        return remote(self.src(peer), self.dst(self.pln), self.sems.at[0, offset], self.sems.at[1, offset], {"pln": peer})

    def keep(self):
        return pltpu.make_async_copy(self.src(self.pln), self.dst(self.pln), self.sems.at[0, 0])

    def begin(self):
        for offset in (2, 3, 1):
            self.copy(offset).start()
        self.keep().start()

    def arrived(self, offset):
        self.keep().wait() if offset == 0 else self.copy(offset).wait_recv()

    def finish(self):
        for offset in (1, 2, 3):
            self.copy(offset).wait_send()


def pack_vectors(refs, pack):
    pack[...] = jnp.zeros_like(pack)
    at = 0
    for ref in refs:
        length = ref.shape[0]
        width = min(128, length)
        line = ref[...].astype(jnp.float32).reshape(1, length)
        for start in range(0, length, width):
            pack[at : at + 1, :width] = line[:, start : start + width]
            at += 1


def columns_of(ref, block):
    at = pl.multiple_of(block * 128, 128)
    line = ref[0:1, pl.ds(at, 128)].astype(jnp.float32)
    return jnp.transpose(jnp.broadcast_to(line, (128, 128)))


def make_marks(lens_ref, ranks_ref, limits_ref, base, self_keys, cross_keys, self_queries, cross_queries):
    docs = lens_ref.shape[1]
    lane = lax.rem(lax.broadcasted_iota(jnp.int32, (128, 128), 1), 64)
    stat = jnp.where(jnp.logical_and(lane >= STAT, lane < STAT + 3), -1.0, 0.0)

    def document(place):
        doc, opened, total = jnp.zeros((128, 128), jnp.int32), place == 0, 0
        for d in range(docs):
            total = total + lens_ref[0, d]
            doc = doc + jnp.where(place >= total, 1, 0)
            if d < docs - 1:
                opened = jnp.logical_or(opened, place == total)
        return doc, opened

    def keys(block, _):
        place = block * 128 + lax.broadcasted_iota(jnp.int32, (128, 128), 0)
        doc, opened = document(place)
        rank = jnp.where(opened, 0, columns_of(ranks_ref, block).astype(jnp.int32) + 1)
        marks = jnp.where(lane == doc, 1.0, stat)
        there = pl.ds(pl.multiple_of(block * 128, 128), 128)
        cross_keys[there, :] = marks.astype(jnp.bfloat16)
        self_keys[there, :] = jnp.where(lane == rank + 16, 1.0, marks).astype(jnp.bfloat16)
        return 0

    def queries(block, _):
        place = base + block * 128 + lax.broadcasted_iota(jnp.int32, (128, 128), 0)
        doc, _ = document(place)
        limit = columns_of(limits_ref, base // 128 + block).astype(jnp.int32)
        marks = jnp.where(jnp.logical_and(lane < docs, lane != doc), HIDE, 0.0)
        ranks = jnp.logical_and(lane >= 16, jnp.logical_and(lane < 33, lane - 17 >= limit))
        there = pl.ds(pl.multiple_of(block * 128, 128), 128)
        cross_queries[there, :] = marks.astype(jnp.bfloat16)
        self_queries[there, :] = jnp.where(ranks, HIDE, marks).astype(jnp.bfloat16)
        return 0

    lax.fori_loop(0, self_keys.shape[0] // 128, keys, 0)
    lax.fori_loop(0, self_queries.shape[0] // 128, queries, 0)


def vector_row(pack_ref, wa_count, start, length):
    width = min(128, length)
    pieces = []
    for wa in range(wa_count):
        for row in range(length // width):
            pieces.append(pack_ref[wa, start + row : start + row + 1, :width])
    return jnp.concatenate(pieces, axis=1)


def split_pairs(value, buffer, column):
    for pair in range(PLANE):
        buffer[pair, :, column : column + 128] = value[:, pair * 128 : pair * 128 + 128]


def flat_pairs(buffer):
    return jnp.concatenate([buffer[p] for p in range(PLANE)], axis=1)


class Looking:
    def __init__(self, ranked, lens, q, qm, kv, km, peaks, acc, base):
        self.ranked, self.lens, self.base = ranked, lens, base
        self.q, self.qm, self.kv, self.km, self.peaks, self.acc = q, qm, kv, km, peaks, acc
        self.rows = q.shape[0]

    def clear(self):
        self.peaks[...] = jnp.full_like(self.peaks, NEGATIVE)
        self.acc[...] = jnp.zeros_like(self.acc)

    def group(self, owner, diagonal=False):
        size = self.rows
        at = pl.multiple_of(owner * size, size)
        there = pl.ds(at, size)
        half = left_half((QUERIES, 128))
        khalf = left_half((size, 128))
        one = jnp.ones((size, 128), jnp.bfloat16)
        k, v, km = self.kv[there, :128], self.kv[there, 128:], self.km[there, :]
        keys = (jnp.where(khalf, k, km), jnp.where(khalf, km, k))
        values = (jnp.where(khalf, v, one), jnp.where(khalf, one, v))

        def one_block(block, _):
            start = pl.multiple_of(block * QUERIES, QUERIES)
            here = pl.ds(start, QUERIES)
            q, qm = self.q[here, :], self.qm[here, :]
            queries = (jnp.where(half, q, qm), jnp.where(half, qm, q))
            scores = [dot(queries[h], keys[h], 1, 1) for h in (0, 1)]
            if diagonal and self.ranked:
                place = start + lax.broadcasted_iota(jnp.int32, (QUERIES, size), 0)
                other = lax.broadcasted_iota(jnp.int32, (QUERIES, size), 1)
                column = start + lax.broadcasted_iota(jnp.int32, (QUERIES, 1), 0)
                banned = jnp.where(openings(self.lens, self.base + column), -1, place) == other
                scores = [jnp.where(banned, HIDE, s) for s in scores]
            for h in (0, 1):
                peak = self.peaks[h, here, :]
                new = jnp.maximum(peak, jnp.max(scores[h], axis=1, keepdims=True))
                p = jnp.exp(scores[h] - new).astype(jnp.bfloat16)
                self.acc[h, here, :] = self.acc[h, here, :] * jnp.exp(peak - new) + dot(p, values[h], 1, 0)
                self.peaks[h, here, :] = new
            return 0

        lax.fori_loop(0, self.rows // QUERIES, one_block, 0)

    def aside(self, offset, grp, grp_count):
        for owner in (grp + offset, grp - offset):
            @pl.when(jnp.logical_and(owner >= 0, owner < grp_count))
            def _():
                self.group(owner)

    def end(self, o_ref, lse_ref):
        half = left_half((self.rows, 128))
        total = jnp.where(half, self.acc[1], self.acc[0])
        mixed = jnp.where(half, self.acc[0], self.acc[1])
        o_ref[...] = mixed / pltpu.roll(total, 64, 1)
        lse_ref[...] = jnp.where(half, self.peaks[1], self.peaks[0]) + jnp.log(total)


def front_kernel(grp_count, wa_count, reach, count, vec_at, lens_ref, ranks_ref, limits_ref, content_ref, query_ref,
                 encoder_ref, *refs):
    refs = list(refs)
    take = lambda n: [refs.pop(0) for _ in range(n)]
    vecs, shards, wide_shards = take(len(vec_at)), take(count), take(2)
    fulls, wide_fulls = take(count), take(2)
    vec_out, q_out, q2_out, kv_out, kv2_out = take(5)
    mark_outs = take(4)
    o_out, lse_out, o2_out, lse2_out, hidden_ref, normed_ref, inverse_ref, mixed_ref = take(8)
    marks, (vec_ref, held, vec_all, kvbuf, kvbuf2, qbuf, qbuf2, sendbuf, mixbuf) = take(4), take(9)
    kv_all, kv2_all, q_all, q2_all, peaks, acc, stage_a, stage_b = take(8)
    row_sems, wide_sems, vec_sems, line_sems, swap_sems, out_sems, last_sems = refs
    grp, pln, wa = lax.axis_index("grp"), lax.axis_index("pln"), lax.axis_index("wa")
    tok = content_ref.shape[0]
    base = grp * PLANE * tok
    gathers = [Rows(shards[i], held.at[i], row_sems, i, wa_count) for i in range(count)]
    wide = [Rows(wide_shards[0], wide_fulls[0], wide_sems, 0, wa_count, stage_a),
            Rows(wide_shards[1], wide_fulls[1], wide_sems, 1, wa_count, stage_b)]
    pack_vectors(vecs, vec_ref)
    greet(grp_count, wa_count)
    vec_keep = pltpu.make_async_copy(vec_ref, vec_all.at[wa], vec_sems.at[0, 0])
    vec_keep.start()
    pushes = [remote(vec_ref, vec_all.at[wa], vec_sems.at[0, o], vec_sems.at[1, o], {"wa": lax.rem(wa + o, wa_count)})
              for o in range(1, wa_count)]
    for g in gathers[:2]:
        g.begin()
    for p in pushes:
        p.start()
    for g in gathers[:2]:
        g.pass_on()
    for g in gathers[2:5]:
        g.begin()
    vec_keep.wait()
    for p in pushes:
        p.wait_recv()
    for g in gathers[:2]:
        g.arrived()
    row = lambda i: vector_row(vec_all, wa_count, *vec_at[i])
    content = content_ref[...]
    split_pairs(matmul(content, held[0]).astype(jnp.bfloat16), kvbuf, 0)
    split_pairs((matmul(content, held[1]) + row(1)).astype(jnp.bfloat16), kvbuf, 128)
    line = Line(kv_all, line_sems.at[0], grp_count, reach, tok)
    spot = lambda ref: lambda p: ref.at[pl.ds(pl.multiple_of((grp * PLANE + p) * tok, 16), tok)]
    flat = lambda ref: lambda p: ref.at[pl.ds(pl.multiple_of(p * tok, 16), tok)]
    swap = Swap(lambda p: kvbuf.at[p], spot(kv_all), swap_sems.at[0])
    swap.begin()
    line.send(1, pln, kvbuf.at[pln])
    swap.arrived(1)
    line.send(1, across(pln, 1))
    for g in gathers[2:5]:
        g.pass_on()
    for g in gathers[5:]:
        g.begin()
    for offset in (2, 3):
        swap.arrived(offset)
        line.send(1, across(pln, offset))
    for g in gathers[2:5]:
        g.arrived()
    outs = [pltpu.make_async_copy(held.at[i], fulls[i], out_sems.at[i]) for i in range(count)]
    for o in outs[:5]:
        o.start()
    saves = [pltpu.make_async_copy(vec_all, vec_out, out_sems.at[count])]
    saves[0].start()
    query = (matmul(query_ref[...], held[2]) + row(0)).astype(jnp.bfloat16) * 0.125
    for pair in range(PLANE):
        qbuf[pair] = query[:, pair * 128 : pair * 128 + 128]
    swap_q = Swap(lambda p: qbuf.at[p], flat(q_all), swap_sems.at[1])
    swap_q.begin()
    encoder = encoder_ref[...]
    split_pairs(matmul(encoder, held[3]).astype(jnp.bfloat16), kvbuf2, 0)
    split_pairs((matmul(encoder, held[4]) + row(2)).astype(jnp.bfloat16), kvbuf2, 128)
    swap_2 = Swap(lambda p: kvbuf2.at[p], spot(kv2_all), swap_sems.at[2])
    swap_2.begin()
    make_marks(lens_ref, ranks_ref, limits_ref, base, *marks)
    mark_saves = [pltpu.make_async_copy(m, o, out_sems.at[count + 1 + i]) for i, (m, o) in enumerate(zip(marks, mark_outs))]
    for m in mark_saves:
        m.start()
    look = Looking(True, lens_ref, q_all, marks[2], kv_all, marks[0], peaks, acc, base)
    look.clear()
    swap.arrived(0)
    for offset in range(4):
        swap_q.arrived(offset)
    look.group(grp, True)
    line.forward(1)
    for g in gathers[5:]:
        g.pass_on()
    for w in wide:
        w.begin()
    line_2 = Line(kv2_all, line_sems.at[1], grp_count, reach, tok)
    for offset in range(4):
        swap_2.arrived(offset)
    for block in range(PLANE):
        line_2.send(1, block)
    look.aside(1, grp, grp_count)
    for w in wide:
        w.staged()
    for step in range(2, reach + 1):
        line.forward(step)
        look.aside(step, grp, grp_count)
    look.end(o_out, lse_out)
    for p in range(PLANE):
        sendbuf[p] = o_out[p * tok : p * tok + tok, :].astype(jnp.bfloat16)
    swap_o = Swap(lambda p: sendbuf.at[p], lambda p: mixbuf.at[p], swap_sems.at[3])
    swap_o.begin()
    more = [pltpu.make_async_copy(kv_all, kv_out, last_sems.at[0]), pltpu.make_async_copy(q_all, q_out, last_sems.at[1])]
    for m in more:
        m.start()
    for g in gathers[5:]:
        g.arrived()
    for o in outs[5:]:
        o.start()
    for offset in range(4):
        swap_o.arrived(offset)
    mixed = flat_pairs(mixbuf)
    mixed_ref[...] = mixed
    value = query_ref[...].astype(jnp.float32) + matmul(mixed, held[5]) + row(3)
    hidden, normed, inverse = norm_forward(value, row(4), row(5))
    query = (matmul(hidden.astype(jnp.bfloat16), held[6]) + row(6)).astype(jnp.bfloat16) * 0.125
    for pair in range(PLANE):
        qbuf2[pair] = query[:, pair * 128 : pair * 128 + 128]
    swap_q2 = Swap(lambda p: qbuf2.at[p], flat(q2_all), swap_sems.at[4])
    swap_q2.begin()
    hidden_ref[...] = hidden
    normed_ref[...] = normed
    inverse_ref[...] = jnp.broadcast_to(inverse, inverse_ref.shape)
    line_2.forward(1)
    look_2 = Looking(False, lens_ref, q2_all, marks[3], kv2_all, marks[1], peaks, acc, base)
    look_2.clear()
    for w in wide:
        w.pass_on()
    for offset in range(4):
        swap_q2.arrived(offset)
    more.append(pltpu.make_async_copy(q2_all, q2_out, last_sems.at[2]))
    more[-1].start()
    look_2.group(grp)
    look_2.aside(1, grp, grp_count)
    for step in range(2, reach + 1):
        line_2.forward(step)
        look_2.aside(step, grp, grp_count)
    more.append(pltpu.make_async_copy(kv2_all, kv2_out, last_sems.at[3]))
    more[-1].start()
    look_2.end(o2_out, lse2_out)
    for w in wide:
        w.arrived()
    for g in gathers + wide:
        g.finish()
    for p in pushes:
        p.wait_send()
    for c in outs + saves + mark_saves + more:
        c.wait()
    line.finish()
    line_2.finish()
    for s in (swap, swap_q, swap_2, swap_o, swap_q2):
        s.finish()


def run_front(grp_count, wa_count, lens, ranks, limits, content, query, encoder, vecs, mats, wide, vec_at):
    tok = content.shape[0]
    reach = min(grp_count - 1, (DOCLEN + PLANE * tok - 2) // (PLANE * tok))
    count = len(mats)
    low, full = jnp.bfloat16, jnp.float32
    shape = jax.ShapeDtypeStruct
    rows, keys = PLANE * tok, grp_count * PLANE * tok
    used = sum(length // min(128, length) for _, length in vec_at)
    pack = (used + -used % 16, 128)
    marks = [(keys, 128), (keys, 128), (rows, 128), (rows, 128)]
    out_shape = [shape((m.shape[0] * wa_count, m.shape[1]), low) for m in mats + wide]
    out_shape += [shape((wa_count,) + pack, full), shape((rows, 128), low), shape((rows, 128), low), shape((keys, 256), low),
                  shape((keys, 256), low)]
    out_shape += [shape(m, low) for m in marks]
    inner = [shape((rows, 128), full)] * 4 + [shape((tok, 512), full), shape((tok, 512), full), shape((tok, 128), full),
                                              shape((tok, 512), low)]
    pairs = pltpu.VMEM((PLANE, tok, 128), low)
    doubles = pltpu.VMEM((PLANE, tok, 256), low)
    return pl.pallas_call(
        functools.partial(front_kernel, grp_count, wa_count, reach, count, vec_at),
        out_shape=tuple(out_shape + inner),
        in_specs=[SMEM] + [VMEM] * (5 + len(vecs)) + [ANY] * (count + 2),
        out_specs=tuple([ANY] * len(out_shape) + [VMEM] * len(inner)),
        scratch_shapes=[pltpu.VMEM(m, low) for m in marks] + [
            pltpu.VMEM(pack, full), pltpu.VMEM((count, 512, 512), low), pltpu.VMEM((wa_count,) + pack, full),
            doubles, doubles, pairs, pairs, pairs, pairs,
            pltpu.VMEM((keys, 256), low), pltpu.VMEM((keys, 256), low), pltpu.VMEM((rows, 128), low),
            pltpu.VMEM((rows, 128), low), pltpu.VMEM((2, rows, 1), full), pltpu.VMEM((2, rows, 128), full),
            pltpu.VMEM(wide[0].shape, low), pltpu.VMEM(wide[1].shape, low),
            DMA((5, count, max(1, wa_count - 1))), DMA((5, 2, max(1, wa_count - 1))), DMA((2, wa_count)),
            DMA((2, 2, 2, reach, PLANE)), DMA((5, 2, 4)), DMA((count + 5,)), DMA((4,))],
        compiler_params=pltpu.CompilerParams(collective_id=1, has_side_effects=True, vmem_limit_bytes=60 << 20),
    )(lens, ranks, limits, content, query, encoder, *vecs, *mats, *wide)


class Fold:
    def __init__(self, partial, mine, sendbuf, getbuf, sems, load_sems, grp_count, reach, block):
        self.partial, self.mine, self.sendbuf, self.getbuf = partial, mine, sendbuf, getbuf
        self.sems, self.load_sems = sems, load_sems
        self.count, self.reach, self.block = grp_count, reach, block
        self.grp = lax.axis_index("grp")

    def toward(self, side):
        return 1 if side == 0 else -1

    def rows(self, owner, block):
        return pl.ds(pl.multiple_of((owner * PLANE + block) * self.block, 16), self.block)

    def part(self, block):
        return pl.ds(block * self.block, self.block)

    def sends(self, side, stage):
        return self.grp + stage < self.count if side == 0 else self.grp - stage >= 0

    def receives(self, side, stage):
        if side == 0:
            return jnp.logical_and(self.grp >= 1, self.grp - 1 + stage < self.count)
        return jnp.logical_and(self.grp + 1 < self.count, self.grp + 1 - stage >= 0)

    def copy(self, side, stage, block, back=False):
        source = self.sendbuf.at[side, stage - 1, self.part(block)]
        if stage == self.reach and not back:
            source = self.partial.at[self.rows(self.grp + self.toward(side) * stage, block)]
        peer = self.grp + (-self.toward(side) if back else self.toward(side))
        return remote(source, self.getbuf.at[side, stage - 1, self.part(block)], self.sems.at[0, side, stage - 1, block],
                      self.sems.at[1, side, stage - 1, block], {"grp": peer})

    def load(self, side, stage):
        size = PLANE * self.block
        rows = pl.ds(pl.multiple_of((self.grp + self.toward(side) * stage) * size, 16), size)
        return pltpu.make_async_copy(self.partial.at[rows], self.mine.at[side, stage - 1], self.load_sems.at[side, stage - 1])

    def begin(self):
        for block in range(PLANE):
            for side in (0, 1):
                @pl.when(self.sends(side, self.reach))
                def _():
                    self.copy(side, self.reach, block).start()
        for stage in range(1, self.reach):
            for side in (0, 1):
                @pl.when(self.sends(side, stage))
                def _():
                    self.load(side, stage).start()

    def grow(self, stage):
        for side in (0, 1):
            @pl.when(self.sends(side, stage))
            def _():
                self.load(side, stage).wait()
        for block in range(PLANE):
            part = self.part(block)
            for side in (0, 1):
                @pl.when(self.sends(side, stage))
                def _():
                    self.sendbuf[side, stage - 1, part, :] = self.mine[side, stage - 1, part, :]

                    @pl.when(self.receives(side, stage + 1))
                    def _():
                        self.copy(side, stage + 1, block, True).wait_recv()
                        total = self.mine[side, stage - 1, part, :].astype(jnp.float32)
                        total = total + self.getbuf[side, stage, part, :].astype(jnp.float32)
                        self.sendbuf[side, stage - 1, part, :] = total.astype(jnp.bfloat16)

                    self.copy(side, stage, block).start()

    def total(self, own, out):
        for block in range(PLANE):
            part = self.part(block)
            for side in (0, 1):
                @pl.when(self.receives(side, 1))
                def _():
                    self.copy(side, 1, block, True).wait_recv()
                    own[part, :] = own[part, :] + self.getbuf[side, 0, part, :].astype(jnp.float32)
            out[block] = own[part, :].astype(jnp.bfloat16)

    def finish(self):
        for stage in range(1, self.reach + 1):
            for block in range(PLANE):
                for side in (0, 1):
                    @pl.when(self.sends(side, stage))
                    def _():
                        self.copy(side, stage, block, True).wait_send()


def store_blocks(buffer, value):
    for c in range(PLANE):
        buffer[c] = value[:, c * 128 : c * 128 + 128].astype(jnp.bfloat16)


def halves(buffer):
    keys = jnp.concatenate([buffer[p, :, :128] for p in range(PLANE)], axis=1)
    values = jnp.concatenate([buffer[p, :, 128:] for p in range(PLANE)], axis=1)
    return keys, values


class Reduce:
    def __init__(self, index, source, parts, got, kept, sems, wa_count, place=None):
        self.index, self.source, self.sems, self.wa_count = index, source, sems, wa_count
        self.parts, (self.got_core, self.got_wa, self.got_row) = parts, got
        self.by_core, self.by_wa, self.by_row = kept
        self.place = index if place is None else place
        self.wa, self.pln = lax.axis_index("wa"), lax.axis_index("pln")
        self.core = lax.rem(self.pln, 2)
        self.row = self.pln // 2
        self.size = 512 // wa_count

    def core_copy(self, row):
        return remote(self.source.at[row * 2 + 1 - self.core], self.got_core.at[self.index, row],
                      self.sems.at[0, self.index, row], self.sems.at[1, self.index, row], {"pln": across(self.pln, 1)})

    def rows_of(self, wa):
        return pl.ds(pl.multiple_of(wa * self.size, 16), self.size)

    def wa_copy(self, offset):
        peer = lax.rem(self.wa + offset, self.wa_count)
        return remote(self.by_core.at[self.index, :, self.rows_of(peer)], self.got_wa.at[offset - 1, self.index],
                      self.sems.at[0, self.index, 1 + offset], self.sems.at[1, self.index, 1 + offset], {"wa": peer})

    def row_copy(self):
        return remote(self.by_wa.at[self.index, 1 - self.row], self.got_row.at[self.index],
                      self.sems.at[0, self.index, 1 + self.wa_count], self.sems.at[1, self.index, 1 + self.wa_count],
                      {"pln": across(self.pln, 2)})

    def begin(self):
        for row in (0, 1):
            self.core_copy(row).start()

    def after_core(self):
        for row in (0, 1):
            self.core_copy(row).wait_recv()
            mine = self.parts[row * 2 + self.core].astype(jnp.float32)
            total = mine + self.got_core[self.index, row].astype(jnp.float32)
            self.by_core[self.index, row] = total.astype(jnp.bfloat16)
        for offset in range(1, self.wa_count):
            self.wa_copy(offset).start()

    def after_wa(self):
        for offset in range(1, self.wa_count):
            self.wa_copy(offset).wait_recv()
        for row in (0, 1):
            total = self.by_core[self.index, row, self.rows_of(self.wa), :].astype(jnp.float32)
            for offset in range(1, self.wa_count):
                total = total + self.got_wa[offset - 1, self.index, row].astype(jnp.float32)
            self.by_wa[self.index, row] = total.astype(jnp.bfloat16)
        self.row_copy().start()

    def after_row(self):
        self.row_copy().wait_recv()
        total = self.by_wa[self.index, self.row].astype(jnp.float32) + self.got_row[self.index].astype(jnp.float32)
        self.by_row[self.place] = total.astype(jnp.bfloat16)

    def finish(self):
        for row in (0, 1):
            self.core_copy(row).wait_send()
        for offset in range(1, self.wa_count):
            self.wa_copy(offset).wait_send()
        self.row_copy().wait_send()


def turn_kernel(grp_count, wa_count, reach, vec_at, dq_ref, dkv_ref, own_ref, back_ref, normed_ref, inverse_ref, hidden_ref,
                mixed_one_ref, mixed_two_ref, branch_two_ref, encoder_ref, query_mat_ref, out_mat_ref, vec_ref, vg_ref, wide_ref,
                do_out, back_out, kv_out, grads_out, vg_out, wide_out,
                dqsend, dqget, dosend, doget, kvsend, kvget, total, mine, foldsend, foldget, grads, parts, got_core, got_wa,
                got_row, by_core, by_wa, by_row, fold_sems, load_sems, swap_sems, out_sems, part_sems, red_sems):
    tok = back_ref.shape[0]
    for p in range(PLANE):
        dqsend[p] = dq_ref[p * tok : p * tok + tok, :]
    wide = wide_ref.shape[0]
    loads = [pltpu.make_async_copy(wide_ref.at[i], parts.at[i], part_sems.at[i]) for i in range(wide)]
    for l in loads:
        l.start()
    greet(grp_count, wa_count)
    swap_dq = Swap(lambda p: dqsend.at[p], lambda p: dqget.at[p], swap_sems.at[0])
    swap_dq.begin()
    fold = Fold(dkv_ref, mine, foldsend, foldget, fold_sems, load_sems, grp_count, reach, tok)
    fold.begin()
    reds = [Reduce(i, wide_ref.at[i], parts.at[i], (got_core, got_wa, got_row), (by_core, by_wa, by_row), red_sems, wa_count)
            for i in range(wide)]
    for r in reds:
        r.begin()
    row = lambda i: vector_row(vec_ref, wa_count, *vec_at[i])
    vg_out[...] = vg_ref[...]
    saves = [pltpu.make_async_copy(grads.at[i], grads_out.at[i], out_sems.at[i]) for i in range(5)]
    total[...] = own_ref[...]
    store_blocks(grads.at[0], dot(mixed_two_ref[...], branch_two_ref[...], 0, 0))
    saves[0].start()
    for l in loads:
        l.wait()
    for r in reds:
        r.after_core()
    for offset in range(4):
        swap_dq.arrived(offset)
    dq = flat_pairs(dqget)
    incoming = back_ref[...] + dot(dq, query_mat_ref[...], 1, 1)
    back, gain_grad, shift_grad = norm_backward(incoming, normed_ref[...], inverse_ref[:, :1], row(4))
    back_out[...] = back
    branch = back.astype(jnp.bfloat16)
    do = dot(branch, out_mat_ref[...], 1, 1).astype(jnp.bfloat16)
    for p in range(PLANE):
        dosend[p] = do[:, p * 128 : p * 128 + 128]
    swap_do = Swap(lambda p: dosend.at[p], lambda p: doget.at[p], swap_sems.at[1])
    swap_do.begin()
    vg_out[10:11, :] = gain_grad.reshape(1, 512)
    vg_out[11:12, :] = shift_grad.reshape(1, 512)
    vg_out[12:13, :] = column_sum(branch).reshape(1, 512)
    vg_out[13:14, :] = column_sum(dq).reshape(1, 512)
    store_blocks(grads.at[1], dot(hidden_ref[...].astype(jnp.bfloat16), dq, 0, 0))
    saves[1].start()
    store_blocks(grads.at[2], dot(mixed_one_ref[...], branch, 0, 0))
    saves[2].start()
    for stage in range(reach - 1, 0, -1):
        fold.grow(stage)
    for offset in range(4):
        swap_do.arrived(offset)
    for p in range(PLANE):
        do_out[p * tok : p * tok + tok, :] = doget[p]
    for r in reds:
        r.after_wa()
    fold.total(total, kvsend)
    swap_kv = Swap(lambda p: kvsend.at[p], lambda p: kvget.at[p], swap_sems.at[2])
    swap_kv.begin()
    for offset in range(4):
        swap_kv.arrived(offset)
    keys, values = halves(kvget)
    kv_out[:, :512] = keys
    kv_out[:, 512:] = values
    encoder = encoder_ref[...]
    store_blocks(grads.at[3], dot(encoder, keys, 0, 0))
    saves[3].start()
    store_blocks(grads.at[4], dot(encoder, values, 0, 0))
    saves[4].start()
    vg_out[14:15, :] = column_sum(values).reshape(1, 512)
    for r in reds:
        r.after_row()
    wide_save = pltpu.make_async_copy(by_row, wide_out, part_sems.at[0])
    wide_save.start()
    for s in saves:
        s.wait()
    for r in reds:
        r.finish()
    wide_save.wait()
    fold.finish()
    for s in (swap_dq, swap_do, swap_kv):
        s.finish()


def fold_scratch(tok, reach):
    low = jnp.bfloat16
    size = PLANE * tok
    return [pltpu.VMEM((PLANE, tok, 256), low), pltpu.VMEM((PLANE, tok, 256), low), pltpu.VMEM((size, 256), jnp.float32),
            pltpu.VMEM((2, max(1, reach - 1), size, 256), low), pltpu.VMEM((2, reach, size, 256), low),
            pltpu.VMEM((2, reach, size, 256), low)]


def run_turn(grp_count, wa_count, vec_at, dq, dkv, own, back, normed, inverse, hidden, mixed_one, mixed_two, branch_two,
             encoder, query_mat, out_mat, vecs, vg, wide):
    tok = back.shape[0]
    reach = min(grp_count - 1, (DOCLEN + PLANE * tok - 2) // (PLANE * tok))
    low, full = jnp.bfloat16, jnp.float32
    shape = jax.ShapeDtypeStruct
    pairs = pltpu.VMEM((PLANE, tok, 128), low)
    count, size = wide.shape[0], 512 // wa_count
    return pl.pallas_call(
        functools.partial(turn_kernel, grp_count, wa_count, reach, vec_at),
        out_shape=(shape((PLANE * tok, 128), low), shape((tok, 512), full), shape((tok, 1024), low),
                   shape((5, PLANE, 512, 128), low), shape(vg.shape, full), shape((count, size, 128), low)),
        in_specs=[VMEM, ANY] + [VMEM] * 13 + [ANY],
        out_specs=(VMEM, VMEM, VMEM, ANY, VMEM, ANY),
        scratch_shapes=[pairs] * 4 + fold_scratch(tok, reach) + [
            pltpu.VMEM((5, PLANE, 512, 128), low), pltpu.VMEM((count, PLANE, 512, 128), low),
            pltpu.VMEM((count, 2, 512, 128), low), pltpu.VMEM((max(1, wa_count - 1), count, 2, size, 128), low),
            pltpu.VMEM((count, size, 128), low), pltpu.VMEM((count, 2, 512, 128), low), pltpu.VMEM((count, 2, size, 128), low),
            pltpu.VMEM((count, size, 128), low), DMA((2, 2, reach, PLANE)), DMA((2, max(1, reach - 1))), DMA((3, 2, 4)),
            DMA((5,)), DMA((count,)), DMA((2, count, wa_count + 2))],
        cost_estimate=pl.CostEstimate(flops=32000000000, bytes_accessed=0, transcendentals=0),
        compiler_params=pltpu.CompilerParams(collective_id=8, has_side_effects=True, vmem_limit_bytes=60 << 20),
    )(dq, dkv, own, back, normed, inverse, hidden, mixed_one, mixed_two, branch_two, encoder, query_mat, out_mat, vecs, vg,
      wide)


def greet_all(grp_count, wa_count):
    barrier = pltpu.get_barrier_semaphore()
    grp, pln, wa = lax.axis_index("grp"), lax.axis_index("pln"), lax.axis_index("wa")
    peers = [{"pln": across(pln, o)} for o in (1, 2, 3)]
    peers += [{"wa": lax.rem(wa + o, wa_count)} for o in range(1, wa_count)]
    peers += [{"grp": lax.rem(grp + o, grp_count)} for o in range(1, grp_count)]
    for where in peers:
        pl.semaphore_signal(barrier, inc=1, device_id=where, device_id_type=MESH)
    pl.semaphore_wait(barrier, len(peers))


def closing_kernel(grp_count, wa_count, reach, count, dq_ref, dkv_ref, own_ref, query_ref, content_ref, early_ref, wide_ref, vg_ref,
                   dq_out, kv_out, out_ref, vg_out,
                   dqsend, dqget, kvsend, kvget, total, mine, foldsend, foldget, parts, got_core, got_wa, got_row,
                   by_core, by_wa, by_row, got_grp, final, vsum, vgot, vall,
                   fold_sems, load_sems, swap_sems, part_sems, wide_sem, red_sems, vec_sems, grp_sems, share_sems):
    grp, pln, wa = lax.axis_index("grp"), lax.axis_index("pln"), lax.axis_index("wa")
    tok = query_ref.shape[0]
    early = early_ref.shape[0]
    wide = wide_ref.shape[0]
    sets = ((0, wide), (wide, early + 1), (wide + early + 1, count - early - 1))
    size = 512 // wa_count
    slab = size // grp_count
    for p in range(PLANE):
        dqsend[p] = dq_ref[p * tok : p * tok + tok, :]
    greet_all(grp_count, wa_count)
    swap_dq = Swap(lambda p: dqsend.at[p], lambda p: dqget.at[p], swap_sems.at[0])
    swap_dq.begin()
    fold = Fold(dkv_ref, mine, foldsend, foldget, fold_sems, load_sems, grp_count, reach, tok)
    fold.begin()
    loads = [pltpu.make_async_copy(early_ref.at[i], parts.at[i], part_sems.at[i]) for i in range(early)]
    for l in loads:
        l.start()
    wide_load = pltpu.make_async_copy(wide_ref, by_row.at[pl.ds(0, wide)], wide_sem)
    wide_load.start()
    got, kept = (got_core, got_wa, got_row), (by_core, by_wa, by_row)
    reds = [Reduce(i, early_ref.at[i] if i < early else parts.at[i], parts.at[i], got, kept, red_sems, wa_count,
                   wide + i) for i in range(count)]
    for r in reds[:early]:
        r.begin()
    total[...] = own_ref[...]
    vsum[0] = vg_ref[...]
    for offset in range(4):
        swap_dq.arrived(offset)
    dq = flat_pairs(dqget)
    dq_out[...] = dq
    store_blocks(parts.at[early], dot(query_ref[...], dq, 0, 0))
    vsum[0, 15:16, :] = column_sum(dq).reshape(1, 512)
    reds[early].begin()
    for l in loads:
        l.wait()
    for r in reds[: early + 1]:
        r.after_core()
    for stage in range(reach - 1, 0, -1):
        fold.grow(stage)
    wide_load.wait()

    def grp_copy(set_at, offset):
        start, length = sets[set_at]
        peer = lax.rem(grp + offset, grp_count)
        some = pl.ds(start, length)
        rows = pl.ds(pl.multiple_of(peer * slab, 8), slab)
        return remote(by_row.at[some, rows], got_grp.at[offset - 1, some], grp_sems.at[0, set_at, offset - 1],
                      grp_sems.at[1, set_at, offset - 1], {"grp": peer})

    offsets = range(1, grp_count)
    for o in offsets:
        grp_copy(0, o).start()
    for r in reds[: early + 1]:
        r.after_wa()
    fold.total(total, kvsend)
    swap_kv = Swap(lambda p: kvsend.at[p], lambda p: kvget.at[p], swap_sems.at[1])
    swap_kv.begin()
    for r in reds[: early + 1]:
        r.after_row()
    for o in offsets:
        grp_copy(1, o).start()
    for offset in range(4):
        swap_kv.arrived(offset)
    keys, values = halves(kvget)
    content = content_ref[...]
    store_blocks(parts.at[early + 1], dot(content, keys, 0, 0))
    reds[early + 1].begin()
    store_blocks(parts.at[early + 2], dot(content, values, 0, 0))
    reds[early + 2].begin()
    vsum[0, 16:17, :] = column_sum(values).reshape(1, 512)
    vec_core = remote(vsum.at[0], vgot.at[0], vec_sems.at[0, 0], vec_sems.at[1, 0], {"pln": across(pln, 1)})
    vec_core.start()
    kv_out[:, :512] = keys
    kv_out[:, 512:] = values

    for r in reds[early + 1 :]:
        r.after_core()
    vec_core.wait_recv()
    vsum[1] = vsum[0] + vgot[0]
    vec_wa = [remote(vsum.at[1], vgot.at[o], vec_sems.at[0, o], vec_sems.at[1, o], {"wa": lax.rem(wa + o, wa_count)})
              for o in range(1, wa_count)]
    for v in vec_wa:
        v.start()
    for r in reds[early + 1 :]:
        r.after_wa()
    for v in vec_wa:
        v.wait_recv()
    vall[wa] = vsum[1]
    for o in range(1, wa_count):
        vall[lax.rem(wa + wa_count - o, wa_count)] = vgot[o]
    joined = vall[0]
    for o in range(1, wa_count):
        joined = joined + vall[o]
    vsum[2] = joined
    vec_row = remote(vsum.at[2], vgot.at[wa_count], vec_sems.at[0, wa_count], vec_sems.at[1, wa_count],
                     {"pln": across(pln, 2)})
    vec_row.start()
    own_rows = pl.ds(pl.multiple_of(grp * slab, 8), slab)

    def settle(set_at):
        start, length = sets[set_at]
        some = pl.ds(start, length)
        for o in offsets:
            grp_copy(set_at, o).wait_recv()
        value = by_row[some, own_rows, :].astype(jnp.float32)
        for o in offsets:
            value = value + got_grp[o - 1, some].astype(jnp.float32)
        final[some] = value.astype(jnp.bfloat16)

    def spot(column, source, some):
        return out_ref.at[column, some, pl.ds(pl.multiple_of(source * slab, 8), slab)]

    def spread(set_at, offset):
        start, length = sets[set_at]
        some = pl.ds(start, length)
        return remote(final.at[some], spot(pln, grp, some), share_sems.at[0, set_at, 0, offset],
                      share_sems.at[1, set_at, 0, offset], {"grp": lax.rem(grp + offset, grp_count)})

    def keep(set_at):
        start, length = sets[set_at]
        some = pl.ds(start, length)
        return pltpu.make_async_copy(final.at[some], spot(pln, grp, some), share_sems.at[0, set_at, 0, 0])

    def give(set_at, kind, offset):
        start, length = sets[set_at]
        some = pl.ds(start, length)
        source = lax.rem(grp + grp_count - offset, grp_count)
        column = pln if kind < 3 else across(pln, 2)
        there = spot(column, source, some)
        return remote(there, there, share_sems.at[0, set_at, kind, offset], share_sems.at[1, set_at, kind, offset],
                      {"pln": across(pln, 2 if kind == 1 else 1)})

    def share(set_at):
        settle(set_at)
        keep(set_at).start()
        for o in offsets:
            spread(set_at, o).start()

    share(0)
    share(1)
    for r in reds[early + 1 :]:
        r.after_row()
    for o in offsets:
        grp_copy(2, o).start()
    vec_row.wait_recv()
    vsum[3] = vsum[2] + vgot[wa_count]
    vec_grp = [remote(vsum.at[3], vall.at[wa_count + o], vec_sems.at[0, wa_count + o], vec_sems.at[1, wa_count + o],
                      {"grp": lax.rem(grp + o, grp_count)}) for o in offsets]
    for v in vec_grp:
        v.start()
    everyone = range(grp_count)

    def hand_out(set_at, offset):
        if offset == 0:
            keep(set_at).wait()
        else:
            spread(set_at, offset).wait_recv()
        give(set_at, 1, offset).start()
        give(set_at, 2, offset).start()

    def cross_over(set_at):
        for o in everyone:
            give(set_at, 1, o).wait_recv()
            give(set_at, 3, o).start()

    for o in everyone:
        hand_out(0, o)
    for o in everyone:
        hand_out(1, o)
    share(2)
    cross_over(0)
    cross_over(1)
    for o in everyone:
        hand_out(2, o)
    for v in vec_grp:
        v.wait_recv()
    ordered = jnp.zeros_like(vsum[3])
    for g in everyone:
        piece = jnp.where(grp == g, vsum[3], 0.0)
        for o in offsets:
            piece = piece + jnp.where(lax.rem(grp + grp_count - o, grp_count) == g, vall[wa_count + o], 0.0)
        ordered = ordered + piece
    vg_out[...] = ordered
    cross_over(2)
    for set_at in range(3):
        for o in everyone:
            give(set_at, 2, o).wait_recv()
            give(set_at, 3, o).wait_recv()
    for set_at in range(3):
        for o in everyone:
            for kind in (1, 2, 3):
                give(set_at, kind, o).wait_send()
        for o in offsets:
            spread(set_at, o).wait_send()
            grp_copy(set_at, o).wait_send()
    for v in [vec_core, vec_row] + vec_wa + vec_grp:
        v.wait_send()
    for r in reds:
        r.finish()
    fold.finish()
    swap_dq.finish()
    swap_kv.finish()


def run_closing(grp_count, wa_count, dq, dkv, own, query, content, early, wide, vg):
    tok = query.shape[0]
    count = early.shape[0] + 3
    every = count + wide.shape[0]
    reach = min(grp_count - 1, (DOCLEN + PLANE * tok - 2) // (PLANE * tok))
    size = 512 // wa_count
    slab = size // grp_count
    low, full = jnp.bfloat16, jnp.float32
    shape = jax.ShapeDtypeStruct
    pairs = pltpu.VMEM((PLANE, tok, 128), low)
    steps = wa_count + 2
    return pl.pallas_call(
        functools.partial(closing_kernel, grp_count, wa_count, reach, count),
        out_shape=(shape((tok, 512), low), shape((tok, 1024), low), shape((PLANE, every, size, 128), low),
                   shape(vg.shape, full)),
        in_specs=[VMEM, ANY, VMEM, VMEM, VMEM, ANY, ANY, VMEM],
        out_specs=(VMEM, VMEM, ANY, VMEM),
        scratch_shapes=[pairs] * 2 + fold_scratch(tok, reach) + [
            pltpu.VMEM((count, PLANE, 512, 128), low), pltpu.VMEM((count, 2, 512, 128), low),
            pltpu.VMEM((max(1, wa_count - 1), count, 2, size, 128), low), pltpu.VMEM((count, size, 128), low),
            pltpu.VMEM((count, 2, 512, 128), low), pltpu.VMEM((count, 2, size, 128), low), pltpu.VMEM((every, size, 128), low),
            pltpu.VMEM((grp_count - 1, every, slab, 128), low), pltpu.VMEM((every, slab, 128), low),
            pltpu.VMEM((4,) + vg.shape, full), pltpu.VMEM((wa_count + 1,) + vg.shape, full),
            pltpu.VMEM((wa_count + grp_count,) + vg.shape, full),
            DMA((2, 2, reach, PLANE)), DMA((2, max(1, reach - 1))), DMA((2, 2, 4)), DMA((early.shape[0],)), DMA,
            DMA((2, count, steps)), DMA((2, wa_count + grp_count)), DMA((2, 3, grp_count - 1)), DMA((2, 3, 4, grp_count))],
        cost_estimate=pl.CostEstimate(flops=75000000000, bytes_accessed=0, transcendentals=0),
        compiler_params=pltpu.CompilerParams(collective_id=9, has_side_effects=True, vmem_limit_bytes=60 << 20),
    )(dq, dkv, own, query, content, early, wide, vg)


def centre_kernel(wa_count, vec_at, attended_ref, hidden_ref, cotangent_ref, out_mat_ref, expand_ref, shrink_ref, vec_ref,
                  layer_out, mixed_out, back_out, branch_out, do_out, grads_out, vg_out,
                  sendbuf, getbuf, dosend, doget, slopes, actives, grads, swap_sems, out_sems):
    tok = hidden_ref.shape[0]
    for p in range(PLANE):
        sendbuf[p] = attended_ref[p * tok : p * tok + tok, :].astype(jnp.bfloat16)
    greet(1, 1, groups=False, rows=False)
    swap = Swap(lambda p: sendbuf.at[p], lambda p: getbuf.at[p], swap_sems.at[0])
    swap.begin()
    row = lambda i: vector_row(vec_ref, wa_count, *vec_at[i])
    vg_out[...] = jnp.zeros_like(vg_out)
    for offset in range(4):
        swap.arrived(offset)
    mixed = flat_pairs(getbuf)
    mixed_out[...] = mixed
    value = hidden_ref[...] + matmul(mixed, out_mat_ref[...]) + row(7)
    hidden, normed_two, inverse_two = norm_forward(value, row(8), row(9))
    low = hidden.astype(jnp.bfloat16)
    expand_row = row(10)
    total = hidden + row(11)
    width = 512
    chunks = expand_ref.shape[1] // width
    for c in range(chunks):
        span = slice(c * width, c * width + width)
        u = matmul(low, expand_ref[:, span]) + expand_row[:, span]
        cumulative = 0.5 * (1.0 + lax.erf(u * ROOT_HALF))
        active = (u * cumulative).astype(jnp.bfloat16)
        actives[:, span] = active
        slopes[:, span] = cumulative + u * jnp.exp(-0.5 * u * u) * INV_ROOT_TWO_PI
        total = total + matmul(active, shrink_ref[span, :])
    out, normed_three, inverse_three = norm_forward(total, row(12), row(13))
    layer_out[...] = out
    cotangent = cotangent_ref[...].astype(jnp.float32)
    back, gain_grad, shift_grad = norm_backward(cotangent, normed_three, inverse_three, row(12))
    vg_out[0:1, :] = gain_grad.reshape(1, 512)
    vg_out[1:2, :] = shift_grad.reshape(1, 512)
    grad = back.astype(jnp.bfloat16)
    vg_out[2:3, :] = column_sum(grad).reshape(1, 512)
    incoming = back
    steps = []
    for c in range(chunks):
        span = slice(c * width, c * width + width)
        du = (dot(grad, shrink_ref[span, :], 1, 1) * slopes[:, span]).astype(jnp.bfloat16)
        vg_out[3 + c : 4 + c, :] = column_sum(du).reshape(1, 512)
        incoming = incoming + dot(du, expand_ref[:, span], 1, 1)
        steps.append(du)
    back, gain_grad, shift_grad = norm_backward(incoming, normed_two, inverse_two, row(8))
    back_out[...] = back
    branch = back.astype(jnp.bfloat16)
    branch_out[...] = branch
    do = dot(branch, out_mat_ref[...], 1, 1).astype(jnp.bfloat16)
    for p in range(PLANE):
        dosend[p] = do[:, p * 128 : p * 128 + 128]
    swap_do = Swap(lambda p: dosend.at[p], lambda p: doget.at[p], swap_sems.at[1])
    swap_do.begin()
    vg_out[7:8, :] = gain_grad.reshape(1, 512)
    vg_out[8:9, :] = shift_grad.reshape(1, 512)
    vg_out[9:10, :] = column_sum(branch).reshape(1, 512)
    size = 512 // wa_count
    saves = [pltpu.make_async_copy(grads.at[i], grads_out.at[i], out_sems.at[i]) for i in range(2 * chunks)]
    for c in range(chunks):
        span = slice(c * width, c * width + width)
        store_blocks(grads.at[c], dot(low, steps[c], 0, 0))
        saves[c].start()
        value = dot(actives[:, span], grad, 0, 0).astype(jnp.bfloat16)
        for piece in range(width // size):
            owner, index = divmod(c * (width // size) + piece, chunks)
            for column in range(PLANE):
                grads[chunks + index, column, owner * size : owner * size + size, :] = value[
                    piece * size : piece * size + size, column * 128 : column * 128 + 128]
    for c in range(chunks):
        saves[chunks + c].start()
    for offset in range(4):
        swap_do.arrived(offset)
    for p in range(PLANE):
        do_out[p * tok : p * tok + tok, :] = doget[p]
    for save in saves:
        save.wait()
    swap.finish()
    swap_do.finish()


def run_centre(wa_count, vec_at, attended, hidden, cotangent, out_mat, expand, shrink, vecs):
    tok = hidden.shape[0]
    low, full = jnp.bfloat16, jnp.float32
    shape = jax.ShapeDtypeStruct
    pairs = pltpu.VMEM((PLANE, tok, 128), low)
    wide = expand.shape[1]
    return pl.pallas_call(
        functools.partial(centre_kernel, wa_count, vec_at),
        out_shape=(shape((tok, 512), full), shape((tok, 512), low), shape((tok, 512), full), shape((tok, 512), low),
                   shape((PLANE * tok, 128), low), shape((2 * wide // 512, PLANE, 512, 128), low), shape((24, 512), full)),
        in_specs=[VMEM] * 7,
        out_specs=(VMEM,) * 5 + (ANY, VMEM),
        scratch_shapes=[pairs] * 4 + [pltpu.VMEM((tok, wide), full), pltpu.VMEM((tok, wide), low),
            pltpu.VMEM((2 * wide // 512, PLANE, 512, 128), low), DMA((2, 2, 4)), DMA((2 * wide // 512,))],
        compiler_params=pltpu.CompilerParams(collective_id=3, has_side_effects=True, vmem_limit_bytes=60 << 20),
    )(attended, hidden, cotangent, out_mat, expand, shrink, vecs)


def last_kernel(wa_count, shares, at_ref, late_ref, sums_ref, dq_ref, dkv_ref, back_ref, query_mat, key_mat, value_mat,
                query_out, content_out, expand_out, shrink_out, *outs):
    wide = expand_out.shape[1] // 512
    size = late_ref.shape[2]
    count = late_ref.shape[1] - 2 * wide
    for c in range(PLANE):
        span = slice(c * 128, c * 128 + 128)
        for i in range(count):
            outs[i][:, span] = late_ref[c, 2 * wide + i].astype(jnp.float32)
        for i in range(wide):
            expand_out[:, i * 512 + c * 128 : i * 512 + c * 128 + 128] = late_ref[c, i].astype(jnp.float32)
            shrink_out[i * size : i * size + size, span] = late_ref[c, wide + i].astype(jnp.float32)
    query_out[...] = back_ref[...] + dot(dq_ref[...], query_mat[...], 1, 1)
    content_out[...] = dot(dkv_ref[:, :512], key_mat[...], 1, 1) + dot(dkv_ref[:, 512:], value_mat[...], 1, 1)
    at = 0
    for i, share in enumerate(shares):
        used = share * wa_count // 512
        line = jnp.concatenate([sums_ref[at + r : at + r + 1, :] for r in range(used)], axis=1)
        at += used
        mine = line[:, :share]
        for w in range(1, wa_count):
            mine = jnp.where(at_ref[0] == w, line[:, w * share : w * share + share], mine)
        outs[count + i][...] = mine.reshape(share)


def run_last(wa_count, wide, shares, at, late, sums, dq, dkv, back, query_mat, key_mat, value_mat):
    full = jnp.float32
    shape = jax.ShapeDtypeStruct
    tok = dq.shape[0]
    out_shape = [shape((tok, 512), full), shape((tok, 512), full), shape((late.shape[2], wide), full),
                 shape((wide // wa_count, 512), full)]
    out_shape += [shape((late.shape[2], 512), full)] * (late.shape[1] - wide // 256) + [shape((s,), full) for s in shares]
    return pl.pallas_call(
        functools.partial(last_kernel, wa_count, shares),
        out_shape=tuple(out_shape),
        in_specs=[SMEM] + [VMEM] * 8,
        out_specs=tuple([VMEM] * len(out_shape)),
        compiler_params=pltpu.CompilerParams(vmem_limit_bytes=60 << 20),
    )(at, late, sums, dq, dkv, back, query_mat, key_mat, value_mat)


def shards(
    query_in,
    content_in,
    encoder_in,
    out_grad,
    document_lengths,
    key_ranks,
    query_limits,
    self_query_weight,
    self_query_bias,
    self_key_weight,
    self_value_weight,
    self_value_bias,
    self_out_weight,
    self_out_bias,
    norm_one_gain,
    norm_one_shift,
    cross_query_weight,
    cross_query_bias,
    cross_key_weight,
    cross_value_weight,
    cross_value_bias,
    cross_out_weight,
    cross_out_bias,
    norm_two_gain,
    norm_two_shift,
    expand_weight,
    expand_bias,
    shrink_weight,
    shrink_bias,
    norm_three_gain,
    norm_three_shift,
):
    grp_count = lax.axis_size("grp")
    own = lax.axis_index("grp")[None].astype(jnp.int32)
    lens = document_lengths


    wa_count = lax.axis_size("wa")
    vectors = (self_query_bias, self_value_bias, cross_value_bias, self_out_bias, norm_one_gain, norm_one_shift,
        cross_query_bias, cross_out_bias, norm_two_gain, norm_two_shift, expand_bias, shrink_bias, norm_three_gain,
        norm_three_shift)
    vec_at, at = [], 0
    for v in vectors:
        vec_at.append((at, v.shape[0]))
        at += v.shape[0] // min(128, v.shape[0])
    vec_at = tuple(vec_at)
    mats = (self_key_weight, self_value_weight, self_query_weight, cross_key_weight, cross_value_weight, self_out_weight,
        cross_query_weight, cross_out_weight)
    (self_key_matrix, self_value_mat, self_query_mat, cross_key_matrix, cross_value_mat, self_out_mat, cross_query_mat,
        cross_out_mat, expand_mat, shrink_mat, vec_all, pair_one, pair_two, kv_one, kv_two, self_keys, cross_keys, self_marks,
        cross_marks, attended_one, total_one, attended_two, total_two, hidden_one, normed_one, inverse_one, mixed_one) = \
        run_front(grp_count, wa_count, lens, key_ranks, query_limits, content_in[0], query_in[0], encoder_in[0], vectors,
            mats, (expand_weight, shrink_weight), vec_at)
    source = query_in[0]
    content_states = content_in[0]
    encoder_output = encoder_in[0]
    layer_out, mixed_two, back_two, branch_two, do_two, wide, lines = run_centre(
        wa_count, vec_at, attended_two, hidden_one, out_grad[0], cross_out_mat, expand_mat, shrink_mat, vec_all)
    dq_two, dkv_two, own_two = attend_backward(False, lens, own, pair_two, cross_marks, kv_two, cross_keys,
        attended_two, total_two, do_two)
    do_one, back_one, kv_two_grad, early, lines, wide = run_turn(grp_count, wa_count, vec_at, dq_two, dkv_two, own_two, back_two,
        normed_one, inverse_one, hidden_one, mixed_one, mixed_two, branch_two, encoder_output, cross_query_mat, self_out_mat,
        vec_all, lines, wide)
    key_two_low, value_two_low = kv_two_grad[:, :512], kv_two_grad[:, 512:]
    encoder_grad = right_product(key_two_low, cross_key_matrix) + right_product(value_two_low, cross_value_mat)
    dq_one, dkv_one, own_one = attend_backward(True, lens, own, pair_one, self_marks, kv_one, self_keys,
        attended_one, total_one, do_one)
    query_one_low, kv_one_grad, late, sums = run_closing(grp_count, wa_count, dq_one, dkv_one, own_one, source,
        content_states, early, wide, lines)
    shares = tuple(v.shape[0] for v in (norm_three_gain, norm_three_shift, shrink_bias, expand_bias, norm_two_gain,
        norm_two_shift, cross_out_bias, norm_one_gain, norm_one_shift, self_out_bias, cross_query_bias, cross_value_bias,
        self_query_bias, self_value_bias))
    query_grad, content_grad, expand_grad, shrink_grad, *rest = run_last(wa_count, expand_weight.shape[1], shares,
        lax.axis_index("wa")[None].astype(jnp.int32), late, sums, query_one_low, kv_one_grad, back_one, self_query_mat,
        self_key_matrix, self_value_mat)
    names = ("cross_out", "cross_query", "self_out", "cross_key", "cross_value", "self_query", "self_key", "self_value")
    mat = dict(zip(names, rest))
    names = ("gain_three", "shift_three", "shrink", "expand", "gain_two", "shift_two", "cross_out", "gain_one", "shift_one",
        "self_out", "cross_query", "cross_value", "self_query", "self_value")
    vec = dict(zip(names, rest[len(mat):]))
    grads = (mat["self_query"], vec["self_query"], mat["self_key"], mat["self_value"], vec["self_value"], mat["self_out"],
        vec["self_out"], vec["gain_one"], vec["shift_one"], mat["cross_query"], vec["cross_query"], mat["cross_key"],
        mat["cross_value"], vec["cross_value"], mat["cross_out"], vec["cross_out"], vec["gain_two"], vec["shift_two"],
        expand_grad, vec["expand"], shrink_grad, vec["shrink"], vec["gain_three"], vec["shift_three"])
    return (layer_out[None], query_grad[None], content_grad[None], encoder_grad[None]) + grads


def solution(mesh):
    ctx, wa = mesh.devices.shape
    mesh = Mesh(mesh.devices.reshape(ctx // PLANE, PLANE, wa), ("grp", "pln", "wa"))
    in_specs = (
        P("wa", ("grp", "pln"), None),
        P("wa", ("grp", "pln"), None),
        P("wa", ("grp", "pln"), None),
        P("wa", ("grp", "pln"), None),
        P("wa", None),
        P("wa", None),
        P("wa", None),
        P("wa", None),
        P("wa"),
        P("wa", None),
        P("wa", None),
        P("wa"),
        P("wa", None),
        P("wa"),
        P("wa"),
        P("wa"),
        P("wa", None),
        P("wa"),
        P("wa", None),
        P("wa", None),
        P("wa"),
        P("wa", None),
        P("wa"),
        P("wa"),
        P("wa"),
        P("wa", None),
        P("wa"),
        P("wa", None),
        P("wa"),
        P("wa"),
        P("wa"),
    )
    out_specs = (
        P("wa", ("grp", "pln"), None),
        P("wa", ("grp", "pln"), None),
        P("wa", ("grp", "pln"), None),
        P("wa", ("grp", "pln"), None),
        P("wa", None),
        P("wa"),
        P("wa", None),
        P("wa", None),
        P("wa"),
        P("wa", None),
        P("wa"),
        P("wa"),
        P("wa"),
        P("wa", None),
        P("wa"),
        P("wa", None),
        P("wa", None),
        P("wa"),
        P("wa", None),
        P("wa"),
        P("wa"),
        P("wa"),
        P("wa", None),
        P("wa"),
        P("wa", None),
        P("wa"),
        P("wa"),
        P("wa"),
    )
    return jax.shard_map(shards, mesh=mesh, in_specs=in_specs, out_specs=out_specs, check_vma=False)
```

```python
import functools
import jax
import jax.numpy as jnp
from jax import lax
from jax.experimental import pallas as pl
from jax.experimental.pallas import tpu as pltpu
from jax.sharding import Mesh
from jax.sharding import PartitionSpec as P

PLANE = 4
DOCLEN = 2048
EPSILON = 1e-05
ROOT_HALF = 0.7071067811865476
INV_ROOT_TWO_PI = 0.3989422804014327
NEGATIVE = -1e29
HIDE = -(2.0 ** 100)
BLOCK = 512
QUERIES = 512
KEYS = 512
STAT = 40


def dot(a, b, ca, cb):
    return lax.dot_general(a, b, (((ca,), (cb,)), ((), ())), preferred_element_type=jnp.float32)


def left_half(shape):
    return lax.broadcasted_iota(jnp.int32, shape, 1) < 64


def openings(lens_ref, places):
    total, found = 0, places == 0
    for d in range(lens_ref.shape[1] - 1):
        total = total + lens_ref[0, d]
        found = jnp.logical_or(found, places == total)
    return found


def turned(value, eye):
    return dot(eye, value, 1, 1).astype(jnp.bfloat16)


def unit_matrix():
    row = lax.broadcasted_iota(jnp.int32, (128, 128), 0)
    lane = lax.broadcasted_iota(jnp.int32, (128, 128), 1)
    return jnp.where(row == lane, 1.0, 0.0).astype(jnp.bfloat16)


def with_stat(marks, stat, lane, at):
    high = stat.astype(jnp.bfloat16)
    rest = stat - high.astype(jnp.float32)
    middle = rest.astype(jnp.bfloat16)
    tail = (rest - middle.astype(jnp.float32)).astype(jnp.bfloat16)
    side = jnp.where(lane == at, high, jnp.where(lane == at + 1, middle, jnp.where(lane == at + 2, tail, marks)))
    return side


def matmul(left, right):
    return jnp.dot(left, right, preferred_element_type=jnp.float32)


def left_product(left, right):
    return jnp.einsum("ta,tb->ab", left, right, preferred_element_type=jnp.float32)


def right_product(left, right):
    return jnp.einsum("ta,ba->tb", left, right, preferred_element_type=jnp.float32)


def column_sum(value):
    return jnp.sum(value.astype(jnp.float32), axis=0)


def gelu_slope(value):
    cumulative = 0.5 * (1.0 + lax.erf(value * ROOT_HALF))
    return cumulative + value * jnp.exp(-0.5 * value * value) * INV_ROOT_TWO_PI


def norm_forward(value, gain_row, shift_row):
    middle = jnp.mean(value, axis=-1, keepdims=True)
    centred = value - middle
    spread = jnp.mean(centred * centred, axis=-1, keepdims=True)
    inverse = lax.rsqrt(spread + EPSILON)
    normed = centred * inverse
    return (normed * gain_row + shift_row, normed, inverse)


def norm_backward(incoming, normed, inverse, gain_row):
    scaled = incoming * gain_row
    centred = (
        scaled
        - jnp.mean(scaled, axis=-1, keepdims=True)
        - normed * jnp.mean(scaled * normed, axis=-1, keepdims=True)
    )
    return (inverse * centred, jnp.sum(incoming * normed, axis=0), jnp.sum(incoming, axis=0))


MESH = pl.DeviceIdType.MESH
ANY = pl.BlockSpec(memory_space=pltpu.HBM)
VMEM = pl.BlockSpec(memory_space=pltpu.VMEM)
SMEM = pl.BlockSpec(memory_space=pltpu.SMEM)
DMA = pltpu.SemaphoreType.DMA


def across(place, offset):
    if offset == 1:
        return place + 1 - 2 * lax.rem(place, 2)
    if offset == 2:
        return lax.rem(place + 2, 4)
    return 3 - place


def remote(src, dst, sends, recvs, where):
    return pltpu.make_async_remote_copy(
        src_ref=src, dst_ref=dst, send_sem=sends, recv_sem=recvs, device_id=where, device_id_type=MESH)


def greet(grp_count, wa_count, plane=True, groups=True, rows=True):
    barrier = pltpu.get_barrier_semaphore()
    grp, pln, wa = lax.axis_index("grp"), lax.axis_index("pln"), lax.axis_index("wa")

    def hello(where):
        pl.semaphore_signal(barrier, inc=1, device_id=where, device_id_type=MESH)

    count = 0
    if plane:
        for offset in (1, 2, 3):
            hello({"pln": across(pln, offset)})
        count += 3
    if rows:
        for offset in range(1, wa_count):
            hello({"wa": lax.rem(wa + offset, wa_count)})
        count += wa_count - 1
    if groups:
        @pl.when(grp > 0)
        def _():
            hello({"grp": grp - 1})

        @pl.when(grp < grp_count - 1)
        def _():
            hello({"grp": grp + 1})

        count = count + jnp.where(grp > 0, 1, 0) + jnp.where(grp < grp_count - 1, 1, 0)
    pl.semaphore_wait(barrier, count)


class Rows:
    def __init__(self, shard, full, sems, index, wa_count, stage=None):
        self.shard, self.full, self.sems, self.index, self.wa_count = shard, full, sems, index, wa_count
        self.stage = stage
        self.size = shard.shape[0]
        self.half = self.size // 2
        self.wa, self.pln = lax.axis_index("wa"), lax.axis_index("pln")
        self.core = lax.rem(self.pln, 2)

    def part(self, owner, core):
        return pl.ds(pl.multiple_of(owner * self.size + core * self.half, 16), self.half)

    def keep(self):
        own = pl.ds(pl.multiple_of(self.wa * self.size, 16), self.size)
        source = self.shard if self.stage is None else self.stage
        return pltpu.make_async_copy(source, self.full.at[own], self.sems.at[0, self.index, 0])

    def load(self):
        return pltpu.make_async_copy(self.shard, self.stage, self.sems.at[0, self.index, 0])

    def push(self, offset):
        mine = pl.ds(pl.multiple_of(self.core * self.half, 16), self.half)
        return remote(self.shard.at[mine], self.full.at[self.part(self.wa, self.core)],
                      self.sems.at[1, self.index, offset - 1], self.sems.at[2, self.index, offset - 1],
                      {"wa": lax.rem(self.wa + offset, self.wa_count)})

    def hand(self, offset):
        owner = lax.rem(self.wa + self.wa_count - offset, self.wa_count)
        spot = self.full.at[self.part(owner, self.core)]
        return remote(spot, spot, self.sems.at[3, self.index, offset - 1], self.sems.at[4, self.index, offset - 1],
                      {"pln": across(self.pln, 1)})

    def begin(self):
        if self.stage is None:
            self.keep().start()
        else:
            self.load().start()
        for offset in range(1, self.wa_count):
            self.push(offset).start()

    def staged(self):
        self.load().wait()
        self.keep().start()

    def pass_on(self):
        for offset in range(1, self.wa_count):
            self.push(offset).wait_recv()
            self.hand(offset).start()

    def arrived(self):
        self.keep().wait()
        for offset in range(1, self.wa_count):
            self.hand(offset).wait_recv()

    def finish(self):
        for offset in range(1, self.wa_count):
            self.push(offset).wait_send()
            self.hand(offset).wait_send()


class Line:
    def __init__(self, full, sems, grp_count, reach, block):
        self.full, self.sems, self.count, self.reach, self.block = full, sems, grp_count, reach, block
        self.grp = lax.axis_index("grp")

    def rows(self, owner, block):
        return pl.ds(pl.multiple_of((owner * PLANE + block) * self.block, 16), self.block)

    def copy(self, side, step, block, source=None):
        toward = 1 if side == 0 else -1
        owner = self.grp - toward * (step - 1)
        spot = self.full.at[self.rows(owner, block)]
        return remote(spot if source is None else source, spot, self.sems.at[0, side, step - 1, block],
                      self.sems.at[1, side, step - 1, block], {"grp": self.grp + toward})

    def sends(self, side, step):
        if side == 0:
            return jnp.logical_and(self.grp - step + 1 >= 0, self.grp + 1 < self.count)
        return jnp.logical_and(self.grp + step - 1 < self.count, self.grp - 1 >= 0)

    def receives(self, side, step):
        return self.grp - step >= 0 if side == 0 else self.grp + step < self.count

    def send(self, step, block, source=None):
        for side in (0, 1):
            @pl.when(self.sends(side, step))
            def _():
                self.copy(side, step, block, source).start()

    def arrival(self, side, step, block):
        toward = 1 if side == 0 else -1
        spot = self.full.at[self.rows(self.grp - toward * step, block)]
        return remote(spot, spot, self.sems.at[0, side, step - 1, block], self.sems.at[1, side, step - 1, block],
                      {"grp": self.grp - toward})

    def forward(self, step):
        for block in range(PLANE):
            for side in (0, 1):
                @pl.when(self.receives(side, step))
                def _():
                    self.arrival(side, step, block).wait_recv()

                    if step < self.reach:
                        @pl.when(self.sends(side, step + 1))
                        def _():
                            self.copy(side, step + 1, block).start()

    def finish(self, source=None):
        for step in range(1, self.reach + 1):
            for block in range(PLANE):
                for side in (0, 1):
                    @pl.when(self.sends(side, step))
                    def _():
                        self.copy(side, step, block, source[block] if source and step == 1 else None).wait_send()


class Swap:
    def __init__(self, src, dst, sems):
        self.src, self.dst, self.sems = src, dst, sems
        self.pln = lax.axis_index("pln")

    def copy(self, offset):
        peer = across(self.pln, offset)
        return remote(self.src(peer), self.dst(self.pln), self.sems.at[0, offset], self.sems.at[1, offset], {"pln": peer})

    def keep(self):
        return pltpu.make_async_copy(self.src(self.pln), self.dst(self.pln), self.sems.at[0, 0])

    def begin(self):
        for offset in (2, 3, 1):
            self.copy(offset).start()
        self.keep().start()

    def arrived(self, offset):
        self.keep().wait() if offset == 0 else self.copy(offset).wait_recv()

    def finish(self):
        for offset in (1, 2, 3):
            self.copy(offset).wait_send()


def pack_vectors(refs, pack):
    pack[...] = jnp.zeros_like(pack)
    at = 0
    for ref in refs:
        length = ref.shape[0]
        width = min(128, length)
        line = ref[...].astype(jnp.float32).reshape(1, length)
        for start in range(0, length, width):
            pack[at : at + 1, :width] = line[:, start : start + width]
            at += 1


def columns_of(ref, block):
    at = pl.multiple_of(block * 128, 128)
    line = ref[0:1, pl.ds(at, 128)].astype(jnp.float32)
    return jnp.transpose(jnp.broadcast_to(line, (128, 128)))


def make_marks(lens_ref, ranks_ref, limits_ref, base, self_keys, cross_keys, self_queries, cross_queries):
    docs = lens_ref.shape[1]
    lane = lax.rem(lax.broadcasted_iota(jnp.int32, (128, 128), 1), 64)
    stat = jnp.where(jnp.logical_and(lane >= STAT, lane < STAT + 3), -1.0, 0.0)

    def document(place):
        doc, opened, total = jnp.zeros((128, 128), jnp.int32), place == 0, 0
        for d in range(docs):
            total = total + lens_ref[0, d]
            doc = doc + jnp.where(place >= total, 1, 0)
            if d < docs - 1:
                opened = jnp.logical_or(opened, place == total)
        return doc, opened

    def keys(block, _):
        place = block * 128 + lax.broadcasted_iota(jnp.int32, (128, 128), 0)
        doc, opened = document(place)
        rank = jnp.where(opened, 0, columns_of(ranks_ref, block).astype(jnp.int32) + 1)
        marks = jnp.where(lane == doc, 1.0, stat)
        there = pl.ds(pl.multiple_of(block * 128, 128), 128)
        cross_keys[there, :] = marks.astype(jnp.bfloat16)
        self_keys[there, :] = jnp.where(lane == rank + 16, 1.0, marks).astype(jnp.bfloat16)
        return 0

    def queries(block, _):
        place = base + block * 128 + lax.broadcasted_iota(jnp.int32, (128, 128), 0)
        doc, _ = document(place)
        limit = columns_of(limits_ref, base // 128 + block).astype(jnp.int32)
        marks = jnp.where(jnp.logical_and(lane < docs, lane != doc), HIDE, 0.0)
        ranks = jnp.logical_and(lane >= 16, jnp.logical_and(lane < 33, lane - 17 >= limit))
        there = pl.ds(pl.multiple_of(block * 128, 128), 128)
        cross_queries[there, :] = marks.astype(jnp.bfloat16)
        self_queries[there, :] = jnp.where(ranks, HIDE, marks).astype(jnp.bfloat16)
        return 0

    lax.fori_loop(0, self_keys.shape[0] // 128, keys, 0)
    lax.fori_loop(0, self_queries.shape[0] // 128, queries, 0)


def vector_row(pack_ref, wa_count, start, length):
    width = min(128, length)
    pieces = []
    for wa in range(wa_count):
        for row in range(length // width):
            pieces.append(pack_ref[wa, start + row : start + row + 1, :width])
    return jnp.concatenate(pieces, axis=1)


def split_pairs(value, buffer, column):
    for pair in range(PLANE):
        buffer[pair, :, column : column + 128] = value[:, pair * 128 : pair * 128 + 128]


def flat_pairs(buffer):
    return jnp.concatenate([buffer[p] for p in range(PLANE)], axis=1)


class Looking:
    def __init__(self, ranked, lens, q, qm, kv, km, peaks, acc, base):
        self.ranked, self.lens, self.base = ranked, lens, base
        self.q, self.qm, self.kv, self.km, self.peaks, self.acc = q, qm, kv, km, peaks, acc
        self.rows = q.shape[0]

    def clear(self):
        self.peaks[...] = jnp.full_like(self.peaks, NEGATIVE)
        self.acc[...] = jnp.zeros_like(self.acc)

    def group(self, owner, diagonal=False):
        size = self.rows
        at = pl.multiple_of(owner * size, size)
        there = pl.ds(at, size)
        half = left_half((QUERIES, 128))
        khalf = left_half((size, 128))
        one = jnp.ones((size, 128), jnp.bfloat16)
        k, v, km = self.kv[there, :128], self.kv[there, 128:], self.km[there, :]
        keys = (jnp.where(khalf, k, km), jnp.where(khalf, km, k))
        values = (jnp.where(khalf, v, one), jnp.where(khalf, one, v))

        def one_block(block, _):
            start = pl.multiple_of(block * QUERIES, QUERIES)
            here = pl.ds(start, QUERIES)
            q, qm = self.q[here, :], self.qm[here, :]
            queries = (jnp.where(half, q, qm), jnp.where(half, qm, q))
            scores = [dot(queries[h], keys[h], 1, 1) for h in (0, 1)]
            if diagonal and self.ranked:
                place = start + lax.broadcasted_iota(jnp.int32, (QUERIES, size), 0)
                other = lax.broadcasted_iota(jnp.int32, (QUERIES, size), 1)
                column = start + lax.broadcasted_iota(jnp.int32, (QUERIES, 1), 0)
                banned = jnp.where(openings(self.lens, self.base + column), -1, place) == other
                scores = [jnp.where(banned, HIDE, s) for s in scores]
            for h in (0, 1):
                peak = self.peaks[h, here, :]
                new = jnp.maximum(peak, jnp.max(scores[h], axis=1, keepdims=True))
                p = jnp.exp(scores[h] - new).astype(jnp.bfloat16)
                self.acc[h, here, :] = self.acc[h, here, :] * jnp.exp(peak - new) + dot(p, values[h], 1, 0)
                self.peaks[h, here, :] = new
            return 0

        lax.fori_loop(0, self.rows // QUERIES, one_block, 0)

    def aside(self, offset, grp, grp_count):
        for owner in (grp + offset, grp - offset):
            @pl.when(jnp.logical_and(owner >= 0, owner < grp_count))
            def _():
                self.group(owner)

    def end(self, o_ref, lse_ref):
        half = left_half((self.rows, 128))
        total = jnp.where(half, self.acc[1], self.acc[0])
        mixed = jnp.where(half, self.acc[0], self.acc[1])
        o_ref[...] = mixed / pltpu.roll(total, 64, 1)
        lse_ref[...] = jnp.where(half, self.peaks[1], self.peaks[0]) + jnp.log(total)


def front_kernel(grp_count, wa_count, reach, count, vec_at, lens_ref, ranks_ref, limits_ref, content_ref, query_ref,
                 encoder_ref, *refs):
    refs = list(refs)
    take = lambda n: [refs.pop(0) for _ in range(n)]
    vecs, shards, wide_shards = take(len(vec_at)), take(count), take(2)
    fulls, wide_fulls = take(count), take(2)
    vec_out, q_out, q2_out, kv_out, kv2_out = take(5)
    mark_outs = take(4)
    o_out, lse_out, o2_out, lse2_out, hidden_ref, normed_ref, inverse_ref, mixed_ref = take(8)
    marks, (vec_ref, held, vec_all, kvbuf, kvbuf2, qbuf, qbuf2, sendbuf, mixbuf) = take(4), take(9)
    kv_all, kv2_all, q_all, q2_all, peaks, acc, stage_a, stage_b = take(8)
    row_sems, wide_sems, vec_sems, line_sems, swap_sems, out_sems, last_sems = refs
    grp, pln, wa = lax.axis_index("grp"), lax.axis_index("pln"), lax.axis_index("wa")
    tok = content_ref.shape[0]
    base = grp * PLANE * tok
    gathers = [Rows(shards[i], held.at[i], row_sems, i, wa_count) for i in range(count)]
    wide = [Rows(wide_shards[0], wide_fulls[0], wide_sems, 0, wa_count, stage_a),
            Rows(wide_shards[1], wide_fulls[1], wide_sems, 1, wa_count, stage_b)]
    pack_vectors(vecs, vec_ref)
    greet(grp_count, wa_count)
    vec_keep = pltpu.make_async_copy(vec_ref, vec_all.at[wa], vec_sems.at[0, 0])
    vec_keep.start()
    pushes = [remote(vec_ref, vec_all.at[wa], vec_sems.at[0, o], vec_sems.at[1, o], {"wa": lax.rem(wa + o, wa_count)})
              for o in range(1, wa_count)]
    for g in gathers[:2]:
        g.begin()
    for p in pushes:
        p.start()
    for g in gathers[:2]:
        g.pass_on()
    for g in gathers[2:5]:
        g.begin()
    vec_keep.wait()
    for p in pushes:
        p.wait_recv()
    for g in gathers[:2]:
        g.arrived()
    row = lambda i: vector_row(vec_all, wa_count, *vec_at[i])
    content = content_ref[...]
    split_pairs(matmul(content, held[0]).astype(jnp.bfloat16), kvbuf, 0)
    split_pairs((matmul(content, held[1]) + row(1)).astype(jnp.bfloat16), kvbuf, 128)
    line = Line(kv_all, line_sems.at[0], grp_count, reach, tok)
    spot = lambda ref: lambda p: ref.at[pl.ds(pl.multiple_of((grp * PLANE + p) * tok, 16), tok)]
    flat = lambda ref: lambda p: ref.at[pl.ds(pl.multiple_of(p * tok, 16), tok)]
    swap = Swap(lambda p: kvbuf.at[p], spot(kv_all), swap_sems.at[0])
    swap.begin()
    line.send(1, pln, kvbuf.at[pln])
    swap.arrived(1)
    line.send(1, across(pln, 1))
    for g in gathers[2:5]:
        g.pass_on()
    for g in gathers[5:]:
        g.begin()
    for offset in (2, 3):
        swap.arrived(offset)
        line.send(1, across(pln, offset))
    for g in gathers[2:5]:
        g.arrived()
    outs = [pltpu.make_async_copy(held.at[i], fulls[i], out_sems.at[i]) for i in range(count)]
    for o in outs[:5]:
        o.start()
    saves = [pltpu.make_async_copy(vec_all, vec_out, out_sems.at[count])]
    saves[0].start()
    query = (matmul(query_ref[...], held[2]) + row(0)).astype(jnp.bfloat16) * 0.125
    for pair in range(PLANE):
        qbuf[pair] = query[:, pair * 128 : pair * 128 + 128]
    swap_q = Swap(lambda p: qbuf.at[p], flat(q_all), swap_sems.at[1])
    swap_q.begin()
    encoder = encoder_ref[...]
    split_pairs(matmul(encoder, held[3]).astype(jnp.bfloat16), kvbuf2, 0)
    split_pairs((matmul(encoder, held[4]) + row(2)).astype(jnp.bfloat16), kvbuf2, 128)
    swap_2 = Swap(lambda p: kvbuf2.at[p], spot(kv2_all), swap_sems.at[2])
    swap_2.begin()
    make_marks(lens_ref, ranks_ref, limits_ref, base, *marks)
    mark_saves = [pltpu.make_async_copy(m, o, out_sems.at[count + 1 + i]) for i, (m, o) in enumerate(zip(marks, mark_outs))]
    for m in mark_saves:
        m.start()
    look = Looking(True, lens_ref, q_all, marks[2], kv_all, marks[0], peaks, acc, base)
    look.clear()
    swap.arrived(0)
    for offset in range(4):
        swap_q.arrived(offset)
    look.group(grp, True)
    line.forward(1)
    for g in gathers[5:]:
        g.pass_on()
    for w in wide:
        w.begin()
    line_2 = Line(kv2_all, line_sems.at[1], grp_count, reach, tok)
    for offset in range(4):
        swap_2.arrived(offset)
    for block in range(PLANE):
        line_2.send(1, block)
    look.aside(1, grp, grp_count)
    for w in wide:
        w.staged()
    for step in range(2, reach + 1):
        line.forward(step)
        look.aside(step, grp, grp_count)
    look.end(o_out, lse_out)
    for p in range(PLANE):
        sendbuf[p] = o_out[p * tok : p * tok + tok, :].astype(jnp.bfloat16)
    swap_o = Swap(lambda p: sendbuf.at[p], lambda p: mixbuf.at[p], swap_sems.at[3])
    swap_o.begin()
    more = [pltpu.make_async_copy(kv_all, kv_out, last_sems.at[0]), pltpu.make_async_copy(q_all, q_out, last_sems.at[1])]
    for m in more:
        m.start()
    for g in gathers[5:]:
        g.arrived()
    for o in outs[5:]:
        o.start()
    for offset in range(4):
        swap_o.arrived(offset)
    mixed = flat_pairs(mixbuf)
    mixed_ref[...] = mixed
    value = query_ref[...].astype(jnp.float32) + matmul(mixed, held[5]) + row(3)
    hidden, normed, inverse = norm_forward(value, row(4), row(5))
    query = (matmul(hidden.astype(jnp.bfloat16), held[6]) + row(6)).astype(jnp.bfloat16) * 0.125
    for pair in range(PLANE):
        qbuf2[pair] = query[:, pair * 128 : pair * 128 + 128]
    swap_q2 = Swap(lambda p: qbuf2.at[p], flat(q2_all), swap_sems.at[4])
    swap_q2.begin()
    hidden_ref[...] = hidden
    normed_ref[...] = normed
    inverse_ref[...] = jnp.broadcast_to(inverse, inverse_ref.shape)
    line_2.forward(1)
    look_2 = Looking(False, lens_ref, q2_all, marks[3], kv2_all, marks[1], peaks, acc, base)
    look_2.clear()
    for w in wide:
        w.pass_on()
    for offset in range(4):
        swap_q2.arrived(offset)
    more.append(pltpu.make_async_copy(q2_all, q2_out, last_sems.at[2]))
    more[-1].start()
    look_2.group(grp)
    look_2.aside(1, grp, grp_count)
    for step in range(2, reach + 1):
        line_2.forward(step)
        look_2.aside(step, grp, grp_count)
    more.append(pltpu.make_async_copy(kv2_all, kv2_out, last_sems.at[3]))
    more[-1].start()
    look_2.end(o2_out, lse2_out)
    for w in wide:
        w.arrived()
    for g in gathers + wide:
        g.finish()
    for p in pushes:
        p.wait_send()
    for c in outs + saves + mark_saves + more:
        c.wait()
    line.finish()
    line_2.finish()
    for s in (swap, swap_q, swap_2, swap_o, swap_q2):
        s.finish()


def run_front(grp_count, wa_count, lens, ranks, limits, content, query, encoder, vecs, mats, wide, vec_at):
    tok = content.shape[0]
    reach = min(grp_count - 1, (DOCLEN + PLANE * tok - 2) // (PLANE * tok))
    count = len(mats)
    low, full = jnp.bfloat16, jnp.float32
    shape = jax.ShapeDtypeStruct
    rows, keys = PLANE * tok, grp_count * PLANE * tok
    used = sum(length // min(128, length) for _, length in vec_at)
    pack = (used + -used % 16, 128)
    marks = [(keys, 128), (keys, 128), (rows, 128), (rows, 128)]
    out_shape = [shape((m.shape[0] * wa_count, m.shape[1]), low) for m in mats + wide]
    out_shape += [shape((wa_count,) + pack, full), shape((rows, 128), low), shape((rows, 128), low), shape((keys, 256), low),
                  shape((keys, 256), low)]
    out_shape += [shape(m, low) for m in marks]
    inner = [shape((rows, 128), full)] * 4 + [shape((tok, 512), full), shape((tok, 512), full), shape((tok, 128), full),
                                              shape((tok, 512), low)]
    pairs = pltpu.VMEM((PLANE, tok, 128), low)
    doubles = pltpu.VMEM((PLANE, tok, 256), low)
    return pl.pallas_call(
        functools.partial(front_kernel, grp_count, wa_count, reach, count, vec_at),
        out_shape=tuple(out_shape + inner),
        in_specs=[SMEM] + [VMEM] * (5 + len(vecs)) + [ANY] * (count + 2),
        out_specs=tuple([ANY] * len(out_shape) + [VMEM] * len(inner)),
        scratch_shapes=[pltpu.VMEM(m, low) for m in marks] + [
            pltpu.VMEM(pack, full), pltpu.VMEM((count, 512, 512), low), pltpu.VMEM((wa_count,) + pack, full),
            doubles, doubles, pairs, pairs, pairs, pairs,
            pltpu.VMEM((keys, 256), low), pltpu.VMEM((keys, 256), low), pltpu.VMEM((rows, 128), low),
            pltpu.VMEM((rows, 128), low), pltpu.VMEM((2, rows, 1), full), pltpu.VMEM((2, rows, 128), full),
            pltpu.VMEM(wide[0].shape, low), pltpu.VMEM(wide[1].shape, low),
            DMA((5, count, max(1, wa_count - 1))), DMA((5, 2, max(1, wa_count - 1))), DMA((2, wa_count)),
            DMA((2, 2, 2, reach, PLANE)), DMA((5, 2, 4)), DMA((count + 5,)), DMA((4,))],
        compiler_params=pltpu.CompilerParams(collective_id=1, has_side_effects=True, vmem_limit_bytes=60 << 20),
    )(lens, ranks, limits, content, query, encoder, *vecs, *mats, *wide)


class Backing:
    def __init__(self, ranked, lens, q, qm, kv, km, o, lse, do, sides, dqt, base):
        self.ranked, self.lens, self.base = ranked, lens, base
        self.q, self.qm, self.kv, self.km, self.o, self.lse, self.do = q, qm, kv, km, o, lse, do
        self.sides, self.dqt = sides, dqt
        self.rows = q.shape[0]

    def prepare(self):
        half = left_half((BLOCK, 128))
        lane = lax.rem(lax.broadcasted_iota(jnp.int32, (BLOCK, 128), 1), 64)
        zero = jnp.zeros((BLOCK, 128), jnp.bfloat16)

        def one_block(block, _):
            here = pl.ds(pl.multiple_of(block * BLOCK, BLOCK), BLOCK)
            q, do = self.q[here, :], self.do[here, :]
            shared = do.astype(jnp.float32) * self.o[here, :]
            delta0 = jnp.sum(jnp.where(half, shared, 0.0), axis=1, keepdims=True)
            delta1 = jnp.sum(jnp.where(half, 0.0, shared), axis=1, keepdims=True)
            side = with_stat(self.qm[here, :], self.lse[here, :], lane, STAT)
            self.sides[0, here, :] = jnp.where(half, q, side)
            self.sides[1, here, :] = jnp.where(half, side, q)
            side = with_stat(zero, -jnp.where(half, delta1, delta0), lane, STAT)
            self.sides[2, here, :] = jnp.where(half, do, side)
            self.sides[3, here, :] = jnp.where(half, side, do)
            self.sides[4, here, :] = jnp.where(half, q, zero)
            self.sides[5, here, :] = jnp.where(half, zero, q)
            self.sides[6, here, :] = jnp.where(half, do, zero)
            self.sides[7, here, :] = jnp.where(half, zero, do)
            return 0

        lax.fori_loop(0, self.rows // BLOCK, one_block, 0)
        self.dqt[...] = jnp.zeros_like(self.dqt)

    def group(self, owner, store, diagonal=False):
        khalf = left_half((KEYS, 128))
        one = jnp.ones((KEYS, 128), jnp.bfloat16)
        tops = lax.broadcasted_iota(jnp.int32, (128, KEYS), 0) < 64
        none = jnp.zeros((128, KEYS), jnp.bfloat16)
        eye = unit_matrix()

        def keys_block(index, _):
            at = pl.multiple_of(owner * self.rows + index * KEYS, KEYS)
            there = pl.ds(at, KEYS)
            k, v, km = self.kv[there, :128], self.kv[there, 128:], self.km[there, :]
            keys = (jnp.where(khalf, k, km), jnp.where(khalf, km, k))
            values = (jnp.where(khalf, v, one), jnp.where(khalf, one, v))
            kt = turned(k, eye)
            kts = (jnp.where(tops, kt, none), jnp.where(tops, none, kt))

            def queries_block(block, carry):
                dk, dv = carry
                start = pl.multiple_of(block * BLOCK, BLOCK)
                here = pl.ds(start, BLOCK)
                scores = [dot(keys[h], self.sides[h, here, :], 1, 1) for h in (0, 1)]
                if diagonal and self.ranked:
                    other = at + lax.broadcasted_iota(jnp.int32, (KEYS, BLOCK), 0)
                    row = self.base + start + lax.broadcasted_iota(jnp.int32, (1, BLOCK), 1)
                    banned = other == jnp.where(openings(self.lens, row), -1, row)
                    scores = [jnp.where(banned, HIDE, s) for s in scores]
                ps = [jnp.exp(scores[h]) for h in (0, 1)]
                ds = [(ps[h] * dot(values[h], self.sides[2 + h, here, :], 1, 1)).astype(jnp.bfloat16) for h in (0, 1)]
                ps = [p.astype(jnp.bfloat16) for p in ps]
                both_q = jnp.concatenate([self.sides[4, here, :], self.sides[5, here, :]], axis=0)
                both_do = jnp.concatenate([self.sides[6, here, :], self.sides[7, here, :]], axis=0)
                dv = dv + dot(jnp.concatenate(ps, axis=1), both_do, 1, 0)
                dk = dk + dot(jnp.concatenate(ds, axis=1), both_q, 1, 0)
                self.dqt[:, here] = self.dqt[:, here] + dot(kts[0], ds[0], 1, 0) + dot(kts[1], ds[1], 1, 0)
                return dk, dv

            zero = jnp.zeros((KEYS, 128), jnp.float32)
            dk, dv = lax.fori_loop(0, self.rows // BLOCK, queries_block, (zero, zero))
            store(pl.ds(pl.multiple_of(index * KEYS, KEYS), KEYS), dk, dv)
            return 0

        lax.fori_loop(0, self.rows // KEYS, keys_block, 0)

    def query_grad(self, out, tok):
        for p in range(PLANE):
            out[p] = jnp.transpose(self.dqt[:, p * tok : p * tok + tok] * 0.125).astype(jnp.bfloat16)


def into(ref):
    def store(rows, dk, dv):
        ref[rows, :128] = dk.astype(ref.dtype)
        ref[rows, 128:] = dv.astype(ref.dtype)

    return store


class Fold:
    def __init__(self, mine, sendbuf, getbuf, sems, grp_count, reach, block):
        self.mine, self.sendbuf, self.getbuf, self.sems = mine, sendbuf, getbuf, sems
        self.count, self.reach, self.block = grp_count, reach, block
        self.grp = lax.axis_index("grp")

    def toward(self, side):
        return 1 if side == 0 else -1

    def part(self, block):
        return pl.ds(block * self.block, self.block)

    def sends(self, side, stage):
        return self.grp + stage < self.count if side == 0 else self.grp - stage >= 0

    def receives(self, side, stage):
        if side == 0:
            return jnp.logical_and(self.grp >= 1, self.grp - 1 + stage < self.count)
        return jnp.logical_and(self.grp + 1 < self.count, self.grp + 1 - stage >= 0)

    def copy(self, side, stage, block, back=False):
        peer = self.grp + (-self.toward(side) if back else self.toward(side))
        return remote(self.sendbuf.at[side, stage - 1, self.part(block)], self.getbuf.at[side, stage - 1, self.part(block)],
                      self.sems.at[0, side, stage - 1, block], self.sems.at[1, side, stage - 1, block], {"grp": peer})

    def run(self, side, stage, backing):
        @pl.when(self.sends(side, stage))
        def _():
            owner = self.grp + self.toward(side) * stage
            if stage == self.reach:
                backing.group(owner, into(self.sendbuf.at[side, stage - 1]))
                for block in range(PLANE):
                    self.copy(side, stage, block).start()
            else:
                backing.group(owner, into(self.mine.at[side]))
                for block in range(PLANE):
                    part = self.part(block)
                    self.sendbuf[side, stage - 1, part, :] = self.mine[side, part, :]

                    @pl.when(self.receives(side, stage + 1))
                    def _():
                        self.copy(side, stage + 1, block, True).wait_recv()
                        total = self.mine[side, part, :].astype(jnp.float32)
                        total = total + self.getbuf[side, stage, part, :].astype(jnp.float32)
                        self.sendbuf[side, stage - 1, part, :] = total.astype(jnp.bfloat16)

                    self.copy(side, stage, block).start()

    def total(self, own, out):
        for block in range(PLANE):
            part = self.part(block)
            for side in (0, 1):
                @pl.when(self.receives(side, 1))
                def _():
                    self.copy(side, 1, block, True).wait_recv()
                    own[part, :] = own[part, :] + self.getbuf[side, 0, part, :].astype(jnp.float32)
            out[block] = own[part, :].astype(jnp.bfloat16)

    def finish(self):
        for stage in range(1, self.reach + 1):
            for block in range(PLANE):
                for side in (0, 1):
                    @pl.when(self.sends(side, stage))
                    def _():
                        self.copy(side, stage, block, True).wait_send()


def back_scratch(tok, reach):
    low = jnp.bfloat16
    size = PLANE * tok
    pairs = pltpu.VMEM((PLANE, tok, 128), low)
    doubles = pltpu.VMEM((PLANE, tok, 256), low)
    return [pltpu.VMEM((8, size, 128), low), pltpu.VMEM((128, size), jnp.float32), pairs, pairs, doubles, doubles,
            pltpu.VMEM((size, 256), jnp.float32), pltpu.VMEM((2, size, 256), low), pltpu.VMEM((2, reach, size, 256), low),
            pltpu.VMEM((2, reach, size, 256), low)]


def store_blocks(buffer, value):
    for c in range(PLANE):
        buffer[c] = value[:, c * 128 : c * 128 + 128].astype(jnp.bfloat16)


def halves(buffer):
    keys = jnp.concatenate([buffer[p, :, :128] for p in range(PLANE)], axis=1)
    values = jnp.concatenate([buffer[p, :, 128:] for p in range(PLANE)], axis=1)
    return keys, values


class Reduce:
    def __init__(self, index, source, parts, got, kept, sems, wa_count, place=None):
        self.index, self.source, self.sems, self.wa_count = index, source, sems, wa_count
        self.parts, (self.got_core, self.got_wa, self.got_row) = parts, got
        self.by_core, self.by_wa, self.by_row = kept
        self.place = index if place is None else place
        self.wa, self.pln = lax.axis_index("wa"), lax.axis_index("pln")
        self.core = lax.rem(self.pln, 2)
        self.row = self.pln // 2
        self.size = 512 // wa_count

    def core_copy(self, row):
        return remote(self.source.at[row * 2 + 1 - self.core], self.got_core.at[self.index, row],
                      self.sems.at[0, self.index, row], self.sems.at[1, self.index, row], {"pln": across(self.pln, 1)})

    def rows_of(self, wa):
        return pl.ds(pl.multiple_of(wa * self.size, 16), self.size)

    def wa_copy(self, offset):
        peer = lax.rem(self.wa + offset, self.wa_count)
        return remote(self.by_core.at[self.index, :, self.rows_of(peer)], self.got_wa.at[offset - 1, self.index],
                      self.sems.at[0, self.index, 1 + offset], self.sems.at[1, self.index, 1 + offset], {"wa": peer})

    def row_copy(self):
        return remote(self.by_wa.at[self.index, 1 - self.row], self.got_row.at[self.index],
                      self.sems.at[0, self.index, 1 + self.wa_count], self.sems.at[1, self.index, 1 + self.wa_count],
                      {"pln": across(self.pln, 2)})

    def begin(self):
        for row in (0, 1):
            self.core_copy(row).start()

    def after_core(self):
        for row in (0, 1):
            self.core_copy(row).wait_recv()
            mine = self.parts[row * 2 + self.core].astype(jnp.float32)
            total = mine + self.got_core[self.index, row].astype(jnp.float32)
            self.by_core[self.index, row] = total.astype(jnp.bfloat16)
        for offset in range(1, self.wa_count):
            self.wa_copy(offset).start()

    def after_wa(self):
        for offset in range(1, self.wa_count):
            self.wa_copy(offset).wait_recv()
        for row in (0, 1):
            total = self.by_core[self.index, row, self.rows_of(self.wa), :].astype(jnp.float32)
            for offset in range(1, self.wa_count):
                total = total + self.got_wa[offset - 1, self.index, row].astype(jnp.float32)
            self.by_wa[self.index, row] = total.astype(jnp.bfloat16)
        self.row_copy().start()

    def after_row(self):
        self.row_copy().wait_recv()
        total = self.by_wa[self.index, self.row].astype(jnp.float32) + self.got_row[self.index].astype(jnp.float32)
        self.by_row[self.place] = total.astype(jnp.bfloat16)

    def finish(self):
        for row in (0, 1):
            self.core_copy(row).wait_send()
        for offset in range(1, self.wa_count):
            self.wa_copy(offset).wait_send()
        self.row_copy().wait_send()


def turn_kernel(grp_count, wa_count, reach, vec_at, lens_ref, q_ref, qm_ref, kv_ref, km_ref, o_ref, lse_ref, do_ref, back_ref,
                normed_ref, inverse_ref, hidden_ref, mixed_one_ref, mixed_two_ref, branch_two_ref, encoder_ref, query_mat_ref,
                out_mat_ref, vec_ref, vg_ref, wide_ref,
                do_out, back_out, kv_out, grads_out, vg_out, wide_out,
                sides, dqt, dqsend, dqget, kvsend, kvget, total, mine, foldsend, foldget, dosend, doget, grads, parts, got_core,
                got_wa, got_row, by_core, by_wa, by_row, fold_sems, swap_sems, out_sems, part_sems, red_sems):
    tok = back_ref.shape[0]
    grp = lax.axis_index("grp")
    wide = wide_ref.shape[0]
    loads = [pltpu.make_async_copy(wide_ref.at[i], parts.at[i], part_sems.at[i]) for i in range(wide)]
    for l in loads:
        l.start()
    greet(grp_count, wa_count)
    reds = [Reduce(i, wide_ref.at[i], parts.at[i], (got_core, got_wa, got_row), (by_core, by_wa, by_row), red_sems, wa_count)
            for i in range(wide)]
    for r in reds:
        r.begin()
    backing = Backing(False, lens_ref, q_ref, qm_ref, kv_ref, km_ref, o_ref, lse_ref, do_ref, sides, dqt, grp * PLANE * tok)
    backing.prepare()
    for l in loads:
        l.wait()
    for r in reds[: wide // 2]:
        r.after_core()
    fold = Fold(mine, foldsend, foldget, fold_sems, grp_count, reach, tok)
    for side in (0, 1):
        fold.run(side, reach, backing)
    for r in reds[wide // 2 :]:
        r.after_core()
    for stage in range(reach - 1, 0, -1):
        for side in (0, 1):
            fold.run(side, stage, backing)
    for r in reds[: wide // 2]:
        r.after_wa()
    backing.group(grp, into(total), True)
    backing.query_grad(dqsend, tok)
    swap_dq = Swap(lambda p: dqsend.at[p], lambda p: dqget.at[p], swap_sems.at[0])
    swap_dq.begin()
    row = lambda i: vector_row(vec_ref, wa_count, *vec_at[i])
    vg_out[...] = vg_ref[...]
    saves = [pltpu.make_async_copy(grads.at[i], grads_out.at[i], out_sems.at[i]) for i in range(5)]
    store_blocks(grads.at[0], dot(mixed_two_ref[...], branch_two_ref[...], 0, 0))
    saves[0].start()
    for r in reds[wide // 2 :]:
        r.after_wa()
    for offset in range(4):
        swap_dq.arrived(offset)
    dq = flat_pairs(dqget)
    incoming = back_ref[...] + dot(dq, query_mat_ref[...], 1, 1)
    back, gain_grad, shift_grad = norm_backward(incoming, normed_ref[...], inverse_ref[:, :1], row(4))
    back_out[...] = back
    branch = back.astype(jnp.bfloat16)
    do = dot(branch, out_mat_ref[...], 1, 1).astype(jnp.bfloat16)
    for p in range(PLANE):
        dosend[p] = do[:, p * 128 : p * 128 + 128]
    swap_do = Swap(lambda p: dosend.at[p], lambda p: doget.at[p], swap_sems.at[1])
    swap_do.begin()
    fold.total(total, kvsend)
    swap_kv = Swap(lambda p: kvsend.at[p], lambda p: kvget.at[p], swap_sems.at[2])
    swap_kv.begin()
    vg_out[10:11, :] = gain_grad.reshape(1, 512)
    vg_out[11:12, :] = shift_grad.reshape(1, 512)
    vg_out[12:13, :] = column_sum(branch).reshape(1, 512)
    vg_out[13:14, :] = column_sum(dq).reshape(1, 512)
    store_blocks(grads.at[1], dot(hidden_ref[...].astype(jnp.bfloat16), dq, 0, 0))
    saves[1].start()
    store_blocks(grads.at[2], dot(mixed_one_ref[...], branch, 0, 0))
    saves[2].start()
    for offset in range(4):
        swap_do.arrived(offset)
    for p in range(PLANE):
        do_out[p * tok : p * tok + tok, :] = doget[p]
    for offset in range(4):
        swap_kv.arrived(offset)
    keys, values = halves(kvget)
    kv_out[:, :512] = keys
    kv_out[:, 512:] = values
    encoder = encoder_ref[...]
    store_blocks(grads.at[3], dot(encoder, keys, 0, 0))
    saves[3].start()
    store_blocks(grads.at[4], dot(encoder, values, 0, 0))
    saves[4].start()
    vg_out[14:15, :] = column_sum(values).reshape(1, 512)
    for r in reds:
        r.after_row()
    wide_save = pltpu.make_async_copy(by_row, wide_out, part_sems.at[0])
    wide_save.start()
    for s in saves:
        s.wait()
    for r in reds:
        r.finish()
    wide_save.wait()
    fold.finish()
    for s in (swap_dq, swap_do, swap_kv):
        s.finish()


def run_turn(grp_count, wa_count, vec_at, lens, q, qm, kv, km, o, lse, do, back, normed, inverse, hidden, mixed_one, mixed_two, branch_two,
             encoder, query_mat, out_mat, vecs, vg, wide):
    tok = back.shape[0]
    reach = min(grp_count - 1, (DOCLEN + PLANE * tok - 2) // (PLANE * tok))
    low, full = jnp.bfloat16, jnp.float32
    shape = jax.ShapeDtypeStruct
    pairs = pltpu.VMEM((PLANE, tok, 128), low)
    count, size = wide.shape[0], 512 // wa_count
    return pl.pallas_call(
        functools.partial(turn_kernel, grp_count, wa_count, reach, vec_at),
        out_shape=(shape((PLANE * tok, 128), low), shape((tok, 512), full), shape((tok, 1024), low),
                   shape((5, PLANE, 512, 128), low), shape(vg.shape, full), shape((count, size, 128), low)),
        in_specs=[SMEM] + [VMEM] * 19 + [ANY],
        out_specs=(VMEM, VMEM, VMEM, ANY, VMEM, ANY),
        scratch_shapes=back_scratch(tok, reach) + [pairs] * 2 + [
            pltpu.VMEM((5, PLANE, 512, 128), low), pltpu.VMEM((count, PLANE, 512, 128), low),
            pltpu.VMEM((count, 2, 512, 128), low), pltpu.VMEM((max(1, wa_count - 1), count, 2, size, 128), low),
            pltpu.VMEM((count, size, 128), low), pltpu.VMEM((count, 2, 512, 128), low), pltpu.VMEM((count, 2, size, 128), low),
            pltpu.VMEM((count, size, 128), low), DMA((2, 2, reach, PLANE)), DMA((3, 2, 4)),
            DMA((5,)), DMA((count,)), DMA((2, count, wa_count + 2))],
        cost_estimate=pl.CostEstimate(flops=32000000000, bytes_accessed=0, transcendentals=0),
        compiler_params=pltpu.CompilerParams(collective_id=8, has_side_effects=True, vmem_limit_bytes=60 << 20),
    )(lens, q, qm, kv, km, o, lse, do, back, normed, inverse, hidden, mixed_one, mixed_two, branch_two, encoder, query_mat, out_mat, vecs, vg,
      wide)


def greet_all(grp_count, wa_count):
    barrier = pltpu.get_barrier_semaphore()
    grp, pln, wa = lax.axis_index("grp"), lax.axis_index("pln"), lax.axis_index("wa")
    peers = [{"pln": across(pln, o)} for o in (1, 2, 3)]
    peers += [{"wa": lax.rem(wa + o, wa_count)} for o in range(1, wa_count)]
    peers += [{"grp": lax.rem(grp + o, grp_count)} for o in range(1, grp_count)]
    for where in peers:
        pl.semaphore_signal(barrier, inc=1, device_id=where, device_id_type=MESH)
    pl.semaphore_wait(barrier, len(peers))


def closing_kernel(grp_count, wa_count, reach, count, lens_ref, q_ref, qm_ref, kv_ref, km_ref, o_ref, lse_ref, do_ref,
                   query_ref, content_ref, early_ref, wide_ref, vg_ref,
                   dq_out, kv_out, out_ref, vg_out,
                   sides, dqt, dqsend, dqget, kvsend, kvget, total, mine, foldsend, foldget, parts, got_core, got_wa, got_row,
                   by_core, by_wa, by_row, got_grp, final, vsum, vgot, vall,
                   fold_sems, swap_sems, part_sems, wide_sem, red_sems, vec_sems, grp_sems, share_sems):
    grp, pln, wa = lax.axis_index("grp"), lax.axis_index("pln"), lax.axis_index("wa")
    tok = query_ref.shape[0]
    early = early_ref.shape[0]
    wide = wide_ref.shape[0]
    sets = ((0, wide), (wide, early), (wide + early, count - early))
    size = 512 // wa_count
    slab = size // grp_count
    loads = [pltpu.make_async_copy(early_ref.at[i], parts.at[i], part_sems.at[i]) for i in range(early)]
    for l in loads:
        l.start()
    wide_load = pltpu.make_async_copy(wide_ref, by_row.at[pl.ds(0, wide)], wide_sem)
    wide_load.start()
    greet_all(grp_count, wa_count)
    got, kept = (got_core, got_wa, got_row), (by_core, by_wa, by_row)
    reds = [Reduce(i, early_ref.at[i] if i < early else parts.at[i], parts.at[i], got, kept, red_sems, wa_count,
                   wide + i) for i in range(count)]
    for r in reds[:early]:
        r.begin()
    wide_load.wait()

    def grp_copy(set_at, offset):
        start, length = sets[set_at]
        peer = lax.rem(grp + offset, grp_count)
        some = pl.ds(start, length)
        rows = pl.ds(pl.multiple_of(peer * slab, 8), slab)
        return remote(by_row.at[some, rows], got_grp.at[offset - 1, some], grp_sems.at[0, set_at, offset - 1],
                      grp_sems.at[1, set_at, offset - 1], {"grp": peer})

    offsets = range(1, grp_count)
    own_rows = pl.ds(pl.multiple_of(grp * slab, 8), slab)

    def settle(set_at):
        start, length = sets[set_at]
        some = pl.ds(start, length)
        for o in offsets:
            grp_copy(set_at, o).wait_recv()
        value = by_row[some, own_rows, :].astype(jnp.float32)
        for o in offsets:
            value = value + got_grp[o - 1, some].astype(jnp.float32)
        final[some] = value.astype(jnp.bfloat16)

    def spot(column, source, some):
        return out_ref.at[column, some, pl.ds(pl.multiple_of(source * slab, 8), slab)]

    def spread(set_at, offset):
        start, length = sets[set_at]
        some = pl.ds(start, length)
        return remote(final.at[some], spot(pln, grp, some), share_sems.at[0, set_at, 0, offset],
                      share_sems.at[1, set_at, 0, offset], {"grp": lax.rem(grp + offset, grp_count)})

    def keep(set_at):
        start, length = sets[set_at]
        some = pl.ds(start, length)
        return pltpu.make_async_copy(final.at[some], spot(pln, grp, some), share_sems.at[0, set_at, 0, 0])

    def give(set_at, kind, offset):
        start, length = sets[set_at]
        some = pl.ds(start, length)
        source = lax.rem(grp + grp_count - offset, grp_count)
        column = pln if kind < 3 else across(pln, 2)
        there = spot(column, source, some)
        return remote(there, there, share_sems.at[0, set_at, kind, offset], share_sems.at[1, set_at, kind, offset],
                      {"pln": across(pln, 2 if kind == 1 else 1)})

    def share(set_at):
        settle(set_at)
        keep(set_at).start()
        for o in offsets:
            spread(set_at, o).start()

    everyone = range(grp_count)

    def hand_out(set_at, offset):
        if offset == 0:
            keep(set_at).wait()
        else:
            spread(set_at, offset).wait_recv()
        give(set_at, 1, offset).start()
        give(set_at, 2, offset).start()

    def cross_over(set_at):
        for o in everyone:
            give(set_at, 1, o).wait_recv()
            give(set_at, 3, o).start()

    for o in offsets:
        grp_copy(0, o).start()
    backing = Backing(True, lens_ref, q_ref, qm_ref, kv_ref, km_ref, o_ref, lse_ref, do_ref, sides, dqt, grp * PLANE * tok)
    backing.prepare()
    for l in loads:
        l.wait()
    for r in reds[:early]:
        r.after_core()
    fold = Fold(mine, foldsend, foldget, fold_sems, grp_count, reach, tok)
    for side in (0, 1):
        fold.run(side, reach, backing)
    for stage in range(reach - 1, 0, -1):
        for side in (0, 1):
            fold.run(side, stage, backing)
    for r in reds[:early]:
        r.after_wa()
    backing.group(grp, into(total), True)
    backing.query_grad(dqsend, tok)
    swap_dq = Swap(lambda p: dqsend.at[p], lambda p: dqget.at[p], swap_sems.at[0])
    swap_dq.begin()
    vsum[0] = vg_ref[...]
    for r in reds[:early]:
        r.after_row()
    for o in offsets:
        grp_copy(1, o).start()
    fold.total(total, kvsend)
    swap_kv = Swap(lambda p: kvsend.at[p], lambda p: kvget.at[p], swap_sems.at[1])
    swap_kv.begin()
    share(0)
    for offset in range(4):
        swap_dq.arrived(offset)
    dq = flat_pairs(dqget)
    dq_out[...] = dq
    store_blocks(parts.at[early], dot(query_ref[...], dq, 0, 0))
    vsum[0, 15:16, :] = column_sum(dq).reshape(1, 512)
    reds[early].begin()
    for offset in range(4):
        swap_kv.arrived(offset)
    keys, values = halves(kvget)
    content = content_ref[...]
    store_blocks(parts.at[early + 1], dot(content, keys, 0, 0))
    reds[early + 1].begin()
    store_blocks(parts.at[early + 2], dot(content, values, 0, 0))
    reds[early + 2].begin()
    vsum[0, 16:17, :] = column_sum(values).reshape(1, 512)
    vec_core = remote(vsum.at[0], vgot.at[0], vec_sems.at[0, 0], vec_sems.at[1, 0], {"pln": across(pln, 1)})
    vec_core.start()
    kv_out[:, :512] = keys
    kv_out[:, 512:] = values

    for r in reds[early:]:
        r.after_core()
    vec_core.wait_recv()
    vsum[1] = vsum[0] + vgot[0]
    vec_wa = [remote(vsum.at[1], vgot.at[o], vec_sems.at[0, o], vec_sems.at[1, o], {"wa": lax.rem(wa + o, wa_count)})
              for o in range(1, wa_count)]
    for v in vec_wa:
        v.start()
    for r in reds[early:]:
        r.after_wa()
    for v in vec_wa:
        v.wait_recv()
    vall[wa] = vsum[1]
    for o in range(1, wa_count):
        vall[lax.rem(wa + wa_count - o, wa_count)] = vgot[o]
    joined = vall[0]
    for o in range(1, wa_count):
        joined = joined + vall[o]
    vsum[2] = joined
    vec_row = remote(vsum.at[2], vgot.at[wa_count], vec_sems.at[0, wa_count], vec_sems.at[1, wa_count],
                     {"pln": across(pln, 2)})
    vec_row.start()
    for o in everyone:
        hand_out(0, o)
    share(1)
    for r in reds[early:]:
        r.after_row()
    for o in offsets:
        grp_copy(2, o).start()
    cross_over(0)
    vec_row.wait_recv()
    vsum[3] = vsum[2] + vgot[wa_count]
    vec_grp = [remote(vsum.at[3], vall.at[wa_count + o], vec_sems.at[0, wa_count + o], vec_sems.at[1, wa_count + o],
                      {"grp": lax.rem(grp + o, grp_count)}) for o in offsets]
    for v in vec_grp:
        v.start()
    for o in everyone:
        hand_out(1, o)
    share(2)
    cross_over(1)
    for o in everyone:
        hand_out(2, o)
    for v in vec_grp:
        v.wait_recv()
    ordered = jnp.zeros_like(vsum[3])
    for g in everyone:
        piece = jnp.where(grp == g, vsum[3], 0.0)
        for o in offsets:
            piece = piece + jnp.where(lax.rem(grp + grp_count - o, grp_count) == g, vall[wa_count + o], 0.0)
        ordered = ordered + piece
    vg_out[...] = ordered
    cross_over(2)
    for set_at in range(3):
        for o in everyone:
            give(set_at, 2, o).wait_recv()
            give(set_at, 3, o).wait_recv()
    for set_at in range(3):
        for o in everyone:
            for kind in (1, 2, 3):
                give(set_at, kind, o).wait_send()
        for o in offsets:
            spread(set_at, o).wait_send()
            grp_copy(set_at, o).wait_send()
    for v in [vec_core, vec_row] + vec_wa + vec_grp:
        v.wait_send()
    for r in reds:
        r.finish()
    fold.finish()
    swap_dq.finish()
    swap_kv.finish()


def run_closing(grp_count, wa_count, lens, q, qm, kv, km, o, lse, do, query, content, early, wide, vg):
    tok = query.shape[0]
    count = early.shape[0] + 3
    every = count + wide.shape[0]
    reach = min(grp_count - 1, (DOCLEN + PLANE * tok - 2) // (PLANE * tok))
    size = 512 // wa_count
    slab = size // grp_count
    low, full = jnp.bfloat16, jnp.float32
    shape = jax.ShapeDtypeStruct
    steps = wa_count + 2
    return pl.pallas_call(
        functools.partial(closing_kernel, grp_count, wa_count, reach, count),
        out_shape=(shape((tok, 512), low), shape((tok, 1024), low), shape((PLANE, every, size, 128), low),
                   shape(vg.shape, full)),
        in_specs=[SMEM] + [VMEM] * 9 + [ANY, ANY, VMEM],
        out_specs=(VMEM, VMEM, ANY, VMEM),
        scratch_shapes=back_scratch(tok, reach) + [
            pltpu.VMEM((count, PLANE, 512, 128), low), pltpu.VMEM((count, 2, 512, 128), low),
            pltpu.VMEM((max(1, wa_count - 1), count, 2, size, 128), low), pltpu.VMEM((count, size, 128), low),
            pltpu.VMEM((count, 2, 512, 128), low), pltpu.VMEM((count, 2, size, 128), low), pltpu.VMEM((every, size, 128), low),
            pltpu.VMEM((grp_count - 1, every, slab, 128), low), pltpu.VMEM((every, slab, 128), low),
            pltpu.VMEM((4,) + vg.shape, full), pltpu.VMEM((wa_count + 1,) + vg.shape, full),
            pltpu.VMEM((wa_count + grp_count,) + vg.shape, full),
            DMA((2, 2, reach, PLANE)), DMA((2, 2, 4)), DMA((early.shape[0],)), DMA,
            DMA((2, count, steps)), DMA((2, wa_count + grp_count)), DMA((2, 3, grp_count - 1)), DMA((2, 3, 4, grp_count))],
        cost_estimate=pl.CostEstimate(flops=75000000000, bytes_accessed=0, transcendentals=0),
        compiler_params=pltpu.CompilerParams(collective_id=9, has_side_effects=True, vmem_limit_bytes=60 << 20),
    )(lens, q, qm, kv, km, o, lse, do, query, content, early, wide, vg)


def centre_kernel(wa_count, vec_at, attended_ref, hidden_ref, cotangent_ref, out_mat_ref, expand_ref, shrink_ref, vec_ref,
                  layer_out, mixed_out, back_out, branch_out, do_out, grads_out, vg_out,
                  sendbuf, getbuf, dosend, doget, slopes, actives, grads, swap_sems, out_sems):
    tok = hidden_ref.shape[0]
    for p in range(PLANE):
        sendbuf[p] = attended_ref[p * tok : p * tok + tok, :].astype(jnp.bfloat16)
    greet(1, 1, groups=False, rows=False)
    swap = Swap(lambda p: sendbuf.at[p], lambda p: getbuf.at[p], swap_sems.at[0])
    swap.begin()
    row = lambda i: vector_row(vec_ref, wa_count, *vec_at[i])
    vg_out[...] = jnp.zeros_like(vg_out)
    for offset in range(4):
        swap.arrived(offset)
    mixed = flat_pairs(getbuf)
    mixed_out[...] = mixed
    value = hidden_ref[...] + matmul(mixed, out_mat_ref[...]) + row(7)
    hidden, normed_two, inverse_two = norm_forward(value, row(8), row(9))
    low = hidden.astype(jnp.bfloat16)
    expand_row = row(10)
    total = hidden + row(11)
    width = 512
    chunks = expand_ref.shape[1] // width
    for c in range(chunks):
        span = slice(c * width, c * width + width)
        u = matmul(low, expand_ref[:, span]) + expand_row[:, span]
        cumulative = 0.5 * (1.0 + lax.erf(u * ROOT_HALF))
        active = (u * cumulative).astype(jnp.bfloat16)
        actives[:, span] = active
        slopes[:, span] = cumulative + u * jnp.exp(-0.5 * u * u) * INV_ROOT_TWO_PI
        total = total + matmul(active, shrink_ref[span, :])
    out, normed_three, inverse_three = norm_forward(total, row(12), row(13))
    layer_out[...] = out
    cotangent = cotangent_ref[...].astype(jnp.float32)
    back, gain_grad, shift_grad = norm_backward(cotangent, normed_three, inverse_three, row(12))
    vg_out[0:1, :] = gain_grad.reshape(1, 512)
    vg_out[1:2, :] = shift_grad.reshape(1, 512)
    grad = back.astype(jnp.bfloat16)
    vg_out[2:3, :] = column_sum(grad).reshape(1, 512)
    incoming = back
    steps = []
    for c in range(chunks):
        span = slice(c * width, c * width + width)
        du = (dot(grad, shrink_ref[span, :], 1, 1) * slopes[:, span]).astype(jnp.bfloat16)
        vg_out[3 + c : 4 + c, :] = column_sum(du).reshape(1, 512)
        incoming = incoming + dot(du, expand_ref[:, span], 1, 1)
        steps.append(du)
    back, gain_grad, shift_grad = norm_backward(incoming, normed_two, inverse_two, row(8))
    back_out[...] = back
    branch = back.astype(jnp.bfloat16)
    branch_out[...] = branch
    do = dot(branch, out_mat_ref[...], 1, 1).astype(jnp.bfloat16)
    for p in range(PLANE):
        dosend[p] = do[:, p * 128 : p * 128 + 128]
    swap_do = Swap(lambda p: dosend.at[p], lambda p: doget.at[p], swap_sems.at[1])
    swap_do.begin()
    vg_out[7:8, :] = gain_grad.reshape(1, 512)
    vg_out[8:9, :] = shift_grad.reshape(1, 512)
    vg_out[9:10, :] = column_sum(branch).reshape(1, 512)
    size = 512 // wa_count
    saves = [pltpu.make_async_copy(grads.at[i], grads_out.at[i], out_sems.at[i]) for i in range(2 * chunks)]
    for c in range(chunks):
        span = slice(c * width, c * width + width)
        store_blocks(grads.at[c], dot(low, steps[c], 0, 0))
        saves[c].start()
        value = dot(actives[:, span], grad, 0, 0).astype(jnp.bfloat16)
        for piece in range(width // size):
            owner, index = divmod(c * (width // size) + piece, chunks)
            for column in range(PLANE):
                grads[chunks + index, column, owner * size : owner * size + size, :] = value[
                    piece * size : piece * size + size, column * 128 : column * 128 + 128]
    for c in range(chunks):
        saves[chunks + c].start()
    for offset in range(4):
        swap_do.arrived(offset)
    for p in range(PLANE):
        do_out[p * tok : p * tok + tok, :] = doget[p]
    for save in saves:
        save.wait()
    swap.finish()
    swap_do.finish()


def run_centre(wa_count, vec_at, attended, hidden, cotangent, out_mat, expand, shrink, vecs):
    tok = hidden.shape[0]
    low, full = jnp.bfloat16, jnp.float32
    shape = jax.ShapeDtypeStruct
    pairs = pltpu.VMEM((PLANE, tok, 128), low)
    wide = expand.shape[1]
    return pl.pallas_call(
        functools.partial(centre_kernel, wa_count, vec_at),
        out_shape=(shape((tok, 512), full), shape((tok, 512), low), shape((tok, 512), full), shape((tok, 512), low),
                   shape((PLANE * tok, 128), low), shape((2 * wide // 512, PLANE, 512, 128), low), shape((24, 512), full)),
        in_specs=[VMEM] * 7,
        out_specs=(VMEM,) * 5 + (ANY, VMEM),
        scratch_shapes=[pairs] * 4 + [pltpu.VMEM((tok, wide), full), pltpu.VMEM((tok, wide), low),
            pltpu.VMEM((2 * wide // 512, PLANE, 512, 128), low), DMA((2, 2, 4)), DMA((2 * wide // 512,))],
        compiler_params=pltpu.CompilerParams(collective_id=3, has_side_effects=True, vmem_limit_bytes=60 << 20),
    )(attended, hidden, cotangent, out_mat, expand, shrink, vecs)


def last_kernel(wa_count, shares, at_ref, late_ref, sums_ref, dq_ref, dkv_ref, back_ref, query_mat, key_mat, value_mat,
                query_out, content_out, expand_out, shrink_out, *outs):
    wide = expand_out.shape[1] // 512
    size = late_ref.shape[2]
    count = late_ref.shape[1] - 2 * wide
    for c in range(PLANE):
        span = slice(c * 128, c * 128 + 128)
        for i in range(count):
            outs[i][:, span] = late_ref[c, 2 * wide + i].astype(jnp.float32)
        for i in range(wide):
            expand_out[:, i * 512 + c * 128 : i * 512 + c * 128 + 128] = late_ref[c, i].astype(jnp.float32)
            shrink_out[i * size : i * size + size, span] = late_ref[c, wide + i].astype(jnp.float32)
    query_out[...] = back_ref[...] + dot(dq_ref[...], query_mat[...], 1, 1)
    content_out[...] = dot(dkv_ref[:, :512], key_mat[...], 1, 1) + dot(dkv_ref[:, 512:], value_mat[...], 1, 1)
    at = 0
    for i, share in enumerate(shares):
        used = share * wa_count // 512
        line = jnp.concatenate([sums_ref[at + r : at + r + 1, :] for r in range(used)], axis=1)
        at += used
        mine = line[:, :share]
        for w in range(1, wa_count):
            mine = jnp.where(at_ref[0] == w, line[:, w * share : w * share + share], mine)
        outs[count + i][...] = mine.reshape(share)


def run_last(wa_count, wide, shares, at, late, sums, dq, dkv, back, query_mat, key_mat, value_mat):
    full = jnp.float32
    shape = jax.ShapeDtypeStruct
    tok = dq.shape[0]
    out_shape = [shape((tok, 512), full), shape((tok, 512), full), shape((late.shape[2], wide), full),
                 shape((wide // wa_count, 512), full)]
    out_shape += [shape((late.shape[2], 512), full)] * (late.shape[1] - wide // 256) + [shape((s,), full) for s in shares]
    return pl.pallas_call(
        functools.partial(last_kernel, wa_count, shares),
        out_shape=tuple(out_shape),
        in_specs=[SMEM] + [VMEM] * 8,
        out_specs=tuple([VMEM] * len(out_shape)),
        compiler_params=pltpu.CompilerParams(vmem_limit_bytes=60 << 20),
    )(at, late, sums, dq, dkv, back, query_mat, key_mat, value_mat)


def shards(
    query_in,
    content_in,
    encoder_in,
    out_grad,
    document_lengths,
    key_ranks,
    query_limits,
    self_query_weight,
    self_query_bias,
    self_key_weight,
    self_value_weight,
    self_value_bias,
    self_out_weight,
    self_out_bias,
    norm_one_gain,
    norm_one_shift,
    cross_query_weight,
    cross_query_bias,
    cross_key_weight,
    cross_value_weight,
    cross_value_bias,
    cross_out_weight,
    cross_out_bias,
    norm_two_gain,
    norm_two_shift,
    expand_weight,
    expand_bias,
    shrink_weight,
    shrink_bias,
    norm_three_gain,
    norm_three_shift,
):
    grp_count = lax.axis_size("grp")
    lens = document_lengths


    wa_count = lax.axis_size("wa")
    vectors = (self_query_bias, self_value_bias, cross_value_bias, self_out_bias, norm_one_gain, norm_one_shift,
        cross_query_bias, cross_out_bias, norm_two_gain, norm_two_shift, expand_bias, shrink_bias, norm_three_gain,
        norm_three_shift)
    vec_at, at = [], 0
    for v in vectors:
        vec_at.append((at, v.shape[0]))
        at += v.shape[0] // min(128, v.shape[0])
    vec_at = tuple(vec_at)
    mats = (self_key_weight, self_value_weight, self_query_weight, cross_key_weight, cross_value_weight, self_out_weight,
        cross_query_weight, cross_out_weight)
    (self_key_matrix, self_value_mat, self_query_mat, cross_key_matrix, cross_value_mat, self_out_mat, cross_query_mat,
        cross_out_mat, expand_mat, shrink_mat, vec_all, pair_one, pair_two, kv_one, kv_two, self_keys, cross_keys, self_marks,
        cross_marks, attended_one, total_one, attended_two, total_two, hidden_one, normed_one, inverse_one, mixed_one) = \
        run_front(grp_count, wa_count, lens, key_ranks, query_limits, content_in[0], query_in[0], encoder_in[0], vectors,
            mats, (expand_weight, shrink_weight), vec_at)
    source = query_in[0]
    content_states = content_in[0]
    encoder_output = encoder_in[0]
    layer_out, mixed_two, back_two, branch_two, do_two, wide, lines = run_centre(
        wa_count, vec_at, attended_two, hidden_one, out_grad[0], cross_out_mat, expand_mat, shrink_mat, vec_all)
    do_one, back_one, kv_two_grad, early, lines, wide = run_turn(grp_count, wa_count, vec_at, lens, pair_two, cross_marks,
        kv_two, cross_keys, attended_two, total_two, do_two, back_two, normed_one, inverse_one, hidden_one, mixed_one,
        mixed_two, branch_two, encoder_output, cross_query_mat, self_out_mat, vec_all, lines, wide)
    key_two_low, value_two_low = kv_two_grad[:, :512], kv_two_grad[:, 512:]
    encoder_grad = right_product(key_two_low, cross_key_matrix) + right_product(value_two_low, cross_value_mat)
    query_one_low, kv_one_grad, late, sums = run_closing(grp_count, wa_count, lens, pair_one, self_marks, kv_one, self_keys,
        attended_one, total_one, do_one, source, content_states, early, wide, lines)
    shares = tuple(v.shape[0] for v in (norm_three_gain, norm_three_shift, shrink_bias, expand_bias, norm_two_gain,
        norm_two_shift, cross_out_bias, norm_one_gain, norm_one_shift, self_out_bias, cross_query_bias, cross_value_bias,
        self_query_bias, self_value_bias))
    query_grad, content_grad, expand_grad, shrink_grad, *rest = run_last(wa_count, expand_weight.shape[1], shares,
        lax.axis_index("wa")[None].astype(jnp.int32), late, sums, query_one_low, kv_one_grad, back_one, self_query_mat,
        self_key_matrix, self_value_mat)
    names = ("cross_out", "cross_query", "self_out", "cross_key", "cross_value", "self_query", "self_key", "self_value")
    mat = dict(zip(names, rest))
    names = ("gain_three", "shift_three", "shrink", "expand", "gain_two", "shift_two", "cross_out", "gain_one", "shift_one",
        "self_out", "cross_query", "cross_value", "self_query", "self_value")
    vec = dict(zip(names, rest[len(mat):]))
    grads = (mat["self_query"], vec["self_query"], mat["self_key"], mat["self_value"], vec["self_value"], mat["self_out"],
        vec["self_out"], vec["gain_one"], vec["shift_one"], mat["cross_query"], vec["cross_query"], mat["cross_key"],
        mat["cross_value"], vec["cross_value"], mat["cross_out"], vec["cross_out"], vec["gain_two"], vec["shift_two"],
        expand_grad, vec["expand"], shrink_grad, vec["shrink"], vec["gain_three"], vec["shift_three"])
    return (layer_out[None], query_grad[None], content_grad[None], encoder_grad[None]) + grads


def solution(mesh):
    ctx, wa = mesh.devices.shape
    mesh = Mesh(mesh.devices.reshape(ctx // PLANE, PLANE, wa), ("grp", "pln", "wa"))
    in_specs = (
        P("wa", ("grp", "pln"), None),
        P("wa", ("grp", "pln"), None),
        P("wa", ("grp", "pln"), None),
        P("wa", ("grp", "pln"), None),
        P("wa", None),
        P("wa", None),
        P("wa", None),
        P("wa", None),
        P("wa"),
        P("wa", None),
        P("wa", None),
        P("wa"),
        P("wa", None),
        P("wa"),
        P("wa"),
        P("wa"),
        P("wa", None),
        P("wa"),
        P("wa", None),
        P("wa", None),
        P("wa"),
        P("wa", None),
        P("wa"),
        P("wa"),
        P("wa"),
        P("wa", None),
        P("wa"),
        P("wa", None),
        P("wa"),
        P("wa"),
        P("wa"),
    )
    out_specs = (
        P("wa", ("grp", "pln"), None),
        P("wa", ("grp", "pln"), None),
        P("wa", ("grp", "pln"), None),
        P("wa", ("grp", "pln"), None),
        P("wa", None),
        P("wa"),
        P("wa", None),
        P("wa", None),
        P("wa"),
        P("wa", None),
        P("wa"),
        P("wa"),
        P("wa"),
        P("wa", None),
        P("wa"),
        P("wa", None),
        P("wa", None),
        P("wa"),
        P("wa", None),
        P("wa"),
        P("wa"),
        P("wa"),
        P("wa", None),
        P("wa"),
        P("wa", None),
        P("wa"),
        P("wa"),
        P("wa"),
    )
    return jax.shard_map(shards, mesh=mesh, in_specs=in_specs, out_specs=out_specs, check_vma=False)
```
